32 devices in a mesh: rep: 4 (over y, x), fsdp: 8 (over z, core).
Axes of the slice: x: 2, y: 2, z: 4, core: 2. Of those that a mesh axis runs over, the one named last changes fastest.
Arguments:
- global_views: bfloat16 [320, 14, 14, 1024], P(('rep', 'fsdp')), may hold values from -6 to 6
- local_views: bfloat16 [640, 6, 6, 1024], P(('rep', 'fsdp')), may hold values from -6 to 6
- live_images: int32 [32], P(('rep', 'fsdp')), may hold values from 1 to 5, as said below
- first_reduce: bfloat16 [1024, 256], P(None, 'fsdp'), may hold values from -0.1875 to 0.1875
- first_spatial: bfloat16 [2304, 256], P(None, 'fsdp'), may hold values from -0.125 to 0.125
- first_expand: bfloat16 [256, 1024], P(None, 'fsdp'), may hold values from -0.375 to 0.375
- first_norms: bfloat16 [2, 1536], P(None, 'fsdp'), may hold values from 0.3984375 to 1.3984375
- second_reduce: bfloat16 [1024, 512], P(None, 'fsdp'), may hold values from -0.1875 to 0.1875
- second_spatial: bfloat16 [4608, 512], P(None, 'fsdp'), may hold values from -0.09375 to 0.09375
- second_expand: bfloat16 [512, 2048], P(None, 'fsdp'), may hold values from -0.25 to 0.25
- second_short: bfloat16 [1024, 2048], P(None, 'fsdp'), may hold values from -0.1875 to 0.1875
- second_norms: bfloat16 [2, 5120], P(None, 'fsdp'), may hold values from 0.3984375 to 1.3984375
- global_cotan: bfloat16 [320, 7, 7, 2048], P(('rep', 'fsdp')), may hold values from -6 to 6
- local_cotan: bfloat16 [640, 3, 3, 2048], P(('rep', 'fsdp')), may hold values from -6 to 6
Outputs:
- first_global: bfloat16 [320, 14, 14, 1024], P(('rep', 'fsdp'))
- first_local: bfloat16 [640, 6, 6, 1024], P(('rep', 'fsdp'))
- second_global: bfloat16 [320, 7, 7, 2048], P(('rep', 'fsdp'))
- second_local: bfloat16 [640, 3, 3, 2048], P(('rep', 'fsdp'))
- global_grad: float32 [320, 14, 14, 1024], P(('rep', 'fsdp'))
- local_grad: float32 [640, 6, 6, 1024], P(('rep', 'fsdp'))
- grad_first_reduce: float32 [1024, 256], P(None, 'fsdp')
- grad_first_spatial: float32 [2304, 256], P(None, 'fsdp')
- grad_first_expand: float32 [256, 1024], P(None, 'fsdp')
- grad_first_norms: float32 [2, 1536], P(None, 'fsdp')
- grad_second_reduce: float32 [1024, 512], P(None, 'fsdp')
- grad_second_spatial: float32 [4608, 512], P(None, 'fsdp')
- grad_second_expand: float32 [512, 2048], P(None, 'fsdp')
- grad_second_short: float32 [1024, 2048], P(None, 'fsdp')
- grad_second_norms: float32 [2, 5120], P(None, 'fsdp')
- pooled_std: float32 [], replicated
The draws below stay inside these ranges and needn't reach their ends.
Inputs may be any that keep to these rules, and one draw needn't show every extreme that they name: `live_images`: A device with n live images holds their 2 n global and 4 n local views in its first slots; some device holds 5 images.
All inputs are finite; a program needn't handle non-finite values.
Results may differ from the reference program's by a relative error of at most 0.025.
Values may be sent and summed in bfloat16 or wider, within the bound.
A program may use at most 320 MiB of HBM per device.

```python
import jax
import jax.numpy as jnp
from jax import lax

C_IN = 1024
MID1 = 256
MID2 = 512
C_OUT = 2048
IMG_CAP = 5
HG = 14
HL = 6
GOUT = 7
LOUT = 3
GVIEWS = 320
LVIEWS = 640
DEVICES = 32


def draw_live_images(key, part):
    key_counts, key_top = jax.random.split(jax.random.fold_in(key, 17))
    counts = jax.random.randint(key_counts, (DEVICES,), 1, IMG_CAP + 1)
    chosen = jax.random.randint(key_top, (), 0, DEVICES)
    return jnp.where(jnp.arange(DEVICES) == chosen, IMG_CAP, counts).astype(jnp.int32)


def levels(key, extent, cuts, smallest, high):
    level = 1.0
    for position, blocks in cuts:
        draws = jax.random.uniform(jax.random.fold_in(jax.random.fold_in(key, 6), position), (blocks,), jnp.float32, smallest / len(cuts), high / len(cuts))
        level = level * jnp.repeat(jnp.exp(draws), extent[position] // blocks).reshape((-1,) + (1,) * (len(extent) - 1 - position))
    return level


def scatter_about(stream_key, shape, width, bound, cuts=(), held_as=jnp.bfloat16):
    result = width * jax.random.normal(stream_key, shape, jnp.float32)
    if cuts:
        result = result * levels(stream_key, shape, cuts, -0.22, 0.18)
    return jnp.clip(result, -bound, bound).astype(held_as)


def setup_inputs(seed: int = 0) -> dict:
    streams_of = jax.random.split(jax.random.key(seed), 15)
    return {
        "global_views": scatter_about(streams_of[0], (GVIEWS, HG, HG, C_IN), 1.0, 6.0, ((0, 32),)),
        "local_views": scatter_about(streams_of[1], (LVIEWS, HL, HL, C_IN), 1.0, 6.0, ((0, 32),)),
        "live_images": draw_live_images(jax.random.fold_in(streams_of[14], 71), 0),
        "first_reduce": scatter_about(streams_of[3], (C_IN, MID1), C_IN ** -0.5, 0.1875, ((1, 8),)),
        "first_spatial": scatter_about(streams_of[4], (9 * MID1, MID1), (9 * MID1) ** -0.5, 0.125, ((1, 8),)),
        "first_expand": scatter_about(streams_of[5], (MID1, C_IN), MID1 ** -0.5, 0.375, ((1, 8),)),
        "first_norms": jnp.clip(0.3984375 + 1.0 * jax.random.uniform(streams_of[6], (2, 2 * MID1 + C_IN), jnp.float32) ** levels(streams_of[6], (2, 2 * MID1 + C_IN), ((1, 8),), -0.2, 0.2), 0.3984375, 1.3984375).astype(jnp.bfloat16),
        "second_reduce": scatter_about(streams_of[7], (C_IN, MID2), C_IN ** -0.5, 0.1875, ((1, 8),)),
        "second_spatial": scatter_about(streams_of[8], (9 * MID2, MID2), (9 * MID2) ** -0.5, 0.09375, ((1, 8),)),
        "second_expand": scatter_about(streams_of[9], (MID2, C_OUT), MID2 ** -0.5, 0.25, ((1, 8),)),
        "second_short": scatter_about(streams_of[10], (C_IN, C_OUT), C_IN ** -0.5, 0.1875, ((1, 8),)),
        "second_norms": jnp.clip(0.3984375 + 1.0 * jax.random.uniform(streams_of[11], (2, 2 * MID2 + 2 * C_OUT), jnp.float32) ** levels(streams_of[11], (2, 2 * MID2 + 2 * C_OUT), ((1, 8),), -0.2, 0.2), 0.3984375, 1.3984375).astype(jnp.bfloat16),
        "global_cotan": scatter_about(streams_of[12], (GVIEWS, GOUT, GOUT, C_OUT), 1.0, 6.0, ((0, 32),)),
        "local_cotan": scatter_about(streams_of[13], (LVIEWS, LOUT, LOUT, C_OUT), 1.0, 6.0, ((0, 32),)),
    }


EPSILON = 1e-05

@jax.custom_vjp
def low(v):
    return lax.optimization_barrier(v.astype(jnp.bfloat16)).astype(jnp.float32)

@jax.custom_vjp
def low_back(v):
    return v

def low_keep(v):
    return (low(v), None)

def low_pass(kept, grad):
    return (grad,)

def back_keep(v):
    return (v, None)

def back_low(kept, grad):
    return (low(grad),)
low.defvjp(low_keep, low_pass)
low_back.defvjp(back_keep, back_low)

def sigmoid_linear(values):
    return values * jax.nn.sigmoid(values)

def patches(feature, stride):
    padded = jnp.pad(feature, ((0, 0), (1, 1), (1, 1), (0, 0)))
    batch_views = feature.shape[0]
    out_rows = (feature.shape[1] - 1) // stride + 1
    out_cols = (feature.shape[2] - 1) // stride + 1
    pieces = []
    for shift_row in range(3):
        for shift_col in range(3):
            pieces.append(lax.slice(padded, (0, shift_row, shift_col, 0), (batch_views, shift_row + stride * (out_rows - 1) + 1, shift_col + stride * (out_cols - 1) + 1, feature.shape[3]), (1, stride, stride, 1)))
    return jnp.concatenate(pieces, axis=3)

def project_high(operand, weight):
    return jnp.einsum('vhwc,cd->vhwd', operand, weight, precision=lax.Precision.HIGHEST)

def batch_norm(conv_out, norm_params, live_mask, view_total):
    weighted = conv_out * live_mask[:, None, None, None]
    pixels = view_total * (conv_out.shape[1] * conv_out.shape[2])
    center = lax.optimization_barrier(jnp.sum(weighted, axis=(0, 1, 2))) / pixels
    spread = lax.optimization_barrier(jnp.sum(weighted * conv_out, axis=(0, 1, 2))) / pixels - center * center
    scaled = (conv_out - center) * lax.rsqrt(spread + EPSILON)
    return norm_params[0] * scaled + norm_params[1]

def single_class(source, live_mask, view_total, params):
    first_reduce, first_spatial, first_expand, first_norms, second_reduce, second_spatial, second_expand, second_short, second_norms = params
    conv_a = low_back(project_high(source, first_reduce))
    act_a = low(sigmoid_linear(batch_norm(conv_a, first_norms[:, :MID1], live_mask, view_total)))
    conv_b = low_back(project_high(patches(act_a, 1), first_spatial))
    act_b = low(sigmoid_linear(batch_norm(conv_b, first_norms[:, MID1:2 * MID1], live_mask, view_total)))
    conv_c = low_back(project_high(act_b, first_expand))
    hidden = sigmoid_linear(batch_norm(conv_c, first_norms[:, 2 * MID1:], live_mask, view_total) + source)
    hidden_low = low(hidden)
    conv_d = low_back(project_high(hidden_low, second_reduce))
    act_d = low(sigmoid_linear(batch_norm(conv_d, second_norms[:, :MID2], live_mask, view_total)))
    conv_e = low_back(project_high(patches(act_d, 2), second_spatial))
    act_e = low(sigmoid_linear(batch_norm(conv_e, second_norms[:, MID2:2 * MID2], live_mask, view_total)))
    conv_f = low_back(project_high(act_e, second_expand))
    conv_s = low_back(project_high(hidden_low[:, ::2, ::2, :], second_short))
    joined = batch_norm(conv_f, second_norms[:, 2 * MID2:2 * MID2 + C_OUT], live_mask, view_total) + batch_norm(conv_s, second_norms[:, 2 * MID2 + C_OUT:], live_mask, view_total)
    return (sigmoid_linear(joined) * live_mask[:, None, None, None], hidden)

def pooled_terms(block_out, live_mask):
    pooled = lax.optimization_barrier(jnp.mean(block_out, axis=(1, 2)))
    normed = pooled * lax.rsqrt(lax.optimization_barrier(jnp.mean(pooled * pooled, axis=1, keepdims=True)) + 1e-06)
    weighted = normed * live_mask[:, None]
    return (lax.optimization_barrier(jnp.sum(weighted, axis=0)), lax.optimization_barrier(jnp.sum(weighted * normed, axis=0)))

def reference(global_views, local_views, live_images, first_reduce, first_spatial, first_expand, first_norms, second_reduce, second_spatial, second_expand, second_short, second_norms, global_cotan, local_cotan):
    global_slots = jnp.arange(GVIEWS)
    global_owner = global_slots // (2 * IMG_CAP)
    global_mask = (global_slots % (2 * IMG_CAP) // 2 < live_images[global_owner]).astype(jnp.float32)
    local_slots = jnp.arange(LVIEWS)
    local_owner = local_slots // (4 * IMG_CAP)
    local_mask = (local_slots % (4 * IMG_CAP) // 4 < live_images[local_owner]).astype(jnp.float32)
    global_total = jnp.sum(global_mask)
    local_total = jnp.sum(local_mask)
    params = tuple((item.astype(jnp.float32) for item in (first_reduce, first_spatial, first_expand, first_norms, second_reduce, second_spatial, second_expand, second_short, second_norms)))

    def forward(glob_value, loc_value, *weights):
        out_glob, hid_glob = single_class(glob_value, global_mask, global_total, weights)
        out_loc, hid_loc = single_class(loc_value, local_mask, local_total, weights)
        return ((out_glob, out_loc), (hid_glob, hid_loc))
    outputs, pullback, hidden = jax.vjp(forward, global_views.astype(jnp.float32), local_views.astype(jnp.float32), *params, has_aux=True)
    gradients = pullback((global_cotan.astype(jnp.float32), local_cotan.astype(jnp.float32)))
    first_global = (hidden[0] * global_mask[:, None, None, None]).astype(jnp.bfloat16)
    first_local = (hidden[1] * local_mask[:, None, None, None]).astype(jnp.bfloat16)
    glob_first, glob_second = pooled_terms(outputs[0], global_mask)
    loc_first, loc_second = pooled_terms(outputs[1], local_mask)
    total_views = global_total + local_total
    center = (glob_first + loc_first) / total_views
    spread = (glob_second + loc_second) / total_views - center * center
    pooled_std = jnp.mean(jnp.sqrt(spread + 1e-06))
    return (first_global, first_local, outputs[0].astype(jnp.bfloat16), outputs[1].astype(jnp.bfloat16), gradients[0], gradients[1], gradients[2], gradients[3], gradients[4], gradients[5], gradients[6], gradients[7], gradients[8], gradients[9], gradients[10], pooled_std)
```

```python
import functools

import jax
import jax.numpy as jnp
from jax import lax
from jax.experimental import pallas as pl
from jax.experimental.pallas import tpu as pltpu
from jax.sharding import PartitionSpec as P

EPSILON = 1e-05
F32 = jnp.float32
BF16 = jnp.bfloat16
MESH = pl.DeviceIdType.MESH
CELLS = 16


def nt(left, right):
    return lax.dot_general(left, right, (((1,), (1,)), ((), ())), preferred_element_type=F32)


def nn(left, right):
    return lax.dot_general(left, right, (((1,), (0,)), ((), ())), preferred_element_type=F32)


def tn(left, right):
    return lax.dot_general(left, right, (((0,), (0,)), ((), ())), preferred_element_type=F32)


def sig(values):
    return 0.5 * jnp.tanh(0.5 * values) + 0.5


def silu(values):
    return values * sig(values)


def slope(values):
    gate = sig(values)
    held = values * gate
    return gate + held - held * gate


def lanes(tile, width):
    return jnp.concatenate([tile] * (width // tile.shape[1]), axis=1)


def fold(values):
    return jnp.sum(values.reshape(values.shape[0] // 8, 8, values.shape[1]), axis=0)


class Geometry:
    def __init__(self, views, side_global, side_local):
        self.slabs = views
        self.hg, self.hl = side_global, side_local
        assert side_global < CELLS and side_local < CELLS // 2
        self.rg, self.rl = side_global * CELLS, side_local * CELLS
        self.rows = self.rg + self.rl
        self.og, self.ol = (side_global - 1) // 2 + 1, (side_local - 1) // 2 + 1
        self.sg, self.sl = self.og * 8, self.ol * 8
        self.small = self.sg + self.sl
        self.total, self.small_total = self.slabs * self.rows, self.slabs * self.small
        self.halo = self.rows + 2 * CELLS
        self.halo_total = self.slabs * self.halo + CELLS
        self.chunk = 32
        assert self.rg % self.chunk == 0 and self.rl % self.chunk == 0 and self.small % 16 == 0

    def pieces(self, width):
        if width <= 256:
            return [(0, self.rg, 0), (self.rg, self.rl, 1)]
        step = self.chunk
        return [(start, step, 0) for start in range(0, self.rg, step)] + [
            (start, step, 1) for start in range(self.rg, self.rows, step)
        ]

    def mask(self, count, group, width):
        row = lax.broadcasted_iota(jnp.int32, (count, 128), 0)
        if group == 0:
            keep = (row & (CELLS - 1)) < self.hg
        else:
            keep = (row & (CELLS // 2 - 1)) < self.hl
        return lanes(keep.astype(F32), width)

    def small_mask(self, group, width):
        count = self.sl if group else self.sg
        row = lax.broadcasted_iota(jnp.int32, (count, 128), 0)
        keep = (row & 3) < self.ol if group else (row & 7) < self.og
        return lanes(keep.astype(F32), width)

    def small_pieces(self):
        return [(0, self.sg, 0), (self.sg, self.sl, 1)]


def alive(live, slab):
    return jnp.where(slab < 2 * live[0], 1.0, 0.0).astype(F32)


def cells(geo, count, group, width, small=False):
    images = lanes(count[8:9, 0:128], width)
    if small:
        return images * float(2 * geo.og * geo.og if group == 0 else 4 * geo.ol * geo.ol)
    return images * float(2 * geo.hg * geo.hg if group == 0 else 4 * geo.hl * geo.hl)


def member(sums, row, width):
    parts = width // sums.shape[1]
    return jnp.concatenate(
        [sums[row * parts + k : row * parts + k + 1, :] for k in range(parts)], axis=1
    )


def norm_terms(stats, norm, number, group):
    width = norm.shape[1]
    mean = member(stats, 2 * group, width) / number
    spread = member(stats, 2 * group + 1, width) / number - mean * mean
    inverse = lax.rsqrt(spread + EPSILON)
    scale = norm[0:1, :] * inverse
    return mean, inverse, scale, norm[1:2, :] - mean * scale


def back_terms(stats, norm, number, group, first, second_raw):
    mean, inverse, scale, unused = norm_terms(stats, norm, number, group)
    second = inverse * (second_raw - mean * first)
    by_value = -scale * inverse * (second / number)
    constant = -scale * (first / number) - by_value * mean
    return scale, by_value, constant, second


def forward_terms(geo, count, stats, norm, width, small=False):
    return [
        norm_terms(stats, norm, cells(geo, count, group, width, small), group)[2:]
        for group in range(2)
    ]


def backward_terms(geo, count, stats, norm, sums, out, width, small=False, rows=((0, 1), (2, 3))):
    terms = []
    seconds = []
    for group in range(2):
        number = cells(geo, count, group, width, small)
        first = member(sums, rows[group][0], width)
        raw = member(sums, rows[group][1], width)
        scale, by_value, constant, second = back_terms(stats, norm, number, group, first, raw)
        terms.append((scale, by_value, constant))
        seconds.append((second, first))
    out[...] = jnp.zeros(out.shape, F32)
    out[0:1, :] = seconds[0][0] + seconds[1][0]
    out[1:2, :] = seconds[0][1] + seconds[1][1]
    return terms


def finish(stats, acc, members, begin=0):
    part = stats.shape[1]
    parts = acc.shape[2] // part
    for row in range(members):
        total = jnp.sum(acc[begin + row], axis=0, keepdims=True)
        for k in range(parts):
            stats[row * parts + k : row * parts + k + 1, :] = total[:, k * part : (k + 1) * part]


def put(store, place, values):
    for k in range(store.shape[0]):
        store[k, place, :] = values[:, k * 128 : (k + 1) * 128]


def take(store, place):
    return jnp.concatenate([store[k, place, :] for k in range(store.shape[0])], axis=1)


def put_pieces(pieces, first, values, begin=0):
    cores, chips, reps, size = pieces.shape[:4]
    cols = slice(begin, begin + values.shape[1])
    for k in range(values.shape[0] // size):
        index = first // size + k
        shard, rep = index // reps, index % reps
        part = values[k * size : (k + 1) * size]
        pieces[shard % cores, shard // cores, rep, :, cols] = part.astype(BF16)


def loop(count, step):
    def one(index, carry):
        step(index)
        return carry

    lax.fori_loop(0, count, one, 0)


def at(index, size):
    return pl.ds(pl.multiple_of(index * size, size), size)


def stage_a(geo, net, live, xg, xl, packed, conv, acc, weight, own_g, own_l, arrive):
    loads = (
        pltpu.make_async_copy(xg, own_g, arrive.at[0]),
        pltpu.make_async_copy(xl, own_l, arrive.at[1]),
    )
    for load in loads:
        load.start()
    net.open()
    acc[...] = jnp.zeros(acc.shape, F32)
    blank = jnp.zeros((CELLS, packed.shape[1]), BF16)
    half = CELLS // 2
    for load in loads:
        load.wait()

    def pack(s):
        base = s * geo.rows
        keep = alive(live, s).astype(BF16)
        for i in range(geo.hg):
            start = pl.multiple_of(base + i * CELLS, CELLS)
            packed[pl.ds(start, CELLS), :] = blank
            packed[pl.ds(start, geo.hg), :] = own_g[s, i] * keep
        for i in range(geo.hl):
            start = pl.multiple_of(base + geo.rg + i * CELLS, CELLS)
            packed[pl.ds(start, CELLS), :] = blank
            for side in range(2):
                place = pl.multiple_of(start + side * half, half)
                packed[pl.ds(place, geo.hl), :] = own_l[2 * s + side, i] * keep

    third = geo.slabs // 3
    loop(third, pack)
    net.turn(1)
    loop(third, lambda s: pack(s + third))
    net.turn(2)
    loop(geo.slabs - 2 * third, lambda s: pack(s + 2 * third))
    net.turn(3)
    gathered = net.job_out(2)
    weight[...] = gathered[...].astype(F32).reshape(weight.shape).astype(BF16)

    def slab(s):
        result = nt(packed[at(s, geo.rows), :], weight[...])
        conv[at(s, geo.rows), :] = result.astype(BF16)
        for start, size, group in geo.pieces(256):
            piece = result[start : start + size]
            acc[2 * group] += fold(piece)
            acc[2 * group + 1] += fold(piece * piece)

    loop(geo.slabs, slab)
    finish(net.own, acc, 4)
    net.own[8:16, :] = jnp.full((8, net.own.shape[1]), live[0], jnp.int32).astype(F32)
    net.begin()
    net.turn(4)
    net.middle()
    net.turn(5)
    net.end()


def spread_taps(geo, store, s, values, reverse):
    width = values[0].shape[1]
    for group in range(2):
        rows = values[group]
        size = rows.shape[0]
        start = pl.multiple_of(s * geo.halo + CELLS + group * (geo.rg + CELLS), CELLS)
        before = pltpu.roll(rows, 1, 0)
        after = pltpu.roll(rows, size - 1, 0)
        order = (after, rows, before) if reverse else (before, rows, after)
        for tap in range(3):
            store[pl.ds(start, size), tap * width : (tap + 1) * width] = order[tap].astype(BF16)


def clear_halo(geo, store):
    blank = jnp.zeros((CELLS, store.shape[1]), BF16)

    def slab(s):
        store[pl.ds(pl.multiple_of(s * geo.halo, CELLS), CELLS), :] = blank
        store[pl.ds(pl.multiple_of(s * geo.halo + CELLS + geo.rg, CELLS), CELLS), :] = blank

    loop(geo.slabs, slab)
    store[geo.slabs * geo.halo : geo.slabs * geo.halo + CELLS, :] = blank


def activate(geo, live, conv, s, terms):
    values = []
    width = conv.shape[1]
    keep = alive(live, s)
    for group in range(2):
        start, size = (geo.rg, geo.rl) if group else (0, geo.rg)
        rows = conv[pl.ds(pl.multiple_of(s * geo.rows + start, CELLS), size), :].astype(F32)
        scale, shift = terms[group]
        values.append(silu(rows * scale + shift) * (geo.mask(size, group, width) * keep))
    return values


def stage_b(geo, net, live, count, za, stats_a, norm, weight, conv, taps, acc):
    net.open()
    acc[...] = jnp.zeros(acc.shape, F32)
    width = za.shape[1]
    terms = forward_terms(geo, count, stats_a, norm, width)
    clear_halo(geo, taps)
    loop(
        geo.slabs,
        lambda s: spread_taps(geo, taps, s, activate(geo, live, za, s, terms), False),
    )
    net.turn(1)
    span = geo.halo - CELLS

    def slab(s):
        result = None
        for dy in range(3):
            rows = taps[pl.ds(pl.multiple_of(s * geo.halo + dy * CELLS, CELLS), span), :]
            term = nt(rows, weight[:, dy * 3 * width : (dy + 1) * 3 * width])
            result = term if result is None else result + term
        keep = alive(live, s)
        for group, (begin, size) in enumerate(((0, geo.rg), (geo.rg + CELLS, geo.rl))):
            piece = result[begin : begin + size]
            start = pl.multiple_of(s * geo.rows + group * geo.rg, CELLS)
            conv[pl.ds(start, size), :] = piece.astype(BF16)
            piece = piece * (geo.mask(size, group, width) * keep)
            acc[2 * group] += fold(piece)
            acc[2 * group + 1] += fold(piece * piece)

    loop(geo.slabs, slab)
    finish(net.own, acc, 4)
    net.run()


def stage_c(geo, net, live, count, zb, stats_b, norm, weight, conv, act, acc):
    net.open()
    acc[...] = jnp.zeros(acc.shape, F32)
    terms = forward_terms(geo, count, stats_b, norm, zb.shape[1])
    step = 256

    def slab(s):
        values = activate(geo, live, zb, s, terms)
        act[0 : geo.rg, :] = values[0].astype(BF16)
        act[geo.rg : geo.rows, :] = values[1].astype(BF16)
        for c in range(0, weight.shape[0], step):
            result = nt(act[...], weight[c : c + step, :])
            conv[at(s, geo.rows), c : c + step] = result.astype(BF16)
            for start, size, group in geo.pieces(256):
                piece = result[start : start + size]
                acc[2 * group, :, c : c + step] += fold(piece)
                acc[2 * group + 1, :, c : c + step] += fold(piece * piece)

    loop(geo.slabs, slab)
    finish(net.own, acc, 4)
    net.run()


def even_rows(geo):
    return [2 * i * CELLS for i in range(geo.og)] + [
        geo.rg + 2 * i * CELLS for i in range(geo.ol)
    ]


def stage_d(
    geo, net, live, count, zc, stats_c, norm, packed, weight, short, hid, outg, outl, conv, conv_s,
    sub, stats_s, full, acc, acc_s,
):
    net.open()
    acc[...] = jnp.zeros(acc.shape, F32)
    acc_s[...] = jnp.zeros(acc_s.shape, F32)
    width = zc.shape[1]
    terms = forward_terms(geo, count, stats_c, norm, width)

    def slab(s):
        keep = alive(live, s)
        for start, size, group in geo.pieces(width):
            rows = pl.ds(pl.multiple_of(s * geo.rows + start, CELLS), size)
            scale, shift = terms[group]
            joined = zc[rows, :].astype(F32) * scale + shift + packed[rows, :].astype(F32)
            value = silu(joined) * (geo.mask(size, group, width) * keep)
            put(full, pl.ds(start, size), value)
            low = value.astype(BF16)
            hid[rows, :] = low
            for k in range(size // CELLS):
                i = (start - group * geo.rg) // CELLS + k
                if group == 0:
                    outg[s, i] = low[k * CELLS : k * CELLS + geo.hg]
                else:
                    for side in range(2):
                        begin = k * CELLS + side * CELLS // 2
                        outl[2 * s + side, i] = low[begin : begin + geo.hl]
        picked = [take(full, pl.ds(start, 8, stride=2)) for start in even_rows(geo)]
        sub[at(s, geo.small), :] = jnp.concatenate(picked, axis=0).astype(BF16)
        result = nt(hid[at(s, geo.rows), :], weight[...])
        conv[at(s, geo.rows), :] = result.astype(BF16)
        for start, size, group in geo.pieces(256):
            piece = result[start : start + size]
            acc[2 * group] += fold(piece)
            acc[2 * group + 1] += fold(piece * piece)

    loop(geo.slabs, slab)
    finish(net.own, acc, 4)
    net.begin()
    half = short.shape[0] // 2
    small_product(geo, sub, short, conv_s, acc_s, 0, half)
    net.middle()
    small_product(geo, sub, short, conv_s, acc_s, half, 2 * half)
    finish(stats_s, acc_s, 4)
    net.end()


def small_product(geo, left, weight, conv, acc, first, last):
    step = 256
    for c in range(first, last, step):
        result = nt(left[...], weight[c : c + step, :])
        conv[:, c : c + step] = result.astype(BF16)
        for s in range(geo.slabs):
            for start, size, group in geo.small_pieces():
                piece = result[s * geo.small + start : s * geo.small + start + size]
                acc[2 * group, :, c : c + step] += fold(piece)
                acc[2 * group + 1, :, c : c + step] += fold(piece * piece)


def gather_taps(geo, live, zd, terms, full, taps):
    width = zd.shape[1]
    blank = jnp.zeros((8, width), F32)
    full[:, 0:CELLS, :] = jnp.zeros((width // 128, CELLS, 128), F32)
    full[:, CELLS + geo.rg : 2 * CELLS + geo.rg, :] = jnp.zeros((width // 128, CELLS, 128), F32)

    def slab(s):
        keep = alive(live, s)
        for start, size, group in geo.pieces(width):
            rows = pl.ds(pl.multiple_of(s * geo.rows + start, CELLS), size)
            scale, shift = terms[group]
            value = silu(zd[rows, :].astype(F32) * scale + shift)
            begin = CELLS + start + group * CELLS
            put(full, pl.ds(begin, size), value * (geo.mask(size, group, width) * keep))
        for dy in range(3):
            for dx in range(3):
                picked = []
                for group in range(2):
                    for i in range(geo.ol if group else geo.og):
                        line = 2 * i + dy - 1
                        if line < 0:
                            picked.append(blank)
                            continue
                        begin = CELLS + group * (geo.rg + CELLS) + line * CELLS + dx - 1
                        picked.append(take(full, pl.ds(begin, 8, stride=2)))
                tap = dy * 3 + dx
                taps[at(s, geo.small), tap * width : (tap + 1) * width] = jnp.concatenate(
                    picked, axis=0
                ).astype(BF16)

    loop(geo.slabs, slab)


def stage_e(geo, net, live, count, zd, stats_d, norm, weight, conv, full, taps, acc):
    net.open()
    net.side.begin()
    acc[...] = jnp.zeros(acc.shape, F32)
    terms = forward_terms(geo, count, stats_d, norm, zd.shape[1])
    gather_taps(geo, live, zd, terms, full, taps)
    net.side.middle()
    step = 256
    for c in range(0, weight.shape[0], step):
        result = nt(taps[...], weight[c : c + step, :])
        conv[:, c : c + step] = result.astype(BF16)
        for s in range(geo.slabs):
            keep = alive(live, s)
            for start, size, group in geo.small_pieces():
                piece = result[s * geo.small + start : s * geo.small + start + size]
                piece = piece * (geo.small_mask(group, step) * keep)
                acc[2 * group, :, c : c + step] += fold(piece)
                acc[2 * group + 1, :, c : c + step] += fold(piece * piece)
    net.side.end()
    finish(net.own, acc, 4)
    net.run()


def stage_f(geo, net, live, count, ze, stats_e, norm, weight, act, conv, acc):
    acc[...] = jnp.zeros(acc.shape, F32)
    width = ze.shape[1]
    terms = forward_terms(geo, count, stats_e, norm, width, True)

    def slab(s):
        keep = alive(live, s)
        rows = ze[at(s, geo.small), :].astype(F32)
        parts = []
        for start, size, group in geo.small_pieces():
            scale, shift = terms[group]
            value = silu(rows[start : start + size] * scale + shift)
            parts.append(value * (geo.small_mask(group, width) * keep))
        act[at(s, geo.small), :] = jnp.concatenate(parts, axis=0).astype(BF16)

    loop(geo.slabs, slab)
    small_product(geo, act, weight, conv, acc, 0, weight.shape[0])
    finish(net.own, acc, 4)
    net.run()


def stage_out(
    geo, net, live, count, zf, zs, stats_f, stats_s, norm_f, norm_s, cotg, cotl, outg, outl, grad,
    pooled_sums, pool, cot, acc,
):
    acc[...] = jnp.zeros(acc.shape, F32)
    cot[...] = jnp.zeros(cot.shape, F32)
    pool[...] = jnp.zeros(pool.shape, F32)
    width = zf.shape[1]
    step = 512
    terms_f = forward_terms(geo, count, stats_f, norm_f, width, True)
    terms_s = forward_terms(geo, count, stats_s, norm_s, width, True)

    def slab(s):
        keep = alive(live, s)
        for c in range(0, width, step):
            cols = slice(c, c + step)
            for i in range(geo.og):
                cot[i * 8 : i * 8 + geo.og, :] = cotg[s, i, :, cols].astype(F32)
            for i in range(geo.ol):
                for side in range(2):
                    begin = geo.sg + i * 8 + side * 4
                    cot[begin : begin + geo.ol, :] = cotl[2 * s + side, i, :, cols].astype(F32)
            rows_f = zf[at(s, geo.small), cols].astype(F32)
            rows_s = zs[at(s, geo.small), cols].astype(F32)
            grads = []
            for start, size, group in geo.small_pieces():
                part = slice(start, start + size)
                vf, vs = rows_f[part], rows_s[part]
                scale_f, shift_f = (item[:, cols] for item in terms_f[group])
                scale_s, shift_s = (item[:, cols] for item in terms_s[group])
                joined = vf * scale_f + vs * scale_s + (shift_f + shift_s)
                mask = geo.small_mask(group, step) * keep
                gate = sig(joined)
                held = joined * gate
                value = held * mask
                low = value.astype(BF16)
                dy = cot[part, :] * ((gate + held - held * gate) * mask)
                grads.append(dy)
                acc[3 * group, :, cols] += fold(dy)
                acc[3 * group + 1, :, cols] += fold(dy * vf)
                acc[3 * group + 2, :, cols] += fold(dy * vs)
                summed = fold(value)
                if group == 0:
                    for i in range(geo.og):
                        outg[s, i, :, cols] = value[i * 8 : i * 8 + geo.og].astype(BF16)
                    pool[s, 0:1, cols] = jnp.sum(summed, axis=0, keepdims=True) * (
                        1.0 / (geo.og * geo.og)
                    )
                else:
                    row = lax.broadcasted_iota(jnp.int32, (8, step), 0)
                    for side in range(2):
                        own = jnp.where((row >= 4) == (side == 1), summed, 0.0)
                        pool[s, 1 + side : 2 + side, cols] = jnp.sum(
                            own, axis=0, keepdims=True
                        ) * (1.0 / (geo.ol * geo.ol))
                        for i in range(geo.ol):
                            begin = i * 8 + side * 4
                            outl[2 * s + side, i, :, cols] = value[begin : begin + geo.ol].astype(
                                BF16
                            )
            grad[at(s, geo.small), cols] = jnp.concatenate(grads, axis=0).astype(BF16)
        pooled = pool[s]
        square = jnp.mean(pooled * pooled, axis=1, keepdims=True)
        normed = pooled * lax.rsqrt(square + 1e-06)
        acc[6] += normed
        acc[7] += normed * normed

    loop(geo.slabs, slab)
    finish(net.own, acc, 6)
    net.begin()
    finish(pooled_sums, acc, 2, 6)
    net.middle()
    net.end()


def small_back(geo, live, s, grad, conv, terms, width, cols):
    keep = alive(live, s)
    rows_g = grad[at(s, geo.small), cols].astype(F32)
    rows_z = conv[at(s, geo.small), cols].astype(F32)
    parts = []
    for start, size, group in geo.small_pieces():
        scale, by_value, constant = (item[:, cols] for item in terms[group])
        part = slice(start, start + size)
        value = rows_g[part] * scale + rows_z[part] * by_value + constant
        parts.append(value * (geo.small_mask(group, width) * keep))
    return jnp.concatenate(parts, axis=0).astype(BF16)


def stage_f_back(
    geo, net, live, count, zf, zs, stats_f, stats_s, norm_f, norm_s, grad, sums, act, sub, weight,
    short, ze, stats_e, norm_e, wgrad_f, wgrad_s, back_sub, back_e, ngrad_f, ngrad_s, dzf, dzs, acc,
):
    acc[...] = jnp.zeros(acc.shape, F32)
    width = zf.shape[1]
    step = 512
    rows_f, rows_s = ((0, 1), (3, 4)), ((0, 2), (3, 5))
    terms_f = backward_terms(geo, count, stats_f, norm_f, sums, ngrad_f, width, True, rows_f)
    terms_s = backward_terms(geo, count, stats_s, norm_s, sums, ngrad_s, width, True, rows_s)

    def slab(s):
        for c in range(0, width, step):
            cols = slice(c, c + step)
            dzf[at(s, geo.small), cols] = small_back(geo, live, s, grad, zf, terms_f, step, cols)
            dzs[at(s, geo.small), cols] = small_back(geo, live, s, grad, zs, terms_s, step, cols)

    loop(geo.slabs, slab)
    net.open()
    net.side.begin()
    block = 256
    terms_e = forward_terms(geo, count, stats_e, norm_e, ze.shape[1], True)
    for c in range(0, act.shape[1], block):
        cols = slice(c, c + block)
        result = nn(dzf[...], weight[:, cols])
        for s in range(geo.slabs):
            keep = alive(live, s)
            rows = ze[s * geo.small : (s + 1) * geo.small, cols].astype(F32)
            parts = []
            for start, size, group in geo.small_pieces():
                scale, shift = (item[:, cols] for item in terms_e[group])
                value = rows[start : start + size]
                mask = geo.small_mask(group, block) * keep
                piece = result[s * geo.small + start : s * geo.small + start + size]
                piece = piece * (slope(value * scale + shift) * mask)
                parts.append(piece)
                acc[2 * group, :, cols] += fold(piece)
                acc[2 * group + 1, :, cols] += fold(piece * value)
            back_e[s * geo.small : (s + 1) * geo.small, cols] = jnp.concatenate(
                parts, axis=0
            ).astype(BF16)
    finish(net.own, acc, 4)
    net.begin()
    for c in range(0, width, block):
        cols = slice(c, c + block)
        put_pieces(wgrad_f, c, tn(dzf[:, cols], act[...]))
    net.side.middle()
    net.middle()
    for c in range(0, width, block):
        cols = slice(c, c + block)
        put_pieces(wgrad_s, c, tn(dzs[:, cols], sub[...]))
    for c in range(0, sub.shape[1], block):
        cols = slice(c, c + block)
        back_sub[:, cols] = nn(dzs[...], short[:, cols]).astype(BF16)
    net.side.end()
    net.end()


def stage_e_back(
    geo, net, live, count, ze, stats_e, norm_e, back_e, sums_e, zd, stats_d, norm_d, weight, wgrad,
    back_d, ngrad, full, taps, dze, moved, parity, acc,
):
    acc[...] = jnp.zeros(acc.shape, F32)
    width = ze.shape[1]
    terms_e = backward_terms(geo, count, stats_e, norm_e, sums_e, ngrad, width, True)
    terms_d = forward_terms(geo, count, stats_d, norm_d, width)
    gather_taps(geo, live, zd, terms_d, full, taps)
    net.open()

    def shift(s):
        value = small_back(geo, live, s, back_e, ze, terms_e, width, slice(0, width)).astype(F32)
        blank = jnp.zeros((8, width), F32)
        down = jnp.concatenate(
            [value[8 : geo.sg], blank, value[geo.sg + 8 :], blank], axis=0
        )
        size = geo.small
        dze[at(s, size), :] = value.astype(BF16)
        moved[0, at(s, size), :] = pltpu.roll(value, size - 1, 0).astype(BF16)
        moved[1, at(s, size), :] = down.astype(BF16)
        moved[2, at(s, size), :] = pltpu.roll(down, size - 1, 0).astype(BF16)

    loop(geo.slabs, shift)

    def tap(dy, dx):
        return weight[:, (dy * 3 + dx) * width : (dy * 3 + dx + 1) * width]

    def grads(first, last):
        for t in range(first, last):
            result = tn(dze[...], taps[:, t * width : (t + 1) * width])
            put_pieces(wgrad, 0, result, t * width)

    parity[0] = nn(dze[...], tap(1, 1))
    parity[1] = nn(dze[...], tap(1, 2)) + nn(moved[0], tap(1, 0))
    parity[2] = nn(dze[...], tap(2, 1)) + nn(moved[1], tap(0, 1))
    parity[3] = (
        nn(dze[...], tap(2, 2))
        + nn(moved[0], tap(2, 0))
        + nn(moved[1], tap(0, 2))
        + nn(moved[2], tap(0, 0))
    )

    def slab(s):
        keep = alive(live, s)
        for group in range(2):
            for i in range(geo.ol if group else geo.og):
                for a in range(2):
                    for b in range(2):
                        begin = group * geo.rg + (2 * i + a) * CELLS + b
                        source = s * geo.small + group * geo.sg + i * 8
                        part = parity[2 * a + b, pl.ds(pl.multiple_of(source, 8), 8), :]
                        put(full, pl.ds(begin, 8, stride=2), part)
        for start, size, group in geo.pieces(width):
            rows = pl.ds(pl.multiple_of(s * geo.rows + start, CELLS), size)
            scale, shift_d = terms_d[group]
            value = zd[rows, :].astype(F32)
            mask = geo.mask(size, group, width) * keep
            piece = take(full, pl.ds(start, size)) * (slope(value * scale + shift_d) * mask)
            back_d[rows, :] = piece.astype(BF16)
            acc[2 * group] += fold(piece)
            acc[2 * group + 1] += fold(piece * value)

    loop(geo.slabs, slab)
    finish(net.own, acc, 4)
    net.begin()
    grads(0, 4)
    net.middle()
    grads(4, 9)
    net.end()


def wide_back(geo, live, s, grad, conv, terms, low):
    width = conv.shape[1]
    keep = alive(live, s)
    for start, size, group in geo.pieces(width):
        rows = pl.ds(pl.multiple_of(s * geo.rows + start, CELLS), size)
        scale, by_value, constant = terms[group]
        value = grad[rows, :].astype(F32) * scale + conv[rows, :].astype(F32) * by_value + constant
        low[rows, :] = (value * (geo.mask(size, group, width) * keep)).astype(BF16)


def stage_d_back(
    geo, net, live, count, zd, stats_d, norm_d, back_d, sums_d, hid, packed, zc, stats_c, norm_c,
    back_sub, weight, wgrad, joined, ngrad, dzd, full, acc,
):
    acc[...] = jnp.zeros(acc.shape, F32)
    width = zc.shape[1]
    terms_d = backward_terms(geo, count, stats_d, norm_d, sums_d, ngrad, zd.shape[1])
    terms_c = forward_terms(geo, count, stats_c, norm_c, width)

    net.open()

    def slab(s):
        wide_back(geo, live, s, back_d, zd, terms_d, dzd)
        put(full, pl.ds(0, geo.rows), nn(dzd[at(s, geo.rows), :], weight[...]))
        extra = back_sub[at(s, geo.small), :].astype(F32)
        for k, start in enumerate(even_rows(geo)):
            place = pl.ds(start, 8, stride=2)
            put(full, place, take(full, place) + extra[k * 8 : k * 8 + 8])
        keep = alive(live, s)
        for start, size, group in geo.pieces(width):
            rows = pl.ds(pl.multiple_of(s * geo.rows + start, CELLS), size)
            scale, shift = terms_c[group]
            value = zc[rows, :].astype(F32)
            pre = value * scale + shift + packed[rows, :].astype(F32)
            mask = geo.mask(size, group, width) * keep
            piece = take(full, pl.ds(start, size)) * (slope(pre) * mask)
            joined[rows, :] = piece.astype(BF16)
            acc[2 * group] += fold(piece)
            acc[2 * group + 1] += fold(piece * value)

    loop(geo.slabs, slab)
    finish(net.own, acc, 4)
    block = 256
    net.begin()
    for c in range(0, dzd.shape[1], block):
        put_pieces(wgrad, c, tn(dzd[:, c : c + block], hid[...]))
        if c == 0:
            net.middle()
    net.end()


def stage_c_back(
    geo, net, live, count, zc, stats_c, norm_c, joined, sums_c, zb, stats_b, norm_b, weight, wgrad,
    back_b, ngrad, dzc, act, acc,
):
    acc[...] = jnp.zeros(acc.shape, F32)
    terms_c = backward_terms(geo, count, stats_c, norm_c, sums_c, ngrad, zc.shape[1])
    terms_b = forward_terms(geo, count, stats_b, norm_b, zb.shape[1])
    width = zb.shape[1]

    net.open()

    def slab(s):
        wide_back(geo, live, s, joined, zc, terms_c, dzc)
        result = nn(dzc[at(s, geo.rows), :], weight[...])
        keep = alive(live, s)
        for start, size, group in geo.pieces(width):
            rows = pl.ds(pl.multiple_of(s * geo.rows + start, CELLS), size)
            scale, shift = terms_b[group]
            value = zb[rows, :].astype(F32)
            pre = value * scale + shift
            mask = geo.mask(size, group, width) * keep
            gate = sig(pre)
            held = pre * gate
            act[rows, :] = (held * mask).astype(BF16)
            piece = result[start : start + size] * ((gate + held - held * gate) * mask)
            back_b[rows, :] = piece.astype(BF16)
            acc[2 * group] += fold(piece)
            acc[2 * group + 1] += fold(piece * value)

    loop(geo.slabs, slab)
    finish(net.own, acc, 4)
    net.begin()
    half = dzc.shape[1] // 2
    put_pieces(wgrad, 0, tn(dzc[:, 0:half], act[...]))
    net.middle()
    put_pieces(wgrad, half, tn(dzc[:, half:], act[...]))
    net.end()


def stage_b_back(
    geo, net, live, count, zb, stats_b, norm_b, back_b, sums_b, za, stats_a, norm_a, weight, wgrad,
    back_a, ngrad, taps, dtaps, stacked, total, acc,
):
    acc[...] = jnp.zeros(acc.shape, F32)
    width = za.shape[1]
    terms_b = backward_terms(geo, count, stats_b, norm_b, sums_b, ngrad, width)
    terms_a = forward_terms(geo, count, stats_a, norm_a, width)
    clear_halo(geo, taps)
    clear_halo(geo, dtaps)
    for t in range(9):
        stacked[t * width : (t + 1) * width, :] = weight[:, t * width : (t + 1) * width]

    def fill(s):
        spread_taps(geo, taps, s, activate(geo, live, za, s, terms_a), False)
        keep = alive(live, s)
        values = []
        for start, size, group in geo.pieces(width):
            rows = pl.ds(pl.multiple_of(s * geo.rows + start, CELLS), size)
            scale, by_value, constant = terms_b[group]
            value = back_b[rows, :].astype(F32) * scale + zb[rows, :].astype(F32) * by_value
            values.append((value + constant) * (geo.mask(size, group, width) * keep))
        spread_taps(geo, dtaps, s, values, True)

    loop(geo.slabs, fill)
    net.open()
    span = geo.halo - CELLS
    total[...] = jnp.zeros(total.shape, F32)

    def slab(s):
        result = None
        for dy in range(3):
            begin = pl.multiple_of(s * geo.halo + (2 - dy) * CELLS, CELLS)
            term = nn(
                dtaps[pl.ds(begin, span), :], stacked[dy * 3 * width : (dy + 1) * 3 * width, :]
            )
            result = term if result is None else result + term
        keep = alive(live, s)
        for group, (begin, size) in enumerate(((0, geo.rg), (geo.rg + CELLS, geo.rl))):
            rows = pl.ds(pl.multiple_of(s * geo.rows + group * geo.rg, CELLS), size)
            scale, shift = terms_a[group]
            value = za[rows, :].astype(F32)
            mask = geo.mask(size, group, width) * keep
            piece = result[begin : begin + size] * (slope(value * scale + shift) * mask)
            back_a[rows, :] = piece.astype(BF16)
            acc[2 * group] += fold(piece)
            acc[2 * group + 1] += fold(piece * value)

    def grads(s):
        own = dtaps[
            pl.ds(pl.multiple_of(s * geo.halo + CELLS, CELLS), span), width : 2 * width
        ]
        for dy in range(3):
            begin = pl.multiple_of(s * geo.halo + dy * CELLS, CELLS)
            total[:, dy * 3 * width : (dy + 1) * 3 * width] += tn(own, taps[pl.ds(begin, span), :])

    loop(geo.slabs, slab)
    finish(net.own, acc, 4)
    half = geo.slabs // 2
    net.begin()
    loop(half, grads)
    net.middle()
    loop(geo.slabs - half, lambda s: grads(s + half))
    put_pieces(wgrad, 0, total[...])
    net.end()


def stage_a_back(
    geo, net, live, count, za, stats_a, norm_a, back_a, sums_a, packed, joined, weight, wgrad, dxg, dxl,
    ngrad, dza,
):
    terms_a = backward_terms(geo, count, stats_a, norm_a, sums_a, ngrad, za.shape[1])

    net.open()

    def slab(s):
        wide_back(geo, live, s, back_a, za, terms_a, dza)
        result = nn(dza[at(s, geo.rows), :], weight[...])
        half = CELLS // 2
        for i in range(geo.hg):
            rows = pl.ds(pl.multiple_of(s * geo.rows + i * CELLS, CELLS), CELLS)
            value = result[i * CELLS : (i + 1) * CELLS] + joined[rows, :].astype(F32)
            dxg[s, i] = value[0 : geo.hg]
        for i in range(geo.hl):
            begin = geo.rg + i * CELLS
            rows = pl.ds(pl.multiple_of(s * geo.rows + begin, CELLS), CELLS)
            value = result[begin : begin + CELLS] + joined[rows, :].astype(F32)
            for side in range(2):
                dxl[2 * s + side, i] = value[side * half : side * half + geo.hl]

    loop(geo.slabs, slab)
    put_pieces(wgrad, 0, tn(dza[...], packed[...]))
    net.close()


class Sums:
    def __init__(self, reps, shards, own, out, first, second, sems):
        self.reps, self.shards = reps, shards
        self.own, self.out, self.first, self.second = own, out, first, second
        self.sems = sems
        self.rep, self.shard = lax.axis_index("rep"), lax.axis_index("fsdp")
        self.copies = []

    def begin(self):
        self.copies = []
        for hop in range(1, self.shards):
            copy = pltpu.make_async_remote_copy(
                self.own, self.first.at[self.shard], self.sems[0].at[hop], self.sems[1].at[hop],
                device_id={"fsdp": lax.rem(self.shard + hop, self.shards)}, device_id_type=MESH,
            )
            copy.start()
            self.copies.append(copy)
        self.first[self.shard] = self.own[...]

    def middle(self):
        for copy in self.copies:
            copy.wait()
        total = self.first[0]
        for k in range(1, self.shards):
            total = total + self.first[k]
        self.second[self.rep] = total
        self.copies = []
        for hop in range(1, self.reps):
            place = self.second.at[self.rep]
            copy = pltpu.make_async_remote_copy(
                place, place, self.sems[2].at[hop], self.sems[3].at[hop],
                device_id={"rep": lax.rem(self.rep + hop, self.reps)}, device_id_type=MESH,
            )
            copy.start()
            self.copies.append(copy)

    def end(self):
        for copy in self.copies:
            copy.wait()
        total = self.second[0]
        for k in range(1, self.reps):
            total = total + self.second[k]
        self.out[...] = total


class Net:
    def __init__(self, reps, shards, sums=None, side=None, jobs=(), plans=()):
        self.reps, self.shards = reps, shards
        self.sums, self.side, self.jobs, self.plans = sums, side, jobs, plans
        self.own = None if sums is None else sums.own
        self.opened = False
        self.started, self.finished = set(), set()

    def enter(self):
        rep, shard = lax.axis_index("rep"), lax.axis_index("fsdp")
        barrier = pltpu.get_barrier_semaphore()
        for hop in range(1, self.shards):
            other = {"fsdp": lax.rem(shard + hop, self.shards)}
            pl.semaphore_signal(barrier, inc=1, device_id=other, device_id_type=MESH)
        for hop in range(1, self.reps):
            other = {"rep": lax.rem(rep + hop, self.reps)}
            pl.semaphore_signal(barrier, inc=1, device_id=other, device_id_type=MESH)

    def open(self):
        if not self.opened:
            self.opened = True
            pl.semaphore_wait(pltpu.get_barrier_semaphore(), self.shards + self.reps - 2)
            self.turn(0)

    def turn(self, number):
        for k, (start, end) in enumerate(self.plans):
            if end == number:
                self.finish(k)
        for k, (start, end) in enumerate(self.plans):
            if start == number:
                self.started.add(k)
                self.jobs[k].start()

    def finish(self, k):
        assert k in self.started and k not in self.finished
        self.finished.add(k)
        self.jobs[k].finish()

    def job_out(self, k):
        return self.jobs[k].out

    def begin(self):
        self.open()
        self.sums.begin()

    def middle(self):
        self.sums.middle()

    def end(self):
        self.sums.end()
        self.close()

    def run(self):
        self.begin()
        self.middle()
        self.end()

    def close(self):
        for k in range(len(self.jobs)):
            if k not in self.finished:
                self.finish(k)


class Job:
    def __init__(self, kind, reps, shards, sources, out, held, send, recv):
        self.kind, self.source, self.out, self.held = kind, sources[0], out, held
        self.sources = sources
        self.send, self.recv = send, recv
        self.reps, self.chips = reps, shards // 2
        self.rep, shard = lax.axis_index("rep"), lax.axis_index("fsdp")
        self.chip, self.core = shard // 2, lax.rem(shard, 2)
        if kind in ("pair", "join"):
            self.members, self.me = 2, self.core
            self.address = lambda k: {"fsdp": self.chip * 2 + k}
        elif kind in ("line", "spread"):
            self.members, self.me = self.chips, self.chip
            self.address = lambda k: {"fsdp": k * 2 + self.core}
        elif kind == "all":
            self.members, self.me = shards, shard
            self.address = lambda k: {"fsdp": k}
        else:
            self.members, self.me = reps, self.rep
            self.address = lambda k: {"rep": k}

    def give(self, source, target, hop):
        other = lax.rem(self.me + hop, self.members)
        k = len(self.copies)
        if hop == 0:
            copy = pltpu.make_async_copy(source, target, self.send.at[k])
        else:
            copy = pltpu.make_async_remote_copy(
                source, target, self.send.at[k], self.recv.at[k],
                device_id=self.address(other), device_id_type=MESH,
            )
        copy.start()
        self.copies.append(copy)

    def start(self):
        self.copies = []
        kind, out = self.kind, self.out
        order = list(range(1, self.members)) + [0]
        if kind == "spread":
            for hop in order:
                self.give(self.source.at[self.rep], out.at[self.chip], hop)
        elif kind == "fan":
            for hop in order:
                for step in range(1, self.chips):
                    chip = lax.rem(self.chip + step, self.chips)
                    self.give(self.source.at[chip], out.at[chip, self.rep], hop)
            self.give(self.sources[1], out.at[self.chip], 0)
        elif kind == "join":
            for hop in order:
                for chip in range(self.chips):
                    self.give(self.source.at[chip], out.at[chip, self.core], hop)
        elif kind == "all":
            for hop in order:
                self.give(self.source, out.at[self.me], hop)
        else:
            for hop in order:
                other = lax.rem(self.me + hop, self.members)
                block = self.source if kind == "share" else self.source.at[other]
                self.give(block, self.held.at[self.me], hop)

    def finish(self):
        for copy in self.copies:
            copy.wait()
        held, out = self.held, self.out
        if held is None:
            return
        if self.kind == "share":
            for k in range(self.members):
                out[k] = held[k].astype(F32)
            return
        blocks = held.shape[1:-2]

        def one(index):
            place = (index // blocks[-1], lax.rem(index, blocks[-1])) if len(blocks) == 2 else (
                (index,) if blocks else ()
            )
            total = held[(0,) + place].astype(F32)
            for k in range(1, self.members):
                total = total + held[(k,) + place].astype(F32)
            out[place[::-1]] = total.astype(BF16)

        if blocks:
            loop(blocks[0] * (blocks[1] if len(blocks) == 2 else 1), one)
        else:
            total = held[0].astype(F32)
            for k in range(1, self.members):
                total = total + held[k].astype(F32)
            out[...] = total.astype(BF16)


def job_shapes(kind, reps, shards, shape):
    chips = shards // 2
    if kind == "spread":
        return None, (chips,) + shape[1:], chips
    if kind == "fan":
        return None, (chips, reps) + shape[1:], reps * (chips - 1) + 1
    if kind == "join":
        return None, (chips, 2) + shape[1:], 2 * chips
    if kind == "all":
        return None, (shards,) + shape, shards
    if kind == "pair":
        return shape, (shape[2], shape[1]) + shape[3:], 2
    if kind == "share":
        return (reps,) + shape, (reps,) + shape, reps
    return shape, shape[1:], shape[0]


VMEM_CAP = 60 << 20
FAR = ("spread", "fan")


def sums_scratch(reps, shards, shape, own):
    return [pltpu.VMEM(shape, F32)] * own + [
        pltpu.VMEM((shards,) + shape, F32),
        pltpu.VMEM((reps,) + shape, F32),
        pltpu.SemaphoreType.DMA((shards,)),
        pltpu.SemaphoreType.DMA((shards,)),
        pltpu.SemaphoreType.DMA((reps,)),
        pltpu.SemaphoreType.DMA((reps,)),
    ]


def run(name, kernel, geo, reps, shards, number, live, operands, results, scratch, sums, jobs, side, far=()):
    own_results = len(results)
    results = list(results)
    spaces = [pltpu.VMEM] * own_results
    extra = []
    arrays = []
    shapes = []
    for kind, sources, start, end in jobs:
        source = sources[0]
        if isinstance(source, int):
            shape, dtype = shapes[source]
        else:
            shape, dtype = source.shape, source.dtype
        arrays += [item for item in sources if not isinstance(item, int)]
        held, out, copies = job_shapes(kind, reps, shards, shape)
        shapes.append((out, F32 if kind == "share" else dtype))
        results.append(shapes[-1])
        spaces.append(pl.ANY if kind in FAR else pltpu.VMEM)
        extra += [] if held is None else [pltpu.VMEM(held, BF16)]
        extra += [pltpu.SemaphoreType.DMA((copies,))] * 2
    operands = tuple(operands)
    near = len(operands)
    if side is not None:
        operands += (side,)
        results.append((side.shape, F32))
        spaces.append(pltpu.VMEM)
        extra += sums_scratch(reps, shards, side.shape, 0)
    if sums is not None:
        results.append((sums, F32))
        spaces.append(pltpu.VMEM)
        extra += sums_scratch(reps, shards, sums, 1)
    inputs = 1 + len(operands)
    remote = bool(jobs) or sums is not None

    def whole(*refs):
        sources_in = list(refs[inputs : inputs + len(arrays)])
        first_out = inputs + len(arrays)
        outs = refs[first_out : first_out + len(results)]
        more = list(refs[first_out + len(results) :])
        made = []
        for k, (kind, sources, start, end) in enumerate(jobs):
            refs_of = [
                made[item].out if isinstance(item, int) else sources_in.pop(0) for item in sources
            ]
            held = more.pop(0) if job_shapes(kind, reps, shards, refs_of[0].shape)[0] else None
            made.append(
                Job(kind, reps, shards, refs_of, outs[own_results + k], held, more.pop(0), more.pop(0))
            )
        beside, main = None, None
        place = own_results + len(jobs)
        if side is not None:
            beside = Sums(reps, shards, refs[near + 1], outs[place], more[0], more[1], more[2:6])
            more = more[6:]
        if sums is not None:
            main = Sums(reps, shards, more[0], outs[-1], more[1], more[2], more[3:7])
            more = more[7:]
        net = None
        if remote:
            plans = [(start, end) for unused, unused_too, start, end in jobs]
            net = Net(reps, shards, main, beside, made, plans)
            net.enter()
        kernel(geo, net, *refs[: near + 1], *outs[:own_results], *more)

    params = {"collective_id": number, "has_side_effects": True} if remote else {}
    return pl.pallas_call(
        whole,
        out_shape=[jax.ShapeDtypeStruct(shape, dtype) for shape, dtype in results],
        in_specs=[pl.BlockSpec(memory_space=pltpu.SMEM)]
        + [pl.BlockSpec(memory_space=pl.ANY if k in far else pltpu.VMEM) for k in range(len(operands))]
        + [pl.BlockSpec(memory_space=pl.ANY)] * len(arrays),
        out_specs=[pl.BlockSpec(memory_space=space) for space in spaces],
        scratch_shapes=extra
        + [item if not isinstance(item, tuple) else pltpu.VMEM(*item) for item in scratch],
        compiler_params=pltpu.CompilerParams(vmem_limit_bytes=VMEM_CAP, **params),
        name=name,
    )(live, *operands, *arrays)


def tail_kernel(reps, shards, plan, *refs):
    count = len(plan)
    current = list(refs[:count])
    outs, more = refs[count : 2 * count], list(refs[2 * count :])
    net = Net(reps, shards)
    net.enter()
    net.open()
    for turn in range(max(len(kinds) for kinds in plan)):
        active = []
        for k, kinds in enumerate(plan):
            if turn >= len(kinds):
                continue
            held, send, recv = more[:3]
            more = more[3:]
            target = outs[k]
            if turn < len(kinds) - 1:
                target = more.pop(0)
            job = Job(kinds[turn], reps, shards, (current[k],), target, held, send, recv)
            job.start()
            active.append((k, job))
        for k, job in active:
            job.finish()
            current[k] = job.out


def run_tail(reps, shards, number, entries):
    shapes = [source.shape for unused, source in entries]
    plan = [kinds for kinds, unused in entries]
    scratch = []
    for turn in range(max(len(kinds) for kinds in plan)):
        for k, kinds in enumerate(plan):
            if turn >= len(kinds):
                continue
            held, out, copies = job_shapes(kinds[turn], reps, shards, shapes[k])
            scratch += [pltpu.VMEM(held, BF16)] + [pltpu.SemaphoreType.DMA((copies,))] * 2
            if turn < len(kinds) - 1:
                scratch.append(pltpu.VMEM(out, BF16))
            shapes[k] = out
    return pl.pallas_call(
        functools.partial(tail_kernel, reps, shards, plan),
        out_shape=[jax.ShapeDtypeStruct(shape, F32) for shape in shapes],
        in_specs=[pl.BlockSpec(memory_space=pl.ANY)] * len(entries),
        out_specs=[pl.BlockSpec(memory_space=pltpu.VMEM)] * len(entries),
        scratch_shapes=scratch,
        compiler_params=pltpu.CompilerParams(
            vmem_limit_bytes=VMEM_CAP, collective_id=number, has_side_effects=True
        ),
        name="tail",
    )(*[source for unused, source in entries])


def columns_of(rows):
    return rows.reshape(-1, rows.shape[-1]).T


def own_norms(first, second):
    flat = jnp.concatenate([first.reshape(-1), second.reshape(-1)]).astype(F32)
    size = -(-flat.shape[0] // 1024) * 1024
    return jnp.pad(flat, (0, size - flat.shape[0])).reshape(8, -1)


def all_norms(gathered, first, second):
    shards = gathered.shape[0]
    flat = gathered.reshape(shards, -1)
    split, last = first.size, first.size + second.size

    def whole(part):
        return part.reshape(shards, 2, -1).transpose(1, 0, 2).reshape(2, -1)

    return whole(flat[:, :split]), whole(flat[:, split:last])


def body(reps, shards, *arguments):
    (
        global_views, local_views, live, first_reduce, first_spatial, first_expand, first_norms,
        second_reduce, second_spatial, second_expand, second_short, second_norms, global_cotan,
        local_cotan,
    ) = arguments
    geo = Geometry(global_views.shape[0], global_views.shape[1], local_views.shape[1])
    assert local_views.shape[0] == 2 * geo.slabs
    channels = global_views.shape[3]
    ha, hb, hc, hd, he, hf, hs = (
        item.T.reshape(reps, -1, item.shape[0])
        for item in (
            first_reduce, first_spatial, first_expand, second_reduce, second_spatial,
            second_expand, second_short,
        )
    )
    mid_1, mid_2 = first_reduce.shape[1] * shards, second_reduce.shape[1] * shards
    wide = second_expand.shape[1] * shards

    def rows_of(gathered):
        return gathered.reshape(-1, gathered.shape[-1])

    big, small = geo.total, geo.small_total

    numbers = iter(range(100))

    def go(name, kernel, operands, results, scratch, width=None, members=4, jobs=(), side=None, far=()):
        parts = {4: 2, 6: 4, 8: 2}[members]
        sums = None if width is None else (members * parts, width // parts)
        return run(
            name, kernel, geo, reps, shards, next(numbers), live, operands, results, scratch, sums,
            jobs, side, far,
        )

    def pieces(weight):
        size = weight.shape[0] // (shards * reps)
        return ((2, shards // 2, reps, size, weight.shape[1]), BF16)

    def acc(width, members=4):
        return ((members, 8, width), F32)

    def stat(width):
        return ((8, width), F32)

    (
        packed, za, spread_a, fan_a, wa, spread_b, fan_b, wb, norms, spread_c, spread_d, spread_s, sa,
    ) = go(
        "stage_a", stage_a, (global_views, local_views),
        [((big, channels), BF16), ((big, mid_1), BF16)],
        [
            acc(mid_1), ((mid_1, channels), BF16), (global_views.shape, BF16),
            (local_views.shape, BF16), pltpu.SemaphoreType.DMA((2,)),
        ],
        mid_1, 8,
        jobs=(
            ("spread", (ha,), 0, 1), ("fan", (0, ha), 1, 2), ("join", (1,), 2, 3),
            ("spread", (hb,), 0, 2), ("fan", (3, hb), 2, 4), ("join", (4,), 4, 5),
            ("all", (own_norms(first_norms, second_norms),), 1, None),
            ("spread", (hc,), 2, None), ("spread", (hd,), 3, None), ("spread", (hs,), 3, None),
        ),
        far=(0, 1),
    )
    count = sa
    wa, wb = rows_of(wa), rows_of(wb)
    norms_1, norms_2 = all_norms(norms, first_norms, second_norms)
    na, nb, nc = norms_1[:, :mid_1], norms_1[:, mid_1 : 2 * mid_1], norms_1[:, 2 * mid_1 :]
    nd, ne = norms_2[:, :mid_2], norms_2[:, mid_2 : 2 * mid_2]
    nf, ns = norms_2[:, 2 * mid_2 : 2 * mid_2 + wide], norms_2[:, 2 * mid_2 + wide :]
    zb, fan_c, wc, fan_d, fan_s, spread_e, sb = go(
        "stage_b", stage_b, (count, za, sa, na, wb), [((big, mid_1), BF16)],
        [((geo.halo_total, 3 * mid_1), BF16), acc(mid_1)], mid_1,
        jobs=(
            ("fan", (spread_c, hc), 0, 1), ("join", (0,), 1, None), ("fan", (spread_d, hd), 0, None),
            ("fan", (spread_s, hs), 0, None), ("spread", (he,), 0, None),
        ),
    )
    wc = rows_of(wc)
    zc, wd, ws, spread_f, fan_e, sc = go(
        "stage_c", stage_c, (count, zb, sb, nb, wc), [((big, channels), BF16)],
        [((geo.rows, mid_1), BF16), acc(channels)], channels,
        jobs=(
            ("join", (fan_d,), 0, None), ("join", (fan_s,), 0, None), ("spread", (hf,), 0, None),
            ("fan", (spread_e, he), 0, None),
        ),
    )
    wd, ws = rows_of(wd), rows_of(ws)
    hid, first_g, first_l, zd, zs, sub, local_s, we, fan_f, sd = go(
        "stage_d", stage_d, (count, zc, sc, nc, packed, wd, ws),
        [
            ((big, channels), BF16), (global_views.shape, BF16), (local_views.shape, BF16),
            ((big, mid_2), BF16), ((small, wide), BF16), ((small, channels), BF16), stat(wide // 2),
        ],
        [((channels // 128, geo.rows, 128), F32), acc(mid_2), acc(wide)], mid_2,
        jobs=(("join", (fan_e,), 0, None), ("fan", (spread_f, hf), 0, None)),
    )
    we = rows_of(we)
    ze, wf, ss, se = go(
        "stage_e", stage_e, (count, zd, sd, nd, we), [((small, mid_2), BF16)],
        [((mid_2 // 128, geo.halo, 128), F32), ((small, 9 * mid_2), BF16), acc(mid_2)], mid_2,
        jobs=(("join", (fan_f,), 0, None),), side=local_s,
    )
    wf = rows_of(wf)
    act_e, zf, sf = go(
        "stage_f", stage_f, (count, ze, se, ne, wf),
        [((small, mid_2), BF16), ((small, wide), BF16)], [acc(wide)], wide,
    )
    second_g, second_l, grad, local_pool, so = go(
        "stage_out", stage_out,
        (count, zf, zs, sf, ss, nf, ns, global_cotan, local_cotan),
        [
            (global_cotan.shape, BF16), (local_cotan.shape, BF16), ((small, wide), BF16),
            stat(wide // 4),
        ],
        [((geo.slabs, 8, wide), F32), ((geo.small, 512), F32), acc(wide, 8)], wide, 6,
    )
    wgrad_f, wgrad_s, back_sub, back_e, ngrad_f, ngrad_s, pool, qe = go(
        "stage_f_back", stage_f_back,
        (count, zf, zs, sf, ss, nf, ns, grad, so, act_e, sub, wf, ws, ze, se, ne),
        [
            pieces(wf), pieces(ws), ((small, channels), BF16), ((small, mid_2), BF16),
            stat(wide), stat(wide),
        ],
        [((small, wide), BF16), ((small, wide), BF16), acc(mid_2)], mid_2, side=local_pool,
    )
    views = count[8, 0] * 6.0
    pool = pool.reshape(2, wide)
    center = pool[0] / views
    spread = pool[1] / views - center * center
    pooled_std = jnp.mean(jnp.sqrt(spread + 1e-06))
    wgrad_e, back_d, ngrad_e, pair_f, pair_s, qd = go(
        "stage_e_back", stage_e_back,
        (count, ze, se, ne, back_e, qe, zd, sd, nd, we),
        [pieces(we), ((big, mid_2), BF16), stat(mid_2)],
        [
            ((mid_2 // 128, geo.halo, 128), F32), ((small, 9 * mid_2), BF16),
            ((small, mid_2), BF16), ((3, small, mid_2), BF16), ((4, small, mid_2), F32),
            acc(mid_2),
        ],
        mid_2, jobs=(("pair", (wgrad_f,), 0, None), ("pair", (wgrad_s,), 0, None)),
    )
    wgrad_d, joined, ngrad_d, rep_f, rep_s, pair_e, qc = go(
        "stage_d_back", stage_d_back,
        (count, zd, sd, nd, back_d, qd, hid, packed, zc, sc, nc, back_sub, wd),
        [pieces(wd), ((big, channels), BF16), stat(mid_2)],
        [((big, mid_2), BF16), ((channels // 128, geo.rows, 128), F32), acc(channels)], channels,
        jobs=(("rep", (pair_f,), 0, None), ("rep", (pair_s,), 0, None), ("pair", (wgrad_e,), 0, None)),
    )
    wgrad_c, back_b, ngrad_c, line_f, line_s, rep_e, pair_d, qb = go(
        "stage_c_back", stage_c_back,
        (count, zc, sc, nc, joined, qc, zb, sb, nb, wc),
        [pieces(wc), ((big, mid_1), BF16), stat(channels)],
        [((big, channels), BF16), ((big, mid_1), BF16), acc(mid_1)], mid_1,
        jobs=(("line", (rep_f,), 0, None), ("line", (rep_s,), 0, None), ("rep", (pair_e,), 0, None), ("pair", (wgrad_d,), 0, None)),
    )
    wgrad_b, back_a, ngrad_b, out_f, out_s, line_e, rep_d, pair_c, qa = go(
        "stage_b_back", stage_b_back,
        (count, zb, sb, nb, back_b, qb, za, sa, na, wb),
        [pieces(wb), ((big, mid_1), BF16), stat(mid_1)],
        [
            ((geo.halo_total, 3 * mid_1), BF16), ((geo.halo_total, 3 * mid_1), BF16),
            ((9 * mid_1, mid_1), BF16), (wb.shape, F32), acc(mid_1),
        ],
        mid_1,
        jobs=(
            ("share", (line_f,), 0, None), ("share", (line_s,), 0, None), ("line", (rep_e,), 0, None), ("rep", (pair_d,), 0, None), ("pair", (wgrad_c,), 0, None),
        ),
    )
    wgrad_a, grad_g, grad_l, ngrad_a, out_e, line_d, rep_c, pair_b = go(
        "stage_a_back", stage_a_back,
        (count, za, sa, na, back_a, qa, packed, joined, wa),
        [pieces(wa), (global_views.shape, F32), (local_views.shape, F32), stat(mid_1)],
        [((big, mid_1), BF16)],
        jobs=(("share", (line_e,), 0, None), ("line", (rep_d,), 0, None), ("rep", (pair_c,), 0, None), ("pair", (wgrad_b,), 0, None)),
    )
    out_a, out_b, out_c, out_d = run_tail(
        reps, shards, next(numbers),
        (
            (("pair", "rep", "line", "share"), wgrad_a), (("rep", "line", "share"), pair_b),
            (("line", "share"), rep_c), (("share",), line_d),
        ),
    )
    shard = lax.axis_index("fsdp")

    def own_columns(parts, width):
        whole = jnp.concatenate([part[0:2] for part in parts], axis=1)
        return lax.dynamic_slice_in_dim(whole, shard * width, width, 1)

    return (
        first_g, first_l, second_g, second_l, grad_g, grad_l,
        columns_of(out_a), columns_of(out_b), columns_of(out_c),
        own_columns((ngrad_a, ngrad_b, ngrad_c), first_norms.shape[1]),
        columns_of(out_d), columns_of(out_e), columns_of(out_f), columns_of(out_s),
        own_columns((ngrad_d, ngrad_e, ngrad_f, ngrad_s), second_norms.shape[1]),
        pooled_std,
    )


def solution(mesh):
    views = P(("rep", "fsdp"), None, None, None)
    columns = P(None, "fsdp")
    return jax.shard_map(
        functools.partial(body, mesh.shape["rep"], mesh.shape["fsdp"]),
        mesh=mesh,
        in_specs=(views, views, P(("rep", "fsdp"))) + (columns,) * 9 + (views, views),
        out_specs=(views,) * 6 + (columns,) * 9 + (P(),),
        check_vma=False,
    )
```

```python
import functools

import jax
import jax.numpy as jnp
from jax import lax
from jax.experimental import pallas as pl
from jax.experimental.pallas import tpu as pltpu
from jax.sharding import PartitionSpec as P

EPSILON = 1e-05
F32 = jnp.float32
BF16 = jnp.bfloat16
MESH = pl.DeviceIdType.MESH
CELLS = 16


def nt(left, right):
    return lax.dot_general(left, right, (((1,), (1,)), ((), ())), preferred_element_type=F32)


def nn(left, right):
    return lax.dot_general(left, right, (((1,), (0,)), ((), ())), preferred_element_type=F32)


def tn(left, right):
    return lax.dot_general(left, right, (((0,), (0,)), ((), ())), preferred_element_type=F32)


def sig(values):
    return 0.5 * jnp.tanh(0.5 * values) + 0.5


def silu(values):
    return values * sig(values)


def slope(values):
    gate = sig(values)
    held = values * gate
    return gate + held - held * gate


def lanes(tile, width):
    return jnp.concatenate([tile] * (width // tile.shape[1]), axis=1)


def fold(values):
    return jnp.sum(values.reshape(values.shape[0] // 8, 8, values.shape[1]), axis=0)


class Geometry:
    def __init__(self, views, side_global, side_local):
        self.slabs = views
        self.hg, self.hl = side_global, side_local
        assert side_global < CELLS and side_local < CELLS // 2
        self.rg, self.rl = side_global * CELLS, side_local * CELLS
        self.rows = self.rg + self.rl
        self.og, self.ol = (side_global - 1) // 2 + 1, (side_local - 1) // 2 + 1
        self.sg, self.sl = self.og * 8, self.ol * 8
        self.small = self.sg + self.sl
        self.total, self.small_total = self.slabs * self.rows, self.slabs * self.small
        self.halo = self.rows + 2 * CELLS
        self.halo_total = self.slabs * self.halo + CELLS
        self.chunk = 32
        assert self.rg % self.chunk == 0 and self.rl % self.chunk == 0 and self.small % 16 == 0

    def pieces(self, width):
        if width <= 256:
            return [(0, self.rg, 0), (self.rg, self.rl, 1)]
        step = self.chunk
        return [(start, step, 0) for start in range(0, self.rg, step)] + [
            (start, step, 1) for start in range(self.rg, self.rows, step)
        ]

    def mask(self, count, group, width):
        row = lax.broadcasted_iota(jnp.int32, (count, 128), 0)
        if group == 0:
            keep = (row & (CELLS - 1)) < self.hg
        else:
            keep = (row & (CELLS // 2 - 1)) < self.hl
        return lanes(keep.astype(F32), width)

    def small_mask(self, group, width):
        count = self.sl if group else self.sg
        row = lax.broadcasted_iota(jnp.int32, (count, 128), 0)
        keep = (row & 3) < self.ol if group else (row & 7) < self.og
        return lanes(keep.astype(F32), width)

    def small_pieces(self):
        return [(0, self.sg, 0), (self.sg, self.sl, 1)]


def alive(live, slab):
    return jnp.where(slab < 2 * live[0], 1.0, 0.0).astype(F32)


def cells(geo, count, group, width, small=False):
    images = lanes(count[8:9, 0:128], width)
    if small:
        return images * float(2 * geo.og * geo.og if group == 0 else 4 * geo.ol * geo.ol)
    return images * float(2 * geo.hg * geo.hg if group == 0 else 4 * geo.hl * geo.hl)


def member(sums, row, width):
    parts = width // sums.shape[1]
    return jnp.concatenate(
        [sums[row * parts + k : row * parts + k + 1, :] for k in range(parts)], axis=1
    )


def norm_terms(stats, norm, number, group):
    width = norm.shape[1]
    mean = member(stats, 2 * group, width) / number
    spread = member(stats, 2 * group + 1, width) / number - mean * mean
    inverse = lax.rsqrt(spread + EPSILON)
    scale = norm[0:1, :] * inverse
    return mean, inverse, scale, norm[1:2, :] - mean * scale


def back_terms(stats, norm, number, group, first, second_raw):
    mean, inverse, scale, unused = norm_terms(stats, norm, number, group)
    second = inverse * (second_raw - mean * first)
    by_value = -scale * inverse * (second / number)
    constant = -scale * (first / number) - by_value * mean
    return scale, by_value, constant, second


def forward_terms(geo, count, stats, norm, width, small=False):
    return [
        norm_terms(stats, norm, cells(geo, count, group, width, small), group)[2:]
        for group in range(2)
    ]


def backward_terms(geo, count, stats, norm, sums, out, width, small=False, rows=((0, 1), (2, 3))):
    terms = []
    seconds = []
    for group in range(2):
        number = cells(geo, count, group, width, small)
        first = member(sums, rows[group][0], width)
        raw = member(sums, rows[group][1], width)
        scale, by_value, constant, second = back_terms(stats, norm, number, group, first, raw)
        terms.append((scale, by_value, constant))
        seconds.append((second, first))
    out[0:1, :] = seconds[0][0] + seconds[1][0]
    out[1:2, :] = seconds[0][1] + seconds[1][1]
    return terms


def finish(stats, acc, members, begin=0):
    part = stats.shape[1]
    parts = acc.shape[2] // part
    for row in range(members):
        total = jnp.sum(acc[begin + row], axis=0, keepdims=True)
        for k in range(parts):
            stats[row * parts + k : row * parts + k + 1, :] = total[:, k * part : (k + 1) * part]


def put(store, place, values):
    for k in range(store.shape[0]):
        store[k, place, :] = values[:, k * 128 : (k + 1) * 128]


def take(store, place):
    return jnp.concatenate([store[k, place, :] for k in range(store.shape[0])], axis=1)


def put_pieces(pieces, first, values, begin=0):
    cores, chips, reps, size = pieces.shape[:4]
    cols = slice(begin, begin + values.shape[1])
    for k in range(values.shape[0] // size):
        index = first // size + k
        shard, rep = index // reps, index % reps
        part = values[k * size : (k + 1) * size]
        pieces[shard % cores, shard // cores, rep, :, cols] = part.astype(BF16)


def loop(count, step):
    def one(index, carry):
        step(index)
        return carry

    lax.fori_loop(0, count, one, 0)


def at(index, size):
    return pl.ds(pl.multiple_of(index * size, size), size)


def stage_a(geo, net, live, xg, xl, packed, conv, acc, weight, own_g, own_l, arrive):
    loads = (
        pltpu.make_async_copy(xg, own_g, arrive.at[0]),
        pltpu.make_async_copy(xl, own_l, arrive.at[1]),
    )
    for load in loads:
        load.start()
    net.open()
    acc[...] = jnp.zeros(acc.shape, F32)
    blank = jnp.zeros((CELLS, packed.shape[1]), BF16)
    half = CELLS // 2
    for load in loads:
        load.wait()

    def pack(s):
        base = s * geo.rows
        keep = alive(live, s).astype(BF16)
        for i in range(geo.hg):
            start = pl.multiple_of(base + i * CELLS, CELLS)
            packed[pl.ds(start, CELLS), :] = blank
            packed[pl.ds(start, geo.hg), :] = own_g[s, i] * keep
        for i in range(geo.hl):
            start = pl.multiple_of(base + geo.rg + i * CELLS, CELLS)
            packed[pl.ds(start, CELLS), :] = blank
            for side in range(2):
                place = pl.multiple_of(start + side * half, half)
                packed[pl.ds(place, geo.hl), :] = own_l[2 * s + side, i] * keep

    third = geo.slabs // 3
    loop(third, pack)
    net.turn(1)
    loop(third, lambda s: pack(s + third))
    net.turn(2)
    loop(geo.slabs - 2 * third, lambda s: pack(s + 2 * third))
    net.turn(3)
    gathered = net.job_out(2)
    weight[...] = gathered[...].astype(F32).reshape(weight.shape).astype(BF16)

    def slab(s):
        result = nt(packed[at(s, geo.rows), :], weight[...])
        conv[at(s, geo.rows), :] = result.astype(BF16)
        for start, size, group in geo.pieces(256):
            piece = result[start : start + size]
            acc[2 * group] += fold(piece)
            acc[2 * group + 1] += fold(piece * piece)

    loop(geo.slabs, slab)
    finish(net.own, acc, 4)
    net.own[8:16, :] = jnp.full((8, net.own.shape[1]), live[0], jnp.int32).astype(F32)
    net.begin()
    net.turn(4)
    net.middle()
    net.turn(5)
    net.end()


def spread_taps(geo, store, s, values, reverse):
    width = values[0].shape[1]
    for group in range(2):
        rows = values[group]
        size = rows.shape[0]
        start = pl.multiple_of(s * geo.halo + CELLS + group * (geo.rg + CELLS), CELLS)
        before = pltpu.roll(rows, 1, 0)
        after = pltpu.roll(rows, size - 1, 0)
        order = (after, rows, before) if reverse else (before, rows, after)
        for tap in range(3):
            store[pl.ds(start, size), tap * width : (tap + 1) * width] = order[tap].astype(BF16)


def clear_halo(geo, store):
    blank = jnp.zeros((CELLS, store.shape[1]), BF16)

    def slab(s):
        store[pl.ds(pl.multiple_of(s * geo.halo, CELLS), CELLS), :] = blank
        store[pl.ds(pl.multiple_of(s * geo.halo + CELLS + geo.rg, CELLS), CELLS), :] = blank

    loop(geo.slabs, slab)
    store[geo.slabs * geo.halo : geo.slabs * geo.halo + CELLS, :] = blank


def activate(geo, live, conv, s, terms):
    values = []
    width = conv.shape[1]
    keep = alive(live, s)
    for group in range(2):
        start, size = (geo.rg, geo.rl) if group else (0, geo.rg)
        rows = conv[pl.ds(pl.multiple_of(s * geo.rows + start, CELLS), size), :].astype(F32)
        scale, shift = terms[group]
        values.append(silu(rows * scale + shift) * (geo.mask(size, group, width) * keep))
    return values


def stage_b(geo, net, live, count, za, stats_a, norm, weight, conv, taps, acc):
    net.open()
    acc[...] = jnp.zeros(acc.shape, F32)
    width = za.shape[1]
    terms = forward_terms(geo, count, stats_a, norm, width)
    clear_halo(geo, taps)
    loop(
        geo.slabs,
        lambda s: spread_taps(geo, taps, s, activate(geo, live, za, s, terms), False),
    )
    net.turn(1)
    span = geo.halo - CELLS

    def slab(s):
        result = None
        for dy in range(3):
            rows = taps[pl.ds(pl.multiple_of(s * geo.halo + dy * CELLS, CELLS), span), :]
            term = nt(rows, weight[:, dy * 3 * width : (dy + 1) * 3 * width])
            result = term if result is None else result + term
        keep = alive(live, s)
        for group, (begin, size) in enumerate(((0, geo.rg), (geo.rg + CELLS, geo.rl))):
            piece = result[begin : begin + size]
            start = pl.multiple_of(s * geo.rows + group * geo.rg, CELLS)
            conv[pl.ds(start, size), :] = piece.astype(BF16)
            piece = piece * (geo.mask(size, group, width) * keep)
            acc[2 * group] += fold(piece)
            acc[2 * group + 1] += fold(piece * piece)

    loop(geo.slabs, slab)
    finish(net.own, acc, 4)
    net.run()


def stage_c(geo, net, live, count, zb, stats_b, norm, weight, conv, act, acc):
    net.open()
    acc[...] = jnp.zeros(acc.shape, F32)
    terms = forward_terms(geo, count, stats_b, norm, zb.shape[1])
    step = 256

    def slab(s):
        values = activate(geo, live, zb, s, terms)
        act[0 : geo.rg, :] = values[0].astype(BF16)
        act[geo.rg : geo.rows, :] = values[1].astype(BF16)
        for c in range(0, weight.shape[0], step):
            result = nt(act[...], weight[c : c + step, :])
            conv[at(s, geo.rows), c : c + step] = result.astype(BF16)
            for start, size, group in geo.pieces(256):
                piece = result[start : start + size]
                acc[2 * group, :, c : c + step] += fold(piece)
                acc[2 * group + 1, :, c : c + step] += fold(piece * piece)

    loop(geo.slabs, slab)
    finish(net.own, acc, 4)
    net.run()


def even_rows(geo):
    return [2 * i * CELLS for i in range(geo.og)] + [
        geo.rg + 2 * i * CELLS for i in range(geo.ol)
    ]


def stage_d(
    geo, net, live, count, zc, stats_c, norm, packed, weight, hid, outg, outl, conv, sub, full, acc,
):
    net.open()
    acc[...] = jnp.zeros(acc.shape, F32)
    width = zc.shape[1]
    terms = forward_terms(geo, count, stats_c, norm, width)

    def slab(s):
        keep = alive(live, s)
        for start, size, group in geo.pieces(width):
            rows = pl.ds(pl.multiple_of(s * geo.rows + start, CELLS), size)
            scale, shift = terms[group]
            joined = zc[rows, :].astype(F32) * scale + shift + packed[rows, :].astype(F32)
            value = silu(joined) * (geo.mask(size, group, width) * keep)
            put(full, pl.ds(start, size), value)
            hid[rows, :] = value.astype(BF16)
        picked = [take(full, pl.ds(start, 8, stride=2)) for start in even_rows(geo)]
        sub[at(s, geo.small), :] = jnp.concatenate(picked, axis=0).astype(BF16)
        result = nt(hid[at(s, geo.rows), :], weight[...])
        conv[at(s, geo.rows), :] = result.astype(BF16)
        for start, size, group in geo.pieces(256):
            piece = result[start : start + size]
            acc[2 * group] += fold(piece)
            acc[2 * group + 1] += fold(piece * piece)

    def emit(s):
        for i in range(geo.hg):
            start = pl.multiple_of(s * geo.rows + i * CELLS, CELLS)
            outg[s, i] = hid[pl.ds(start, CELLS), :][0 : geo.hg]
        for i in range(geo.hl):
            start = pl.multiple_of(s * geo.rows + geo.rg + i * CELLS, CELLS)
            rows = hid[pl.ds(start, CELLS), :]
            for side in range(2):
                begin = side * CELLS // 2
                outl[2 * s + side, i] = rows[begin : begin + geo.hl]

    half = geo.slabs // 2
    loop(half, slab)
    net.turn(1)
    loop(geo.slabs - half, lambda s: slab(s + half))
    net.turn(2)
    finish(net.own, acc, 4)
    net.begin()
    loop(half, emit)
    net.middle()
    loop(geo.slabs - half, lambda s: emit(s + half))
    net.end()


def small_product(geo, left, weight, conv, acc, first, last):
    step = 256
    for c in range(first, last, step):
        result = nt(left[...], weight[c : c + step, :])
        conv[:, c : c + step] = result.astype(BF16)
        for s in range(geo.slabs):
            for start, size, group in geo.small_pieces():
                piece = result[s * geo.small + start : s * geo.small + start + size]
                acc[2 * group, :, c : c + step] += fold(piece)
                acc[2 * group + 1, :, c : c + step] += fold(piece * piece)


def gather_taps(geo, live, zd, terms, full, taps):
    width = zd.shape[1]
    blank = jnp.zeros((8, width), F32)
    full[:, 0:CELLS, :] = jnp.zeros((width // 128, CELLS, 128), F32)
    full[:, CELLS + geo.rg : 2 * CELLS + geo.rg, :] = jnp.zeros((width // 128, CELLS, 128), F32)

    def slab(s):
        keep = alive(live, s)
        for start, size, group in geo.pieces(width):
            rows = pl.ds(pl.multiple_of(s * geo.rows + start, CELLS), size)
            scale, shift = terms[group]
            value = silu(zd[rows, :].astype(F32) * scale + shift)
            begin = CELLS + start + group * CELLS
            put(full, pl.ds(begin, size), value * (geo.mask(size, group, width) * keep))
        for dy in range(3):
            for dx in range(3):
                picked = []
                for group in range(2):
                    for i in range(geo.ol if group else geo.og):
                        line = 2 * i + dy - 1
                        if line < 0:
                            picked.append(blank)
                            continue
                        begin = CELLS + group * (geo.rg + CELLS) + line * CELLS + dx - 1
                        picked.append(take(full, pl.ds(begin, 8, stride=2)))
                tap = dy * 3 + dx
                taps[at(s, geo.small), tap * width : (tap + 1) * width] = jnp.concatenate(
                    picked, axis=0
                ).astype(BF16)

    loop(geo.slabs, slab)


def stage_e(
    geo, net, live, count, zd, stats_d, norm, weight, sub, short, conv, conv_s, stats_s, full, taps,
    acc, acc_s,
):
    net.open()
    acc[...] = jnp.zeros(acc.shape, F32)
    acc_s[...] = jnp.zeros(acc_s.shape, F32)
    terms = forward_terms(geo, count, stats_d, norm, zd.shape[1])
    gather_taps(geo, live, zd, terms, full, taps)
    net.turn(1)
    step = 256
    for c in range(0, weight.shape[0], step):
        result = nt(taps[...], weight[c : c + step, :])
        conv[:, c : c + step] = result.astype(BF16)
        for s in range(geo.slabs):
            keep = alive(live, s)
            for start, size, group in geo.small_pieces():
                piece = result[s * geo.small + start : s * geo.small + start + size]
                piece = piece * (geo.small_mask(group, step) * keep)
                acc[2 * group, :, c : c + step] += fold(piece)
                acc[2 * group + 1, :, c : c + step] += fold(piece * piece)
    net.turn(2)
    finish(net.own, acc, 4)
    net.begin()
    half = short.shape[0] // 2
    small_product(geo, sub, short, conv_s, acc_s, 0, half)
    net.middle()
    small_product(geo, sub, short, conv_s, acc_s, half, 2 * half)
    finish(stats_s, acc_s, 4)
    net.end()


def stage_f(geo, net, live, count, ze, stats_e, norm, weight, act, conv, acc):
    net.open()
    net.side.begin()
    acc[...] = jnp.zeros(acc.shape, F32)
    width = ze.shape[1]
    terms = forward_terms(geo, count, stats_e, norm, width, True)

    def slab(s):
        keep = alive(live, s)
        rows = ze[at(s, geo.small), :].astype(F32)
        parts = []
        for start, size, group in geo.small_pieces():
            scale, shift = terms[group]
            value = silu(rows[start : start + size] * scale + shift)
            parts.append(value * (geo.small_mask(group, width) * keep))
        act[at(s, geo.small), :] = jnp.concatenate(parts, axis=0).astype(BF16)

    loop(geo.slabs, slab)
    half = weight.shape[0] // 2
    small_product(geo, act, weight, conv, acc, 0, half)
    net.side.middle()
    small_product(geo, act, weight, conv, acc, half, 2 * half)
    net.side.end()
    finish(net.own, acc, 4)
    net.run()


def stage_out(
    geo, net, live, count, zf, zs, stats_f, stats_s, norm_f, norm_s, cotg, cotl, outg, outl, grad,
    pooled_sums, pool, cot, acc,
):
    acc[...] = jnp.zeros(acc.shape, F32)
    cot[...] = jnp.zeros(cot.shape, F32)
    pool[...] = jnp.zeros(pool.shape, F32)
    width = zf.shape[1]
    step = 512
    terms_f = forward_terms(geo, count, stats_f, norm_f, width, True)
    terms_s = forward_terms(geo, count, stats_s, norm_s, width, True)

    def slab(s):
        keep = alive(live, s)
        for c in range(0, width, step):
            cols = slice(c, c + step)
            for i in range(geo.og):
                cot[i * 8 : i * 8 + geo.og, :] = cotg[s, i, :, cols].astype(F32)
            for i in range(geo.ol):
                for side in range(2):
                    begin = geo.sg + i * 8 + side * 4
                    cot[begin : begin + geo.ol, :] = cotl[2 * s + side, i, :, cols].astype(F32)
            rows_f = zf[at(s, geo.small), cols].astype(F32)
            rows_s = zs[at(s, geo.small), cols].astype(F32)
            grads = []
            for start, size, group in geo.small_pieces():
                part = slice(start, start + size)
                vf, vs = rows_f[part], rows_s[part]
                scale_f, shift_f = (item[:, cols] for item in terms_f[group])
                scale_s, shift_s = (item[:, cols] for item in terms_s[group])
                joined = vf * scale_f + vs * scale_s + (shift_f + shift_s)
                mask = geo.small_mask(group, step) * keep
                gate = sig(joined)
                held = joined * gate
                value = held * mask
                low = value.astype(BF16)
                dy = cot[part, :] * ((gate + held - held * gate) * mask)
                grads.append(dy)
                acc[3 * group, :, cols] += fold(dy)
                acc[3 * group + 1, :, cols] += fold(dy * vf)
                acc[3 * group + 2, :, cols] += fold(dy * vs)
                summed = fold(value)
                if group == 0:
                    for i in range(geo.og):
                        outg[s, i, :, cols] = value[i * 8 : i * 8 + geo.og].astype(BF16)
                    pool[s, 0:1, cols] = jnp.sum(summed, axis=0, keepdims=True) * (
                        1.0 / (geo.og * geo.og)
                    )
                else:
                    row = lax.broadcasted_iota(jnp.int32, (8, step), 0)
                    for side in range(2):
                        own = jnp.where((row >= 4) == (side == 1), summed, 0.0)
                        pool[s, 1 + side : 2 + side, cols] = jnp.sum(
                            own, axis=0, keepdims=True
                        ) * (1.0 / (geo.ol * geo.ol))
                        for i in range(geo.ol):
                            begin = i * 8 + side * 4
                            outl[2 * s + side, i, :, cols] = value[begin : begin + geo.ol].astype(
                                BF16
                            )
            grad[at(s, geo.small), cols] = jnp.concatenate(grads, axis=0).astype(BF16)
        pooled = pool[s]
        square = jnp.mean(pooled * pooled, axis=1, keepdims=True)
        normed = pooled * lax.rsqrt(square + 1e-06)
        acc[6] += normed
        acc[7] += normed * normed

    loop(geo.slabs, slab)
    finish(net.own, acc, 6)
    net.begin()
    finish(pooled_sums, acc, 2, 6)
    net.middle()
    net.end()


def small_back(geo, live, s, grad, conv, terms, width, cols):
    keep = alive(live, s)
    rows_g = grad[at(s, geo.small), cols].astype(F32)
    rows_z = conv[at(s, geo.small), cols].astype(F32)
    parts = []
    for start, size, group in geo.small_pieces():
        scale, by_value, constant = (item[:, cols] for item in terms[group])
        part = slice(start, start + size)
        value = rows_g[part] * scale + rows_z[part] * by_value + constant
        parts.append(value * (geo.small_mask(group, width) * keep))
    return jnp.concatenate(parts, axis=0).astype(BF16)


def stage_f_back(
    geo, net, live, count, zf, zs, stats_f, stats_s, norm_f, norm_s, grad, sums, act, sub, weight,
    short, ze, stats_e, norm_e, wgrad_f, wgrad_s, back_sub, back_e, ngrad_f, ngrad_s, dzf, dzs, acc,
):
    acc[...] = jnp.zeros(acc.shape, F32)
    width = zf.shape[1]
    step = 512
    rows_f, rows_s = ((0, 1), (3, 4)), ((0, 2), (3, 5))
    terms_f = backward_terms(geo, count, stats_f, norm_f, sums, ngrad_f, width, True, rows_f)
    terms_s = backward_terms(geo, count, stats_s, norm_s, sums, ngrad_s, width, True, rows_s)

    def slab(s):
        for c in range(0, width, step):
            cols = slice(c, c + step)
            dzf[at(s, geo.small), cols] = small_back(geo, live, s, grad, zf, terms_f, step, cols)
            dzs[at(s, geo.small), cols] = small_back(geo, live, s, grad, zs, terms_s, step, cols)

    loop(geo.slabs, slab)
    net.open()
    net.side.begin()
    block = 256
    terms_e = forward_terms(geo, count, stats_e, norm_e, ze.shape[1], True)
    for c in range(0, act.shape[1], block):
        cols = slice(c, c + block)
        result = nn(dzf[...], weight[:, cols])
        for s in range(geo.slabs):
            keep = alive(live, s)
            rows = ze[s * geo.small : (s + 1) * geo.small, cols].astype(F32)
            parts = []
            for start, size, group in geo.small_pieces():
                scale, shift = (item[:, cols] for item in terms_e[group])
                value = rows[start : start + size]
                mask = geo.small_mask(group, block) * keep
                piece = result[s * geo.small + start : s * geo.small + start + size]
                piece = piece * (slope(value * scale + shift) * mask)
                parts.append(piece)
                acc[2 * group, :, cols] += fold(piece)
                acc[2 * group + 1, :, cols] += fold(piece * value)
            back_e[s * geo.small : (s + 1) * geo.small, cols] = jnp.concatenate(
                parts, axis=0
            ).astype(BF16)
    finish(net.own, acc, 4)
    net.begin()
    for c in range(0, width, block):
        cols = slice(c, c + block)
        put_pieces(wgrad_f, c, tn(dzf[:, cols], act[...]))
    net.turn(1)
    net.side.middle()
    net.middle()
    for c in range(0, width, block):
        cols = slice(c, c + block)
        put_pieces(wgrad_s, c, tn(dzs[:, cols], sub[...]))
    net.turn(2)
    for c in range(0, sub.shape[1], block):
        cols = slice(c, c + block)
        back_sub[:, cols] = nn(dzs[...], short[:, cols]).astype(BF16)
    net.side.end()
    net.end()


def stage_e_back(
    geo, net, live, count, ze, stats_e, norm_e, back_e, sums_e, zd, stats_d, norm_d, weight, wgrad,
    back_d, ngrad, full, taps, dze, moved, parity, acc,
):
    net.open()
    acc[...] = jnp.zeros(acc.shape, F32)
    width = ze.shape[1]
    terms_e = backward_terms(geo, count, stats_e, norm_e, sums_e, ngrad, width, True)
    terms_d = forward_terms(geo, count, stats_d, norm_d, width)
    gather_taps(geo, live, zd, terms_d, full, taps)

    def shift(s):
        value = small_back(geo, live, s, back_e, ze, terms_e, width, slice(0, width)).astype(F32)
        blank = jnp.zeros((8, width), F32)
        down = jnp.concatenate(
            [value[8 : geo.sg], blank, value[geo.sg + 8 :], blank], axis=0
        )
        size = geo.small
        dze[at(s, size), :] = value.astype(BF16)
        moved[0, at(s, size), :] = pltpu.roll(value, size - 1, 0).astype(BF16)
        moved[1, at(s, size), :] = down.astype(BF16)
        moved[2, at(s, size), :] = pltpu.roll(down, size - 1, 0).astype(BF16)

    loop(geo.slabs, shift)

    def tap(dy, dx):
        return weight[:, (dy * 3 + dx) * width : (dy * 3 + dx + 1) * width]

    def grads(first, last):
        for t in range(first, last):
            result = tn(dze[...], taps[:, t * width : (t + 1) * width])
            put_pieces(wgrad, 0, result, t * width)

    parity[0] = nn(dze[...], tap(1, 1))
    parity[1] = nn(dze[...], tap(1, 2)) + nn(moved[0], tap(1, 0))
    parity[2] = nn(dze[...], tap(2, 1)) + nn(moved[1], tap(0, 1))
    parity[3] = (
        nn(dze[...], tap(2, 2))
        + nn(moved[0], tap(2, 0))
        + nn(moved[1], tap(0, 2))
        + nn(moved[2], tap(0, 0))
    )

    def slab(s):
        keep = alive(live, s)
        for group in range(2):
            for i in range(geo.ol if group else geo.og):
                for a in range(2):
                    for b in range(2):
                        begin = group * geo.rg + (2 * i + a) * CELLS + b
                        source = s * geo.small + group * geo.sg + i * 8
                        part = parity[2 * a + b, pl.ds(pl.multiple_of(source, 8), 8), :]
                        put(full, pl.ds(begin, 8, stride=2), part)
        for start, size, group in geo.pieces(width):
            rows = pl.ds(pl.multiple_of(s * geo.rows + start, CELLS), size)
            scale, shift_d = terms_d[group]
            value = zd[rows, :].astype(F32)
            mask = geo.mask(size, group, width) * keep
            piece = take(full, pl.ds(start, size)) * (slope(value * scale + shift_d) * mask)
            back_d[rows, :] = piece.astype(BF16)
            acc[2 * group] += fold(piece)
            acc[2 * group + 1] += fold(piece * value)

    loop(geo.slabs, slab)
    net.turn(1)
    finish(net.own, acc, 4)
    net.begin()
    grads(0, 4)
    net.middle()
    grads(4, 9)
    net.end()


def wide_back(geo, live, s, grad, conv, terms, low):
    width = conv.shape[1]
    keep = alive(live, s)
    for start, size, group in geo.pieces(width):
        rows = pl.ds(pl.multiple_of(s * geo.rows + start, CELLS), size)
        scale, by_value, constant = terms[group]
        value = grad[rows, :].astype(F32) * scale + conv[rows, :].astype(F32) * by_value + constant
        low[rows, :] = (value * (geo.mask(size, group, width) * keep)).astype(BF16)


def stage_d_back(
    geo, net, live, count, zd, stats_d, norm_d, back_d, sums_d, hid, packed, zc, stats_c, norm_c,
    back_sub, weight, wgrad, joined, ngrad, dzd, full, acc,
):
    acc[...] = jnp.zeros(acc.shape, F32)
    width = zc.shape[1]
    terms_d = backward_terms(geo, count, stats_d, norm_d, sums_d, ngrad, zd.shape[1])
    terms_c = forward_terms(geo, count, stats_c, norm_c, width)

    net.open()

    def slab(s):
        wide_back(geo, live, s, back_d, zd, terms_d, dzd)
        put(full, pl.ds(0, geo.rows), nn(dzd[at(s, geo.rows), :], weight[...]))
        extra = back_sub[at(s, geo.small), :].astype(F32)
        for k, start in enumerate(even_rows(geo)):
            place = pl.ds(start, 8, stride=2)
            put(full, place, take(full, place) + extra[k * 8 : k * 8 + 8])
        keep = alive(live, s)
        for start, size, group in geo.pieces(width):
            rows = pl.ds(pl.multiple_of(s * geo.rows + start, CELLS), size)
            scale, shift = terms_c[group]
            value = zc[rows, :].astype(F32)
            pre = value * scale + shift + packed[rows, :].astype(F32)
            mask = geo.mask(size, group, width) * keep
            piece = take(full, pl.ds(start, size)) * (slope(pre) * mask)
            joined[rows, :] = piece.astype(BF16)
            acc[2 * group] += fold(piece)
            acc[2 * group + 1] += fold(piece * value)

    third = geo.slabs // 3
    loop(third, slab)
    net.turn(1)
    loop(geo.slabs - third, lambda s: slab(s + third))
    net.turn(2)
    finish(net.own, acc, 4)
    block = 256
    net.begin()
    for c in range(0, dzd.shape[1], block):
        put_pieces(wgrad, c, tn(dzd[:, c : c + block], hid[...]))
        if c == 0:
            net.middle()
    net.end()


def stage_c_back(
    geo, net, live, count, zc, stats_c, norm_c, joined, sums_c, zb, stats_b, norm_b, weight, wgrad,
    back_b, ngrad, dzc, act, acc,
):
    acc[...] = jnp.zeros(acc.shape, F32)
    terms_c = backward_terms(geo, count, stats_c, norm_c, sums_c, ngrad, zc.shape[1])
    terms_b = forward_terms(geo, count, stats_b, norm_b, zb.shape[1])
    width = zb.shape[1]

    net.open()

    def slab(s):
        wide_back(geo, live, s, joined, zc, terms_c, dzc)
        result = nn(dzc[at(s, geo.rows), :], weight[...])
        keep = alive(live, s)
        for start, size, group in geo.pieces(width):
            rows = pl.ds(pl.multiple_of(s * geo.rows + start, CELLS), size)
            scale, shift = terms_b[group]
            value = zb[rows, :].astype(F32)
            pre = value * scale + shift
            mask = geo.mask(size, group, width) * keep
            gate = sig(pre)
            held = pre * gate
            act[rows, :] = (held * mask).astype(BF16)
            piece = result[start : start + size] * ((gate + held - held * gate) * mask)
            back_b[rows, :] = piece.astype(BF16)
            acc[2 * group] += fold(piece)
            acc[2 * group + 1] += fold(piece * value)

    half = geo.slabs // 2
    loop(half, slab)
    net.turn(1)
    loop(geo.slabs - half, lambda s: slab(s + half))
    net.turn(2)
    finish(net.own, acc, 4)
    net.begin()
    half = dzc.shape[1] // 2
    put_pieces(wgrad, 0, tn(dzc[:, 0:half], act[...]))
    net.middle()
    put_pieces(wgrad, half, tn(dzc[:, half:], act[...]))
    net.end()


def stage_b_back(
    geo, net, live, count, zb, stats_b, norm_b, back_b, sums_b, za, stats_a, norm_a, weight, wgrad,
    back_a, ngrad, taps, dtaps, stacked, total, acc,
):
    acc[...] = jnp.zeros(acc.shape, F32)
    width = za.shape[1]
    terms_b = backward_terms(geo, count, stats_b, norm_b, sums_b, ngrad, width)
    terms_a = forward_terms(geo, count, stats_a, norm_a, width)
    clear_halo(geo, taps)
    clear_halo(geo, dtaps)
    for t in range(9):
        stacked[t * width : (t + 1) * width, :] = weight[:, t * width : (t + 1) * width]

    def fill(s):
        spread_taps(geo, taps, s, activate(geo, live, za, s, terms_a), False)
        keep = alive(live, s)
        values = []
        for start, size, group in geo.pieces(width):
            rows = pl.ds(pl.multiple_of(s * geo.rows + start, CELLS), size)
            scale, by_value, constant = terms_b[group]
            value = back_b[rows, :].astype(F32) * scale + zb[rows, :].astype(F32) * by_value
            values.append((value + constant) * (geo.mask(size, group, width) * keep))
        spread_taps(geo, dtaps, s, values, True)

    net.open()
    loop(geo.slabs, fill)
    net.turn(1)
    span = geo.halo - CELLS
    total[...] = jnp.zeros(total.shape, F32)

    def slab(s):
        result = None
        for dy in range(3):
            begin = pl.multiple_of(s * geo.halo + (2 - dy) * CELLS, CELLS)
            term = nn(
                dtaps[pl.ds(begin, span), :], stacked[dy * 3 * width : (dy + 1) * 3 * width, :]
            )
            result = term if result is None else result + term
        keep = alive(live, s)
        for group, (begin, size) in enumerate(((0, geo.rg), (geo.rg + CELLS, geo.rl))):
            rows = pl.ds(pl.multiple_of(s * geo.rows + group * geo.rg, CELLS), size)
            scale, shift = terms_a[group]
            value = za[rows, :].astype(F32)
            mask = geo.mask(size, group, width) * keep
            piece = result[begin : begin + size] * (slope(value * scale + shift) * mask)
            back_a[rows, :] = piece.astype(BF16)
            acc[2 * group] += fold(piece)
            acc[2 * group + 1] += fold(piece * value)

    def grads(s):
        own = dtaps[
            pl.ds(pl.multiple_of(s * geo.halo + CELLS, CELLS), span), width : 2 * width
        ]
        for dy in range(3):
            begin = pl.multiple_of(s * geo.halo + dy * CELLS, CELLS)
            total[:, dy * 3 * width : (dy + 1) * 3 * width] += tn(own, taps[pl.ds(begin, span), :])

    loop(geo.slabs, slab)
    net.turn(2)
    finish(net.own, acc, 4)
    half = geo.slabs // 2
    net.begin()
    loop(half, grads)
    net.middle()
    loop(geo.slabs - half, lambda s: grads(s + half))
    put_pieces(wgrad, 0, total[...])
    net.end()


def stage_a_back(
    geo, net, live, count, za, stats_a, norm_a, back_a, sums_a, packed, wgrad, dza, ngrad,
):
    net.open()
    terms_a = backward_terms(geo, count, stats_a, norm_a, sums_a, ngrad, za.shape[1])
    loop(geo.slabs, lambda s: wide_back(geo, live, s, back_a, za, terms_a, dza))
    put_pieces(wgrad, 0, tn(dza[...], packed[...]))
    for number in range(1, 8):
        net.turn(number)
    net.close()


def last_kernel(geo, joined, dza, weight, *refs):
    count = (len(refs) - 2) // 2
    rows_in, dxg, dxl, columns = refs[:count], refs[count], refs[count + 1], refs[count + 2 :]
    result = nn(dza[...], weight[...]) + joined[...].astype(F32)
    half = CELLS // 2
    for i in range(geo.hg):
        dxg[0, i] = result[i * CELLS : i * CELLS + geo.hg]
    for i in range(geo.hl):
        for side in range(2):
            begin = geo.rg + i * CELLS + side * half
            dxl[side, i] = result[begin : begin + geo.hl]

    def turn_over(k):
        @pl.when(pl.program_id(0) == k % geo.slabs)
        def write():
            source, target = rows_in[k], columns[k]
            size = target.shape[1]
            whole = source[...].astype(F32).reshape(size, target.shape[0])
            target[...] = whole.T

    for k in range(count):
        turn_over(k)


def run_last(geo, joined, dza, weight, parts, global_shape, local_shape):
    def whole(shape):
        return pl.BlockSpec(shape, lambda s: (0,) * len(shape))

    shapes = [(part.shape[-1], part.shape[0] * part.shape[1]) for part in parts]
    return pl.pallas_call(
        functools.partial(last_kernel, geo),
        grid=(geo.slabs,),
        out_shape=[jax.ShapeDtypeStruct(global_shape, F32), jax.ShapeDtypeStruct(local_shape, F32)]
        + [jax.ShapeDtypeStruct(shape, F32) for shape in shapes],
        in_specs=[
            pl.BlockSpec((geo.rows, joined.shape[1]), lambda s: (s, 0)),
            pl.BlockSpec((geo.rows, dza.shape[1]), lambda s: (s, 0)),
            whole(weight.shape),
        ]
        + [whole(part.shape) for part in parts],
        out_specs=[
            pl.BlockSpec((1,) + global_shape[1:], lambda s: (s, 0, 0, 0)),
            pl.BlockSpec((2,) + local_shape[1:], lambda s: (s, 0, 0, 0)),
        ]
        + [whole(shape) for shape in shapes],
        compiler_params=pltpu.CompilerParams(vmem_limit_bytes=VMEM_CAP),
        name="last",
    )(joined, dza, weight, *parts)


class Sums:
    def __init__(self, reps, shards, own, out, first, second, sems):
        self.reps, self.shards = reps, shards
        self.own, self.out, self.first, self.second = own, out, first, second
        self.sems = sems
        self.rep, self.shard = lax.axis_index("rep"), lax.axis_index("fsdp")
        self.copies = []

    def begin(self):
        self.copies = []
        for hop in range(1, self.shards):
            copy = pltpu.make_async_remote_copy(
                self.own, self.first.at[self.shard], self.sems[0].at[hop], self.sems[1].at[hop],
                device_id={"fsdp": lax.rem(self.shard + hop, self.shards)}, device_id_type=MESH,
            )
            copy.start()
            self.copies.append(copy)
        self.first[self.shard] = self.own[...]

    def middle(self):
        for copy in self.copies:
            copy.wait()
        total = self.first[0]
        for k in range(1, self.shards):
            total = total + self.first[k]
        self.second[self.rep] = total
        self.copies = []
        for hop in range(1, self.reps):
            place = self.second.at[self.rep]
            copy = pltpu.make_async_remote_copy(
                place, place, self.sems[2].at[hop], self.sems[3].at[hop],
                device_id={"rep": lax.rem(self.rep + hop, self.reps)}, device_id_type=MESH,
            )
            copy.start()
            self.copies.append(copy)

    def end(self):
        for copy in self.copies:
            copy.wait()
        total = self.second[0]
        for k in range(1, self.reps):
            total = total + self.second[k]
        self.out[...] = total


class Net:
    def __init__(self, reps, shards, sums=None, side=None, jobs=(), plans=()):
        self.reps, self.shards = reps, shards
        self.sums, self.side, self.jobs, self.plans = sums, side, jobs, plans
        self.own = None if sums is None else sums.own
        self.opened = False
        self.started, self.finished = set(), set()

    def enter(self):
        rep, shard = lax.axis_index("rep"), lax.axis_index("fsdp")
        barrier = pltpu.get_barrier_semaphore()
        for hop in range(1, self.shards):
            other = {"fsdp": lax.rem(shard + hop, self.shards)}
            pl.semaphore_signal(barrier, inc=1, device_id=other, device_id_type=MESH)
        for hop in range(1, self.reps):
            other = {"rep": lax.rem(rep + hop, self.reps)}
            pl.semaphore_signal(barrier, inc=1, device_id=other, device_id_type=MESH)

    def open(self):
        if not self.opened:
            self.opened = True
            pl.semaphore_wait(pltpu.get_barrier_semaphore(), self.shards + self.reps - 2)
            self.turn(0)

    def turn(self, number):
        for k, (start, middle, end) in enumerate(self.plans):
            if end == number:
                self.finish(k)
        for k, (start, middle, end) in enumerate(self.plans):
            if middle == number:
                self.jobs[k].middle()
        for k, (start, middle, end) in enumerate(self.plans):
            if start == number:
                self.started.add(k)
                self.jobs[k].start()

    def finish(self, k):
        assert k in self.started and k not in self.finished
        self.jobs[k].middle()
        self.finished.add(k)
        self.jobs[k].finish()

    def job_out(self, k):
        return self.jobs[k].out

    def begin(self):
        self.open()
        self.sums.begin()

    def middle(self):
        self.sums.middle()

    def end(self):
        self.sums.end()
        self.close()

    def run(self):
        self.begin()
        self.middle()
        self.end()

    def close(self):
        for k in range(len(self.jobs)):
            if k not in self.finished:
                self.finish(k)


class Job:
    def __init__(self, kind, reps, shards, sources, out, held, send, recv):
        self.kind, self.source, self.out, self.held = kind, sources[0], out, held
        self.sources = sources
        self.send, self.recv = send, recv
        self.reps, self.chips = reps, shards // 2
        self.halving = kind == "rep" and reps == 4
        self.rep, shard = lax.axis_index("rep"), lax.axis_index("fsdp")
        self.chip, self.core = shard // 2, lax.rem(shard, 2)
        if kind in ("pair", "join"):
            self.members, self.me = 2, self.core
            self.address = lambda k: {"fsdp": self.chip * 2 + k}
        elif kind in ("line", "spread"):
            self.members, self.me = self.chips, self.chip
            self.address = lambda k: {"fsdp": k * 2 + self.core}
        elif kind == "all":
            self.members, self.me = shards, shard
            self.address = lambda k: {"fsdp": k}
        else:
            self.members, self.me = reps, self.rep
            self.address = lambda k: {"rep": k}

    def give(self, source, target, hop):
        other = lax.rem(self.me + hop, self.members)
        k = len(self.copies)
        if hop == 0:
            copy = pltpu.make_async_copy(source, target, self.send.at[k])
        else:
            copy = pltpu.make_async_remote_copy(
                source, target, self.send.at[k], self.recv.at[k],
                device_id=self.address(other), device_id_type=MESH,
            )
        copy.start()
        self.copies.append(copy)

    def start(self):
        self.copies = []
        kind, out = self.kind, self.out
        order = list(range(1, self.members)) + [0]
        if kind == "spread":
            for hop in order:
                self.give(self.source.at[self.rep], out.at[self.chip], hop)
        elif kind == "fan":
            for hop in order:
                for step in range(1, self.chips):
                    chip = lax.rem(self.chip + step, self.chips)
                    self.give(self.source.at[chip], out.at[chip, self.rep], hop)
            self.give(self.sources[1], out.at[self.chip], 0)
        elif kind == "join":
            for hop in order:
                for chip in range(self.chips):
                    self.give(self.source.at[chip], out.at[chip, self.core], hop)
        elif kind in ("all", "share"):
            for hop in order:
                self.give(self.source, out.at[self.me], hop)
        elif self.halving:
            low, high = lax.rem(self.rep, 2), self.rep // 2
            first = self.core == 0
            mine = jnp.where(first, low, high)
            self.rest = jnp.where(first, high, low)
            unit, step = jnp.where(first, 1, 2), jnp.where(first, 2, 1)
            self.partners = (
                jnp.where(first, high * 2 + 1 - low, (1 - high) * 2 + low),
                jnp.where(first, (1 - high) * 2 + low, high * 2 + 1 - low),
            )
            for k in range(2):
                self.send_to(
                    self.partners[0], self.source.at[(1 - mine) * unit + k * step],
                    self.held.at[2 + k],
                )
            for k in range(2):
                self.give(self.source.at[mine * unit + k * step], self.held.at[k], 0)
        else:
            for hop in order:
                other = lax.rem(self.me + hop, self.members)
                self.give(self.source.at[other], self.held.at[self.me], hop)
        self.halfway = False

    def send_to(self, rep, source, target):
        k = len(self.copies)
        copy = pltpu.make_async_remote_copy(
            source, target, self.send.at[k], self.recv.at[k], device_id={"rep": rep},
            device_id_type=MESH,
        )
        copy.start()
        self.copies.append(copy)

    def middle(self):
        if not self.halving or self.halfway:
            return
        self.halfway = True
        held = self.held
        for copy in self.copies:
            copy.wait()
        blocks = held.shape[1]

        def one(index):
            k, place = index // blocks, lax.rem(index, blocks)
            total = held[k, place].astype(F32) + held[2 + k, place].astype(F32)
            held[k, place] = total.astype(BF16)

        loop(2 * blocks, one)
        done = len(self.copies)
        self.send_to(self.partners[1], held.at[1 - self.rest], held.at[4])
        self.copies = self.copies[done:]

    def finish(self):
        for copy in self.copies:
            copy.wait()
        held, out = self.held, self.out
        if held is None:
            return
        if self.halving:

            def add(place):
                total = held[self.rest, place].astype(F32) + held[4, place].astype(F32)
                out[place] = total.astype(BF16)

            loop(held.shape[1], add)
            return
        blocks = held.shape[1:-2]

        def one(index):
            place = (index // blocks[-1], lax.rem(index, blocks[-1])) if len(blocks) == 2 else (
                (index,) if blocks else ()
            )
            total = held[(0,) + place].astype(F32)
            for k in range(1, self.members):
                total = total + held[(k,) + place].astype(F32)
            out[place[::-1]] = total.astype(BF16)

        if blocks:
            loop(blocks[0] * (blocks[1] if len(blocks) == 2 else 1), one)
        else:
            total = held[0].astype(F32)
            for k in range(1, self.members):
                total = total + held[k].astype(F32)
            out[...] = total.astype(BF16)


def job_shapes(kind, reps, shards, shape):
    chips = shards // 2
    if kind == "spread":
        return None, (chips,) + shape[1:], chips
    if kind == "fan":
        return None, (chips, reps) + shape[1:], reps * (chips - 1) + 1
    if kind == "join":
        return None, (chips, 2) + shape[1:], 2 * chips
    if kind == "all":
        return None, (shards,) + shape, shards
    if kind == "pair":
        return shape, (shape[2], shape[1]) + shape[3:], 2
    if kind == "share":
        return None, (reps,) + shape, reps
    if kind == "rep" and reps == 4:
        return (5,) + shape[1:], shape[1:], 5
    return shape, shape[1:], shape[0]


VMEM_CAP = 60 << 20
FAR = ("spread", "fan")


def sums_scratch(reps, shards, shape, own):
    return [pltpu.VMEM(shape, F32)] * own + [
        pltpu.VMEM((shards,) + shape, F32),
        pltpu.VMEM((reps,) + shape, F32),
        pltpu.SemaphoreType.DMA((shards,)),
        pltpu.SemaphoreType.DMA((shards,)),
        pltpu.SemaphoreType.DMA((reps,)),
        pltpu.SemaphoreType.DMA((reps,)),
    ]


def run(name, kernel, geo, reps, shards, number, live, operands, results, scratch, sums, jobs, side, far=()):
    own_results = len(results)
    results = list(results)
    spaces = [pltpu.VMEM] * own_results
    extra = []
    arrays = []
    shapes = []
    for kind, sources, start, middle, end in jobs:
        source = sources[0]
        if isinstance(source, int):
            shape, dtype = shapes[source]
        elif isinstance(source, str):
            shape, dtype = results[int(source)]
        else:
            shape, dtype = source.shape, source.dtype
        arrays += [item for item in sources if not isinstance(item, (int, str))]
        held, out, copies = job_shapes(kind, reps, shards, shape)
        shapes.append((out, dtype))
        results.append(shapes[-1])
        spaces.append(pltpu.HBM if kind in FAR else pltpu.VMEM)
        extra += [] if held is None else [pltpu.VMEM(held, BF16)]
        extra += [pltpu.SemaphoreType.DMA((copies,))] * 2
    operands = tuple(operands)
    near = len(operands)
    if side is not None:
        operands += (side,)
        results.append((side.shape, F32))
        spaces.append(pltpu.VMEM)
        extra += sums_scratch(reps, shards, side.shape, 0)
    if sums is not None:
        results.append((sums, F32))
        spaces.append(pltpu.VMEM)
        extra += sums_scratch(reps, shards, sums, 1)
    inputs = 1 + len(operands)
    remote = bool(jobs) or sums is not None

    def whole(*refs):
        sources_in = list(refs[inputs : inputs + len(arrays)])
        first_out = inputs + len(arrays)
        outs = refs[first_out : first_out + len(results)]
        more = list(refs[first_out + len(results) :])
        made = []
        for k, (kind, sources, start, middle, end) in enumerate(jobs):
            refs_of = []
            for item in sources:
                if isinstance(item, int):
                    refs_of.append(made[item].out)
                elif isinstance(item, str):
                    refs_of.append(outs[int(item)])
                else:
                    refs_of.append(sources_in.pop(0))
            held = more.pop(0) if job_shapes(kind, reps, shards, refs_of[0].shape)[0] else None
            made.append(
                Job(kind, reps, shards, refs_of, outs[own_results + k], held, more.pop(0), more.pop(0))
            )
        beside, main = None, None
        place = own_results + len(jobs)
        if side is not None:
            beside = Sums(reps, shards, refs[near + 1], outs[place], more[0], more[1], more[2:6])
            more = more[6:]
        if sums is not None:
            main = Sums(reps, shards, more[0], outs[-1], more[1], more[2], more[3:7])
            more = more[7:]
        net = None
        if remote:
            plans = [job[2:] for job in jobs]
            net = Net(reps, shards, main, beside, made, plans)
            net.enter()
        kernel(geo, net, *refs[: near + 1], *outs[:own_results], *more)

    params = {"collective_id": number, "has_side_effects": True} if remote else {}
    return pl.pallas_call(
        whole,
        out_shape=[jax.ShapeDtypeStruct(shape, dtype) for shape, dtype in results],
        in_specs=[pl.BlockSpec(memory_space=pltpu.SMEM)]
        + [pl.BlockSpec(memory_space=pltpu.HBM if k in far else pltpu.VMEM) for k in range(len(operands))]
        + [pl.BlockSpec(memory_space=pl.ANY)] * len(arrays),
        out_specs=[pl.BlockSpec(memory_space=space) for space in spaces],
        scratch_shapes=extra
        + [item if not isinstance(item, tuple) else pltpu.VMEM(*item) for item in scratch],
        compiler_params=pltpu.CompilerParams(vmem_limit_bytes=VMEM_CAP, **params),
        name=name,
    )(live, *operands, *arrays)


def own_norms(first, second):
    flat = jnp.concatenate([first.reshape(-1), second.reshape(-1)]).astype(F32)
    size = -(-flat.shape[0] // 1024) * 1024
    return jnp.pad(flat, (0, size - flat.shape[0])).reshape(8, -1)


def all_norms(gathered, first, second):
    shards = gathered.shape[0]
    flat = gathered.reshape(shards, -1)
    split, last = first.size, first.size + second.size

    def whole(part):
        return part.reshape(shards, 2, -1).transpose(1, 0, 2).reshape(2, -1)

    return whole(flat[:, :split]), whole(flat[:, split:last])


def body(reps, shards, *arguments):
    (
        global_views, local_views, live, first_reduce, first_spatial, first_expand, first_norms,
        second_reduce, second_spatial, second_expand, second_short, second_norms, global_cotan,
        local_cotan,
    ) = arguments
    geo = Geometry(global_views.shape[0], global_views.shape[1], local_views.shape[1])
    assert local_views.shape[0] == 2 * geo.slabs
    channels = global_views.shape[3]
    ha, hb, hc, hd, he, hf, hs = (
        item.T.reshape(reps, -1, item.shape[0])
        for item in (
            first_reduce, first_spatial, first_expand, second_reduce, second_spatial,
            second_expand, second_short,
        )
    )
    mid_1, mid_2 = first_reduce.shape[1] * shards, second_reduce.shape[1] * shards
    wide = second_expand.shape[1] * shards

    def rows_of(gathered):
        return gathered.reshape(-1, gathered.shape[-1])

    big, small = geo.total, geo.small_total

    numbers = iter(range(100))

    def go(name, kernel, operands, results, scratch, width=None, members=4, jobs=(), side=None, far=()):
        parts = {4: 2, 6: 4, 8: 2}[members]
        sums = None if width is None else (members * parts, width // parts)
        return run(
            name, kernel, geo, reps, shards, next(numbers), live, operands, results, scratch, sums,
            jobs, side, far,
        )

    def pieces(weight):
        size = weight.shape[0] // (shards * reps)
        return ((2, shards // 2, reps, size, weight.shape[1]), BF16)

    def acc(width, members=4):
        return ((members, 8, width), F32)

    def stat(width):
        return ((8, width), F32)

    def both(width):
        return ((2, width), F32)

    (
        packed, za, spread_a, fan_a, wa, spread_b, fan_b, wb, norms, spread_c, spread_d, sa,
    ) = go(
        "stage_a", stage_a, (global_views, local_views),
        [((big, channels), BF16), ((big, mid_1), BF16)],
        [
            acc(mid_1), ((mid_1, channels), BF16), (global_views.shape, BF16),
            (local_views.shape, BF16), pltpu.SemaphoreType.DMA((2,)),
        ],
        mid_1, 8,
        jobs=(
            ("spread", (ha,), 0, None, 1), ("fan", (0, ha), 1, None, 2), ("join", (1,), 2, None, 3),
            ("spread", (hb,), 0, None, 2), ("fan", (3, hb), 2, None, 4), ("join", (4,), 4, None, 5),
            ("all", (own_norms(first_norms, second_norms),), 1, None, None),
            ("spread", (hc,), 2, None, None), ("spread", (hd,), 3, None, None),
        ),
        far=(0, 1),
    )
    count = sa
    wa, wb = rows_of(wa), rows_of(wb)
    norms_1, norms_2 = all_norms(norms, first_norms, second_norms)
    na, nb, nc = norms_1[:, :mid_1], norms_1[:, mid_1 : 2 * mid_1], norms_1[:, 2 * mid_1 :]
    nd, ne = norms_2[:, :mid_2], norms_2[:, mid_2 : 2 * mid_2]
    nf, ns = norms_2[:, 2 * mid_2 : 2 * mid_2 + wide], norms_2[:, 2 * mid_2 + wide :]
    zb, fan_c, wc, fan_d, spread_e, sb = go(
        "stage_b", stage_b, (count, za, sa, na, wb), [((big, mid_1), BF16)],
        [((geo.halo_total, 3 * mid_1), BF16), acc(mid_1)], mid_1,
        jobs=(
            ("fan", (spread_c, hc), 0, None, 1), ("join", (0,), 1, None, None),
            ("fan", (spread_d, hd), 0, None, None), ("spread", (he,), 0, None, None),
        ),
    )
    wc = rows_of(wc)
    zc, wd, fan_e, spread_s, spread_f, sc = go(
        "stage_c", stage_c, (count, zb, sb, nb, wc), [((big, channels), BF16)],
        [((geo.rows, mid_1), BF16), acc(channels)], channels,
        jobs=(
            ("join", (fan_d,), 0, None, None), ("fan", (spread_e, he), 0, None, None),
            ("spread", (hs,), 0, None, None), ("spread", (hf,), 0, None, None),
        ),
    )
    wd = rows_of(wd)
    hid, first_g, first_l, zd, sub, we, fan_s, ws, sd = go(
        "stage_d", stage_d, (count, zc, sc, nc, packed, wd),
        [
            ((big, channels), BF16), (global_views.shape, BF16), (local_views.shape, BF16),
            ((big, mid_2), BF16), ((small, channels), BF16),
        ],
        [((channels // 128, geo.rows, 128), F32), acc(mid_2)], mid_2,
        jobs=(
            ("join", (fan_e,), 0, None, None), ("fan", (spread_s, hs), 0, None, 2),
            ("join", (1,), 2, None, None),
        ),
    )
    we, ws = rows_of(we), rows_of(ws)
    ze, zs, local_s, fan_f, wf, se = go(
        "stage_e", stage_e, (count, zd, sd, nd, we, sub, ws),
        [((small, mid_2), BF16), ((small, wide), BF16), stat(wide // 2)],
        [
            ((mid_2 // 128, geo.halo, 128), F32), ((small, 9 * mid_2), BF16), acc(mid_2), acc(wide),
        ],
        mid_2,
        jobs=(("fan", (spread_f, hf), 0, None, 2), ("join", (0,), 2, None, None)),
    )
    wf = rows_of(wf)
    act_e, zf, ss, sf = go(
        "stage_f", stage_f, (count, ze, se, ne, wf),
        [((small, mid_2), BF16), ((small, wide), BF16)], [acc(wide)], wide, side=local_s,
    )
    second_g, second_l, grad, local_pool, so = go(
        "stage_out", stage_out,
        (count, zf, zs, sf, ss, nf, ns, global_cotan, local_cotan),
        [
            (global_cotan.shape, BF16), (local_cotan.shape, BF16), ((small, wide), BF16),
            stat(wide // 4),
        ],
        [((geo.slabs, 8, wide), F32), ((geo.small, 512), F32), acc(wide, 8)], wide, 6,
    )
    unused, unused, back_sub, back_e, ngrad_f, ngrad_s, pair_f, pair_s, pool, qe = go(
        "stage_f_back", stage_f_back,
        (count, zf, zs, sf, ss, nf, ns, grad, so, act_e, sub, wf, ws, ze, se, ne),
        [
            pieces(wf), pieces(ws), ((small, channels), BF16), ((small, mid_2), BF16),
            both(wide), both(wide),
        ],
        [((small, wide), BF16), ((small, wide), BF16), acc(mid_2)], mid_2,
        jobs=(("pair", ("0",), 1, None, None), ("pair", ("1",), 2, None, None)), side=local_pool,
    )
    views = count[8, 0] * 6.0
    pool = pool.reshape(2, wide)
    center = pool[0] / views
    spread = pool[1] / views - center * center
    pooled_std = jnp.mean(jnp.sqrt(spread + 1e-06))
    wgrad_e, back_d, ngrad_e, rep_f, rep_s, qd = go(
        "stage_e_back", stage_e_back,
        (count, ze, se, ne, back_e, qe, zd, sd, nd, we),
        [pieces(we), ((big, mid_2), BF16), both(mid_2)],
        [
            ((mid_2 // 128, geo.halo, 128), F32), ((small, 9 * mid_2), BF16),
            ((small, mid_2), BF16), ((3, small, mid_2), BF16), ((4, small, mid_2), F32),
            acc(mid_2),
        ],
        mid_2, jobs=(("rep", (pair_f,), 0, 1, None), ("rep", (pair_s,), 0, 1, None)),
    )
    wgrad_d, joined, ngrad_d, unused, rep_e, line_f, line_s, qc = go(
        "stage_d_back", stage_d_back,
        (count, zd, sd, nd, back_d, qd, hid, packed, zc, sc, nc, back_sub, wd),
        [pieces(wd), ((big, channels), BF16), both(mid_2)],
        [((big, mid_2), BF16), ((channels // 128, geo.rows, 128), F32), acc(channels)], channels,
        jobs=(
            ("pair", (wgrad_e,), 0, None, 1), ("rep", (0,), 1, 2, None),
            ("line", (rep_f,), 0, None, None), ("line", (rep_s,), 0, None, None),
        ),
    )
    wgrad_c, back_b, ngrad_c, unused, rep_d, line_e, out_f, out_s, qb = go(
        "stage_c_back", stage_c_back,
        (count, zc, sc, nc, joined, qc, zb, sb, nb, wc),
        [pieces(wc), ((big, mid_1), BF16), both(channels)],
        [((big, channels), BF16), ((big, mid_1), BF16), acc(mid_1)], mid_1,
        jobs=(
            ("pair", (wgrad_d,), 0, None, 1), ("rep", (0,), 1, 2, None),
            ("line", (rep_e,), 0, None, None), ("share", (line_f,), 0, None, None),
            ("share", (line_s,), 0, None, None),
        ),
    )
    wgrad_b, back_a, ngrad_b, unused, rep_c, line_d, out_e, qa = go(
        "stage_b_back", stage_b_back,
        (count, zb, sb, nb, back_b, qb, za, sa, na, wb),
        [pieces(wb), ((big, mid_1), BF16), both(mid_1)],
        [
            ((geo.halo_total, 3 * mid_1), BF16), ((geo.halo_total, 3 * mid_1), BF16),
            ((9 * mid_1, mid_1), BF16), (wb.shape, F32), acc(mid_1),
        ],
        mid_1,
        jobs=(
            ("pair", (wgrad_c,), 0, None, 1), ("rep", (0,), 1, 2, None),
            ("line", (rep_d,), 0, None, None), ("share", (line_e,), 0, None, None),
        ),
    )
    more = go(
        "stage_a_back", stage_a_back, (count, za, sa, na, back_a, qa, packed),
        [pieces(wa), ((big, mid_1), BF16), both(mid_1)], [],
        jobs=(
            ("pair", (wgrad_b,), 0, None, 1), ("rep", (0,), 1, 2, 3), ("line", (1,), 3, None, 4),
            ("share", (2,), 4, None, None),
            ("pair", ("0",), 1, None, 2), ("rep", (4,), 2, 3, 4), ("line", (5,), 4, None, 5),
            ("share", (6,), 5, None, None),
            ("line", (rep_c,), 0, None, 1), ("share", (8,), 1, None, None),
            ("share", (line_d,), 0, None, None),
        ),
    )
    dza, ngrad_a, out_b, out_a, out_c, out_d = (more[k] for k in (1, 2, 6, 10, 12, 13))
    grad_g, grad_l, *columns = run_last(
        geo, joined, dza, wa, (out_a, out_b, out_c, out_d, out_e, out_f, out_s),
        global_views.shape, local_views.shape,
    )
    shard = lax.axis_index("fsdp")

    def own_columns(parts, width):
        whole = jnp.concatenate(parts, axis=1)
        return lax.dynamic_slice_in_dim(whole, shard * width, width, 1)

    return (
        first_g, first_l, second_g, second_l, grad_g, grad_l,
        *columns[0:3],
        own_columns((ngrad_a, ngrad_b, ngrad_c), first_norms.shape[1]),
        *columns[3:7],
        own_columns((ngrad_d, ngrad_e, ngrad_f, ngrad_s), second_norms.shape[1]),
        pooled_std,
    )


def solution(mesh):
    views = P(("rep", "fsdp"), None, None, None)
    columns = P(None, "fsdp")
    return jax.shard_map(
        functools.partial(body, mesh.shape["rep"], mesh.shape["fsdp"]),
        mesh=mesh,
        in_specs=(views, views, P(("rep", "fsdp"))) + (columns,) * 9 + (views, views),
        out_specs=(views,) * 6 + (columns,) * 9 + (P(),),
        check_vma=False,
    )
```

```python
import functools

import jax
import jax.numpy as jnp
from jax import lax
from jax.experimental import pallas as pl
from jax.experimental.pallas import tpu as pltpu
from jax.sharding import PartitionSpec as P

EPSILON = 1e-05
F32 = jnp.float32
BF16 = jnp.bfloat16
MESH = pl.DeviceIdType.MESH
CELLS = 16


def nt(left, right):
    return lax.dot_general(left, right, (((1,), (1,)), ((), ())), preferred_element_type=F32)


def nn(left, right):
    return lax.dot_general(left, right, (((1,), (0,)), ((), ())), preferred_element_type=F32)


def tn(left, right):
    return lax.dot_general(left, right, (((0,), (0,)), ((), ())), preferred_element_type=F32)


def sig(values):
    return 0.5 * jnp.tanh(0.5 * values) + 0.5


def silu(values):
    return values * sig(values)


def slope(values):
    gate = sig(values)
    held = values * gate
    return gate + held - held * gate


def lanes(tile, width):
    return jnp.concatenate([tile] * (width // tile.shape[1]), axis=1)


def fold(values):
    return jnp.sum(values.reshape(values.shape[0] // 8, 8, values.shape[1]), axis=0)


class Geometry:
    def __init__(self, views, side_global, side_local):
        self.slabs = views
        self.hg, self.hl = side_global, side_local
        assert side_global < CELLS and side_local < CELLS // 2
        self.rg, self.rl = side_global * CELLS, side_local * CELLS
        self.rows = self.rg + self.rl
        self.og, self.ol = (side_global - 1) // 2 + 1, (side_local - 1) // 2 + 1
        self.sg, self.sl = self.og * 8, self.ol * 8
        self.small = self.sg + self.sl
        self.total, self.small_total = self.slabs * self.rows, self.slabs * self.small
        self.halo = self.rows + 2 * CELLS
        self.halo_total = self.slabs * self.halo + CELLS
        self.chunk = 32
        assert self.rg % self.chunk == 0 and self.rl % self.chunk == 0 and self.small % 16 == 0

    def pieces(self, width):
        if width <= 256:
            return [(0, self.rg, 0), (self.rg, self.rl, 1)]
        step = self.chunk
        return [(start, step, 0) for start in range(0, self.rg, step)] + [
            (start, step, 1) for start in range(self.rg, self.rows, step)
        ]

    def mask(self, count, group, width):
        row = lax.broadcasted_iota(jnp.int32, (count, 128), 0)
        if group == 0:
            keep = (row & (CELLS - 1)) < self.hg
        else:
            keep = (row & (CELLS // 2 - 1)) < self.hl
        return lanes(keep.astype(F32), width)

    def small_mask(self, group, width):
        count = self.sl if group else self.sg
        row = lax.broadcasted_iota(jnp.int32, (count, 128), 0)
        keep = (row & 3) < self.ol if group else (row & 7) < self.og
        return lanes(keep.astype(F32), width)

    def small_pieces(self):
        return [(0, self.sg, 0), (self.sg, self.sl, 1)]


def alive(live, slab):
    return jnp.where(slab < 2 * live[0], 1.0, 0.0).astype(F32)


def cells(geo, count, group, width, small=False):
    images = lanes(count[8:9, 0:128], width)
    if small:
        return images * float(2 * geo.og * geo.og if group == 0 else 4 * geo.ol * geo.ol)
    return images * float(2 * geo.hg * geo.hg if group == 0 else 4 * geo.hl * geo.hl)


def member(sums, row, width):
    parts = width // sums.shape[1]
    return jnp.concatenate(
        [sums[row * parts + k : row * parts + k + 1, :] for k in range(parts)], axis=1
    )


def norm_terms(stats, norm, number, group):
    width = norm.shape[1]
    mean = member(stats, 2 * group, width) / number
    spread = member(stats, 2 * group + 1, width) / number - mean * mean
    inverse = lax.rsqrt(spread + EPSILON)
    scale = norm[0:1, :] * inverse
    return mean, inverse, scale, norm[1:2, :] - mean * scale


def back_terms(stats, norm, number, group, first, second_raw):
    mean, inverse, scale, unused = norm_terms(stats, norm, number, group)
    second = inverse * (second_raw - mean * first)
    by_value = -scale * inverse * (second / number)
    constant = -scale * (first / number) - by_value * mean
    return scale, by_value, constant, second


def forward_terms(geo, count, stats, norm, width, small=False):
    return [
        norm_terms(stats, norm, cells(geo, count, group, width, small), group)[2:]
        for group in range(2)
    ]


def backward_terms(geo, count, stats, norm, sums, out, width, small=False, rows=((0, 1), (2, 3))):
    terms = []
    seconds = []
    for group in range(2):
        number = cells(geo, count, group, width, small)
        first = member(sums, rows[group][0], width)
        raw = member(sums, rows[group][1], width)
        scale, by_value, constant, second = back_terms(stats, norm, number, group, first, raw)
        terms.append((scale, by_value, constant))
        seconds.append((second, first))
    out[0:1, :] = seconds[0][0] + seconds[1][0]
    out[1:2, :] = seconds[0][1] + seconds[1][1]
    return terms


def finish(stats, acc, members, begin=0):
    part = stats.shape[1]
    parts = acc.shape[2] // part
    for row in range(members):
        total = jnp.sum(acc[begin + row], axis=0, keepdims=True)
        for k in range(parts):
            stats[row * parts + k : row * parts + k + 1, :] = total[:, k * part : (k + 1) * part]


def put(store, place, values):
    for k in range(store.shape[0]):
        store[k, place, :] = values[:, k * 128 : (k + 1) * 128]


def take(store, place):
    return jnp.concatenate([store[k, place, :] for k in range(store.shape[0])], axis=1)


def put_pieces(pieces, first, values, begin=0):
    cores, chips, reps, size = pieces.shape[:4]
    cols = slice(begin, begin + values.shape[1])
    for k in range(values.shape[0] // size):
        index = first // size + k
        shard, rep = index // reps, index % reps
        part = values[k * size : (k + 1) * size]
        pieces[shard % cores, shard // cores, rep, :, cols] = part.astype(BF16)


def loop(count, step):
    def one(index, carry):
        step(index)
        return carry

    lax.fori_loop(0, count, one, 0)


def at(index, size):
    return pl.ds(pl.multiple_of(index * size, size), size)


def stage_a(geo, net, live, xg, xl, packed, conv, acc, weight, own_g, own_l, arrive):
    loads = (
        pltpu.make_async_copy(xg, own_g, arrive.at[0]),
        pltpu.make_async_copy(xl, own_l, arrive.at[1]),
    )
    for load in loads:
        load.start()
    net.open()
    acc[...] = jnp.zeros(acc.shape, F32)
    blank = jnp.zeros((CELLS, packed.shape[1]), BF16)
    half = CELLS // 2
    for load in loads:
        load.wait()

    def pack(s):
        base = s * geo.rows
        keep = alive(live, s).astype(BF16)
        for i in range(geo.hg):
            start = pl.multiple_of(base + i * CELLS, CELLS)
            packed[pl.ds(start, CELLS), :] = blank
            packed[pl.ds(start, geo.hg), :] = own_g[s, i] * keep
        for i in range(geo.hl):
            start = pl.multiple_of(base + geo.rg + i * CELLS, CELLS)
            packed[pl.ds(start, CELLS), :] = blank
            for side in range(2):
                place = pl.multiple_of(start + side * half, half)
                packed[pl.ds(place, geo.hl), :] = own_l[2 * s + side, i] * keep

    third = geo.slabs // 3
    loop(third, pack)
    net.turn(1)
    loop(third, lambda s: pack(s + third))
    net.turn(2)
    loop(geo.slabs - 2 * third, lambda s: pack(s + 2 * third))
    net.turn(3)
    gathered = net.job_out(2)
    weight[...] = gathered[...].astype(F32).reshape(weight.shape).astype(BF16)

    def slab(s):
        result = nt(packed[at(s, geo.rows), :], weight[...])
        conv[at(s, geo.rows), :] = result.astype(BF16)
        for start, size, group in geo.pieces(256):
            piece = result[start : start + size]
            acc[2 * group] += fold(piece)
            acc[2 * group + 1] += fold(piece * piece)

    loop(geo.slabs, slab)
    finish(net.own, acc, 4)
    net.own[8:16, :] = jnp.full((8, net.own.shape[1]), live[0], jnp.int32).astype(F32)
    net.turn(4)
    net.run()


def spread_taps(geo, store, s, values, reverse):
    width = values[0].shape[1]
    for group in range(2):
        rows = values[group]
        size = rows.shape[0]
        start = pl.multiple_of(s * geo.halo + CELLS + group * (geo.rg + CELLS), CELLS)
        before = pltpu.roll(rows, 1, 0)
        after = pltpu.roll(rows, size - 1, 0)
        order = (after, rows, before) if reverse else (before, rows, after)
        for tap in range(3):
            store[pl.ds(start, size), tap * width : (tap + 1) * width] = order[tap].astype(BF16)


def clear_halo(geo, store):
    blank = jnp.zeros((CELLS, store.shape[1]), BF16)

    def slab(s):
        store[pl.ds(pl.multiple_of(s * geo.halo, CELLS), CELLS), :] = blank
        store[pl.ds(pl.multiple_of(s * geo.halo + CELLS + geo.rg, CELLS), CELLS), :] = blank

    loop(geo.slabs, slab)
    store[geo.slabs * geo.halo : geo.slabs * geo.halo + CELLS, :] = blank


def activate(geo, live, conv, s, terms):
    values = []
    width = conv.shape[1]
    keep = alive(live, s)
    for group in range(2):
        start, size = (geo.rg, geo.rl) if group else (0, geo.rg)
        rows = conv[pl.ds(pl.multiple_of(s * geo.rows + start, CELLS), size), :].astype(F32)
        scale, shift = terms[group]
        values.append(silu(rows * scale + shift) * (geo.mask(size, group, width) * keep))
    return values


def stage_b(geo, net, live, count, za, stats_a, norm, weight, conv, taps, acc):
    net.open()
    acc[...] = jnp.zeros(acc.shape, F32)
    width = za.shape[1]
    terms = forward_terms(geo, count, stats_a, norm, width)
    clear_halo(geo, taps)
    loop(
        geo.slabs,
        lambda s: spread_taps(geo, taps, s, activate(geo, live, za, s, terms), False),
    )
    net.turn(1)
    span = geo.halo - CELLS

    def slab(s):
        result = None
        for dy in range(3):
            rows = taps[pl.ds(pl.multiple_of(s * geo.halo + dy * CELLS, CELLS), span), :]
            term = nt(rows, weight[:, dy * 3 * width : (dy + 1) * 3 * width])
            result = term if result is None else result + term
        keep = alive(live, s)
        for group, (begin, size) in enumerate(((0, geo.rg), (geo.rg + CELLS, geo.rl))):
            piece = result[begin : begin + size]
            start = pl.multiple_of(s * geo.rows + group * geo.rg, CELLS)
            conv[pl.ds(start, size), :] = piece.astype(BF16)
            piece = piece * (geo.mask(size, group, width) * keep)
            acc[2 * group] += fold(piece)
            acc[2 * group + 1] += fold(piece * piece)

    loop(geo.slabs, slab)
    net.turn(2)
    finish(net.own, acc, 4)
    net.run()


def stage_c(geo, net, live, count, zb, stats_b, norm, weight, conv, act, acc):
    net.open()
    acc[...] = jnp.zeros(acc.shape, F32)
    terms = forward_terms(geo, count, stats_b, norm, zb.shape[1])
    step = 256

    def slab(s):
        values = activate(geo, live, zb, s, terms)
        act[0 : geo.rg, :] = values[0].astype(BF16)
        act[geo.rg : geo.rows, :] = values[1].astype(BF16)
        for c in range(0, weight.shape[0], step):
            result = nt(act[...], weight[c : c + step, :])
            conv[at(s, geo.rows), c : c + step] = result.astype(BF16)
            for start, size, group in geo.pieces(256):
                piece = result[start : start + size]
                acc[2 * group, :, c : c + step] += fold(piece)
                acc[2 * group + 1, :, c : c + step] += fold(piece * piece)

    loop(geo.slabs, slab)
    net.turn(2)
    finish(net.own, acc, 4)
    net.run()


def even_rows(geo):
    return [2 * i * CELLS for i in range(geo.og)] + [
        geo.rg + 2 * i * CELLS for i in range(geo.ol)
    ]


def stage_d(
    geo, net, live, count, zc, stats_c, norm, packed, weight, hid, conv, sub, full, acc,
):
    net.open()
    acc[...] = jnp.zeros(acc.shape, F32)
    width = zc.shape[1]
    terms = forward_terms(geo, count, stats_c, norm, width)

    def slab(s):
        keep = alive(live, s)
        for start, size, group in geo.pieces(width):
            rows = pl.ds(pl.multiple_of(s * geo.rows + start, CELLS), size)
            scale, shift = terms[group]
            joined = zc[rows, :].astype(F32) * scale + shift + packed[rows, :].astype(F32)
            value = silu(joined) * (geo.mask(size, group, width) * keep)
            put(full, pl.ds(start, size), value)
            hid[rows, :] = value.astype(BF16)
        picked = [take(full, pl.ds(start, 8, stride=2)) for start in even_rows(geo)]
        sub[at(s, geo.small), :] = jnp.concatenate(picked, axis=0).astype(BF16)
        result = nt(hid[at(s, geo.rows), :], weight[...])
        conv[at(s, geo.rows), :] = result.astype(BF16)
        for start, size, group in geo.pieces(256):
            piece = result[start : start + size]
            acc[2 * group] += fold(piece)
            acc[2 * group + 1] += fold(piece * piece)

    loop(geo.slabs, slab)
    net.turn(2)
    finish(net.own, acc, 4)
    net.run()


def small_product(geo, left, pick, step, conv, acc, first, last):
    for c in range(first, last, step):
        result = nt(left[...], pick(c))
        conv[:, c : c + step] = result.astype(BF16)
        for s in range(geo.slabs):
            for start, size, group in geo.small_pieces():
                piece = result[s * geo.small + start : s * geo.small + start + size]
                acc[2 * group, :, c : c + step] += fold(piece)
                acc[2 * group + 1, :, c : c + step] += fold(piece * piece)


def gather_taps(geo, live, zd, terms, full, taps):
    width = zd.shape[1]
    blank = jnp.zeros((8, width), F32)
    full[:, 0:CELLS, :] = jnp.zeros((width // 128, CELLS, 128), F32)
    full[:, CELLS + geo.rg : 2 * CELLS + geo.rg, :] = jnp.zeros((width // 128, CELLS, 128), F32)

    def slab(s):
        keep = alive(live, s)
        for start, size, group in geo.pieces(width):
            rows = pl.ds(pl.multiple_of(s * geo.rows + start, CELLS), size)
            scale, shift = terms[group]
            value = silu(zd[rows, :].astype(F32) * scale + shift)
            begin = CELLS + start + group * CELLS
            put(full, pl.ds(begin, size), value * (geo.mask(size, group, width) * keep))
        for dy in range(3):
            for dx in range(3):
                picked = []
                for group in range(2):
                    for i in range(geo.ol if group else geo.og):
                        line = 2 * i + dy - 1
                        if line < 0:
                            picked.append(blank)
                            continue
                        begin = CELLS + group * (geo.rg + CELLS) + line * CELLS + dx - 1
                        picked.append(take(full, pl.ds(begin, 8, stride=2)))
                tap = dy * 3 + dx
                taps[at(s, geo.small), tap * width : (tap + 1) * width] = jnp.concatenate(
                    picked, axis=0
                ).astype(BF16)

    loop(geo.slabs, slab)


def stage_e(
    geo, net, live, count, zd, stats_d, norm, weight_0, weight_1, weight_2, sub, conv, conv_s,
    stats_s, full, taps, acc, acc_s,
):
    net.open()
    acc[...] = jnp.zeros(acc.shape, F32)
    acc_s[...] = jnp.zeros(acc_s.shape, F32)
    terms = forward_terms(geo, count, stats_d, norm, zd.shape[1])
    gather_taps(geo, live, zd, terms, full, taps)
    net.turn(1)
    step = 256
    third = weight_0.shape[1]
    for c in range(0, weight_0.shape[0], step):
        result = nt(taps[:, 0:third], weight_0[c : c + step, :])
        result = result + nt(taps[:, third : 2 * third], weight_1[c : c + step, :])
        result = result + nt(taps[:, 2 * third :], weight_2[c : c + step, :])
        conv[:, c : c + step] = result.astype(BF16)
        for s in range(geo.slabs):
            keep = alive(live, s)
            for start, size, group in geo.small_pieces():
                piece = result[s * geo.small + start : s * geo.small + start + size]
                piece = piece * (geo.small_mask(group, step) * keep)
                acc[2 * group, :, c : c + step] += fold(piece)
                acc[2 * group + 1, :, c : c + step] += fold(piece * piece)
    net.turn(2)
    finish(net.own, acc, 4)
    net.begin()
    short = net.job_out(0)
    step = short.shape[2] * short.shape[3]

    def pick(c):
        part = c // step
        return short[part // 2, part % 2].reshape(step, short.shape[4])

    half = conv_s.shape[1] // 2
    small_product(geo, sub, pick, step, conv_s, acc_s, 0, half)
    net.middle()
    small_product(geo, sub, pick, step, conv_s, acc_s, half, 2 * half)
    finish(stats_s, acc_s, 4)
    net.end()


def stage_f(geo, net, live, count, ze, stats_e, norm, weight, act, conv, acc):
    net.open()
    net.side.begin()
    acc[...] = jnp.zeros(acc.shape, F32)
    width = ze.shape[1]
    terms = forward_terms(geo, count, stats_e, norm, width, True)

    def slab(s):
        keep = alive(live, s)
        rows = ze[at(s, geo.small), :].astype(F32)
        parts = []
        for start, size, group in geo.small_pieces():
            scale, shift = terms[group]
            value = silu(rows[start : start + size] * scale + shift)
            parts.append(value * (geo.small_mask(group, width) * keep))
        act[at(s, geo.small), :] = jnp.concatenate(parts, axis=0).astype(BF16)

    loop(geo.slabs, slab)
    half, step = weight.shape[0] // 2, 256

    def pick(c):
        return weight[c : c + step, :]

    small_product(geo, act, pick, step, conv, acc, 0, half)
    net.side.middle()
    small_product(geo, act, pick, step, conv, acc, half, 2 * half)
    net.side.end()
    finish(net.own, acc, 4)
    net.run()


def stage_out(
    geo, net, live, count, zf, zs, stats_f, stats_s, norm_f, norm_s, cotg, cotl, outg, outl, grad,
    pooled_sums, pool, cot, acc,
):
    acc[...] = jnp.zeros(acc.shape, F32)
    cot[...] = jnp.zeros(cot.shape, F32)
    pool[...] = jnp.zeros(pool.shape, F32)
    width = zf.shape[1]
    step = 512
    terms_f = forward_terms(geo, count, stats_f, norm_f, width, True)
    terms_s = forward_terms(geo, count, stats_s, norm_s, width, True)

    def slab(s):
        keep = alive(live, s)
        for c in range(0, width, step):
            cols = slice(c, c + step)
            for i in range(geo.og):
                cot[i * 8 : i * 8 + geo.og, :] = cotg[s, i, :, cols].astype(F32)
            for i in range(geo.ol):
                for side in range(2):
                    begin = geo.sg + i * 8 + side * 4
                    cot[begin : begin + geo.ol, :] = cotl[2 * s + side, i, :, cols].astype(F32)
            rows_f = zf[at(s, geo.small), cols].astype(F32)
            rows_s = zs[at(s, geo.small), cols].astype(F32)
            grads = []
            for start, size, group in geo.small_pieces():
                part = slice(start, start + size)
                vf, vs = rows_f[part], rows_s[part]
                scale_f, shift_f = (item[:, cols] for item in terms_f[group])
                scale_s, shift_s = (item[:, cols] for item in terms_s[group])
                joined = vf * scale_f + vs * scale_s + (shift_f + shift_s)
                mask = geo.small_mask(group, step) * keep
                gate = sig(joined)
                held = joined * gate
                value = held * mask
                low = value.astype(BF16)
                dy = cot[part, :] * ((gate + held - held * gate) * mask)
                grads.append(dy)
                acc[3 * group, :, cols] += fold(dy)
                acc[3 * group + 1, :, cols] += fold(dy * vf)
                acc[3 * group + 2, :, cols] += fold(dy * vs)
                summed = fold(value)
                if group == 0:
                    for i in range(geo.og):
                        outg[s, i, :, cols] = value[i * 8 : i * 8 + geo.og].astype(BF16)
                    pool[s, 0:1, cols] = jnp.sum(summed, axis=0, keepdims=True) * (
                        1.0 / (geo.og * geo.og)
                    )
                else:
                    row = lax.broadcasted_iota(jnp.int32, (8, step), 0)
                    for side in range(2):
                        own = jnp.where((row >= 4) == (side == 1), summed, 0.0)
                        pool[s, 1 + side : 2 + side, cols] = jnp.sum(
                            own, axis=0, keepdims=True
                        ) * (1.0 / (geo.ol * geo.ol))
                        for i in range(geo.ol):
                            begin = i * 8 + side * 4
                            outl[2 * s + side, i, :, cols] = value[begin : begin + geo.ol].astype(
                                BF16
                            )
            grad[at(s, geo.small), cols] = jnp.concatenate(grads, axis=0).astype(BF16)
        pooled = pool[s]
        square = jnp.mean(pooled * pooled, axis=1, keepdims=True)
        normed = pooled * lax.rsqrt(square + 1e-06)
        acc[6] += normed
        acc[7] += normed * normed

    loop(geo.slabs, slab)
    finish(net.own, acc, 6)
    net.begin()
    finish(pooled_sums, acc, 2, 6)
    net.middle()
    net.end()


def small_back(geo, live, s, grad, conv, terms, width, cols):
    keep = alive(live, s)
    rows_g = grad[at(s, geo.small), cols].astype(F32)
    rows_z = conv[at(s, geo.small), cols].astype(F32)
    parts = []
    for start, size, group in geo.small_pieces():
        scale, by_value, constant = (item[:, cols] for item in terms[group])
        part = slice(start, start + size)
        value = rows_g[part] * scale + rows_z[part] * by_value + constant
        parts.append(value * (geo.small_mask(group, width) * keep))
    return jnp.concatenate(parts, axis=0).astype(BF16)


def stage_f_back(
    geo, net, live, count, zf, zs, stats_f, stats_s, norm_f, norm_s, grad, sums, act, sub, weight,
    short, ze, stats_e, norm_e, wgrad_f, wgrad_s, back_sub, back_e, ngrad_f, ngrad_s, dzf, dzs, acc,
):
    acc[...] = jnp.zeros(acc.shape, F32)
    width = zf.shape[1]
    step = 512
    rows_f, rows_s = ((0, 1), (3, 4)), ((0, 2), (3, 5))
    terms_f = backward_terms(geo, count, stats_f, norm_f, sums, ngrad_f, width, True, rows_f)
    terms_s = backward_terms(geo, count, stats_s, norm_s, sums, ngrad_s, width, True, rows_s)

    def slab(s):
        for c in range(0, width, step):
            cols = slice(c, c + step)
            dzf[at(s, geo.small), cols] = small_back(geo, live, s, grad, zf, terms_f, step, cols)
            dzs[at(s, geo.small), cols] = small_back(geo, live, s, grad, zs, terms_s, step, cols)

    loop(geo.slabs, slab)
    net.open()
    net.side.begin()
    block = 256
    terms_e = forward_terms(geo, count, stats_e, norm_e, ze.shape[1], True)
    for c in range(0, act.shape[1], block):
        cols = slice(c, c + block)
        result = nn(dzf[...], weight[:, cols])
        for s in range(geo.slabs):
            keep = alive(live, s)
            rows = ze[s * geo.small : (s + 1) * geo.small, cols].astype(F32)
            parts = []
            for start, size, group in geo.small_pieces():
                scale, shift = (item[:, cols] for item in terms_e[group])
                value = rows[start : start + size]
                mask = geo.small_mask(group, block) * keep
                piece = result[s * geo.small + start : s * geo.small + start + size]
                piece = piece * (slope(value * scale + shift) * mask)
                parts.append(piece)
                acc[2 * group, :, cols] += fold(piece)
                acc[2 * group + 1, :, cols] += fold(piece * value)
            back_e[s * geo.small : (s + 1) * geo.small, cols] = jnp.concatenate(
                parts, axis=0
            ).astype(BF16)
    finish(net.own, acc, 4)
    net.begin()
    for c in range(0, width, block):
        cols = slice(c, c + block)
        put_pieces(wgrad_s, c, tn(dzs[:, cols], sub[...]))
    net.side.middle()
    net.middle()
    net.turn(1)
    for c in range(0, width, block):
        cols = slice(c, c + block)
        put_pieces(wgrad_f, c, tn(dzf[:, cols], act[...]))
    net.turn(2)
    for c in range(0, sub.shape[1], block):
        cols = slice(c, c + block)
        back_sub[:, cols] = nn(dzs[...], short[:, cols]).astype(BF16)
    net.side.end()
    net.end()


def stage_e_back(
    geo, net, live, count, ze, stats_e, norm_e, back_e, sums_e, zd, stats_d, norm_d, weight_0, weight_1,
    weight_2, wgrad, back_d, ngrad, full, taps, dze, moved, parity, acc,
):
    net.open()
    acc[...] = jnp.zeros(acc.shape, F32)
    width = ze.shape[1]
    terms_e = backward_terms(geo, count, stats_e, norm_e, sums_e, ngrad, width, True)
    terms_d = forward_terms(geo, count, stats_d, norm_d, width)
    gather_taps(geo, live, zd, terms_d, full, taps)

    def shift(s):
        value = small_back(geo, live, s, back_e, ze, terms_e, width, slice(0, width)).astype(F32)
        blank = jnp.zeros((8, width), F32)
        down = jnp.concatenate(
            [value[8 : geo.sg], blank, value[geo.sg + 8 :], blank], axis=0
        )
        size = geo.small
        dze[at(s, size), :] = value.astype(BF16)
        moved[0, at(s, size), :] = pltpu.roll(value, size - 1, 0).astype(BF16)
        moved[1, at(s, size), :] = down.astype(BF16)
        moved[2, at(s, size), :] = pltpu.roll(down, size - 1, 0).astype(BF16)

    loop(geo.slabs, shift)

    def tap(dy, dx):
        return (weight_0, weight_1, weight_2)[dy][:, dx * width : (dx + 1) * width]

    def grads(first, last):
        for t in range(first, last):
            result = tn(dze[...], taps[:, t * width : (t + 1) * width])
            put_pieces(wgrad, 0, result, t * width)

    parity[0] = nn(dze[...], tap(1, 1))
    parity[1] = nn(dze[...], tap(1, 2)) + nn(moved[0], tap(1, 0))
    parity[2] = nn(dze[...], tap(2, 1)) + nn(moved[1], tap(0, 1))
    parity[3] = (
        nn(dze[...], tap(2, 2))
        + nn(moved[0], tap(2, 0))
        + nn(moved[1], tap(0, 2))
        + nn(moved[2], tap(0, 0))
    )

    def slab(s):
        keep = alive(live, s)
        for group in range(2):
            for i in range(geo.ol if group else geo.og):
                for a in range(2):
                    for b in range(2):
                        begin = group * geo.rg + (2 * i + a) * CELLS + b
                        source = s * geo.small + group * geo.sg + i * 8
                        part = parity[2 * a + b, pl.ds(pl.multiple_of(source, 8), 8), :]
                        put(full, pl.ds(begin, 8, stride=2), part)
        for start, size, group in geo.pieces(width):
            rows = pl.ds(pl.multiple_of(s * geo.rows + start, CELLS), size)
            scale, shift_d = terms_d[group]
            value = zd[rows, :].astype(F32)
            mask = geo.mask(size, group, width) * keep
            piece = take(full, pl.ds(start, size)) * (slope(value * scale + shift_d) * mask)
            back_d[rows, :] = piece.astype(BF16)
            acc[2 * group] += fold(piece)
            acc[2 * group + 1] += fold(piece * value)

    loop(geo.slabs, slab)
    finish(net.own, acc, 4)
    net.begin()
    grads(0, 4)
    net.middle()
    grads(4, 9)
    net.end()


def wide_back(geo, live, s, grad, conv, terms, low):
    width = conv.shape[1]
    keep = alive(live, s)
    for start, size, group in geo.pieces(width):
        rows = pl.ds(pl.multiple_of(s * geo.rows + start, CELLS), size)
        scale, by_value, constant = terms[group]
        value = grad[rows, :].astype(F32) * scale + conv[rows, :].astype(F32) * by_value + constant
        low[rows, :] = (value * (geo.mask(size, group, width) * keep)).astype(BF16)


def stage_d_back(
    geo, net, live, count, zd, stats_d, norm_d, back_d, sums_d, hid, packed, zc, stats_c, norm_c,
    back_sub, weight, wgrad, joined, ngrad, dzd, full, acc,
):
    acc[...] = jnp.zeros(acc.shape, F32)
    width = zc.shape[1]
    terms_d = backward_terms(geo, count, stats_d, norm_d, sums_d, ngrad, zd.shape[1])
    terms_c = forward_terms(geo, count, stats_c, norm_c, width)

    net.open()

    def slab(s):
        wide_back(geo, live, s, back_d, zd, terms_d, dzd)
        put(full, pl.ds(0, geo.rows), nn(dzd[at(s, geo.rows), :], weight[...]))
        extra = back_sub[at(s, geo.small), :].astype(F32)
        for k, start in enumerate(even_rows(geo)):
            place = pl.ds(start, 8, stride=2)
            put(full, place, take(full, place) + extra[k * 8 : k * 8 + 8])
        keep = alive(live, s)
        for start, size, group in geo.pieces(width):
            rows = pl.ds(pl.multiple_of(s * geo.rows + start, CELLS), size)
            scale, shift = terms_c[group]
            value = zc[rows, :].astype(F32)
            pre = value * scale + shift + packed[rows, :].astype(F32)
            mask = geo.mask(size, group, width) * keep
            piece = take(full, pl.ds(start, size)) * (slope(pre) * mask)
            joined[rows, :] = piece.astype(BF16)
            acc[2 * group] += fold(piece)
            acc[2 * group + 1] += fold(piece * value)

    third = geo.slabs // 3
    loop(third, slab)
    net.turn(1)
    loop(geo.slabs - third, lambda s: slab(s + third))
    net.turn(2)
    finish(net.own, acc, 4)
    block = 256
    net.begin()
    for c in range(0, dzd.shape[1], block):
        put_pieces(wgrad, c, tn(dzd[:, c : c + block], hid[...]))
        if c == 0:
            net.middle()
    net.end()


def stage_c_back(
    geo, net, live, count, zc, stats_c, norm_c, joined, sums_c, zb, stats_b, norm_b, weight, wgrad,
    back_b, ngrad, dzc, act, acc,
):
    acc[...] = jnp.zeros(acc.shape, F32)
    terms_c = backward_terms(geo, count, stats_c, norm_c, sums_c, ngrad, zc.shape[1])
    terms_b = forward_terms(geo, count, stats_b, norm_b, zb.shape[1])
    width = zb.shape[1]

    net.open()

    def slab(s):
        wide_back(geo, live, s, joined, zc, terms_c, dzc)
        result = nn(dzc[at(s, geo.rows), :], weight[...])
        keep = alive(live, s)
        for start, size, group in geo.pieces(width):
            rows = pl.ds(pl.multiple_of(s * geo.rows + start, CELLS), size)
            scale, shift = terms_b[group]
            value = zb[rows, :].astype(F32)
            pre = value * scale + shift
            mask = geo.mask(size, group, width) * keep
            gate = sig(pre)
            held = pre * gate
            act[rows, :] = (held * mask).astype(BF16)
            piece = result[start : start + size] * ((gate + held - held * gate) * mask)
            back_b[rows, :] = piece.astype(BF16)
            acc[2 * group] += fold(piece)
            acc[2 * group + 1] += fold(piece * value)

    half = geo.slabs // 2
    loop(half, slab)
    net.turn(1)
    loop(geo.slabs - half, lambda s: slab(s + half))
    net.turn(2)
    finish(net.own, acc, 4)
    net.begin()
    half = dzc.shape[1] // 2
    put_pieces(wgrad, 0, tn(dzc[:, 0:half], act[...]))
    net.middle()
    put_pieces(wgrad, half, tn(dzc[:, half:], act[...]))
    net.end()


def stage_b_back(
    geo, net, live, count, zb, stats_b, norm_b, back_b, sums_b, za, stats_a, norm_a, weight, wgrad,
    back_a, ngrad, taps, dtaps, stacked, total, acc,
):
    acc[...] = jnp.zeros(acc.shape, F32)
    width = za.shape[1]
    terms_b = backward_terms(geo, count, stats_b, norm_b, sums_b, ngrad, width)
    terms_a = forward_terms(geo, count, stats_a, norm_a, width)
    clear_halo(geo, taps)
    clear_halo(geo, dtaps)
    for t in range(9):
        stacked[t * width : (t + 1) * width, :] = weight[:, t * width : (t + 1) * width]

    def fill(s):
        spread_taps(geo, taps, s, activate(geo, live, za, s, terms_a), False)
        keep = alive(live, s)
        values = []
        for start, size, group in geo.pieces(width):
            rows = pl.ds(pl.multiple_of(s * geo.rows + start, CELLS), size)
            scale, by_value, constant = terms_b[group]
            value = back_b[rows, :].astype(F32) * scale + zb[rows, :].astype(F32) * by_value
            values.append((value + constant) * (geo.mask(size, group, width) * keep))
        spread_taps(geo, dtaps, s, values, True)

    net.open()
    loop(geo.slabs, fill)
    net.turn(1)
    span = geo.halo - CELLS
    total[...] = jnp.zeros(total.shape, F32)

    def slab(s):
        result = None
        for dy in range(3):
            begin = pl.multiple_of(s * geo.halo + (2 - dy) * CELLS, CELLS)
            term = nn(
                dtaps[pl.ds(begin, span), :], stacked[dy * 3 * width : (dy + 1) * 3 * width, :]
            )
            result = term if result is None else result + term
        keep = alive(live, s)
        for group, (begin, size) in enumerate(((0, geo.rg), (geo.rg + CELLS, geo.rl))):
            rows = pl.ds(pl.multiple_of(s * geo.rows + group * geo.rg, CELLS), size)
            scale, shift = terms_a[group]
            value = za[rows, :].astype(F32)
            mask = geo.mask(size, group, width) * keep
            piece = result[begin : begin + size] * (slope(value * scale + shift) * mask)
            back_a[rows, :] = piece.astype(BF16)
            acc[2 * group] += fold(piece)
            acc[2 * group + 1] += fold(piece * value)

    def grads(s):
        own = dtaps[
            pl.ds(pl.multiple_of(s * geo.halo + CELLS, CELLS), span), width : 2 * width
        ]
        for dy in range(3):
            begin = pl.multiple_of(s * geo.halo + dy * CELLS, CELLS)
            total[:, dy * 3 * width : (dy + 1) * 3 * width] += tn(own, taps[pl.ds(begin, span), :])

    loop(geo.slabs, slab)
    net.turn(2)
    finish(net.own, acc, 4)
    half = geo.slabs // 2
    net.begin()
    loop(half, grads)
    net.middle()
    loop(geo.slabs - half, lambda s: grads(s + half))
    put_pieces(wgrad, 0, total[...])
    net.end()


def stage_a_back(
    geo, net, live, count, za, stats_a, norm_a, back_a, sums_a, packed, wgrad, dza, ngrad,
):
    net.open()
    terms_a = backward_terms(geo, count, stats_a, norm_a, sums_a, ngrad, za.shape[1])
    loop(geo.slabs, lambda s: wide_back(geo, live, s, back_a, za, terms_a, dza))
    put_pieces(wgrad, 0, tn(dza[...], packed[...]))
    for number in range(1, 8):
        net.turn(number)
    net.close()


def last_kernel(geo, upright, joined, dza, hid, weight, *refs):
    count = len(upright)
    rows_in, refs = refs[:count], refs[count:]
    dxg, dxl, outg, outl = refs[:4]
    targets = refs[4:]
    result = nn(dza[...], weight[...]) + joined[...].astype(F32)
    half = CELLS // 2
    for i in range(geo.hg):
        dxg[0, i] = result[i * CELLS : i * CELLS + geo.hg]
        outg[0, i] = hid[i * CELLS : (i + 1) * CELLS, :][0 : geo.hg]
    for i in range(geo.hl):
        begin = geo.rg + i * CELLS
        low = hid[begin : begin + CELLS, :]
        for side in range(2):
            part = begin + side * half
            dxl[side, i] = result[part : part + geo.hl]
            outl[side, i] = low[side * half : side * half + geo.hl]

    def write(k):
        @pl.when(pl.program_id(0) == k % geo.slabs)
        def one():
            source, target = rows_in[k], targets[k]
            rows = source.shape[0] * source.shape[1]
            whole = source[...].astype(F32).reshape(rows, source.shape[2])
            target[...] = whole.T if upright[k] else whole

    for k in range(count):
        write(k)


def run_last(geo, joined, dza, hid, weight, parts, global_shape, local_shape):
    def whole(shape):
        return pl.BlockSpec(shape, lambda s: (0,) * len(shape))

    upright = [part.shape[0] * part.shape[1] >= 128 for part in parts]
    shapes = []
    for turn, part in zip(upright, parts):
        rows = part.shape[0] * part.shape[1]
        shapes.append((part.shape[2], rows) if turn else (rows, part.shape[2]))
    views = [
        pl.BlockSpec((1,) + global_shape[1:], lambda s: (s, 0, 0, 0)),
        pl.BlockSpec((2,) + local_shape[1:], lambda s: (s, 0, 0, 0)),
    ]
    outs = pl.pallas_call(
        functools.partial(last_kernel, geo, upright),
        grid=(geo.slabs,),
        out_shape=[
            jax.ShapeDtypeStruct(shape, dtype)
            for dtype in (F32, BF16)
            for shape in (global_shape, local_shape)
        ]
        + [jax.ShapeDtypeStruct(shape, F32) for shape in shapes],
        in_specs=[
            pl.BlockSpec((geo.rows, item.shape[1]), lambda s: (s, 0)) for item in (joined, dza, hid)
        ]
        + [whole(weight.shape)]
        + [whole(part.shape) for part in parts],
        out_specs=views + views + [whole(shape) for shape in shapes],
        compiler_params=pltpu.CompilerParams(vmem_limit_bytes=VMEM_CAP),
        name="last",
    )(joined, dza, hid, weight, *parts)
    return outs[:4], [item if turn else item.T for turn, item in zip(upright, outs[4:])]


class Sums:
    def __init__(self, reps, shards, own, out, first, second, sems):
        self.reps, self.shards = reps, shards
        self.own, self.out, self.first, self.second = own, out, first, second
        self.sems = sems
        self.rep, self.shard = lax.axis_index("rep"), lax.axis_index("fsdp")
        self.copies = []

    def begin(self):
        self.copies = []
        for hop in range(1, self.shards):
            copy = pltpu.make_async_remote_copy(
                self.own, self.first.at[self.shard], self.sems[0].at[hop], self.sems[1].at[hop],
                device_id={"fsdp": lax.rem(self.shard + hop, self.shards)}, device_id_type=MESH,
            )
            copy.start()
            self.copies.append(copy)
        self.first[self.shard] = self.own[...]

    def middle(self):
        for copy in self.copies:
            copy.wait()
        total = self.first[0]
        for k in range(1, self.shards):
            total = total + self.first[k]
        self.second[self.rep] = total
        self.copies = []
        for hop in range(1, self.reps):
            place = self.second.at[self.rep]
            copy = pltpu.make_async_remote_copy(
                place, place, self.sems[2].at[hop], self.sems[3].at[hop],
                device_id={"rep": lax.rem(self.rep + hop, self.reps)}, device_id_type=MESH,
            )
            copy.start()
            self.copies.append(copy)

    def end(self):
        for copy in self.copies:
            copy.wait()
        total = self.second[0]
        for k in range(1, self.reps):
            total = total + self.second[k]
        self.out[...] = total


class Net:
    def __init__(self, reps, shards, sums=None, side=None, jobs=(), plans=()):
        self.reps, self.shards = reps, shards
        self.sums, self.side, self.jobs, self.plans = sums, side, jobs, plans
        self.own = None if sums is None else sums.own
        self.opened = False
        self.started, self.finished = set(), set()

    def enter(self):
        rep, shard = lax.axis_index("rep"), lax.axis_index("fsdp")
        barrier = pltpu.get_barrier_semaphore()
        for hop in range(1, self.shards):
            other = {"fsdp": lax.rem(shard + hop, self.shards)}
            pl.semaphore_signal(barrier, inc=1, device_id=other, device_id_type=MESH)
        for hop in range(1, self.reps):
            other = {"rep": lax.rem(rep + hop, self.reps)}
            pl.semaphore_signal(barrier, inc=1, device_id=other, device_id_type=MESH)

    def open(self):
        if not self.opened:
            self.opened = True
            pl.semaphore_wait(pltpu.get_barrier_semaphore(), self.shards + self.reps - 2)
            self.turn(0)

    def turn(self, number):
        for k, (start, end) in enumerate(self.plans):
            if end == number:
                self.finish(k)
        for k, (start, end) in enumerate(self.plans):
            if start == number:
                self.started.add(k)
                self.jobs[k].start()

    def finish(self, k):
        assert k in self.started and k not in self.finished
        self.finished.add(k)
        self.jobs[k].finish()

    def job_out(self, k):
        return self.jobs[k].out

    def begin(self):
        self.open()
        self.sums.begin()

    def middle(self):
        self.sums.middle()

    def end(self):
        self.sums.end()
        self.close()

    def run(self):
        self.begin()
        self.middle()
        self.end()

    def close(self):
        for k in range(len(self.jobs)):
            if k not in self.finished:
                self.finish(k)


class Job:
    def __init__(self, kind, reps, shards, sources, out, held, send, recv):
        self.kind, self.source, self.out, self.held = kind, sources[0], out, held
        self.sources = sources
        self.send, self.recv = send, recv
        self.reps, self.chips = reps, shards // 2
        self.rep, shard = lax.axis_index("rep"), lax.axis_index("fsdp")
        self.chip, self.core = shard // 2, lax.rem(shard, 2)
        if kind in ("pair", "join"):
            self.members, self.me = 2, self.core
            self.address = lambda k: {"fsdp": self.chip * 2 + k}
        elif kind in ("line", "spread"):
            self.members, self.me = self.chips, self.chip
            self.address = lambda k: {"fsdp": k * 2 + self.core}
        elif kind == "all":
            self.members, self.me = shards, shard
            self.address = lambda k: {"fsdp": k}
        elif kind == "half":
            wide = reps // 2
            even = lax.rem(self.rep, 2) == 0
            self.members, self.me = 2, 0
            aside = jnp.where(even, self.rep + 1, self.rep - 1)
            across = lax.rem(self.rep + wide, reps)
            self.address = lambda k: {"rep": jnp.where(self.core == 0, aside, across)}
        elif kind == "rest":
            wide = reps // 2
            low, high = lax.rem(self.rep, 2), self.rep // wide
            first = self.core == 0
            self.members = wide
            self.me = jnp.where(first, self.rep // 2, lax.rem(self.rep, wide))
            self.address = lambda k: {"rep": jnp.where(first, k * 2 + low, high * wide + k)}
        else:
            self.members, self.me = reps, self.rep
            self.address = lambda k: {"rep": k}

    def give(self, source, target, hop):
        other = lax.rem(self.me + hop, self.members)
        k = len(self.copies)
        if hop == 0:
            copy = pltpu.make_async_copy(source, target, self.send.at[k])
        else:
            copy = pltpu.make_async_remote_copy(
                source, target, self.send.at[k], self.recv.at[k],
                device_id=self.address(other), device_id_type=MESH,
            )
        copy.start()
        self.copies.append(copy)

    def start(self):
        self.copies = []
        kind, out = self.kind, self.out
        order = list(range(1, self.members)) + [0]
        if kind == "spread":
            for hop in order:
                self.give(self.source.at[self.rep], out.at[self.chip], hop)
        elif kind == "fan":
            for hop in order:
                for step in range(1, self.chips):
                    chip = lax.rem(self.chip + step, self.chips)
                    self.give(self.source.at[chip], out.at[chip, self.rep], hop)
            self.give(self.sources[1], out.at[self.chip], 0)
        elif kind == "join":
            for hop in order:
                for chip in range(self.chips):
                    self.give(self.source.at[chip], out.at[chip, self.core], hop)
        elif kind in ("all", "share"):
            for hop in order:
                self.give(self.source, out.at[self.me], hop)
        elif kind == "half":
            wide = self.reps // 2
            first = self.core == 0
            low, high = lax.rem(self.rep, 2), self.rep // wide
            mine = jnp.where(first, low, high * wide)
            theirs = jnp.where(first, 1 - low, (1 - high) * wide)
            step = jnp.where(first, 2, 1)
            for k in range(wide):
                self.give(self.source.at[theirs + k * step], self.held.at[1, k], 1)
            for k in range(wide):
                self.give(self.source.at[mine + k * step], self.held.at[0, k], 0)
        else:
            for hop in order:
                other = lax.rem(self.me + hop, self.members)
                self.give(self.source.at[other], self.held.at[self.me], hop)

    def finish(self):
        for copy in self.copies:
            copy.wait()
        held, out = self.held, self.out
        if held is None:
            return
        blocks = held.shape[1:-2]

        def one(index):
            place = (index // blocks[-1], lax.rem(index, blocks[-1])) if len(blocks) == 2 else (
                (index,) if blocks else ()
            )
            total = held[(0,) + place].astype(F32)
            for k in range(1, self.members):
                total = total + held[(k,) + place].astype(F32)
            out[place[::-1] if self.kind == "pair" else place] = total.astype(BF16)

        if blocks:
            loop(blocks[0] * (blocks[1] if len(blocks) == 2 else 1), one)
        else:
            total = held[0].astype(F32)
            for k in range(1, self.members):
                total = total + held[k].astype(F32)
            out[...] = total.astype(BF16)


def job_shapes(kind, reps, shards, shape):
    chips = shards // 2
    if kind == "spread":
        return None, (chips,) + shape[1:], chips
    if kind == "fan":
        return None, (chips, reps) + shape[1:], reps * (chips - 1) + 1
    if kind == "join":
        return None, (chips, 2) + shape[1:], 2 * chips
    if kind == "all":
        return None, (shards,) + shape, shards
    if kind == "pair":
        return shape, (shape[2], shape[1]) + shape[3:], 2
    if kind == "share":
        return None, (reps,) + shape, reps
    if kind == "half":
        return (2, reps // 2) + shape[1:], (reps // 2,) + shape[1:], reps
    return shape, shape[1:], shape[0]


VMEM_CAP = 60 << 20
FAR = ("spread", "fan")


def sums_scratch(reps, shards, shape, own):
    return [pltpu.VMEM(shape, F32)] * own + [
        pltpu.VMEM((shards,) + shape, F32),
        pltpu.VMEM((reps,) + shape, F32),
        pltpu.SemaphoreType.DMA((shards,)),
        pltpu.SemaphoreType.DMA((shards,)),
        pltpu.SemaphoreType.DMA((reps,)),
        pltpu.SemaphoreType.DMA((reps,)),
    ]


def run(name, kernel, geo, reps, shards, number, live, operands, results, scratch, sums, jobs, side, far=()):
    own_results = len(results)
    results = list(results)
    spaces = [pltpu.VMEM] * own_results
    extra = []
    arrays = []
    shapes = []
    for kind, sources, start, end in jobs:
        source = sources[0]
        if isinstance(source, int):
            shape, dtype = shapes[source]
        elif isinstance(source, str):
            shape, dtype = results[int(source)]
        else:
            shape, dtype = source.shape, source.dtype
        arrays += [item for item in sources if not isinstance(item, (int, str))]
        held, out, copies = job_shapes(kind, reps, shards, shape)
        shapes.append((out, dtype))
        results.append(shapes[-1])
        spaces.append(pltpu.HBM if kind in FAR else pltpu.VMEM)
        extra += [] if held is None else [pltpu.VMEM(held, BF16)]
        extra += [pltpu.SemaphoreType.DMA((copies,))] * 2
    operands = tuple(operands)
    near = len(operands)
    if side is not None:
        operands += (side,)
        results.append((side.shape, F32))
        spaces.append(pltpu.VMEM)
        extra += sums_scratch(reps, shards, side.shape, 0)
    if sums is not None:
        results.append((sums, F32))
        spaces.append(pltpu.VMEM)
        extra += sums_scratch(reps, shards, sums, 1)
    inputs = 1 + len(operands)
    remote = bool(jobs) or sums is not None

    def whole(*refs):
        sources_in = list(refs[inputs : inputs + len(arrays)])
        first_out = inputs + len(arrays)
        outs = refs[first_out : first_out + len(results)]
        more = list(refs[first_out + len(results) :])
        made = []
        for k, (kind, sources, start, end) in enumerate(jobs):
            refs_of = []
            for item in sources:
                if isinstance(item, int):
                    refs_of.append(made[item].out)
                elif isinstance(item, str):
                    refs_of.append(outs[int(item)])
                else:
                    refs_of.append(sources_in.pop(0))
            held = more.pop(0) if job_shapes(kind, reps, shards, refs_of[0].shape)[0] else None
            made.append(
                Job(kind, reps, shards, refs_of, outs[own_results + k], held, more.pop(0), more.pop(0))
            )
        beside, main = None, None
        place = own_results + len(jobs)
        if side is not None:
            beside = Sums(reps, shards, refs[near + 1], outs[place], more[0], more[1], more[2:6])
            more = more[6:]
        if sums is not None:
            main = Sums(reps, shards, more[0], outs[-1], more[1], more[2], more[3:7])
            more = more[7:]
        net = None
        if remote:
            plans = [job[2:] for job in jobs]
            net = Net(reps, shards, main, beside, made, plans)
            net.enter()
        kernel(geo, net, *refs[: near + 1], *outs[:own_results], *more)

    params = {"collective_id": number, "has_side_effects": True} if remote else {}
    return pl.pallas_call(
        whole,
        out_shape=[jax.ShapeDtypeStruct(shape, dtype) for shape, dtype in results],
        in_specs=[pl.BlockSpec(memory_space=pltpu.SMEM)]
        + [pl.BlockSpec(memory_space=pltpu.HBM if k in far else pltpu.VMEM) for k in range(len(operands))]
        + [pl.BlockSpec(memory_space=pl.ANY)] * len(arrays),
        out_specs=[pl.BlockSpec(memory_space=space) for space in spaces],
        scratch_shapes=extra
        + [item if not isinstance(item, tuple) else pltpu.VMEM(*item) for item in scratch],
        compiler_params=pltpu.CompilerParams(vmem_limit_bytes=VMEM_CAP, **params),
        name=name,
    )(live, *operands, *arrays)


def own_norms(first, second):
    flat = jnp.concatenate([first.reshape(-1), second.reshape(-1)]).astype(F32)
    size = -(-flat.shape[0] // 1024) * 1024
    return jnp.pad(flat, (0, size - flat.shape[0])).reshape(8, -1)


def all_norms(gathered, first, second):
    shards = gathered.shape[0]
    flat = gathered.reshape(shards, -1)
    split, last = first.size, first.size + second.size

    def whole(part):
        return part.reshape(shards, 2, -1).transpose(1, 0, 2).reshape(2, -1)

    return whole(flat[:, :split]), whole(flat[:, split:last])


def body(reps, shards, *arguments):
    (
        global_views, local_views, live, first_reduce, first_spatial, first_expand, first_norms,
        second_reduce, second_spatial, second_expand, second_short, second_norms, global_cotan,
        local_cotan,
    ) = arguments
    geo = Geometry(global_views.shape[0], global_views.shape[1], local_views.shape[1])
    assert local_views.shape[0] == 2 * geo.slabs
    channels = global_views.shape[3]
    ha, hb, hc, hd, he, hf, hs = (
        item.T.reshape(reps, -1, item.shape[0])
        for item in (
            first_reduce, first_spatial, first_expand, second_reduce, second_spatial,
            second_expand, second_short,
        )
    )
    he_0, he_1, he_2 = (he[:, :, k * he.shape[2] // 3 : (k + 1) * he.shape[2] // 3] for k in range(3))
    mid_1, mid_2 = first_reduce.shape[1] * shards, second_reduce.shape[1] * shards
    wide = second_expand.shape[1] * shards

    def rows_of(gathered):
        return gathered.reshape(-1, gathered.shape[-1])

    big, small = geo.total, geo.small_total

    numbers = iter(range(100))

    def go(name, kernel, operands, results, scratch, width=None, members=4, jobs=(), side=None, far=()):
        parts = {4: 2, 6: 4, 8: 2}[members]
        sums = None if width is None else (members * parts, width // parts)
        return run(
            name, kernel, geo, reps, shards, next(numbers), live, operands, results, scratch, sums,
            jobs, side, far,
        )

    def pieces(rows, columns):
        return ((2, shards // 2, reps, rows // (shards * reps), columns), BF16)

    def acc(width, members=4):
        return ((members, 8, width), F32)

    def stat(width):
        return ((8, width), F32)

    def both(width):
        return ((2, width), F32)

    (
        packed, za, spread_a, fan_a, wa, spread_b, fan_b, wb, norms, unused, unused, wc,
        unused, fan_d, spread_e0, spread_e1, sa,
    ) = go(
        "stage_a", stage_a, (global_views, local_views),
        [((big, channels), BF16), ((big, mid_1), BF16)],
        [
            acc(mid_1), ((mid_1, channels), BF16), (global_views.shape, BF16),
            (local_views.shape, BF16), pltpu.SemaphoreType.DMA((2,)),
        ],
        mid_1, 8,
        jobs=(
            ("spread", (ha,), 0, 1), ("fan", (0, ha), 1, 2), ("join", (1,), 2, 3),
            ("spread", (hb,), 0, 2), ("fan", (3, hb), 2, 4), ("join", (4,), 4, None),
            ("all", (own_norms(first_norms, second_norms),), 1, 4),
            ("spread", (hc,), 0, 3), ("fan", (7, hc), 3, 4), ("join", (8,), 4, None),
            ("spread", (hd,), 0, 3), ("fan", (10, hd), 3, 4),
            ("spread", (he_0,), 3, 4), ("spread", (he_1,), 3, 4),
        ),
        far=(0, 1),
    )
    count = sa
    wa, wb, wc = rows_of(wa), rows_of(wb), rows_of(wc)
    norms_1, norms_2 = all_norms(norms, first_norms, second_norms)
    na, nb, nc = norms_1[:, :mid_1], norms_1[:, mid_1 : 2 * mid_1], norms_1[:, 2 * mid_1 :]
    nd, ne = norms_2[:, :mid_2], norms_2[:, mid_2 : 2 * mid_2]
    nf, ns = norms_2[:, 2 * mid_2 : 2 * mid_2 + wide], norms_2[:, 2 * mid_2 + wide :]
    zb, wd, fan_e0, fan_e1, spread_e2, spread_s, sb = go(
        "stage_b", stage_b, (count, za, sa, na, wb), [((big, mid_1), BF16)],
        [((geo.halo_total, 3 * mid_1), BF16), acc(mid_1)], mid_1,
        jobs=(
            ("join", (fan_d,), 0, 2), ("fan", (spread_e0, he_0), 0, 2),
            ("fan", (spread_e1, he_1), 0, 2), ("spread", (he_2,), 0, 2), ("spread", (hs,), 0, 2),
        ),
    )
    zc, we_0, we_1, fan_e2, spread_f, sc = go(
        "stage_c", stage_c, (count, zb, sb, nb, wc), [((big, channels), BF16)],
        [((geo.rows, mid_1), BF16), acc(channels)], channels,
        jobs=(
            ("join", (fan_e0,), 0, 2), ("join", (fan_e1,), 0, 2),
            ("fan", (spread_e2, he_2), 0, 2), ("spread", (hf,), 0, 2),
        ),
    )
    wd = rows_of(wd)
    hid, zd, sub, we_2, fan_s, sd = go(
        "stage_d", stage_d, (count, zc, sc, nc, packed, wd),
        [((big, channels), BF16), ((big, mid_2), BF16), ((small, channels), BF16)],
        [((channels // 128, geo.rows, 128), F32), acc(mid_2)], mid_2,
        jobs=(("join", (fan_e2,), 0, 2), ("fan", (spread_s, hs), 0, 2)),
    )
    we = tuple(rows_of(item) for item in (we_0, we_1, we_2))
    ze, zs, local_s, ws, fan_f, wf, se = go(
        "stage_e", stage_e, (count, zd, sd, nd, *we, sub),
        [((small, mid_2), BF16), ((small, wide), BF16), stat(wide // 2)],
        [
            ((mid_2 // 128, geo.halo, 128), F32), ((small, 9 * mid_2), BF16), acc(mid_2), acc(wide),
        ],
        mid_2,
        jobs=(
            ("join", (fan_s,), 0, 2), ("fan", (spread_f, hf), 0, 2), ("join", (1,), 2, None),
        ),
    )
    wf, ws = rows_of(wf), rows_of(ws)
    act_e, zf, ss, sf = go(
        "stage_f", stage_f, (count, ze, se, ne, wf),
        [((small, mid_2), BF16), ((small, wide), BF16)], [acc(wide)], wide, side=local_s,
    )
    second_g, second_l, grad, local_pool, so = go(
        "stage_out", stage_out,
        (count, zf, zs, sf, ss, nf, ns, global_cotan, local_cotan),
        [
            (global_cotan.shape, BF16), (local_cotan.shape, BF16), ((small, wide), BF16),
            stat(wide // 4),
        ],
        [((geo.slabs, 8, wide), F32), ((geo.small, 512), F32), acc(wide, 8)], wide, 6,
    )
    unused, unused, back_sub, back_e, ngrad_f, ngrad_s, pair_f, pair_s, pool, qe = go(
        "stage_f_back", stage_f_back,
        (count, zf, zs, sf, ss, nf, ns, grad, so, act_e, sub, wf, ws, ze, se, ne),
        [
            pieces(wide, mid_2), pieces(wide, channels), ((small, channels), BF16), ((small, mid_2), BF16),
            both(wide), both(wide),
        ],
        [((small, wide), BF16), ((small, wide), BF16), acc(mid_2)], mid_2,
        jobs=(("pair", ("0",), 2, None), ("pair", ("1",), 1, None)), side=local_pool,
    )
    views = count[8, 0] * 6.0
    pool = pool.reshape(2, wide)
    center = pool[0] / views
    spread = pool[1] / views - center * center
    pooled_std = jnp.mean(jnp.sqrt(spread + 1e-06))
    wgrad_e, back_d, ngrad_e, half_f, half_s, qd = go(
        "stage_e_back", stage_e_back,
        (count, ze, se, ne, back_e, qe, zd, sd, nd, *we),
        [pieces(mid_2, 9 * mid_2), ((big, mid_2), BF16), both(mid_2)],
        [
            ((mid_2 // 128, geo.halo, 128), F32), ((small, 9 * mid_2), BF16),
            ((small, mid_2), BF16), ((3, small, mid_2), BF16), ((4, small, mid_2), F32),
            acc(mid_2),
        ],
        mid_2, jobs=(("half", (pair_f,), 0, None), ("half", (pair_s,), 0, None)),
    )
    wgrad_d, joined, ngrad_d, unused, half_e, rest_f, rest_s, qc = go(
        "stage_d_back", stage_d_back,
        (count, zd, sd, nd, back_d, qd, hid, packed, zc, sc, nc, back_sub, wd),
        [pieces(mid_2, channels), ((big, channels), BF16), both(mid_2)],
        [((big, mid_2), BF16), ((channels // 128, geo.rows, 128), F32), acc(channels)], channels,
        jobs=(
            ("pair", (wgrad_e,), 0, 1), ("half", (0,), 1, None),
            ("rest", (half_f,), 0, 1), ("rest", (half_s,), 0, 1),
        ),
    )
    wgrad_c, back_b, ngrad_c, pair_d, rest_e, line_f, line_s, qb = go(
        "stage_c_back", stage_c_back,
        (count, zc, sc, nc, joined, qc, zb, sb, nb, wc),
        [pieces(channels, mid_1), ((big, mid_1), BF16), both(channels)],
        [((big, channels), BF16), ((big, mid_1), BF16), acc(mid_1)], mid_1,
        jobs=(
            ("pair", (wgrad_d,), 0, 2), ("rest", (half_e,), 0, 2), ("line", (rest_f,), 0, 2),
            ("line", (rest_s,), 0, 2),
        ),
    )
    wgrad_b, back_a, ngrad_b, unused, rest_d, unused, half_c, line_e, out_f, out_s, qa = go(
        "stage_b_back", stage_b_back,
        (count, zb, sb, nb, back_b, qb, za, sa, na, wb),
        [pieces(mid_1, 9 * mid_1), ((big, mid_1), BF16), both(mid_1)],
        [
            ((geo.halo_total, 3 * mid_1), BF16), ((geo.halo_total, 3 * mid_1), BF16),
            ((9 * mid_1, mid_1), BF16), (wb.shape, F32), acc(mid_1),
        ],
        mid_1,
        jobs=(
            ("half", (pair_d,), 0, 1), ("rest", (0,), 1, 2), ("pair", (wgrad_c,), 0, 1),
            ("half", (2,), 1, 2), ("line", (rest_e,), 0, 2), ("share", (line_f,), 0, 2),
            ("share", (line_s,), 0, 2),
        ),
    )
    more = go(
        "stage_a_back", stage_a_back, (count, za, sa, na, back_a, qa, packed),
        [pieces(mid_1, channels), ((big, mid_1), BF16), both(mid_1)], [],
        jobs=(
            ("pair", (wgrad_b,), 0, 1), ("half", (0,), 1, 2), ("rest", (1,), 2, 3),
            ("line", (2,), 3, 4), ("share", (3,), 4, None),
            ("pair", ("0",), 1, 2), ("half", (5,), 2, 3), ("rest", (6,), 3, 4),
            ("line", (7,), 4, 5), ("share", (8,), 5, None),
            ("rest", (half_c,), 0, 1), ("line", (10,), 1, 2), ("share", (11,), 2, None),
            ("line", (rest_d,), 0, 1), ("share", (13,), 1, None),
            ("share", (line_e,), 0, None),
        ),
    )
    dza, ngrad_a = more[1], more[2]
    out_b, out_a, out_c, out_d, out_e = (more[3 + k] for k in (4, 9, 12, 14, 15))
    (grad_g, grad_l, first_g, first_l), columns = run_last(
        geo, joined, dza, hid, wa, (out_a, out_b, out_c, out_d, out_e, out_f, out_s),
        global_views.shape, local_views.shape,
    )
    shard = lax.axis_index("fsdp")

    def own_columns(parts, width):
        whole = jnp.concatenate(parts, axis=1)
        return lax.dynamic_slice_in_dim(whole, shard * width, width, 1)

    return (
        first_g, first_l, second_g, second_l, grad_g, grad_l,
        *columns[0:3],
        own_columns((ngrad_a, ngrad_b, ngrad_c), first_norms.shape[1]),
        *columns[3:7],
        own_columns((ngrad_d, ngrad_e, ngrad_f, ngrad_s), second_norms.shape[1]),
        pooled_std,
    )


def solution(mesh):
    views = P(("rep", "fsdp"), None, None, None)
    columns = P(None, "fsdp")
    return jax.shard_map(
        functools.partial(body, mesh.shape["rep"], mesh.shape["fsdp"]),
        mesh=mesh,
        in_specs=(views, views, P(("rep", "fsdp"))) + (columns,) * 9 + (views, views),
        out_specs=(views,) * 6 + (columns,) * 9 + (P(),),
        check_vma=False,
    )
```

```python
import functools

import jax
import jax.numpy as jnp
from jax import lax
from jax.experimental import pallas as pl
from jax.experimental.pallas import tpu as pltpu
from jax.sharding import PartitionSpec as P

EPSILON = 1e-05
F32 = jnp.float32
BF16 = jnp.bfloat16
MESH = pl.DeviceIdType.MESH
CELLS = 16


def nt(left, right):
    return lax.dot_general(left, right, (((1,), (1,)), ((), ())), preferred_element_type=F32)


def nn(left, right):
    return lax.dot_general(left, right, (((1,), (0,)), ((), ())), preferred_element_type=F32)


def tn(left, right):
    return lax.dot_general(left, right, (((0,), (0,)), ((), ())), preferred_element_type=F32)


def sig(values):
    return 0.5 * jnp.tanh(0.5 * values) + 0.5


def silu(values):
    return values * sig(values)


def slope(values):
    gate = sig(values)
    held = values * gate
    return gate + held - held * gate


def lanes(tile, width):
    return jnp.concatenate([tile] * (width // tile.shape[1]), axis=1)


def fold(values):
    return jnp.sum(values.reshape(values.shape[0] // 8, 8, values.shape[1]), axis=0)


class Geometry:
    def __init__(self, views, side_global, side_local):
        self.slabs = views
        self.hg, self.hl = side_global, side_local
        assert side_global < CELLS and side_local < CELLS // 2
        self.rg, self.rl = side_global * CELLS, side_local * CELLS
        self.rows = self.rg + self.rl
        self.og, self.ol = (side_global - 1) // 2 + 1, (side_local - 1) // 2 + 1
        self.sg, self.sl = self.og * 8, self.ol * 8
        self.small = self.sg + self.sl
        self.total, self.small_total = self.slabs * self.rows, self.slabs * self.small
        self.halo = self.rows + 2 * CELLS
        self.halo_total = self.slabs * self.halo + CELLS
        self.chunk = 32
        assert self.rg % self.chunk == 0 and self.rl % self.chunk == 0 and self.small % 16 == 0

    def pieces(self, width):
        if width <= 256:
            return [(0, self.rg, 0), (self.rg, self.rl, 1)]
        step = self.chunk
        return [(start, step, 0) for start in range(0, self.rg, step)] + [
            (start, step, 1) for start in range(self.rg, self.rows, step)
        ]

    def mask(self, count, group, width):
        row = lax.broadcasted_iota(jnp.int32, (count, 128), 0)
        if group == 0:
            keep = (row & (CELLS - 1)) < self.hg
        else:
            keep = (row & (CELLS // 2 - 1)) < self.hl
        return lanes(keep.astype(F32), width)

    def small_mask(self, group, width):
        count = self.sl if group else self.sg
        row = lax.broadcasted_iota(jnp.int32, (count, 128), 0)
        keep = (row & 3) < self.ol if group else (row & 7) < self.og
        return lanes(keep.astype(F32), width)

    def small_pieces(self):
        return [(0, self.sg, 0), (self.sg, self.sl, 1)]


def alive(live, slab):
    return jnp.where(slab < 2 * live[0], 1.0, 0.0).astype(F32)


def cells(geo, count, group, width, small=False):
    images = lanes(count[8:9, 0:128], width)
    if small:
        return images * float(2 * geo.og * geo.og if group == 0 else 4 * geo.ol * geo.ol)
    return images * float(2 * geo.hg * geo.hg if group == 0 else 4 * geo.hl * geo.hl)


def member(sums, row, width):
    parts = width // sums.shape[1]
    return jnp.concatenate(
        [sums[row * parts + k : row * parts + k + 1, :] for k in range(parts)], axis=1
    )


def norm_terms(stats, norm, number, group):
    width = norm.shape[1]
    mean = member(stats, 2 * group, width) / number
    spread = member(stats, 2 * group + 1, width) / number - mean * mean
    inverse = lax.rsqrt(spread + EPSILON)
    scale = norm[0:1, :] * inverse
    return mean, inverse, scale, norm[1:2, :] - mean * scale


def back_terms(stats, norm, number, group, first, second_raw):
    mean, inverse, scale, unused = norm_terms(stats, norm, number, group)
    second = inverse * (second_raw - mean * first)
    by_value = -scale * inverse * (second / number)
    constant = -scale * (first / number) - by_value * mean
    return scale, by_value, constant, second


def forward_terms(geo, count, stats, norm, width, small=False):
    return [
        norm_terms(stats, norm, cells(geo, count, group, width, small), group)[2:]
        for group in range(2)
    ]


def backward_terms(geo, count, stats, norm, sums, out, width, small=False, rows=((0, 1), (2, 3))):
    terms = []
    seconds = []
    for group in range(2):
        number = cells(geo, count, group, width, small)
        first = member(sums, rows[group][0], width)
        raw = member(sums, rows[group][1], width)
        scale, by_value, constant, second = back_terms(stats, norm, number, group, first, raw)
        terms.append((scale, by_value, constant))
        seconds.append((second, first))
    out[0:1, :] = seconds[0][0] + seconds[1][0]
    out[1:2, :] = seconds[0][1] + seconds[1][1]
    return terms


def finish(stats, acc, members, begin=0):
    part = stats.shape[1]
    parts = acc.shape[2] // part
    for row in range(members):
        total = jnp.sum(acc[begin + row], axis=0, keepdims=True)
        for k in range(parts):
            stats[row * parts + k : row * parts + k + 1, :] = total[:, k * part : (k + 1) * part]


def put(store, place, values):
    for k in range(store.shape[0]):
        store[k, place, :] = values[:, k * 128 : (k + 1) * 128]


def take(store, place):
    return jnp.concatenate([store[k, place, :] for k in range(store.shape[0])], axis=1)


def put_pieces(pieces, first, values, begin=0):
    cores, chips, reps, size = pieces.shape[:4]
    cols = slice(begin, begin + values.shape[1])
    for k in range(values.shape[0] // size):
        index = first // size + k
        shard, rep = index // reps, index % reps
        part = values[k * size : (k + 1) * size]
        pieces[shard % cores, shard // cores, rep, :, cols] = part.astype(BF16)


def loop(count, step):
    def one(index, carry):
        step(index)
        return carry

    lax.fori_loop(0, count, one, 0)


def at(index, size):
    return pl.ds(pl.multiple_of(index * size, size), size)


def stage_a(geo, net, live, xg, xl, packed, conv, acc, weight, own_g, own_l, arrive):
    loads = (
        pltpu.make_async_copy(xg, own_g, arrive.at[0]),
        pltpu.make_async_copy(xl, own_l, arrive.at[1]),
    )
    for load in loads:
        load.start()
    net.open()
    acc[...] = jnp.zeros(acc.shape, F32)
    blank = jnp.zeros((CELLS, packed.shape[1]), BF16)
    half = CELLS // 2
    for load in loads:
        load.wait()

    def pack(s):
        base = s * geo.rows
        keep = alive(live, s).astype(BF16)
        for i in range(geo.hg):
            start = pl.multiple_of(base + i * CELLS, CELLS)
            packed[pl.ds(start, CELLS), :] = blank
            packed[pl.ds(start, geo.hg), :] = own_g[s, i] * keep
        for i in range(geo.hl):
            start = pl.multiple_of(base + geo.rg + i * CELLS, CELLS)
            packed[pl.ds(start, CELLS), :] = blank
            for side in range(2):
                place = pl.multiple_of(start + side * half, half)
                packed[pl.ds(place, geo.hl), :] = own_l[2 * s + side, i] * keep

    part = geo.slabs // 4
    for number in range(4):
        begin = number * part
        size = part if number < 3 else geo.slabs - begin
        loop(size, lambda s: pack(s + begin))
        net.turn(number + 1)
    gathered = net.job_out(3)
    weight[...] = gathered[...].astype(F32).reshape(weight.shape).astype(BF16)

    def slab(s):
        result = nt(packed[at(s, geo.rows), :], weight[...])
        conv[at(s, geo.rows), :] = result.astype(BF16)
        for start, size, group in geo.pieces(256):
            piece = result[start : start + size]
            acc[2 * group] += fold(piece)
            acc[2 * group + 1] += fold(piece * piece)

    loop(geo.slabs, slab)
    finish(net.own, acc, 4)
    net.own[8:16, :] = jnp.full((8, net.own.shape[1]), live[0], jnp.int32).astype(F32)
    net.turn(5)
    net.run()


def spread_taps(geo, store, s, values, reverse):
    width = values[0].shape[1]
    for group in range(2):
        rows = values[group]
        size = rows.shape[0]
        start = pl.multiple_of(s * geo.halo + CELLS + group * (geo.rg + CELLS), CELLS)
        before = pltpu.roll(rows, 1, 0)
        after = pltpu.roll(rows, size - 1, 0)
        order = (after, rows, before) if reverse else (before, rows, after)
        for tap in range(3):
            store[pl.ds(start, size), tap * width : (tap + 1) * width] = order[tap].astype(BF16)


def clear_halo(geo, store):
    blank = jnp.zeros((CELLS, store.shape[1]), BF16)

    def slab(s):
        store[pl.ds(pl.multiple_of(s * geo.halo, CELLS), CELLS), :] = blank
        store[pl.ds(pl.multiple_of(s * geo.halo + CELLS + geo.rg, CELLS), CELLS), :] = blank

    loop(geo.slabs, slab)
    store[geo.slabs * geo.halo : geo.slabs * geo.halo + CELLS, :] = blank


def activate(geo, live, conv, s, terms):
    values = []
    width = conv.shape[1]
    keep = alive(live, s)
    for group in range(2):
        start, size = (geo.rg, geo.rl) if group else (0, geo.rg)
        rows = conv[pl.ds(pl.multiple_of(s * geo.rows + start, CELLS), size), :].astype(F32)
        scale, shift = terms[group]
        values.append(silu(rows * scale + shift) * (geo.mask(size, group, width) * keep))
    return values


def stage_b(geo, net, live, count, za, stats_a, norm, weight, conv, taps, acc):
    acc[...] = jnp.zeros(acc.shape, F32)
    width = za.shape[1]
    terms = forward_terms(geo, count, stats_a, norm, width)
    clear_halo(geo, taps)

    def fill(s):
        spread_taps(geo, taps, s, activate(geo, live, za, s, terms), False)

    loop(2, fill)
    net.open()
    loop(geo.slabs - 2, lambda s: fill(s + 2))
    span = geo.halo - CELLS

    def slab(s):
        result = None
        for dy in range(3):
            rows = taps[pl.ds(pl.multiple_of(s * geo.halo + dy * CELLS, CELLS), span), :]
            term = nt(rows, weight[:, dy * 3 * width : (dy + 1) * 3 * width])
            result = term if result is None else result + term
        keep = alive(live, s)
        for group, (begin, size) in enumerate(((0, geo.rg), (geo.rg + CELLS, geo.rl))):
            piece = result[begin : begin + size]
            start = pl.multiple_of(s * geo.rows + group * geo.rg, CELLS)
            conv[pl.ds(start, size), :] = piece.astype(BF16)
            piece = piece * (geo.mask(size, group, width) * keep)
            acc[2 * group] += fold(piece)
            acc[2 * group + 1] += fold(piece * piece)

    loop(2, slab)
    net.turn(1)
    loop(geo.slabs - 2, lambda s: slab(s + 2))
    net.turn(2)
    finish(net.own, acc, 4)
    net.run()


def stage_c(geo, net, live, count, zb, stats_b, norm, weight, conv, act, acc):
    acc[...] = jnp.zeros(acc.shape, F32)
    terms = forward_terms(geo, count, stats_b, norm, zb.shape[1])
    step = 256

    def slab(s):
        values = activate(geo, live, zb, s, terms)
        act[0 : geo.rg, :] = values[0].astype(BF16)
        act[geo.rg : geo.rows, :] = values[1].astype(BF16)
        for c in range(0, weight.shape[0], step):
            result = nt(act[...], weight[c : c + step, :])
            conv[at(s, geo.rows), c : c + step] = result.astype(BF16)
            for start, size, group in geo.pieces(256):
                piece = result[start : start + size]
                acc[2 * group, :, c : c + step] += fold(piece)
                acc[2 * group + 1, :, c : c + step] += fold(piece * piece)

    loop(2, slab)
    net.open()
    loop(4, lambda s: slab(s + 2))
    net.turn(1)
    loop(geo.slabs - 6, lambda s: slab(s + 6))
    net.turn(2)
    finish(net.own, acc, 4)
    net.run()


def even_rows(geo):
    return [2 * i * CELLS for i in range(geo.og)] + [
        geo.rg + 2 * i * CELLS for i in range(geo.ol)
    ]


def stage_d(
    geo, net, live, count, zc, stats_c, norm, packed, weight, hid, conv, sub, full, acc,
):
    acc[...] = jnp.zeros(acc.shape, F32)
    width = zc.shape[1]
    terms = forward_terms(geo, count, stats_c, norm, width)

    def slab(s):
        keep = alive(live, s)
        for start, size, group in geo.pieces(width):
            rows = pl.ds(pl.multiple_of(s * geo.rows + start, CELLS), size)
            scale, shift = terms[group]
            joined = zc[rows, :].astype(F32) * scale + shift + packed[rows, :].astype(F32)
            value = silu(joined) * (geo.mask(size, group, width) * keep)
            put(full, pl.ds(start, size), value)
            hid[rows, :] = value.astype(BF16)
        picked = [take(full, pl.ds(start, 8, stride=2)) for start in even_rows(geo)]
        sub[at(s, geo.small), :] = jnp.concatenate(picked, axis=0).astype(BF16)
        result = nt(hid[at(s, geo.rows), :], weight[...])
        conv[at(s, geo.rows), :] = result.astype(BF16)
        for start, size, group in geo.pieces(256):
            piece = result[start : start + size]
            acc[2 * group] += fold(piece)
            acc[2 * group + 1] += fold(piece * piece)

    loop(1, slab)
    net.open()
    loop(4, lambda s: slab(s + 1))
    net.turn(1)
    loop(geo.slabs - 5, lambda s: slab(s + 5))
    net.turn(2)
    finish(net.own, acc, 4)
    net.run()


def small_product(geo, left, pick, step, conv, acc, first, last):
    for c in range(first, last, step):
        result = nt(left[...], pick(c))
        conv[:, c : c + step] = result.astype(BF16)
        for s in range(geo.slabs):
            for start, size, group in geo.small_pieces():
                piece = result[s * geo.small + start : s * geo.small + start + size]
                acc[2 * group, :, c : c + step] += fold(piece)
                acc[2 * group + 1, :, c : c + step] += fold(piece * piece)


def gather_taps(geo, net, live, zd, terms, full, taps):
    width = zd.shape[1]
    blank = jnp.zeros((8, width), F32)
    full[:, 0:CELLS, :] = jnp.zeros((width // 128, CELLS, 128), F32)
    full[:, CELLS + geo.rg : 2 * CELLS + geo.rg, :] = jnp.zeros((width // 128, CELLS, 128), F32)

    def slab(s):
        keep = alive(live, s)
        for start, size, group in geo.pieces(width):
            rows = pl.ds(pl.multiple_of(s * geo.rows + start, CELLS), size)
            scale, shift = terms[group]
            value = silu(zd[rows, :].astype(F32) * scale + shift)
            begin = CELLS + start + group * CELLS
            put(full, pl.ds(begin, size), value * (geo.mask(size, group, width) * keep))
        for dy in range(3):
            for dx in range(3):
                picked = []
                for group in range(2):
                    for i in range(geo.ol if group else geo.og):
                        line = 2 * i + dy - 1
                        if line < 0:
                            picked.append(blank)
                            continue
                        begin = CELLS + group * (geo.rg + CELLS) + line * CELLS + dx - 1
                        picked.append(take(full, pl.ds(begin, 8, stride=2)))
                tap = dy * 3 + dx
                taps[at(s, geo.small), tap * width : (tap + 1) * width] = jnp.concatenate(
                    picked, axis=0
                ).astype(BF16)

    loop(2, slab)
    net.open()
    loop(geo.slabs - 2, lambda s: slab(s + 2))


def stage_e(
    geo, net, live, count, zd, stats_d, norm, weight_0, weight_1, weight_2, sub, conv, conv_s,
    stats_s, full, taps, acc, acc_s,
):
    acc[...] = jnp.zeros(acc.shape, F32)
    acc_s[...] = jnp.zeros(acc_s.shape, F32)
    terms = forward_terms(geo, count, stats_d, norm, zd.shape[1])
    gather_taps(geo, net, live, zd, terms, full, taps)
    net.turn(1)
    step = 256
    third = weight_0.shape[1]
    for c in range(0, weight_0.shape[0], step):
        result = nt(taps[:, 0:third], weight_0[c : c + step, :])
        result = result + nt(taps[:, third : 2 * third], weight_1[c : c + step, :])
        result = result + nt(taps[:, 2 * third :], weight_2[c : c + step, :])
        conv[:, c : c + step] = result.astype(BF16)
        for s in range(geo.slabs):
            keep = alive(live, s)
            for start, size, group in geo.small_pieces():
                piece = result[s * geo.small + start : s * geo.small + start + size]
                piece = piece * (geo.small_mask(group, step) * keep)
                acc[2 * group, :, c : c + step] += fold(piece)
                acc[2 * group + 1, :, c : c + step] += fold(piece * piece)
    net.turn(2)
    finish(net.own, acc, 4)
    net.begin()
    short = net.job_out(0)
    step = short.shape[2] * short.shape[3]

    def pick(c):
        part = c // step
        return short[part // 2, part % 2].reshape(step, short.shape[4])

    width = conv_s.shape[1]
    small_product(geo, sub, pick, step, conv_s, acc_s, 0, width // 4)
    net.step()
    small_product(geo, sub, pick, step, conv_s, acc_s, width // 4, 5 * width // 8)
    net.step()
    small_product(geo, sub, pick, step, conv_s, acc_s, 5 * width // 8, width)
    finish(stats_s, acc_s, 4)
    net.end()


def stage_f(geo, net, live, count, ze, stats_e, norm, weight, act, conv, acc):
    net.open()
    net.side.begin()
    acc[...] = jnp.zeros(acc.shape, F32)
    width = ze.shape[1]
    terms = forward_terms(geo, count, stats_e, norm, width, True)

    def slab(s):
        keep = alive(live, s)
        rows = ze[at(s, geo.small), :].astype(F32)
        parts = []
        for start, size, group in geo.small_pieces():
            scale, shift = terms[group]
            value = silu(rows[start : start + size] * scale + shift)
            parts.append(value * (geo.small_mask(group, width) * keep))
        act[at(s, geo.small), :] = jnp.concatenate(parts, axis=0).astype(BF16)

    loop(geo.slabs, slab)
    net.side.step()
    half, step = weight.shape[0] // 2, 256

    def pick(c):
        return weight[c : c + step, :]

    small_product(geo, act, pick, step, conv, acc, 0, half)
    net.side.step()
    small_product(geo, act, pick, step, conv, acc, half, 2 * half)
    net.side.end()
    finish(net.own, acc, 4)
    net.run()


def stage_out(
    geo, net, live, count, zf, zs, stats_f, stats_s, norm_f, norm_s, cotg, cotl, outg, outl, grad,
    pooled_sums, pool, cot, acc,
):
    acc[...] = jnp.zeros(acc.shape, F32)
    cot[...] = jnp.zeros(cot.shape, F32)
    pool[...] = jnp.zeros(pool.shape, F32)
    width = zf.shape[1]
    step = 512
    terms_f = forward_terms(geo, count, stats_f, norm_f, width, True)
    terms_s = forward_terms(geo, count, stats_s, norm_s, width, True)

    def slab(s):
        keep = alive(live, s)
        for c in range(0, width, step):
            cols = slice(c, c + step)
            for i in range(geo.og):
                cot[i * 8 : i * 8 + geo.og, :] = cotg[s, i, :, cols].astype(F32)
            for i in range(geo.ol):
                for side in range(2):
                    begin = geo.sg + i * 8 + side * 4
                    cot[begin : begin + geo.ol, :] = cotl[2 * s + side, i, :, cols].astype(F32)
            rows_f = zf[at(s, geo.small), cols].astype(F32)
            rows_s = zs[at(s, geo.small), cols].astype(F32)
            grads = []
            for start, size, group in geo.small_pieces():
                part = slice(start, start + size)
                vf, vs = rows_f[part], rows_s[part]
                scale_f, shift_f = (item[:, cols] for item in terms_f[group])
                scale_s, shift_s = (item[:, cols] for item in terms_s[group])
                joined = vf * scale_f + vs * scale_s + (shift_f + shift_s)
                mask = geo.small_mask(group, step) * keep
                gate = sig(joined)
                held = joined * gate
                value = held * mask
                low = value.astype(BF16)
                dy = cot[part, :] * ((gate + held - held * gate) * mask)
                grads.append(dy)
                acc[3 * group, :, cols] += fold(dy)
                acc[3 * group + 1, :, cols] += fold(dy * vf)
                acc[3 * group + 2, :, cols] += fold(dy * vs)
                summed = fold(value)
                if group == 0:
                    for i in range(geo.og):
                        outg[s, i, :, cols] = value[i * 8 : i * 8 + geo.og].astype(BF16)
                    pool[s, 0:1, cols] = jnp.sum(summed, axis=0, keepdims=True) * (
                        1.0 / (geo.og * geo.og)
                    )
                else:
                    row = lax.broadcasted_iota(jnp.int32, (8, step), 0)
                    for side in range(2):
                        own = jnp.where((row >= 4) == (side == 1), summed, 0.0)
                        pool[s, 1 + side : 2 + side, cols] = jnp.sum(
                            own, axis=0, keepdims=True
                        ) * (1.0 / (geo.ol * geo.ol))
                        for i in range(geo.ol):
                            begin = i * 8 + side * 4
                            outl[2 * s + side, i, :, cols] = value[begin : begin + geo.ol].astype(
                                BF16
                            )
            grad[at(s, geo.small), cols] = jnp.concatenate(grads, axis=0).astype(BF16)
        pooled = pool[s]
        square = jnp.mean(pooled * pooled, axis=1, keepdims=True)
        normed = pooled * lax.rsqrt(square + 1e-06)
        acc[6] += normed
        acc[7] += normed * normed

    loop(geo.slabs, slab)
    finish(net.own, acc, 6)
    net.begin()
    finish(pooled_sums, acc, 2, 6)
    net.end()


def small_back(geo, live, s, grad, conv, terms, width, cols):
    keep = alive(live, s)
    rows_g = grad[at(s, geo.small), cols].astype(F32)
    rows_z = conv[at(s, geo.small), cols].astype(F32)
    parts = []
    for start, size, group in geo.small_pieces():
        scale, by_value, constant = (item[:, cols] for item in terms[group])
        part = slice(start, start + size)
        value = rows_g[part] * scale + rows_z[part] * by_value + constant
        parts.append(value * (geo.small_mask(group, width) * keep))
    return jnp.concatenate(parts, axis=0).astype(BF16)


def stage_f_back(
    geo, net, live, count, zf, zs, stats_f, stats_s, norm_f, norm_s, grad, sums, act, sub, weight,
    short, ze, stats_e, norm_e, wgrad_f, wgrad_s, back_sub, back_e, ngrad_f, ngrad_s, dzf, dzs, acc,
):
    acc[...] = jnp.zeros(acc.shape, F32)
    width = zf.shape[1]
    step = 512
    rows_f, rows_s = ((0, 1), (3, 4)), ((0, 2), (3, 5))
    terms_f = backward_terms(geo, count, stats_f, norm_f, sums, ngrad_f, width, True, rows_f)
    terms_s = backward_terms(geo, count, stats_s, norm_s, sums, ngrad_s, width, True, rows_s)

    def slab(s):
        for c in range(0, width, step):
            cols = slice(c, c + step)
            dzf[at(s, geo.small), cols] = small_back(geo, live, s, grad, zf, terms_f, step, cols)
            dzs[at(s, geo.small), cols] = small_back(geo, live, s, grad, zs, terms_s, step, cols)

    loop(geo.slabs, slab)
    net.open()
    net.side.begin()
    block = 256
    terms_e = forward_terms(geo, count, stats_e, norm_e, ze.shape[1], True)
    for c in range(0, act.shape[1], block):
        cols = slice(c, c + block)
        result = nn(dzf[...], weight[:, cols])
        for s in range(geo.slabs):
            keep = alive(live, s)
            rows = ze[s * geo.small : (s + 1) * geo.small, cols].astype(F32)
            parts = []
            for start, size, group in geo.small_pieces():
                scale, shift = (item[:, cols] for item in terms_e[group])
                value = rows[start : start + size]
                mask = geo.small_mask(group, block) * keep
                piece = result[s * geo.small + start : s * geo.small + start + size]
                piece = piece * (slope(value * scale + shift) * mask)
                parts.append(piece)
                acc[2 * group, :, cols] += fold(piece)
                acc[2 * group + 1, :, cols] += fold(piece * value)
            back_e[s * geo.small : (s + 1) * geo.small, cols] = jnp.concatenate(
                parts, axis=0
            ).astype(BF16)
    finish(net.own, acc, 4)
    net.begin()
    for c in range(0, width, block):
        cols = slice(c, c + block)
        put_pieces(wgrad_s, c, tn(dzs[:, cols], sub[...]))
        if c == width // 4:
            net.step()
    net.step()
    net.turn(1)
    for c in range(0, width, block):
        cols = slice(c, c + block)
        put_pieces(wgrad_f, c, tn(dzf[:, cols], act[...]))
        if c == width // 4:
            net.side.step()
    net.side.step()
    net.turn(2)
    for c in range(0, sub.shape[1], block):
        cols = slice(c, c + block)
        back_sub[:, cols] = nn(dzs[...], short[:, cols]).astype(BF16)
    net.side.end()
    net.end()


def stage_e_back(
    geo, net, live, count, ze, stats_e, norm_e, back_e, sums_e, zd, stats_d, norm_d, weight_0, weight_1,
    weight_2, wgrad, back_d, ngrad, full, taps, dze, moved, parity, acc,
):
    acc[...] = jnp.zeros(acc.shape, F32)
    width = ze.shape[1]
    terms_e = backward_terms(geo, count, stats_e, norm_e, sums_e, ngrad, width, True)
    terms_d = forward_terms(geo, count, stats_d, norm_d, width)
    gather_taps(geo, net, live, zd, terms_d, full, taps)

    def shift(s):
        value = small_back(geo, live, s, back_e, ze, terms_e, width, slice(0, width)).astype(F32)
        blank = jnp.zeros((8, width), F32)
        down = jnp.concatenate(
            [value[8 : geo.sg], blank, value[geo.sg + 8 :], blank], axis=0
        )
        size = geo.small
        dze[at(s, size), :] = value.astype(BF16)
        moved[0, at(s, size), :] = pltpu.roll(value, size - 1, 0).astype(BF16)
        moved[1, at(s, size), :] = down.astype(BF16)
        moved[2, at(s, size), :] = pltpu.roll(down, size - 1, 0).astype(BF16)

    loop(geo.slabs, shift)

    def tap(dy, dx):
        return (weight_0, weight_1, weight_2)[dy][:, dx * width : (dx + 1) * width]

    def grads(first, last):
        for t in range(first, last):
            result = tn(dze[...], taps[:, t * width : (t + 1) * width])
            put_pieces(wgrad, 0, result, t * width)

    parity[0] = nn(dze[...], tap(1, 1))
    parity[1] = nn(dze[...], tap(1, 2)) + nn(moved[0], tap(1, 0))
    parity[2] = nn(dze[...], tap(2, 1)) + nn(moved[1], tap(0, 1))
    parity[3] = (
        nn(dze[...], tap(2, 2))
        + nn(moved[0], tap(2, 0))
        + nn(moved[1], tap(0, 2))
        + nn(moved[2], tap(0, 0))
    )

    def slab(s):
        keep = alive(live, s)
        for group in range(2):
            for i in range(geo.ol if group else geo.og):
                for a in range(2):
                    for b in range(2):
                        begin = group * geo.rg + (2 * i + a) * CELLS + b
                        source = s * geo.small + group * geo.sg + i * 8
                        part = parity[2 * a + b, pl.ds(pl.multiple_of(source, 8), 8), :]
                        put(full, pl.ds(begin, 8, stride=2), part)
        for start, size, group in geo.pieces(width):
            rows = pl.ds(pl.multiple_of(s * geo.rows + start, CELLS), size)
            scale, shift_d = terms_d[group]
            value = zd[rows, :].astype(F32)
            mask = geo.mask(size, group, width) * keep
            piece = take(full, pl.ds(start, size)) * (slope(value * scale + shift_d) * mask)
            back_d[rows, :] = piece.astype(BF16)
            acc[2 * group] += fold(piece)
            acc[2 * group + 1] += fold(piece * value)

    loop(geo.slabs, slab)
    finish(net.own, acc, 4)
    net.begin()
    grads(0, 3)
    net.step()
    grads(3, 6)
    net.step()
    grads(6, 9)
    net.end()


def wide_back(geo, live, s, grad, conv, terms, low):
    width = conv.shape[1]
    keep = alive(live, s)
    for start, size, group in geo.pieces(width):
        rows = pl.ds(pl.multiple_of(s * geo.rows + start, CELLS), size)
        scale, by_value, constant = terms[group]
        value = grad[rows, :].astype(F32) * scale + conv[rows, :].astype(F32) * by_value + constant
        low[rows, :] = (value * (geo.mask(size, group, width) * keep)).astype(BF16)


def stage_d_back(
    geo, net, live, count, zd, stats_d, norm_d, back_d, sums_d, hid, packed, zc, stats_c, norm_c,
    back_sub, weight, wgrad, joined, ngrad, dzd, full, acc,
):
    acc[...] = jnp.zeros(acc.shape, F32)
    width = zc.shape[1]
    terms_d = backward_terms(geo, count, stats_d, norm_d, sums_d, ngrad, zd.shape[1])
    terms_c = forward_terms(geo, count, stats_c, norm_c, width)

    def slab(s):
        wide_back(geo, live, s, back_d, zd, terms_d, dzd)
        put(full, pl.ds(0, geo.rows), nn(dzd[at(s, geo.rows), :], weight[...]))
        extra = back_sub[at(s, geo.small), :].astype(F32)
        for k, start in enumerate(even_rows(geo)):
            place = pl.ds(start, 8, stride=2)
            put(full, place, take(full, place) + extra[k * 8 : k * 8 + 8])
        keep = alive(live, s)
        for start, size, group in geo.pieces(width):
            rows = pl.ds(pl.multiple_of(s * geo.rows + start, CELLS), size)
            scale, shift = terms_c[group]
            value = zc[rows, :].astype(F32)
            pre = value * scale + shift + packed[rows, :].astype(F32)
            mask = geo.mask(size, group, width) * keep
            piece = take(full, pl.ds(start, size)) * (slope(pre) * mask)
            joined[rows, :] = piece.astype(BF16)
            acc[2 * group] += fold(piece)
            acc[2 * group + 1] += fold(piece * value)

    loop(1, slab)
    net.open()
    loop(4, lambda s: slab(s + 1))
    net.turn(1)
    loop(geo.slabs - 5, lambda s: slab(s + 5))
    net.turn(2)
    finish(net.own, acc, 4)
    block = 256
    net.begin()
    for c in range(0, dzd.shape[1], block):
        put_pieces(wgrad, c, tn(dzd[:, c : c + block], hid[...]))
        net.step()
    net.end()


def stage_c_back(
    geo, net, live, count, zc, stats_c, norm_c, joined, sums_c, zb, stats_b, norm_b, weight, wgrad,
    back_b, ngrad, dzc, act, acc,
):
    acc[...] = jnp.zeros(acc.shape, F32)
    terms_c = backward_terms(geo, count, stats_c, norm_c, sums_c, ngrad, zc.shape[1])
    terms_b = forward_terms(geo, count, stats_b, norm_b, zb.shape[1])
    width = zb.shape[1]

    def slab(s):
        wide_back(geo, live, s, joined, zc, terms_c, dzc)
        result = nn(dzc[at(s, geo.rows), :], weight[...])
        keep = alive(live, s)
        for start, size, group in geo.pieces(width):
            rows = pl.ds(pl.multiple_of(s * geo.rows + start, CELLS), size)
            scale, shift = terms_b[group]
            value = zb[rows, :].astype(F32)
            pre = value * scale + shift
            mask = geo.mask(size, group, width) * keep
            gate = sig(pre)
            held = pre * gate
            act[rows, :] = (held * mask).astype(BF16)
            piece = result[start : start + size] * ((gate + held - held * gate) * mask)
            back_b[rows, :] = piece.astype(BF16)
            acc[2 * group] += fold(piece)
            acc[2 * group + 1] += fold(piece * value)

    loop(1, slab)
    net.open()
    loop(geo.slabs - 1, lambda s: slab(s + 1))
    net.turn(2)
    finish(net.own, acc, 4)
    net.begin()
    block = 256
    for c in range(0, dzc.shape[1], block):
        put_pieces(wgrad, c, tn(dzc[:, c : c + block], act[...]))
        if c < 2 * block:
            net.step()
    net.end()


def stage_b_back(
    geo, net, live, count, zb, stats_b, norm_b, back_b, sums_b, za, stats_a, norm_a, weight, wgrad,
    back_a, ngrad, taps, dtaps, stacked, total, acc,
):
    acc[...] = jnp.zeros(acc.shape, F32)
    width = za.shape[1]
    terms_b = backward_terms(geo, count, stats_b, norm_b, sums_b, ngrad, width)
    terms_a = forward_terms(geo, count, stats_a, norm_a, width)
    clear_halo(geo, taps)
    clear_halo(geo, dtaps)
    for t in range(9):
        stacked[t * width : (t + 1) * width, :] = weight[:, t * width : (t + 1) * width]

    def fill(s):
        spread_taps(geo, taps, s, activate(geo, live, za, s, terms_a), False)
        keep = alive(live, s)
        values = []
        for start, size, group in geo.pieces(width):
            rows = pl.ds(pl.multiple_of(s * geo.rows + start, CELLS), size)
            scale, by_value, constant = terms_b[group]
            value = back_b[rows, :].astype(F32) * scale + zb[rows, :].astype(F32) * by_value
            values.append((value + constant) * (geo.mask(size, group, width) * keep))
        spread_taps(geo, dtaps, s, values, True)

    loop(2, fill)
    net.open()
    loop(geo.slabs - 2, lambda s: fill(s + 2))
    net.turn(1)
    span = geo.halo - CELLS
    total[...] = jnp.zeros(total.shape, F32)

    def slab(s):
        result = None
        for dy in range(3):
            begin = pl.multiple_of(s * geo.halo + (2 - dy) * CELLS, CELLS)
            term = nn(
                dtaps[pl.ds(begin, span), :], stacked[dy * 3 * width : (dy + 1) * 3 * width, :]
            )
            result = term if result is None else result + term
        keep = alive(live, s)
        for group, (begin, size) in enumerate(((0, geo.rg), (geo.rg + CELLS, geo.rl))):
            rows = pl.ds(pl.multiple_of(s * geo.rows + group * geo.rg, CELLS), size)
            scale, shift = terms_a[group]
            value = za[rows, :].astype(F32)
            mask = geo.mask(size, group, width) * keep
            piece = result[begin : begin + size] * (slope(value * scale + shift) * mask)
            back_a[rows, :] = piece.astype(BF16)
            acc[2 * group] += fold(piece)
            acc[2 * group + 1] += fold(piece * value)

    def grads(s):
        own = dtaps[
            pl.ds(pl.multiple_of(s * geo.halo + CELLS, CELLS), span), width : 2 * width
        ]
        for dy in range(3):
            begin = pl.multiple_of(s * geo.halo + dy * CELLS, CELLS)
            total[:, dy * 3 * width : (dy + 1) * 3 * width] += tn(own, taps[pl.ds(begin, span), :])

    loop(geo.slabs, slab)
    net.turn(2)
    finish(net.own, acc, 4)
    part = geo.slabs // 3
    net.begin()
    loop(part, grads)
    net.step()
    loop(part, lambda s: grads(s + part))
    net.step()
    loop(geo.slabs - 2 * part, lambda s: grads(s + 2 * part))
    put_pieces(wgrad, 0, total[...])
    net.end()


def stage_a_back(
    geo, net, live, count, za, stats_a, norm_a, back_a, sums_a, packed, wgrad, dza, ngrad,
):
    net.open()
    terms_a = backward_terms(geo, count, stats_a, norm_a, sums_a, ngrad, za.shape[1])
    loop(geo.slabs, lambda s: wide_back(geo, live, s, back_a, za, terms_a, dza))
    put_pieces(wgrad, 0, tn(dza[...], packed[...]))
    for number in range(1, 8):
        net.turn(number)
    net.close()


def last_kernel(geo, upright, joined, dza, hid, weight, *refs):
    count = len(upright)
    rows_in, refs = refs[:count], refs[count:]
    dxg, dxl, outg, outl = refs[:4]
    targets = refs[4:]
    result = nn(dza[...], weight[...]) + joined[...].astype(F32)
    half = CELLS // 2
    for i in range(geo.hg):
        dxg[0, i] = result[i * CELLS : i * CELLS + geo.hg]
        outg[0, i] = hid[i * CELLS : (i + 1) * CELLS, :][0 : geo.hg]
    for i in range(geo.hl):
        begin = geo.rg + i * CELLS
        low = hid[begin : begin + CELLS, :]
        for side in range(2):
            part = begin + side * half
            dxl[side, i] = result[part : part + geo.hl]
            outl[side, i] = low[side * half : side * half + geo.hl]

    def write(k):
        @pl.when(pl.program_id(0) == k % geo.slabs)
        def one():
            source, target = rows_in[k], targets[k]
            rows = source.shape[0] * source.shape[1]
            whole = source[...].astype(F32).reshape(rows, source.shape[2])
            target[...] = whole.T if upright[k] else whole

    for k in range(count):
        write(k)


def run_last(geo, joined, dza, hid, weight, parts, global_shape, local_shape):
    def whole(shape):
        return pl.BlockSpec(shape, lambda s: (0,) * len(shape))

    upright = [part.shape[0] * part.shape[1] >= 128 for part in parts]
    shapes = []
    for turn, part in zip(upright, parts):
        rows = part.shape[0] * part.shape[1]
        shapes.append((part.shape[2], rows) if turn else (rows, part.shape[2]))
    views = [
        pl.BlockSpec((1,) + global_shape[1:], lambda s: (s, 0, 0, 0)),
        pl.BlockSpec((2,) + local_shape[1:], lambda s: (s, 0, 0, 0)),
    ]
    outs = pl.pallas_call(
        functools.partial(last_kernel, geo, upright),
        grid=(geo.slabs,),
        out_shape=[
            jax.ShapeDtypeStruct(shape, dtype)
            for dtype in (F32, BF16)
            for shape in (global_shape, local_shape)
        ]
        + [jax.ShapeDtypeStruct(shape, F32) for shape in shapes],
        in_specs=[
            pl.BlockSpec((geo.rows, item.shape[1]), lambda s: (s, 0)) for item in (joined, dza, hid)
        ]
        + [whole(weight.shape)]
        + [whole(part.shape) for part in parts],
        out_specs=views + views + [whole(shape) for shape in shapes],
        compiler_params=pltpu.CompilerParams(vmem_limit_bytes=VMEM_CAP),
        name="last",
    )(joined, dza, hid, weight, *parts)
    return outs[:4], [item if turn else item.T for turn, item in zip(upright, outs[4:])]


class Group:
    def __init__(self, kind, reps, shards):
        rep, shard = lax.axis_index("rep"), lax.axis_index("fsdp")
        chip, core = shard // 2, lax.rem(shard, 2)
        wide = reps // 2
        low, high = lax.rem(rep, 2), rep // wide
        first = core == 0
        if kind == "core":
            self.size, self.me = 2, core
            self.address = lambda k: {"fsdp": chip * 2 + k}
        elif kind == "chips":
            self.size, self.me = shards // 2, chip
            self.address = lambda k: {"fsdp": k * 2 + core}
        elif kind == "shards":
            self.size, self.me = shards, shard
            self.address = lambda k: {"fsdp": k}
        elif kind == "reps":
            self.size, self.me = reps, rep
            self.address = lambda k: {"rep": k}
        elif kind == "near":
            self.size, self.me = 2, jnp.where(first, low, high)
            self.address = lambda k: {
                "rep": jnp.where(first, rep - low + k, rep - high * wide + k * wide)
            }
        else:
            self.size = wide
            self.me = jnp.where(first, rep // 2, lax.rem(rep, wide))
            self.address = lambda k: {"rep": jnp.where(first, k * 2 + low, high * wide + k)}

    def other(self, hop):
        return lax.rem(self.me + hop, self.size)


class Sums:
    def __init__(self, reps, shards, own, out, buffers, sems):
        self.own, self.out, self.buffers, self.sems = own, out, buffers, sems
        self.groups = [Group(kind, reps, shards) for kind in ("core", "chips", "reps")]
        self.phase = 0
        self.copies = []

    def send(self, source):
        group, buffer = self.groups[self.phase], self.buffers[self.phase]
        self.copies = []
        for hop in range(1, group.size):
            copy = pltpu.make_async_remote_copy(
                source, buffer.at[group.me], self.sems[2 * self.phase].at[hop],
                self.sems[2 * self.phase + 1].at[hop], device_id=group.address(group.other(hop)),
                device_id_type=MESH,
            )
            copy.start()
            self.copies.append(copy)

    def begin(self):
        self.send(self.own)
        self.buffers[0][self.groups[0].me] = self.own[...]

    def total(self):
        for copy in self.copies:
            copy.wait()
        buffer = self.buffers[self.phase]
        total = buffer[0]
        for k in range(1, self.groups[self.phase].size):
            total = total + buffer[k]
        return total

    def step(self):
        total = self.total()
        self.phase += 1
        group, buffer = self.groups[self.phase], self.buffers[self.phase]
        buffer[group.me] = total
        self.send(buffer.at[group.me])

    def end(self):
        while self.phase < 2:
            self.step()
        self.out[...] = self.total()


class Net:
    def __init__(self, reps, shards, sums=None, side=None, jobs=(), plans=()):
        self.reps, self.shards = reps, shards
        self.sums, self.side, self.jobs, self.plans = sums, side, jobs, plans
        self.own = None if sums is None else sums.own
        self.opened = False
        self.started, self.finished = set(), set()

    def enter(self):
        rep, shard = lax.axis_index("rep"), lax.axis_index("fsdp")
        barrier = pltpu.get_barrier_semaphore()
        for hop in range(1, self.shards):
            other = {"fsdp": lax.rem(shard + hop, self.shards)}
            pl.semaphore_signal(barrier, inc=1, device_id=other, device_id_type=MESH)
        for hop in range(1, self.reps):
            other = {"rep": lax.rem(rep + hop, self.reps)}
            pl.semaphore_signal(barrier, inc=1, device_id=other, device_id_type=MESH)

    def open(self):
        if not self.opened:
            self.opened = True
            pl.semaphore_wait(pltpu.get_barrier_semaphore(), self.shards + self.reps - 2)
            self.turn(0)

    def turn(self, number):
        for k, (start, end) in enumerate(self.plans):
            if end == number:
                self.finish(k)
        for k, (start, end) in enumerate(self.plans):
            if start == number:
                self.started.add(k)
                self.jobs[k].start()

    def finish(self, k):
        assert k in self.started and k not in self.finished
        self.finished.add(k)
        self.jobs[k].finish()

    def job_out(self, k):
        return self.jobs[k].out

    def begin(self):
        self.open()
        self.sums.begin()

    def step(self):
        self.sums.step()

    def end(self):
        self.sums.end()
        self.close()

    def run(self):
        self.begin()
        self.end()

    def close(self):
        for k in range(len(self.jobs)):
            if k not in self.finished:
                self.finish(k)


class Job:
    GROUPS = {
        "pair": "core", "join": "core", "line": "chips", "spread": "chips", "all": "shards",
        "share": "reps", "half": "near", "near": "near", "rest": "others", "others": "others",
    }

    def __init__(self, kind, reps, shards, sources, out, held, send, recv):
        self.kind, self.sources, self.out, self.held = kind, sources, out, held
        self.send, self.recv = send, recv
        self.reps, self.chips = reps, shards // 2
        self.rep, shard = lax.axis_index("rep"), lax.axis_index("fsdp")
        self.chip, self.core = shard // 2, lax.rem(shard, 2)
        self.group = Group(self.GROUPS[kind], reps, shards)

    def give(self, source, target, hop):
        k = len(self.copies)
        if hop == 0:
            copy = pltpu.make_async_copy(source, target, self.send.at[k])
        else:
            copy = pltpu.make_async_remote_copy(
                source, target, self.send.at[k], self.recv.at[k],
                device_id=self.group.address(self.group.other(hop)), device_id_type=MESH,
            )
        copy.start()
        self.copies.append(copy)

    def start(self):
        self.copies = []
        kind, out, source, group = self.kind, self.out, self.sources[0], self.group
        order = list(range(1, group.size)) + [0]
        wide = self.reps // 2
        first = self.core == 0
        if kind == "spread":
            for hop in order[:-1]:
                self.give(source.at[self.rep], out.at[group.size - hop - 1], hop)
        elif kind == "near":
            self.give(source, out, 1)
        elif kind == "others":
            low, high = lax.rem(self.rep, 2), self.rep // wide
            partner = jnp.where(
                first, self.rep + 1 - 2 * low, self.rep + (1 - 2 * high) * wide
            )
            for hop in order:
                self.give(source, out.at[self.rep], hop)
                self.give(self.sources[1], out.at[partner], hop)
        elif kind == "join":
            for hop in order:
                for step in range(1, self.chips):
                    chip = lax.rem(self.chip + step, self.chips)
                    self.give(source.at[:, step - 1], out.at[chip, self.core], hop)
                self.give(self.sources[1], out.at[self.chip, self.core], hop)
        elif kind in ("all", "share"):
            for hop in order:
                self.give(source, out.at[group.me], hop)
        elif kind == "half":
            low, high = lax.rem(self.rep, 2), self.rep // wide
            mine = jnp.where(first, low, high * wide)
            theirs = jnp.where(first, 1 - low, (1 - high) * wide)
            step = jnp.where(first, 2, 1)
            for k in range(wide):
                self.give(source.at[theirs + k * step], self.held.at[1, k], 1)
            for k in range(wide):
                self.give(source.at[mine + k * step], self.held.at[0, k], 0)
        else:
            for hop in order:
                self.give(source.at[group.other(hop)], self.held.at[group.me], hop)

    def finish(self):
        for copy in self.copies:
            copy.wait()
        held, out = self.held, self.out
        if held is None:
            return
        members = held.shape[0]
        blocks = held.shape[1:-2]

        def one(index):
            place = (index // blocks[-1], lax.rem(index, blocks[-1])) if len(blocks) == 2 else (
                (index,) if blocks else ()
            )
            total = held[(0,) + place].astype(F32)
            for k in range(1, members):
                total = total + held[(k,) + place].astype(F32)
            out[place[::-1] if self.kind == "pair" else place] = total.astype(BF16)

        if blocks:
            loop(blocks[0] * (blocks[1] if len(blocks) == 2 else 1), one)
        else:
            total = held[0].astype(F32)
            for k in range(1, members):
                total = total + held[k].astype(F32)
            out[...] = total.astype(BF16)


def job_shapes(kind, reps, shards, shape):
    chips = shards // 2
    if kind == "spread":
        return None, (chips - 1,) + shape[1:], chips
    if kind == "near":
        return None, shape, 1
    if kind == "others":
        return None, (reps,) + shape, reps
    if kind == "join":
        return None, (chips, 2, reps) + shape[2:], 2 * chips
    if kind == "all":
        return None, (shards,) + shape, shards
    if kind == "pair":
        return shape, (shape[2], shape[1]) + shape[3:], 2
    if kind == "share":
        return None, (reps,) + shape, reps
    if kind == "half":
        return (2, reps // 2) + shape[1:], (reps // 2,) + shape[1:], reps
    return shape, shape[1:], shape[0]


VMEM_CAP = 60 << 20
FAR = ("spread", "near", "others")


def sums_scratch(reps, shards, shape, own):
    sizes = (2, shards // 2, reps)
    return (
        [pltpu.VMEM(shape, F32)] * own
        + [pltpu.VMEM((size,) + shape, F32) for size in sizes]
        + [pltpu.SemaphoreType.DMA((size,)) for size in sizes for unused in range(2)]
    )


def run(name, kernel, geo, reps, shards, number, live, operands, results, scratch, sums, jobs, side, far=()):
    own_results = len(results)
    results = list(results)
    spaces = [pltpu.VMEM] * own_results
    extra = []
    arrays = []
    shapes = []
    for kind, sources, start, end in jobs:
        source = sources[0]
        if isinstance(source, int):
            shape, dtype = shapes[source]
        elif isinstance(source, str):
            shape, dtype = results[int(source)]
        else:
            shape, dtype = source.shape, source.dtype
        arrays += [item for item in sources if not isinstance(item, (int, str))]
        held, out, copies = job_shapes(kind, reps, shards, shape)
        shapes.append((out, dtype))
        results.append(shapes[-1])
        spaces.append(pltpu.HBM if kind in FAR else pltpu.VMEM)
        extra += [] if held is None else [pltpu.VMEM(held, BF16)]
        extra += [pltpu.SemaphoreType.DMA((copies,))] * 2
    operands = tuple(operands)
    near = len(operands)
    if side is not None:
        operands += (side,)
        results.append((side.shape, F32))
        spaces.append(pltpu.VMEM)
        extra += sums_scratch(reps, shards, side.shape, 0)
    if sums is not None:
        results.append((sums, F32))
        spaces.append(pltpu.VMEM)
        extra += sums_scratch(reps, shards, sums, 1)
    inputs = 1 + len(operands)
    remote = bool(jobs) or sums is not None

    def whole(*refs):
        sources_in = list(refs[inputs : inputs + len(arrays)])
        first_out = inputs + len(arrays)
        outs = refs[first_out : first_out + len(results)]
        more = list(refs[first_out + len(results) :])
        made = []
        for k, (kind, sources, start, end) in enumerate(jobs):
            refs_of = []
            for item in sources:
                if isinstance(item, int):
                    refs_of.append(made[item].out)
                elif isinstance(item, str):
                    refs_of.append(outs[int(item)])
                else:
                    refs_of.append(sources_in.pop(0))
            held = more.pop(0) if job_shapes(kind, reps, shards, refs_of[0].shape)[0] else None
            made.append(
                Job(kind, reps, shards, refs_of, outs[own_results + k], held, more.pop(0), more.pop(0))
            )
        beside, main = None, None
        place = own_results + len(jobs)
        if side is not None:
            beside = Sums(reps, shards, refs[near + 1], outs[place], more[0:3], more[3:9])
            more = more[9:]
        if sums is not None:
            main = Sums(reps, shards, more[0], outs[-1], more[1:4], more[4:10])
            more = more[10:]
        net = None
        if remote:
            plans = [job[2:] for job in jobs]
            net = Net(reps, shards, main, beside, made, plans)
            net.enter()
        kernel(geo, net, *refs[: near + 1], *outs[:own_results], *more)

    params = {"collective_id": number, "has_side_effects": True} if remote else {}
    return pl.pallas_call(
        whole,
        out_shape=[jax.ShapeDtypeStruct(shape, dtype) for shape, dtype in results],
        in_specs=[pl.BlockSpec(memory_space=pltpu.SMEM)]
        + [pl.BlockSpec(memory_space=pltpu.HBM if k in far else pltpu.VMEM) for k in range(len(operands))]
        + [pl.BlockSpec(memory_space=pl.ANY)] * len(arrays),
        out_specs=[pl.BlockSpec(memory_space=space) for space in spaces],
        scratch_shapes=extra
        + [item if not isinstance(item, tuple) else pltpu.VMEM(*item) for item in scratch],
        compiler_params=pltpu.CompilerParams(vmem_limit_bytes=VMEM_CAP, **params),
        name=name,
    )(live, *operands, *arrays)


def own_norms(first, second):
    flat = jnp.concatenate([first.reshape(-1), second.reshape(-1)]).astype(F32)
    size = -(-flat.shape[0] // 1024) * 1024
    return jnp.pad(flat, (0, size - flat.shape[0])).reshape(8, -1)


def all_norms(gathered, first, second):
    shards = gathered.shape[0]
    flat = gathered.reshape(shards, -1)
    split, last = first.size, first.size + second.size

    def whole(part):
        return part.reshape(shards, 2, -1).transpose(1, 0, 2).reshape(2, -1)

    return whole(flat[:, :split]), whole(flat[:, split:last])


def body(reps, shards, *arguments):
    (
        global_views, local_views, live, first_reduce, first_spatial, first_expand, first_norms,
        second_reduce, second_spatial, second_expand, second_short, second_norms, global_cotan,
        local_cotan,
    ) = arguments
    geo = Geometry(global_views.shape[0], global_views.shape[1], local_views.shape[1])
    assert local_views.shape[0] == 2 * geo.slabs
    channels = global_views.shape[3]
    ha, hb, hc, hd, he, hf, hs = (
        item.T.reshape(reps, -1, item.shape[0])
        for item in (
            first_reduce, first_spatial, first_expand, second_reduce, second_spatial,
            second_expand, second_short,
        )
    )
    he_0, he_1, he_2 = (he[:, :, k * he.shape[2] // 3 : (k + 1) * he.shape[2] // 3] for k in range(3))
    mid_1, mid_2 = first_reduce.shape[1] * shards, second_reduce.shape[1] * shards
    wide = second_expand.shape[1] * shards

    def rows_of(gathered):
        return gathered.reshape(-1, gathered.shape[-1])

    big, small = geo.total, geo.small_total

    numbers = iter(range(100))

    def go(name, kernel, operands, results, scratch, width=None, members=4, jobs=(), side=None, far=()):
        parts = {4: 2, 6: 4, 8: 2}[members]
        sums = None if width is None else (members * parts, width // parts)
        return run(
            name, kernel, geo, reps, shards, next(numbers), live, operands, results, scratch, sums,
            jobs, side, far,
        )

    def pieces(rows, columns):
        return ((2, shards // 2, reps, rows // (shards * reps), columns), BF16)

    def acc(width, members=4):
        return ((members, 8, width), F32)

    def stat(width):
        return ((8, width), F32)

    def both(width):
        return ((2, width), F32)

    more = go(
        "stage_a", stage_a, (global_views, local_views),
        [((big, channels), BF16), ((big, mid_1), BF16)],
        [
            acc(mid_1), ((mid_1, channels), BF16), (global_views.shape, BF16),
            (local_views.shape, BF16), pltpu.SemaphoreType.DMA((2,)),
        ],
        mid_1, 8,
        jobs=(
            ("spread", (ha,), 0, 1), ("near", (0,), 1, 2), ("others", (0, 1), 2, 3),
            ("join", (2, ha), 3, 4),
            ("spread", (hb,), 0, 2), ("near", (4,), 2, 3), ("others", (4, 5), 3, 5),
            ("join", (6, hb), 5, None),
            ("spread", (hc,), 0, 3), ("near", (8,), 3, 5), ("others", (8, 9), 5, None),
            ("spread", (hd,), 0, 3), ("near", (11,), 3, 5), ("others", (11, 12), 5, None),
            ("all", (own_norms(first_norms, second_norms),), 1, 5),
            ("spread", (he_0,), 3, 5), ("spread", (he_1,), 3, 5),
        ),
        far=(0, 1),
    )
    packed, za, wa, wb = more[0], more[1], more[2 + 3], more[2 + 7]
    far_c, far_d, norms, spread_e0, spread_e1 = (more[2 + k] for k in (10, 13, 14, 15, 16))
    sa = count = more[-1]
    wa, wb = rows_of(wa), rows_of(wb)
    norms_1, norms_2 = all_norms(norms, first_norms, second_norms)
    na, nb, nc = norms_1[:, :mid_1], norms_1[:, mid_1 : 2 * mid_1], norms_1[:, 2 * mid_1 :]
    nd, ne = norms_2[:, :mid_2], norms_2[:, mid_2 : 2 * mid_2]
    nf, ns = norms_2[:, 2 * mid_2 : 2 * mid_2 + wide], norms_2[:, 2 * mid_2 + wide :]
    zb, wc, wd, unused, far_e0, unused, far_e1, spread_e2, spread_f, sb = go(
        "stage_b", stage_b, (count, za, sa, na, wb), [((big, mid_1), BF16)],
        [((geo.halo_total, 3 * mid_1), BF16), acc(mid_1)], mid_1,
        jobs=(
            ("join", (far_c, hc), 0, 2), ("join", (far_d, hd), 0, 2),
            ("near", (spread_e0,), 0, 1), ("others", (spread_e0, 2), 1, 2),
            ("near", (spread_e1,), 0, 1), ("others", (spread_e1, 4), 1, 2),
            ("spread", (he_2,), 0, 2), ("spread", (hf,), 0, 2),
        ),
    )
    wc = rows_of(wc)
    zc, we_0, we_1, unused, far_e2, spread_s, sc = go(
        "stage_c", stage_c, (count, zb, sb, nb, wc), [((big, channels), BF16)],
        [((geo.rows, mid_1), BF16), acc(channels)], channels,
        jobs=(
            ("join", (far_e0, he_0), 0, 2), ("join", (far_e1, he_1), 0, 2),
            ("near", (spread_e2,), 0, 1), ("others", (spread_e2, 2), 1, 2), ("spread", (hs,), 0, 2),
        ),
    )
    wd = rows_of(wd)
    hid, zd, sub, we_2, unused, far_s, near_f, sd = go(
        "stage_d", stage_d, (count, zc, sc, nc, packed, wd),
        [((big, channels), BF16), ((big, mid_2), BF16), ((small, channels), BF16)],
        [((channels // 128, geo.rows, 128), F32), acc(mid_2)], mid_2,
        jobs=(
            ("join", (far_e2, he_2), 0, 2), ("near", (spread_s,), 0, 1),
            ("others", (spread_s, 1), 1, 2), ("near", (spread_f,), 1, 2),
        ),
    )
    we = tuple(rows_of(item) for item in (we_0, we_1, we_2))
    ze, zs, local_s, ws, unused, wf, se = go(
        "stage_e", stage_e, (count, zd, sd, nd, *we, sub),
        [((small, mid_2), BF16), ((small, wide), BF16), stat(wide // 2)],
        [
            ((mid_2 // 128, geo.halo, 128), F32), ((small, 9 * mid_2), BF16), acc(mid_2), acc(wide),
        ],
        mid_2,
        jobs=(
            ("join", (far_s, hs), 0, 2), ("others", (spread_f, near_f), 0, 2),
            ("join", (1, hf), 2, None),
        ),
    )
    wf, ws = rows_of(wf), rows_of(ws)
    act_e, zf, ss, sf = go(
        "stage_f", stage_f, (count, ze, se, ne, wf),
        [((small, mid_2), BF16), ((small, wide), BF16)], [acc(wide)], wide, side=local_s,
    )
    second_g, second_l, grad, local_pool, so = go(
        "stage_out", stage_out,
        (count, zf, zs, sf, ss, nf, ns, global_cotan, local_cotan),
        [
            (global_cotan.shape, BF16), (local_cotan.shape, BF16), ((small, wide), BF16),
            stat(wide // 4),
        ],
        [((geo.slabs, 8, wide), F32), ((geo.small, 512), F32), acc(wide, 8)], wide, 6,
    )
    unused, unused, back_sub, back_e, ngrad_f, ngrad_s, pair_f, pair_s, pool, qe = go(
        "stage_f_back", stage_f_back,
        (count, zf, zs, sf, ss, nf, ns, grad, so, act_e, sub, wf, ws, ze, se, ne),
        [
            pieces(wide, mid_2), pieces(wide, channels), ((small, channels), BF16), ((small, mid_2), BF16),
            both(wide), both(wide),
        ],
        [((small, wide), BF16), ((small, wide), BF16), acc(mid_2)], mid_2,
        jobs=(("pair", ("0",), 2, None), ("pair", ("1",), 1, None)), side=local_pool,
    )
    views = count[8, 0] * 6.0
    pool = pool.reshape(2, wide)
    center = pool[0] / views
    spread = pool[1] / views - center * center
    pooled_std = jnp.mean(jnp.sqrt(spread + 1e-06))
    wgrad_e, back_d, ngrad_e, half_f, half_s, qd = go(
        "stage_e_back", stage_e_back,
        (count, ze, se, ne, back_e, qe, zd, sd, nd, *we),
        [pieces(mid_2, 9 * mid_2), ((big, mid_2), BF16), both(mid_2)],
        [
            ((mid_2 // 128, geo.halo, 128), F32), ((small, 9 * mid_2), BF16),
            ((small, mid_2), BF16), ((3, small, mid_2), BF16), ((4, small, mid_2), F32),
            acc(mid_2),
        ],
        mid_2, jobs=(("half", (pair_f,), 0, None), ("half", (pair_s,), 0, None)),
    )
    wgrad_d, joined, ngrad_d, unused, half_e, rest_f, rest_s, qc = go(
        "stage_d_back", stage_d_back,
        (count, zd, sd, nd, back_d, qd, hid, packed, zc, sc, nc, back_sub, wd),
        [pieces(mid_2, channels), ((big, channels), BF16), both(mid_2)],
        [((big, mid_2), BF16), ((channels // 128, geo.rows, 128), F32), acc(channels)], channels,
        jobs=(
            ("pair", (wgrad_e,), 0, 1), ("half", (0,), 1, None),
            ("rest", (half_f,), 0, 1), ("rest", (half_s,), 0, 1),
        ),
    )
    wgrad_c, back_b, ngrad_c, pair_d, rest_e, line_f, line_s, qb = go(
        "stage_c_back", stage_c_back,
        (count, zc, sc, nc, joined, qc, zb, sb, nb, wc),
        [pieces(channels, mid_1), ((big, mid_1), BF16), both(channels)],
        [((big, channels), BF16), ((big, mid_1), BF16), acc(mid_1)], mid_1,
        jobs=(
            ("pair", (wgrad_d,), 0, 2), ("rest", (half_e,), 0, 2), ("line", (rest_f,), 0, 2),
            ("line", (rest_s,), 0, 2),
        ),
    )
    wgrad_b, back_a, ngrad_b, unused, rest_d, unused, half_c, line_e, out_f, out_s, qa = go(
        "stage_b_back", stage_b_back,
        (count, zb, sb, nb, back_b, qb, za, sa, na, wb),
        [pieces(mid_1, 9 * mid_1), ((big, mid_1), BF16), both(mid_1)],
        [
            ((geo.halo_total, 3 * mid_1), BF16), ((geo.halo_total, 3 * mid_1), BF16),
            ((9 * mid_1, mid_1), BF16), (wb.shape, F32), acc(mid_1),
        ],
        mid_1,
        jobs=(
            ("half", (pair_d,), 0, 1), ("rest", (0,), 1, 2), ("pair", (wgrad_c,), 0, 1),
            ("half", (2,), 1, 2), ("line", (rest_e,), 0, 2), ("share", (line_f,), 0, 2),
            ("share", (line_s,), 0, 2),
        ),
    )
    more = go(
        "stage_a_back", stage_a_back, (count, za, sa, na, back_a, qa, packed),
        [pieces(mid_1, channels), ((big, mid_1), BF16), both(mid_1)], [],
        jobs=(
            ("pair", (wgrad_b,), 0, 1), ("half", (0,), 1, 2), ("rest", (1,), 2, 3),
            ("line", (2,), 3, 4), ("share", (3,), 4, None),
            ("pair", ("0",), 1, 2), ("half", (5,), 2, 3), ("rest", (6,), 3, 4),
            ("line", (7,), 4, 5), ("share", (8,), 5, None),
            ("rest", (half_c,), 0, 1), ("line", (10,), 1, 2), ("share", (11,), 2, None),
            ("line", (rest_d,), 0, 1), ("share", (13,), 1, None),
            ("share", (line_e,), 0, None),
        ),
    )
    dza, ngrad_a = more[1], more[2]
    out_b, out_a, out_c, out_d, out_e = (more[3 + k] for k in (4, 9, 12, 14, 15))
    (grad_g, grad_l, first_g, first_l), columns = run_last(
        geo, joined, dza, hid, wa, (out_a, out_b, out_c, out_d, out_e, out_f, out_s),
        global_views.shape, local_views.shape,
    )
    shard = lax.axis_index("fsdp")

    def own_columns(parts, width):
        whole = jnp.concatenate(parts, axis=1)
        return lax.dynamic_slice_in_dim(whole, shard * width, width, 1)

    return (
        first_g, first_l, second_g, second_l, grad_g, grad_l,
        *columns[0:3],
        own_columns((ngrad_a, ngrad_b, ngrad_c), first_norms.shape[1]),
        *columns[3:7],
        own_columns((ngrad_d, ngrad_e, ngrad_f, ngrad_s), second_norms.shape[1]),
        pooled_std,
    )


def solution(mesh):
    views = P(("rep", "fsdp"), None, None, None)
    columns = P(None, "fsdp")
    return jax.shard_map(
        functools.partial(body, mesh.shape["rep"], mesh.shape["fsdp"]),
        mesh=mesh,
        in_specs=(views, views, P(("rep", "fsdp"))) + (columns,) * 9 + (views, views),
        out_specs=(views,) * 6 + (columns,) * 9 + (P(),),
        check_vma=False,
    )
```

```python
import functools

import jax
import jax.numpy as jnp
from jax import lax
from jax.experimental import pallas as pl
from jax.experimental.pallas import tpu as pltpu
from jax.sharding import PartitionSpec as P

EPSILON = 1e-05
F32 = jnp.float32
BF16 = jnp.bfloat16
MESH = pl.DeviceIdType.MESH
CELLS = 16


def nt(left, right):
    return lax.dot_general(left, right, (((1,), (1,)), ((), ())), preferred_element_type=F32)


def nn(left, right):
    return lax.dot_general(left, right, (((1,), (0,)), ((), ())), preferred_element_type=F32)


def tn(left, right):
    return lax.dot_general(left, right, (((0,), (0,)), ((), ())), preferred_element_type=F32)


def sig(values):
    return 0.5 * jnp.tanh(0.5 * values) + 0.5


def silu(values):
    return values * sig(values)


def slope(values):
    gate = sig(values)
    held = values * gate
    return gate + held - held * gate


def lanes(tile, width):
    return jnp.concatenate([tile] * (width // tile.shape[1]), axis=1)


def fold(values):
    return jnp.sum(values.reshape(values.shape[0] // 8, 8, values.shape[1]), axis=0)


class Geometry:
    def __init__(self, views, side_global, side_local):
        self.slabs = views
        self.hg, self.hl = side_global, side_local
        assert side_global < CELLS and side_local < CELLS // 2
        self.rg, self.rl = side_global * CELLS, side_local * CELLS
        self.rows = self.rg + self.rl
        self.og, self.ol = (side_global - 1) // 2 + 1, (side_local - 1) // 2 + 1
        self.sg, self.sl = self.og * 8, self.ol * 8
        self.small = self.sg + self.sl
        self.total, self.small_total = self.slabs * self.rows, self.slabs * self.small
        self.halo = self.rows + 2 * CELLS
        self.halo_total = self.slabs * self.halo + CELLS
        self.chunk = 32
        assert self.rg % self.chunk == 0 and self.rl % self.chunk == 0 and self.small % 16 == 0

    def pieces(self, width):
        if width <= 256:
            return [(0, self.rg, 0), (self.rg, self.rl, 1)]
        step = self.chunk
        return [(start, step, 0) for start in range(0, self.rg, step)] + [
            (start, step, 1) for start in range(self.rg, self.rows, step)
        ]

    def mask(self, count, group, width):
        row = lax.broadcasted_iota(jnp.int32, (count, 128), 0)
        if group == 0:
            keep = (row & (CELLS - 1)) < self.hg
        else:
            keep = (row & (CELLS // 2 - 1)) < self.hl
        return lanes(keep.astype(F32), width)

    def small_mask(self, group, width):
        count = self.sl if group else self.sg
        row = lax.broadcasted_iota(jnp.int32, (count, 128), 0)
        keep = (row & 3) < self.ol if group else (row & 7) < self.og
        return lanes(keep.astype(F32), width)

    def small_pieces(self):
        return [(0, self.sg, 0), (self.sg, self.sl, 1)]


def alive(live, slab):
    return jnp.where(slab < 2 * live[0], 1.0, 0.0).astype(F32)


def cells(geo, count, group, width, small=False):
    images = lanes(count[8:9, 0:128], width)
    if small:
        return images * float(2 * geo.og * geo.og if group == 0 else 4 * geo.ol * geo.ol)
    return images * float(2 * geo.hg * geo.hg if group == 0 else 4 * geo.hl * geo.hl)


def member(sums, row, width):
    parts = width // sums.shape[1]
    return jnp.concatenate(
        [sums[row * parts + k : row * parts + k + 1, :] for k in range(parts)], axis=1
    )


def norm_terms(stats, norm, number, group):
    width = norm.shape[1]
    mean = member(stats, 2 * group, width) / number
    spread = member(stats, 2 * group + 1, width) / number - mean * mean
    inverse = lax.rsqrt(spread + EPSILON)
    scale = norm[0:1, :] * inverse
    return mean, inverse, scale, norm[1:2, :] - mean * scale


def back_terms(stats, norm, number, group, first, second_raw):
    mean, inverse, scale, unused = norm_terms(stats, norm, number, group)
    second = inverse * (second_raw - mean * first)
    by_value = -scale * inverse * (second / number)
    constant = -scale * (first / number) - by_value * mean
    return scale, by_value, constant, second


def forward_terms(geo, count, stats, norm, width, small=False):
    return [
        norm_terms(stats, norm, cells(geo, count, group, width, small), group)[2:]
        for group in range(2)
    ]


def backward_terms(geo, count, stats, norm, sums, out, width, small=False, rows=((0, 1), (2, 3))):
    terms = []
    seconds = []
    for group in range(2):
        number = cells(geo, count, group, width, small)
        first = member(sums, rows[group][0], width)
        raw = member(sums, rows[group][1], width)
        scale, by_value, constant, second = back_terms(stats, norm, number, group, first, raw)
        terms.append((scale, by_value, constant))
        seconds.append((second, first))
    out[0:1, :] = seconds[0][0] + seconds[1][0]
    out[1:2, :] = seconds[0][1] + seconds[1][1]
    return terms


def finish(stats, acc, members, begin=0):
    part = stats.shape[1]
    parts = acc.shape[2] // part
    for row in range(members):
        total = jnp.sum(acc[begin + row], axis=0, keepdims=True)
        for k in range(parts):
            stats[row * parts + k : row * parts + k + 1, :] = total[:, k * part : (k + 1) * part]


def put(store, place, values):
    for k in range(store.shape[0]):
        store[k, place, :] = values[:, k * 128 : (k + 1) * 128]


def take(store, place):
    return jnp.concatenate([store[k, place, :] for k in range(store.shape[0])], axis=1)


def put_pieces(pieces, first, values, begin=0):
    cores, chips, reps, size = pieces.shape[:4]
    cols = slice(begin, begin + values.shape[1])
    for k in range(values.shape[0] // size):
        index = first // size + k
        shard, rep = index // reps, index % reps
        part = values[k * size : (k + 1) * size]
        pieces[shard % cores, shard // cores, rep, :, cols] = part.astype(BF16)


def loop(count, step):
    def one(index, carry):
        step(index)
        return carry

    lax.fori_loop(0, count, one, 0)


def at(index, size):
    return pl.ds(pl.multiple_of(index * size, size), size)


def stage_a(geo, net, live, xg, xl, packed, conv, acc, weight, own_g, own_l, arrive):
    loads = (
        pltpu.make_async_copy(xg, own_g, arrive.at[0]),
        pltpu.make_async_copy(xl, own_l, arrive.at[1]),
    )
    for load in loads:
        load.start()
    net.open()
    acc[...] = jnp.zeros(acc.shape, F32)
    blank = jnp.zeros((CELLS, packed.shape[1]), BF16)
    half = CELLS // 2
    for load in loads:
        load.wait()

    def pack(s):
        base = s * geo.rows
        keep = alive(live, s).astype(BF16)
        for i in range(geo.hg):
            start = pl.multiple_of(base + i * CELLS, CELLS)
            packed[pl.ds(start, CELLS), :] = blank
            packed[pl.ds(start, geo.hg), :] = own_g[s, i] * keep
        for i in range(geo.hl):
            start = pl.multiple_of(base + geo.rg + i * CELLS, CELLS)
            packed[pl.ds(start, CELLS), :] = blank
            for side in range(2):
                place = pl.multiple_of(start + side * half, half)
                packed[pl.ds(place, geo.hl), :] = own_l[2 * s + side, i] * keep

    part = geo.slabs // 4
    for number in range(4):
        begin = number * part
        size = part if number < 3 else geo.slabs - begin
        loop(size, lambda s: pack(s + begin))
        net.turn(number + 1)
    gathered = net.job_out(3)
    weight[...] = gathered[...].astype(F32).reshape(weight.shape).astype(BF16)

    def slab(s):
        result = nt(packed[at(s, geo.rows), :], weight[...])
        conv[at(s, geo.rows), :] = result.astype(BF16)
        for start, size, group in geo.pieces(256):
            piece = result[start : start + size]
            acc[2 * group] += fold(piece)
            acc[2 * group + 1] += fold(piece * piece)

    loop(geo.slabs, slab)
    finish(net.own, acc, 4)
    net.own[8:16, :] = jnp.full((8, net.own.shape[1]), live[0], jnp.int32).astype(F32)
    net.turn(5)
    net.run()


def spread_taps(geo, store, s, values, reverse):
    width = values[0].shape[1]
    for group in range(2):
        rows = values[group]
        size = rows.shape[0]
        start = pl.multiple_of(s * geo.halo + CELLS + group * (geo.rg + CELLS), CELLS)
        before = pltpu.roll(rows, 1, 0)
        after = pltpu.roll(rows, size - 1, 0)
        order = (after, rows, before) if reverse else (before, rows, after)
        for tap in range(3):
            store[pl.ds(start, size), tap * width : (tap + 1) * width] = order[tap].astype(BF16)


def clear_halo(geo, store):
    blank = jnp.zeros((CELLS, store.shape[1]), BF16)

    def slab(s):
        store[pl.ds(pl.multiple_of(s * geo.halo, CELLS), CELLS), :] = blank
        store[pl.ds(pl.multiple_of(s * geo.halo + CELLS + geo.rg, CELLS), CELLS), :] = blank

    loop(geo.slabs, slab)
    store[geo.slabs * geo.halo : geo.slabs * geo.halo + CELLS, :] = blank


def activate(geo, live, conv, s, terms):
    values = []
    width = conv.shape[1]
    keep = alive(live, s)
    for group in range(2):
        start, size = (geo.rg, geo.rl) if group else (0, geo.rg)
        rows = conv[pl.ds(pl.multiple_of(s * geo.rows + start, CELLS), size), :].astype(F32)
        scale, shift = terms[group]
        values.append(silu(rows * scale + shift) * (geo.mask(size, group, width) * keep))
    return values


def stage_b(geo, net, live, count, za, stats_a, norm, weight, conv, taps, acc):
    acc[...] = jnp.zeros(acc.shape, F32)
    width = za.shape[1]
    terms = forward_terms(geo, count, stats_a, norm, width)
    clear_halo(geo, taps)

    def fill(s):
        spread_taps(geo, taps, s, activate(geo, live, za, s, terms), False)

    loop(2, fill)
    net.open()
    loop(geo.slabs - 2, lambda s: fill(s + 2))
    span = geo.halo - CELLS

    def slab(s):
        result = None
        for dy in range(3):
            rows = taps[pl.ds(pl.multiple_of(s * geo.halo + dy * CELLS, CELLS), span), :]
            term = nt(rows, weight[:, dy * 3 * width : (dy + 1) * 3 * width])
            result = term if result is None else result + term
        keep = alive(live, s)
        for group, (begin, size) in enumerate(((0, geo.rg), (geo.rg + CELLS, geo.rl))):
            piece = result[begin : begin + size]
            start = pl.multiple_of(s * geo.rows + group * geo.rg, CELLS)
            conv[pl.ds(start, size), :] = piece.astype(BF16)
            piece = piece * (geo.mask(size, group, width) * keep)
            acc[2 * group] += fold(piece)
            acc[2 * group + 1] += fold(piece * piece)

    loop(2, slab)
    net.turn(1)
    loop(geo.slabs - 2, lambda s: slab(s + 2))
    net.turn(2)
    finish(net.own, acc, 4)
    net.run()


def stage_c(geo, net, live, count, zb, stats_b, norm, weight, conv, act, acc):
    acc[...] = jnp.zeros(acc.shape, F32)
    terms = forward_terms(geo, count, stats_b, norm, zb.shape[1])
    step = 256

    def slab(s):
        values = activate(geo, live, zb, s, terms)
        act[0 : geo.rg, :] = values[0].astype(BF16)
        act[geo.rg : geo.rows, :] = values[1].astype(BF16)
        for c in range(0, weight.shape[0], step):
            result = nt(act[...], weight[c : c + step, :])
            conv[at(s, geo.rows), c : c + step] = result.astype(BF16)
            for start, size, group in geo.pieces(256):
                piece = result[start : start + size]
                acc[2 * group, :, c : c + step] += fold(piece)
                acc[2 * group + 1, :, c : c + step] += fold(piece * piece)

    loop(2, slab)
    net.open()
    loop(4, lambda s: slab(s + 2))
    net.turn(1)
    loop(geo.slabs - 6, lambda s: slab(s + 6))
    net.turn(2)
    finish(net.own, acc, 4)
    net.run()


def even_rows(geo):
    return [2 * i * CELLS for i in range(geo.og)] + [
        geo.rg + 2 * i * CELLS for i in range(geo.ol)
    ]


def stage_d(
    geo, net, live, count, zc, stats_c, norm, packed, weight, short, hid, conv, sub, conv_s, stats_s,
    full, acc, acc_s,
):
    acc[...] = jnp.zeros(acc.shape, F32)
    width = zc.shape[1]
    terms = forward_terms(geo, count, stats_c, norm, width)

    def slab(s):
        keep = alive(live, s)
        for start, size, group in geo.pieces(width):
            rows = pl.ds(pl.multiple_of(s * geo.rows + start, CELLS), size)
            scale, shift = terms[group]
            joined = zc[rows, :].astype(F32) * scale + shift + packed[rows, :].astype(F32)
            value = silu(joined) * (geo.mask(size, group, width) * keep)
            put(full, pl.ds(start, size), value)
            hid[rows, :] = value.astype(BF16)
        picked = [take(full, pl.ds(start, 8, stride=2)) for start in even_rows(geo)]
        sub[at(s, geo.small), :] = jnp.concatenate(picked, axis=0).astype(BF16)
        result = nt(hid[at(s, geo.rows), :], weight[...])
        conv[at(s, geo.rows), :] = result.astype(BF16)
        for start, size, group in geo.pieces(256):
            piece = result[start : start + size]
            acc[2 * group] += fold(piece)
            acc[2 * group + 1] += fold(piece * piece)

    loop(1, slab)
    net.open()
    loop(4, lambda s: slab(s + 1))
    net.turn(1)
    loop(geo.slabs - 5, lambda s: slab(s + 5))
    net.turn(2)
    finish(net.own, acc, 4)
    net.begin()
    acc_s[...] = jnp.zeros(acc_s.shape, F32)
    wide, step = short.shape[0], 256

    def pick(c):
        return short[c : c + step, :]

    small_product(geo, sub, pick, step, conv_s, acc_s, 0, wide // 4)
    net.step()
    small_product(geo, sub, pick, step, conv_s, acc_s, wide // 4, 5 * wide // 8)
    net.step()
    small_product(geo, sub, pick, step, conv_s, acc_s, 5 * wide // 8, wide)
    finish(stats_s, acc_s, 4)
    net.end()


def small_product(geo, left, pick, step, conv, acc, first, last):
    for c in range(first, last, step):
        result = nt(left[...], pick(c))
        conv[:, c : c + step] = result.astype(BF16)
        for s in range(geo.slabs):
            for start, size, group in geo.small_pieces():
                piece = result[s * geo.small + start : s * geo.small + start + size]
                acc[2 * group, :, c : c + step] += fold(piece)
                acc[2 * group + 1, :, c : c + step] += fold(piece * piece)


def gather_taps(geo, net, live, zd, terms, full, taps):
    width = zd.shape[1]
    blank = jnp.zeros((8, width), F32)
    full[:, 0:CELLS, :] = jnp.zeros((width // 128, CELLS, 128), F32)
    full[:, CELLS + geo.rg : 2 * CELLS + geo.rg, :] = jnp.zeros((width // 128, CELLS, 128), F32)

    def slab(s):
        keep = alive(live, s)
        for start, size, group in geo.pieces(width):
            rows = pl.ds(pl.multiple_of(s * geo.rows + start, CELLS), size)
            scale, shift = terms[group]
            value = silu(zd[rows, :].astype(F32) * scale + shift)
            begin = CELLS + start + group * CELLS
            put(full, pl.ds(begin, size), value * (geo.mask(size, group, width) * keep))
        for dy in range(3):
            for dx in range(3):
                picked = []
                for group in range(2):
                    for i in range(geo.ol if group else geo.og):
                        line = 2 * i + dy - 1
                        if line < 0:
                            picked.append(blank)
                            continue
                        begin = CELLS + group * (geo.rg + CELLS) + line * CELLS + dx - 1
                        picked.append(take(full, pl.ds(begin, 8, stride=2)))
                tap = dy * 3 + dx
                taps[at(s, geo.small), tap * width : (tap + 1) * width] = jnp.concatenate(
                    picked, axis=0
                ).astype(BF16)

    loop(2, slab)
    net.open()
    loop(geo.slabs - 2, lambda s: slab(s + 2))


def stage_e(
    geo, net, live, count, zd, stats_d, norm, weight_0, weight_1, weight_2, conv, full, taps,
    acc,
):
    acc[...] = jnp.zeros(acc.shape, F32)
    terms = forward_terms(geo, count, stats_d, norm, zd.shape[1])
    gather_taps(geo, net, live, zd, terms, full, taps)
    net.turn(1)
    net.side.begin()
    step = 256
    third = weight_0.shape[1]
    for c in range(0, weight_0.shape[0], step):
        if c > 0:
            net.side.step()
        result = nt(taps[:, 0:third], weight_0[c : c + step, :])
        result = result + nt(taps[:, third : 2 * third], weight_1[c : c + step, :])
        result = result + nt(taps[:, 2 * third :], weight_2[c : c + step, :])
        conv[:, c : c + step] = result.astype(BF16)
        for s in range(geo.slabs):
            keep = alive(live, s)
            for start, size, group in geo.small_pieces():
                piece = result[s * geo.small + start : s * geo.small + start + size]
                piece = piece * (geo.small_mask(group, step) * keep)
                acc[2 * group, :, c : c + step] += fold(piece)
                acc[2 * group + 1, :, c : c + step] += fold(piece * piece)
    net.side.step()
    net.turn(2)
    net.side.end()
    finish(net.own, acc, 4)
    net.run()


def stage_f(geo, net, live, count, ze, stats_e, norm, weight, act, conv, acc):
    acc[...] = jnp.zeros(acc.shape, F32)
    width = ze.shape[1]
    terms = forward_terms(geo, count, stats_e, norm, width, True)

    def slab(s):
        keep = alive(live, s)
        rows = ze[at(s, geo.small), :].astype(F32)
        parts = []
        for start, size, group in geo.small_pieces():
            scale, shift = terms[group]
            value = silu(rows[start : start + size] * scale + shift)
            parts.append(value * (geo.small_mask(group, width) * keep))
        act[at(s, geo.small), :] = jnp.concatenate(parts, axis=0).astype(BF16)

    loop(geo.slabs, slab)
    half, step = weight.shape[0] // 2, 256

    def pick(c):
        return weight[c : c + step, :]

    small_product(geo, act, pick, step, conv, acc, 0, half)
    net.open()
    small_product(geo, act, pick, step, conv, acc, half, 2 * half)
    finish(net.own, acc, 4)
    net.run()


def stage_out(
    geo, net, live, count, zf, zs, stats_f, stats_s, norm_f, norm_s, cotg, cotl, outg, outl, grad,
    pooled_sums, pool, cot, acc,
):
    acc[...] = jnp.zeros(acc.shape, F32)
    cot[...] = jnp.zeros(cot.shape, F32)
    pool[...] = jnp.zeros(pool.shape, F32)
    width = zf.shape[1]
    step = 512
    terms_f = forward_terms(geo, count, stats_f, norm_f, width, True)
    terms_s = forward_terms(geo, count, stats_s, norm_s, width, True)

    def slab(s):
        keep = alive(live, s)
        for c in range(0, width, step):
            cols = slice(c, c + step)
            for i in range(geo.og):
                cot[i * 8 : i * 8 + geo.og, :] = cotg[s, i, :, cols].astype(F32)
            for i in range(geo.ol):
                for side in range(2):
                    begin = geo.sg + i * 8 + side * 4
                    cot[begin : begin + geo.ol, :] = cotl[2 * s + side, i, :, cols].astype(F32)
            rows_f = zf[at(s, geo.small), cols].astype(F32)
            rows_s = zs[at(s, geo.small), cols].astype(F32)
            grads = []
            for start, size, group in geo.small_pieces():
                part = slice(start, start + size)
                vf, vs = rows_f[part], rows_s[part]
                scale_f, shift_f = (item[:, cols] for item in terms_f[group])
                scale_s, shift_s = (item[:, cols] for item in terms_s[group])
                joined = vf * scale_f + vs * scale_s + (shift_f + shift_s)
                mask = geo.small_mask(group, step) * keep
                gate = sig(joined)
                held = joined * gate
                value = held * mask
                low = value.astype(BF16)
                dy = cot[part, :] * ((gate + held - held * gate) * mask)
                grads.append(dy)
                acc[3 * group, :, cols] += fold(dy)
                acc[3 * group + 1, :, cols] += fold(dy * vf)
                acc[3 * group + 2, :, cols] += fold(dy * vs)
                summed = fold(value)
                if group == 0:
                    for i in range(geo.og):
                        outg[s, i, :, cols] = value[i * 8 : i * 8 + geo.og].astype(BF16)
                    pool[s, 0:1, cols] = jnp.sum(summed, axis=0, keepdims=True) * (
                        1.0 / (geo.og * geo.og)
                    )
                else:
                    row = lax.broadcasted_iota(jnp.int32, (8, step), 0)
                    for side in range(2):
                        own = jnp.where((row >= 4) == (side == 1), summed, 0.0)
                        pool[s, 1 + side : 2 + side, cols] = jnp.sum(
                            own, axis=0, keepdims=True
                        ) * (1.0 / (geo.ol * geo.ol))
                        for i in range(geo.ol):
                            begin = i * 8 + side * 4
                            outl[2 * s + side, i, :, cols] = value[begin : begin + geo.ol].astype(
                                BF16
                            )
            grad[at(s, geo.small), cols] = jnp.concatenate(grads, axis=0).astype(BF16)
        pooled = pool[s]
        square = jnp.mean(pooled * pooled, axis=1, keepdims=True)
        normed = pooled * lax.rsqrt(square + 1e-06)
        acc[6] += normed
        acc[7] += normed * normed

    loop(geo.slabs, slab)
    finish(net.own, acc, 6)
    net.begin()
    finish(pooled_sums, acc, 2, 6)
    net.end()


def small_back(geo, live, s, grad, conv, terms, width, cols):
    keep = alive(live, s)
    rows_g = grad[at(s, geo.small), cols].astype(F32)
    rows_z = conv[at(s, geo.small), cols].astype(F32)
    parts = []
    for start, size, group in geo.small_pieces():
        scale, by_value, constant = (item[:, cols] for item in terms[group])
        part = slice(start, start + size)
        value = rows_g[part] * scale + rows_z[part] * by_value + constant
        parts.append(value * (geo.small_mask(group, width) * keep))
    return jnp.concatenate(parts, axis=0).astype(BF16)


def stage_f_back(
    geo, net, live, count, zf, zs, stats_f, stats_s, norm_f, norm_s, grad, sums, act, sub, weight,
    short, ze, stats_e, norm_e, wgrad_f, wgrad_s, back_sub, back_e, ngrad_f, ngrad_s, dzf, dzs, acc,
):
    acc[...] = jnp.zeros(acc.shape, F32)
    width = zf.shape[1]
    step = 512
    rows_f, rows_s = ((0, 1), (3, 4)), ((0, 2), (3, 5))
    terms_f = backward_terms(geo, count, stats_f, norm_f, sums, ngrad_f, width, True, rows_f)
    terms_s = backward_terms(geo, count, stats_s, norm_s, sums, ngrad_s, width, True, rows_s)

    def slab(s):
        for c in range(0, width, step):
            cols = slice(c, c + step)
            dzf[at(s, geo.small), cols] = small_back(geo, live, s, grad, zf, terms_f, step, cols)
            dzs[at(s, geo.small), cols] = small_back(geo, live, s, grad, zs, terms_s, step, cols)

    loop(geo.slabs, slab)
    net.open()
    net.side.begin()
    block = 256
    terms_e = forward_terms(geo, count, stats_e, norm_e, ze.shape[1], True)
    for c in range(0, act.shape[1], block):
        cols = slice(c, c + block)
        result = nn(dzf[...], weight[:, cols])
        for s in range(geo.slabs):
            keep = alive(live, s)
            rows = ze[s * geo.small : (s + 1) * geo.small, cols].astype(F32)
            parts = []
            for start, size, group in geo.small_pieces():
                scale, shift = (item[:, cols] for item in terms_e[group])
                value = rows[start : start + size]
                mask = geo.small_mask(group, block) * keep
                piece = result[s * geo.small + start : s * geo.small + start + size]
                piece = piece * (slope(value * scale + shift) * mask)
                parts.append(piece)
                acc[2 * group, :, cols] += fold(piece)
                acc[2 * group + 1, :, cols] += fold(piece * value)
            back_e[s * geo.small : (s + 1) * geo.small, cols] = jnp.concatenate(
                parts, axis=0
            ).astype(BF16)
    finish(net.own, acc, 4)
    net.begin()
    for c in range(0, width, block):
        cols = slice(c, c + block)
        put_pieces(wgrad_s, c, tn(dzs[:, cols], sub[...]))
        if c == width // 4:
            net.step()
    net.step()
    net.turn(1)
    for c in range(0, width, block):
        cols = slice(c, c + block)
        put_pieces(wgrad_f, c, tn(dzf[:, cols], act[...]))
        if c == width // 4:
            net.side.step()
    net.side.step()
    net.turn(2)
    for c in range(0, sub.shape[1], block):
        cols = slice(c, c + block)
        back_sub[:, cols] = nn(dzs[...], short[:, cols]).astype(BF16)
    net.side.end()
    net.end()


def stage_e_back(
    geo, net, live, count, ze, stats_e, norm_e, back_e, sums_e, zd, stats_d, norm_d, weight_0, weight_1,
    weight_2, wgrad, back_d, ngrad, full, taps, dze, moved, parity, acc,
):
    acc[...] = jnp.zeros(acc.shape, F32)
    width = ze.shape[1]
    terms_e = backward_terms(geo, count, stats_e, norm_e, sums_e, ngrad, width, True)
    terms_d = forward_terms(geo, count, stats_d, norm_d, width)
    gather_taps(geo, net, live, zd, terms_d, full, taps)

    def shift(s):
        value = small_back(geo, live, s, back_e, ze, terms_e, width, slice(0, width)).astype(F32)
        blank = jnp.zeros((8, width), F32)
        down = jnp.concatenate(
            [value[8 : geo.sg], blank, value[geo.sg + 8 :], blank], axis=0
        )
        size = geo.small
        dze[at(s, size), :] = value.astype(BF16)
        moved[0, at(s, size), :] = pltpu.roll(value, size - 1, 0).astype(BF16)
        moved[1, at(s, size), :] = down.astype(BF16)
        moved[2, at(s, size), :] = pltpu.roll(down, size - 1, 0).astype(BF16)

    loop(geo.slabs, shift)

    def tap(dy, dx):
        return (weight_0, weight_1, weight_2)[dy][:, dx * width : (dx + 1) * width]

    def grads(first, last):
        for t in range(first, last):
            result = tn(dze[...], taps[:, t * width : (t + 1) * width])
            put_pieces(wgrad, 0, result, t * width)

    parity[0] = nn(dze[...], tap(1, 1))
    parity[1] = nn(dze[...], tap(1, 2)) + nn(moved[0], tap(1, 0))
    parity[2] = nn(dze[...], tap(2, 1)) + nn(moved[1], tap(0, 1))
    parity[3] = (
        nn(dze[...], tap(2, 2))
        + nn(moved[0], tap(2, 0))
        + nn(moved[1], tap(0, 2))
        + nn(moved[2], tap(0, 0))
    )

    def slab(s):
        keep = alive(live, s)
        for group in range(2):
            for i in range(geo.ol if group else geo.og):
                for a in range(2):
                    for b in range(2):
                        begin = group * geo.rg + (2 * i + a) * CELLS + b
                        source = s * geo.small + group * geo.sg + i * 8
                        part = parity[2 * a + b, pl.ds(pl.multiple_of(source, 8), 8), :]
                        put(full, pl.ds(begin, 8, stride=2), part)
        for start, size, group in geo.pieces(width):
            rows = pl.ds(pl.multiple_of(s * geo.rows + start, CELLS), size)
            scale, shift_d = terms_d[group]
            value = zd[rows, :].astype(F32)
            mask = geo.mask(size, group, width) * keep
            piece = take(full, pl.ds(start, size)) * (slope(value * scale + shift_d) * mask)
            back_d[rows, :] = piece.astype(BF16)
            acc[2 * group] += fold(piece)
            acc[2 * group + 1] += fold(piece * value)

    loop(geo.slabs, slab)
    finish(net.own, acc, 4)
    net.begin()
    grads(0, 3)
    net.step()
    grads(3, 6)
    net.step()
    grads(6, 9)
    net.end()


def wide_back(geo, live, s, grad, conv, terms, low):
    width = conv.shape[1]
    keep = alive(live, s)
    for start, size, group in geo.pieces(width):
        rows = pl.ds(pl.multiple_of(s * geo.rows + start, CELLS), size)
        scale, by_value, constant = terms[group]
        value = grad[rows, :].astype(F32) * scale + conv[rows, :].astype(F32) * by_value + constant
        low[rows, :] = (value * (geo.mask(size, group, width) * keep)).astype(BF16)


def stage_d_back(
    geo, net, live, count, zd, stats_d, norm_d, back_d, sums_d, hid, packed, zc, stats_c, norm_c,
    back_sub, weight, wgrad, joined, ngrad, dzd, full, acc,
):
    acc[...] = jnp.zeros(acc.shape, F32)
    width = zc.shape[1]
    terms_d = backward_terms(geo, count, stats_d, norm_d, sums_d, ngrad, zd.shape[1])
    terms_c = forward_terms(geo, count, stats_c, norm_c, width)

    def slab(s):
        wide_back(geo, live, s, back_d, zd, terms_d, dzd)
        put(full, pl.ds(0, geo.rows), nn(dzd[at(s, geo.rows), :], weight[...]))
        extra = back_sub[at(s, geo.small), :].astype(F32)
        for k, start in enumerate(even_rows(geo)):
            place = pl.ds(start, 8, stride=2)
            put(full, place, take(full, place) + extra[k * 8 : k * 8 + 8])
        keep = alive(live, s)
        for start, size, group in geo.pieces(width):
            rows = pl.ds(pl.multiple_of(s * geo.rows + start, CELLS), size)
            scale, shift = terms_c[group]
            value = zc[rows, :].astype(F32)
            pre = value * scale + shift + packed[rows, :].astype(F32)
            mask = geo.mask(size, group, width) * keep
            piece = take(full, pl.ds(start, size)) * (slope(pre) * mask)
            joined[rows, :] = piece.astype(BF16)
            acc[2 * group] += fold(piece)
            acc[2 * group + 1] += fold(piece * value)

    loop(1, slab)
    net.open()
    loop(4, lambda s: slab(s + 1))
    net.turn(1)
    loop(geo.slabs - 5, lambda s: slab(s + 5))
    net.turn(2)
    finish(net.own, acc, 4)
    block = 256
    net.begin()
    for c in range(0, dzd.shape[1], block):
        put_pieces(wgrad, c, tn(dzd[:, c : c + block], hid[...]))
        net.step()
    net.end()


def stage_c_back(
    geo, net, live, count, zc, stats_c, norm_c, joined, sums_c, zb, stats_b, norm_b, weight, wgrad,
    back_b, ngrad, dzc, act, acc,
):
    acc[...] = jnp.zeros(acc.shape, F32)
    terms_c = backward_terms(geo, count, stats_c, norm_c, sums_c, ngrad, zc.shape[1])
    terms_b = forward_terms(geo, count, stats_b, norm_b, zb.shape[1])
    width = zb.shape[1]

    def slab(s):
        wide_back(geo, live, s, joined, zc, terms_c, dzc)
        result = nn(dzc[at(s, geo.rows), :], weight[...])
        keep = alive(live, s)
        for start, size, group in geo.pieces(width):
            rows = pl.ds(pl.multiple_of(s * geo.rows + start, CELLS), size)
            scale, shift = terms_b[group]
            value = zb[rows, :].astype(F32)
            pre = value * scale + shift
            mask = geo.mask(size, group, width) * keep
            gate = sig(pre)
            held = pre * gate
            act[rows, :] = (held * mask).astype(BF16)
            piece = result[start : start + size] * ((gate + held - held * gate) * mask)
            back_b[rows, :] = piece.astype(BF16)
            acc[2 * group] += fold(piece)
            acc[2 * group + 1] += fold(piece * value)

    loop(1, slab)
    net.open()
    loop(geo.slabs - 1, lambda s: slab(s + 1))
    net.turn(2)
    finish(net.own, acc, 4)
    net.begin()
    block = 256
    for c in range(0, dzc.shape[1], block):
        put_pieces(wgrad, c, tn(dzc[:, c : c + block], act[...]))
        if c < 2 * block:
            net.step()
    net.end()


def stage_b_back(
    geo, net, live, count, zb, stats_b, norm_b, back_b, sums_b, za, stats_a, norm_a, weight, wgrad,
    back_a, ngrad, taps, dtaps, stacked, total, acc,
):
    acc[...] = jnp.zeros(acc.shape, F32)
    width = za.shape[1]
    terms_b = backward_terms(geo, count, stats_b, norm_b, sums_b, ngrad, width)
    terms_a = forward_terms(geo, count, stats_a, norm_a, width)
    clear_halo(geo, taps)
    clear_halo(geo, dtaps)
    for t in range(9):
        stacked[t * width : (t + 1) * width, :] = weight[:, t * width : (t + 1) * width]

    def fill(s):
        spread_taps(geo, taps, s, activate(geo, live, za, s, terms_a), False)
        keep = alive(live, s)
        values = []
        for start, size, group in geo.pieces(width):
            rows = pl.ds(pl.multiple_of(s * geo.rows + start, CELLS), size)
            scale, by_value, constant = terms_b[group]
            value = back_b[rows, :].astype(F32) * scale + zb[rows, :].astype(F32) * by_value
            values.append((value + constant) * (geo.mask(size, group, width) * keep))
        spread_taps(geo, dtaps, s, values, True)

    loop(2, fill)
    net.open()
    loop(geo.slabs - 2, lambda s: fill(s + 2))
    net.turn(1)
    span = geo.halo - CELLS
    total[...] = jnp.zeros(total.shape, F32)

    def slab(s):
        result = None
        for dy in range(3):
            begin = pl.multiple_of(s * geo.halo + (2 - dy) * CELLS, CELLS)
            term = nn(
                dtaps[pl.ds(begin, span), :], stacked[dy * 3 * width : (dy + 1) * 3 * width, :]
            )
            result = term if result is None else result + term
        keep = alive(live, s)
        for group, (begin, size) in enumerate(((0, geo.rg), (geo.rg + CELLS, geo.rl))):
            rows = pl.ds(pl.multiple_of(s * geo.rows + group * geo.rg, CELLS), size)
            scale, shift = terms_a[group]
            value = za[rows, :].astype(F32)
            mask = geo.mask(size, group, width) * keep
            piece = result[begin : begin + size] * (slope(value * scale + shift) * mask)
            back_a[rows, :] = piece.astype(BF16)
            acc[2 * group] += fold(piece)
            acc[2 * group + 1] += fold(piece * value)

    def grads(s):
        own = dtaps[
            pl.ds(pl.multiple_of(s * geo.halo + CELLS, CELLS), span), width : 2 * width
        ]
        for dy in range(3):
            begin = pl.multiple_of(s * geo.halo + dy * CELLS, CELLS)
            total[:, dy * 3 * width : (dy + 1) * 3 * width] += tn(own, taps[pl.ds(begin, span), :])

    loop(geo.slabs, slab)
    net.turn(2)
    finish(net.own, acc, 4)
    part = geo.slabs // 3
    net.begin()
    loop(part, grads)
    net.step()
    loop(part, lambda s: grads(s + part))
    net.step()
    loop(geo.slabs - 2 * part, lambda s: grads(s + 2 * part))
    put_pieces(wgrad, 0, total[...])
    net.turn(3)
    net.end()


def stage_a_back(
    geo, net, live, count, za, stats_a, norm_a, back_a, sums_a, packed, joined, weight, wgrad, grad,
    ngrad, dza,
):
    terms_a = backward_terms(geo, count, stats_a, norm_a, sums_a, ngrad, za.shape[1])
    loop(2, lambda s: wide_back(geo, live, s, back_a, za, terms_a, dza))
    net.open()
    loop(geo.slabs - 2, lambda s: wide_back(geo, live, s + 2, back_a, za, terms_a, dza))
    put_pieces(wgrad, 0, tn(dza[...], packed[...]))
    net.turn(1)

    def slab(s):
        result = nn(dza[at(s, geo.rows), :], weight[...])
        rows = at(s, geo.rows)
        grad[rows, :] = (result + joined[rows, :].astype(F32)).astype(BF16)

    part = geo.slabs // 3
    for number in range(3):
        begin = number * part
        size = part if number < 2 else geo.slabs - begin
        loop(size, lambda s: slab(s + begin))
        net.turn(number + 2)
    net.turn(5)
    net.close()


def last_kernel(geo, upright, grad, hid, *refs):
    count = len(upright)
    rows_in, refs = refs[:count], refs[count:]
    dxg, dxl, outg, outl = refs[:4]
    targets = refs[4:]
    result = grad[...].astype(F32)
    half = CELLS // 2
    for i in range(geo.hg):
        dxg[0, i] = result[i * CELLS : i * CELLS + geo.hg]
        outg[0, i] = hid[i * CELLS : (i + 1) * CELLS, :][0 : geo.hg]
    for i in range(geo.hl):
        begin = geo.rg + i * CELLS
        low = hid[begin : begin + CELLS, :]
        for side in range(2):
            part = begin + side * half
            dxl[side, i] = result[part : part + geo.hl]
            outl[side, i] = low[side * half : side * half + geo.hl]

    def write(k):
        @pl.when(pl.program_id(0) == k % geo.slabs)
        def one():
            source, target = rows_in[k], targets[k]
            rows = source.shape[0] * source.shape[1]
            whole = source[...].astype(F32).reshape(rows, source.shape[2])
            target[...] = whole.T if upright[k] else whole

    for k in range(count):
        write(k)


def run_last(geo, grad, hid, parts, global_shape, local_shape):
    def whole(shape):
        return pl.BlockSpec(shape, lambda s: (0,) * len(shape))

    upright = [part.shape[0] * part.shape[1] >= 128 for part in parts]
    shapes = []
    for turn, part in zip(upright, parts):
        rows = part.shape[0] * part.shape[1]
        shapes.append((part.shape[2], rows) if turn else (rows, part.shape[2]))
    views = [
        pl.BlockSpec((1,) + global_shape[1:], lambda s: (s, 0, 0, 0)),
        pl.BlockSpec((2,) + local_shape[1:], lambda s: (s, 0, 0, 0)),
    ]
    outs = pl.pallas_call(
        functools.partial(last_kernel, geo, upright),
        grid=(geo.slabs,),
        out_shape=[
            jax.ShapeDtypeStruct(shape, dtype)
            for dtype in (F32, BF16)
            for shape in (global_shape, local_shape)
        ]
        + [jax.ShapeDtypeStruct(shape, F32) for shape in shapes],
        in_specs=[
            pl.BlockSpec((geo.rows, item.shape[1]), lambda s: (s, 0)) for item in (grad, hid)
        ]
        + [whole(part.shape) for part in parts],
        out_specs=views + views + [whole(shape) for shape in shapes],
        compiler_params=pltpu.CompilerParams(vmem_limit_bytes=VMEM_CAP),
        name="last",
    )(grad, hid, *parts)
    return outs[:4], [item if turn else item.T for turn, item in zip(upright, outs[4:])]


class Group:
    def __init__(self, kind, reps, shards):
        rep, shard = lax.axis_index("rep"), lax.axis_index("fsdp")
        chip, core = shard // 2, lax.rem(shard, 2)
        wide = reps // 2
        low, high = lax.rem(rep, 2), rep // wide
        first = core == 0
        if kind == "core":
            self.size, self.me = 2, core
            self.address = lambda k: {"fsdp": chip * 2 + k}
        elif kind == "chips":
            self.size, self.me = shards // 2, chip
            self.address = lambda k: {"fsdp": k * 2 + core}
        elif kind == "shards":
            self.size, self.me = shards, shard
            self.address = lambda k: {"fsdp": k}
        elif kind == "reps":
            self.size, self.me = reps, rep
            self.address = lambda k: {"rep": k}
        elif kind == "near":
            self.size, self.me = 2, jnp.where(first, low, high)
            self.address = lambda k: {
                "rep": jnp.where(first, rep - low + k, rep - high * wide + k * wide)
            }
        elif kind == "cross":
            self.size = wide * (shards // 2)
            self.me = jnp.where(first, rep // 2, lax.rem(rep, wide)) * (shards // 2) + chip

            def across(k):
                far = k // (shards // 2)
                return {
                    "rep": jnp.where(first, far * 2 + low, high * wide + far),
                    "fsdp": lax.rem(k, shards // 2) * 2 + core,
                }

            self.address = across
        else:
            self.size = wide
            self.me = jnp.where(first, rep // 2, lax.rem(rep, wide))
            self.address = lambda k: {"rep": jnp.where(first, k * 2 + low, high * wide + k)}

    def other(self, hop):
        return lax.rem(self.me + hop, self.size)


class Sums:
    def __init__(self, reps, shards, own, out, buffers, sems):
        self.own, self.out, self.buffers, self.sems = own, out, buffers, sems
        self.groups = [Group(kind, reps, shards) for kind in ("core", "chips", "reps")]
        self.phase = 0
        self.copies = []

    def send(self, source):
        group, buffer = self.groups[self.phase], self.buffers[self.phase]
        self.copies = []
        for hop in range(1, group.size):
            copy = pltpu.make_async_remote_copy(
                source, buffer.at[group.me], self.sems[2 * self.phase].at[hop],
                self.sems[2 * self.phase + 1].at[hop], device_id=group.address(group.other(hop)),
                device_id_type=MESH,
            )
            copy.start()
            self.copies.append(copy)

    def begin(self):
        self.send(self.own)
        self.buffers[0][self.groups[0].me] = self.own[...]

    def total(self):
        for copy in self.copies:
            copy.wait()
        buffer = self.buffers[self.phase]
        total = buffer[0]
        for k in range(1, self.groups[self.phase].size):
            total = total + buffer[k]
        return total

    def step(self):
        total = self.total()
        self.phase += 1
        group, buffer = self.groups[self.phase], self.buffers[self.phase]
        buffer[group.me] = total
        self.send(buffer.at[group.me])

    def end(self):
        while self.phase < 2:
            self.step()
        self.out[...] = self.total()


class Net:
    def __init__(self, reps, shards, sums=None, side=None, jobs=(), plans=()):
        self.reps, self.shards = reps, shards
        self.sums, self.side, self.jobs, self.plans = sums, side, jobs, plans
        self.own = None if sums is None else sums.own
        self.opened = False
        self.started, self.finished = set(), set()

    def enter(self):
        rep, shard = lax.axis_index("rep"), lax.axis_index("fsdp")
        barrier = pltpu.get_barrier_semaphore()
        for hop in range(1, self.shards):
            other = {"fsdp": lax.rem(shard + hop, self.shards)}
            pl.semaphore_signal(barrier, inc=1, device_id=other, device_id_type=MESH)
        for hop in range(1, self.reps):
            other = {"rep": lax.rem(rep + hop, self.reps)}
            pl.semaphore_signal(barrier, inc=1, device_id=other, device_id_type=MESH)
        self.greeted = self.shards + self.reps - 2
        if any(job.kind == "cross" for job in self.jobs):
            group = Group("cross", self.reps, self.shards)
            chips = self.shards // 2
            for far in range(1, self.reps // 2):
                for step in range(1, chips):
                    other = lax.rem(group.me // chips + far, self.reps // 2) * chips
                    other = group.address(other + lax.rem(group.me + step, chips))
                    pl.semaphore_signal(barrier, inc=1, device_id=other, device_id_type=MESH)
                    self.greeted += 1

    def open(self):
        if not self.opened:
            self.opened = True
            pl.semaphore_wait(pltpu.get_barrier_semaphore(), self.greeted)
            self.turn(0)

    def turn(self, number):
        for k, (start, end) in enumerate(self.plans):
            if end == number:
                self.finish(k)
        for k, (start, end) in enumerate(self.plans):
            if start == number:
                self.started.add(k)
                self.jobs[k].start()

    def finish(self, k):
        assert k in self.started and k not in self.finished
        self.finished.add(k)
        self.jobs[k].finish()

    def job_out(self, k):
        return self.jobs[k].out

    def begin(self):
        self.open()
        self.sums.begin()

    def step(self):
        self.sums.step()

    def end(self):
        self.sums.end()
        self.close()

    def run(self):
        self.begin()
        self.end()

    def close(self):
        for k in range(len(self.jobs)):
            if k not in self.finished:
                self.finish(k)


class Job:
    GROUPS = {
        "pair": "core", "join": "core", "line": "chips", "spread": "chips", "all": "shards",
        "share": "reps", "half": "near", "near": "near", "rest": "others", "others": "others",
        "cross": "cross",
    }

    def __init__(self, kind, reps, shards, sources, out, held, send, recv):
        self.kind, self.sources, self.out, self.held = kind, sources, out, held
        self.send, self.recv = send, recv
        self.reps, self.chips = reps, shards // 2
        self.rep, shard = lax.axis_index("rep"), lax.axis_index("fsdp")
        self.chip, self.core = shard // 2, lax.rem(shard, 2)
        self.group = Group(self.GROUPS[kind], reps, shards)

    def give(self, source, target, hop):
        k = len(self.copies)
        if hop == 0:
            copy = pltpu.make_async_copy(source, target, self.send.at[k])
        else:
            copy = pltpu.make_async_remote_copy(
                source, target, self.send.at[k], self.recv.at[k],
                device_id=self.group.address(self.group.other(hop)), device_id_type=MESH,
            )
        copy.start()
        self.copies.append(copy)

    def start(self):
        self.copies = []
        kind, out, source, group = self.kind, self.out, self.sources[0], self.group
        order = list(range(1, group.size)) + [0]
        wide = self.reps // 2
        first = self.core == 0
        if kind == "spread":
            for hop in order[:-1]:
                self.give(source.at[self.rep], out.at[self.rep, group.size - hop - 1], hop)
        elif kind == "near":
            self.give(out.at[self.rep], out.at[self.rep], 1)
        elif kind == "others":
            low, high = lax.rem(self.rep, 2), self.rep // wide
            partner = jnp.where(
                first, self.rep + 1 - 2 * low, self.rep + (1 - 2 * high) * wide
            )
            for hop in order[:-1]:
                for place in (self.rep, partner):
                    self.give(out.at[place], out.at[place], hop)
        elif kind == "join":
            for hop in order:
                for step in range(1, self.chips):
                    chip = lax.rem(self.chip + step, self.chips)
                    self.give(source.at[:, step - 1], out.at[chip, self.core], hop)
                self.give(self.sources[1], out.at[self.chip, self.core], hop)
        elif kind == "cross":
            for hop in order:
                other = group.other(hop)
                block = source.at[other // self.chips, lax.rem(other, self.chips)]
                self.give(block, self.held.at[group.me], hop)
        elif kind in ("all", "share"):
            for hop in order:
                self.give(source, out.at[group.me], hop)
        elif kind == "half":
            low, high = lax.rem(self.rep, 2), self.rep // wide
            mine = jnp.where(first, low, high * wide)
            theirs = jnp.where(first, 1 - low, (1 - high) * wide)
            step = jnp.where(first, 2, 1)
            for k in range(wide):
                self.give(source.at[theirs + k * step], self.held.at[1, k], 1)
            for k in range(wide):
                self.give(source.at[mine + k * step], self.held.at[0, k], 0)
        else:
            for hop in order:
                self.give(source.at[group.other(hop)], self.held.at[group.me], hop)

    def finish(self):
        for copy in self.copies:
            copy.wait()
        held, out = self.held, self.out
        if held is None:
            return
        members = held.shape[0]
        blocks = held.shape[1:-2]

        def one(index):
            place = (index // blocks[-1], lax.rem(index, blocks[-1])) if len(blocks) == 2 else (
                (index,) if blocks else ()
            )
            total = held[(0,) + place].astype(F32)
            for k in range(1, members):
                total = total + held[(k,) + place].astype(F32)
            out[place[::-1] if self.kind == "pair" else place] = total.astype(BF16)

        if blocks:
            loop(blocks[0] * (blocks[1] if len(blocks) == 2 else 1), one)
        else:
            total = held[0].astype(F32)
            for k in range(1, members):
                total = total + held[k].astype(F32)
            out[...] = total.astype(BF16)


def job_shapes(kind, reps, shards, shape):
    chips = shards // 2
    if kind == "spread":
        return None, (reps, chips - 1) + shape[1:], chips
    if kind in ("near", "others"):
        return None, shape, reps
    if kind == "cross":
        return (shape[0] * shape[1],) + shape[2:], shape[2:], shape[0] * shape[1]
    if kind == "join":
        return None, (chips, 2, reps) + shape[2:], 2 * chips
    if kind == "all":
        return None, (shards,) + shape, shards
    if kind == "pair":
        return shape, (shape[2], shape[1]) + shape[3:], 2
    if kind == "share":
        return None, (reps,) + shape, reps
    if kind == "half":
        return (2, reps // 2) + shape[1:], (reps // 2,) + shape[1:], reps
    return shape, shape[1:], shape[0]


VMEM_CAP = 60 << 20
FAR = ("spread", "near", "others")


def sums_scratch(reps, shards, shape, own):
    sizes = (2, shards // 2, reps)
    return (
        [pltpu.VMEM(shape, F32)] * own
        + [pltpu.VMEM((size,) + shape, F32) for size in sizes]
        + [pltpu.SemaphoreType.DMA((size,)) for size in sizes for unused in range(2)]
    )


def run(name, kernel, geo, reps, shards, number, live, operands, results, scratch, sums, jobs, side, far=()):
    own_results = len(results)
    results = list(results)
    spaces = [pltpu.VMEM] * own_results
    extra = []
    arrays = []
    shapes = []
    targets = []
    kept = {}
    for kind, sources, start, end in jobs:
        source = sources[0]
        if isinstance(source, int):
            shape, dtype = shapes[source]
        elif isinstance(source, str):
            shape, dtype = results[int(source)]
        else:
            shape, dtype = source.shape, source.dtype
        held, out, copies = job_shapes(kind, reps, shards, shape)
        shapes.append((out, dtype))
        extra += [] if held is None else [pltpu.VMEM(held, BF16)]
        extra += [pltpu.SemaphoreType.DMA((copies,))] * 2
        if kind in ("near", "others") and isinstance(source, int):
            targets.append(targets[source])
        else:
            if kind in ("near", "others"):
                kept[len(arrays)] = len(results)
            targets.append(len(results))
            results.append(shapes[-1])
            spaces.append(pltpu.HBM if kind in FAR else pltpu.VMEM)
        arrays += [item for item in sources if not isinstance(item, (int, str))]
    own_or_job = len(results)
    operands = tuple(operands)
    near = len(operands)
    if side is not None:
        operands += (side,)
        results.append((side.shape, F32))
        spaces.append(pltpu.VMEM)
        extra += sums_scratch(reps, shards, side.shape, 0)
    if sums is not None:
        results.append((sums, F32))
        spaces.append(pltpu.VMEM)
        extra += sums_scratch(reps, shards, sums, 1)
    inputs = 1 + len(operands)
    remote = bool(jobs) or sums is not None

    def whole(*refs):
        sources_in = list(refs[inputs : inputs + len(arrays)])
        first_out = inputs + len(arrays)
        outs = refs[first_out : first_out + len(results)]
        more = list(refs[first_out + len(results) :])
        made = []
        for k, (kind, sources, start, end) in enumerate(jobs):
            refs_of = []
            for item in sources:
                if isinstance(item, int):
                    refs_of.append(made[item].out)
                elif isinstance(item, str):
                    refs_of.append(outs[int(item)])
                else:
                    refs_of.append(sources_in.pop(0))
            held = more.pop(0) if job_shapes(kind, reps, shards, refs_of[0].shape)[0] else None
            made.append(
                Job(kind, reps, shards, refs_of, outs[targets[k]], held, more.pop(0), more.pop(0))
            )
        beside, main = None, None
        if side is not None:
            beside = Sums(reps, shards, refs[near + 1], outs[own_or_job], more[0:3], more[3:9])
            more = more[9:]
        if sums is not None:
            main = Sums(reps, shards, more[0], outs[-1], more[1:4], more[4:10])
            more = more[10:]
        net = None
        if remote:
            plans = [job[2:] for job in jobs]
            net = Net(reps, shards, main, beside, made, plans)
            net.enter()
        kernel(geo, net, *refs[: near + 1], *outs[:own_results], *more)

    params = {"collective_id": number, "has_side_effects": True} if remote else {}
    return pl.pallas_call(
        whole,
        out_shape=[jax.ShapeDtypeStruct(shape, dtype) for shape, dtype in results],
        in_specs=[pl.BlockSpec(memory_space=pltpu.SMEM)]
        + [pl.BlockSpec(memory_space=pltpu.HBM if k in far else pltpu.VMEM) for k in range(len(operands))]
        + [
            pl.BlockSpec(memory_space=pltpu.HBM if k in kept else pl.ANY) for k in range(len(arrays))
        ],
        out_specs=[pl.BlockSpec(memory_space=space) for space in spaces],
        scratch_shapes=extra
        + [item if not isinstance(item, tuple) else pltpu.VMEM(*item) for item in scratch],
        input_output_aliases={inputs + k: out for k, out in kept.items()},
        compiler_params=pltpu.CompilerParams(vmem_limit_bytes=VMEM_CAP, **params),
        name=name,
    )(live, *operands, *arrays)


def own_norms(first, second):
    flat = jnp.concatenate([first.reshape(-1), second.reshape(-1)]).astype(F32)
    size = -(-flat.shape[0] // 1024) * 1024
    return jnp.pad(flat, (0, size - flat.shape[0])).reshape(8, -1)


def all_norms(gathered, first, second):
    shards = gathered.shape[0]
    flat = gathered.reshape(shards, -1)
    split, last = first.size, first.size + second.size

    def whole(part):
        return part.reshape(shards, 2, -1).transpose(1, 0, 2).reshape(2, -1)

    return whole(flat[:, :split]), whole(flat[:, split:last])


def body(reps, shards, *arguments):
    (
        global_views, local_views, live, first_reduce, first_spatial, first_expand, first_norms,
        second_reduce, second_spatial, second_expand, second_short, second_norms, global_cotan,
        local_cotan,
    ) = arguments
    geo = Geometry(global_views.shape[0], global_views.shape[1], local_views.shape[1])
    assert local_views.shape[0] == 2 * geo.slabs
    channels = global_views.shape[3]
    ha, hb, hc, hd, he, hf, hs = (
        item.T.reshape(reps, -1, item.shape[0])
        for item in (
            first_reduce, first_spatial, first_expand, second_reduce, second_spatial,
            second_expand, second_short,
        )
    )
    he_0, he_1, he_2 = (he[:, :, k * he.shape[2] // 3 : (k + 1) * he.shape[2] // 3] for k in range(3))
    mid_1, mid_2 = first_reduce.shape[1] * shards, second_reduce.shape[1] * shards
    wide = second_expand.shape[1] * shards

    def rows_of(gathered):
        return gathered.reshape(-1, gathered.shape[-1])

    big, small = geo.total, geo.small_total

    numbers = iter(range(100))

    def go(name, kernel, operands, results, scratch, width=None, members=4, jobs=(), side=None, far=()):
        parts = {4: 2, 6: 4, 8: 2}[members]
        sums = None if width is None else (members * parts, width // parts)
        return run(
            name, kernel, geo, reps, shards, next(numbers), live, operands, results, scratch, sums,
            jobs, side, far,
        )

    def pieces(rows, columns):
        return ((2, shards // 2, reps, rows // (shards * reps), columns), BF16)

    def acc(width, members=4):
        return ((members, 8, width), F32)

    def stat(width):
        return ((8, width), F32)

    def both(width):
        return ((2, width), F32)

    more = go(
        "stage_a", stage_a, (global_views, local_views),
        [((big, channels), BF16), ((big, mid_1), BF16)],
        [
            acc(mid_1), ((mid_1, channels), BF16), (global_views.shape, BF16),
            (local_views.shape, BF16), pltpu.SemaphoreType.DMA((2,)),
        ],
        mid_1, 8,
        jobs=(
            ("spread", (ha,), 0, 1), ("near", (0,), 1, 2), ("others", (0,), 2, 3),
            ("join", (0, ha), 3, 4),
            ("spread", (hb,), 0, 2), ("near", (4,), 2, 3), ("others", (4,), 3, 5),
            ("join", (4, hb), 5, None),
            ("spread", (hc,), 0, 3), ("near", (8,), 3, 5), ("others", (8,), 5, None),
            ("spread", (hd,), 0, 3), ("near", (11,), 3, 5), ("others", (11,), 5, None),
            ("all", (own_norms(first_norms, second_norms),), 1, 5), ("spread", (hs,), 3, 5),
        ),
        far=(0, 1),
    )
    packed, za, unused, wa, unused, wb, far_c, far_d, norms, far_s, sa = more
    count = sa
    wa, wb = rows_of(wa), rows_of(wb)
    norms_1, norms_2 = all_norms(norms, first_norms, second_norms)
    na, nb, nc = norms_1[:, :mid_1], norms_1[:, mid_1 : 2 * mid_1], norms_1[:, 2 * mid_1 :]
    nd, ne = norms_2[:, :mid_2], norms_2[:, mid_2 : 2 * mid_2]
    nf, ns = norms_2[:, 2 * mid_2 : 2 * mid_2 + wide], norms_2[:, 2 * mid_2 + wide :]
    zb, wc, wd, far_s, far_e0, far_e1, far_e2, sb = go(
        "stage_b", stage_b, (count, za, sa, na, wb), [((big, mid_1), BF16)],
        [((geo.halo_total, 3 * mid_1), BF16), acc(mid_1)], mid_1,
        jobs=(
            ("join", (far_c, hc), 0, 2), ("join", (far_d, hd), 0, 2),
            ("near", (far_s,), 0, 1), ("others", (2,), 1, 2),
            ("spread", (he_0,), 0, 2), ("spread", (he_1,), 0, 2), ("spread", (he_2,), 0, 2),
        ),
    )
    wc = rows_of(wc)
    zc, ws, far_e0, far_e1, far_f, sc = go(
        "stage_c", stage_c, (count, zb, sb, nb, wc), [((big, channels), BF16)],
        [((geo.rows, mid_1), BF16), acc(channels)], channels,
        jobs=(
            ("join", (far_s, hs), 0, 2), ("near", (far_e0,), 0, 1), ("others", (1,), 1, 2),
            ("near", (far_e1,), 0, 1), ("others", (3,), 1, 2), ("spread", (hf,), 0, 2),
        ),
    )
    wd, ws = rows_of(wd), rows_of(ws)
    hid, zd, sub, zs, local_s, we_0, we_1, far_e2, we_2, far_f, sd = go(
        "stage_d", stage_d, (count, zc, sc, nc, packed, wd, ws),
        [
            ((big, channels), BF16), ((big, mid_2), BF16), ((small, channels), BF16),
            ((small, wide), BF16), stat(wide // 2),
        ],
        [((channels // 128, geo.rows, 128), F32), acc(mid_2), acc(wide)], mid_2,
        jobs=(
            ("join", (far_e0, he_0), 0, 2), ("join", (far_e1, he_1), 0, 2),
            ("near", (far_e2,), 0, 1), ("others", (2,), 1, 2), ("join", (2, he_2), 2, None),
            ("near", (far_f,), 0, 1), ("others", (5,), 1, 2),
        ),
    )
    we = tuple(rows_of(item) for item in (we_0, we_1, we_2))
    ze, wf, ss, se = go(
        "stage_e", stage_e, (count, zd, sd, nd, *we), [((small, mid_2), BF16)],
        [((mid_2 // 128, geo.halo, 128), F32), ((small, 9 * mid_2), BF16), acc(mid_2)], mid_2,
        jobs=(("join", (far_f, hf), 0, 2),), side=local_s,
    )
    wf = rows_of(wf)
    act_e, zf, sf = go(
        "stage_f", stage_f, (count, ze, se, ne, wf),
        [((small, mid_2), BF16), ((small, wide), BF16)], [acc(wide)], wide,
    )
    second_g, second_l, grad, local_pool, so = go(
        "stage_out", stage_out,
        (count, zf, zs, sf, ss, nf, ns, global_cotan, local_cotan),
        [
            (global_cotan.shape, BF16), (local_cotan.shape, BF16), ((small, wide), BF16),
            stat(wide // 4),
        ],
        [((geo.slabs, 8, wide), F32), ((geo.small, 512), F32), acc(wide, 8)], wide, 6,
    )
    unused, unused, back_sub, back_e, ngrad_f, ngrad_s, pair_f, pair_s, pool, qe = go(
        "stage_f_back", stage_f_back,
        (count, zf, zs, sf, ss, nf, ns, grad, so, act_e, sub, wf, ws, ze, se, ne),
        [
            pieces(wide, mid_2), pieces(wide, channels), ((small, channels), BF16), ((small, mid_2), BF16),
            both(wide), both(wide),
        ],
        [((small, wide), BF16), ((small, wide), BF16), acc(mid_2)], mid_2,
        jobs=(("pair", ("0",), 2, None), ("pair", ("1",), 1, None)), side=local_pool,
    )
    views = count[8, 0] * 6.0
    pool = pool.reshape(2, wide)
    center = pool[0] / views
    spread = pool[1] / views - center * center
    pooled_std = jnp.mean(jnp.sqrt(spread + 1e-06))
    wgrad_e, back_d, ngrad_e, half_f, half_s, qd = go(
        "stage_e_back", stage_e_back,
        (count, ze, se, ne, back_e, qe, zd, sd, nd, *we),
        [pieces(mid_2, 9 * mid_2), ((big, mid_2), BF16), both(mid_2)],
        [
            ((mid_2 // 128, geo.halo, 128), F32), ((small, 9 * mid_2), BF16),
            ((small, mid_2), BF16), ((3, small, mid_2), BF16), ((4, small, mid_2), F32),
            acc(mid_2),
        ],
        mid_2, jobs=(("half", (pair_f,), 0, None), ("half", (pair_s,), 0, None)),
    )
    wgrad_d, joined, ngrad_d, unused, half_e, rest_f, rest_s, qc = go(
        "stage_d_back", stage_d_back,
        (count, zd, sd, nd, back_d, qd, hid, packed, zc, sc, nc, back_sub, wd),
        [pieces(mid_2, channels), ((big, channels), BF16), both(mid_2)],
        [((big, mid_2), BF16), ((channels // 128, geo.rows, 128), F32), acc(channels)], channels,
        jobs=(
            ("pair", (wgrad_e,), 0, 1), ("half", (0,), 1, None),
            ("rest", (half_f,), 0, 1), ("rest", (half_s,), 0, 1),
        ),
    )
    wgrad_c, back_b, ngrad_c, pair_d, rest_e, line_f, line_s, qb = go(
        "stage_c_back", stage_c_back,
        (count, zc, sc, nc, joined, qc, zb, sb, nb, wc),
        [pieces(channels, mid_1), ((big, mid_1), BF16), both(channels)],
        [((big, channels), BF16), ((big, mid_1), BF16), acc(mid_1)], mid_1,
        jobs=(
            ("pair", (wgrad_d,), 0, 2), ("rest", (half_e,), 0, 2), ("line", (rest_f,), 0, 2),
            ("line", (rest_s,), 0, 2),
        ),
    )
    wgrad_b, back_a, ngrad_b, unused, rest_d, unused, half_c, line_e, out_f, out_s, pair_b, qa = go(
        "stage_b_back", stage_b_back,
        (count, zb, sb, nb, back_b, qb, za, sa, na, wb),
        [pieces(mid_1, 9 * mid_1), ((big, mid_1), BF16), both(mid_1)],
        [
            ((geo.halo_total, 3 * mid_1), BF16), ((geo.halo_total, 3 * mid_1), BF16),
            ((9 * mid_1, mid_1), BF16), (wb.shape, F32), acc(mid_1),
        ],
        mid_1,
        jobs=(
            ("half", (pair_d,), 0, 1), ("rest", (0,), 1, 2), ("pair", (wgrad_c,), 0, 1),
            ("half", (2,), 1, 2), ("line", (rest_e,), 0, 2), ("share", (line_f,), 0, 2),
            ("share", (line_s,), 0, 2), ("pair", ("0",), 3, None),
        ),
    )
    more = go(
        "stage_a_back", stage_a_back, (count, za, sa, na, back_a, qa, packed, joined, wa),
        [pieces(mid_1, channels), ((big, channels), BF16), both(mid_1)], [((big, mid_1), BF16)],
        jobs=(
            ("half", (pair_b,), 0, 1), ("cross", (0,), 1, 2), ("share", (1,), 2, None),
            ("pair", ("0",), 1, 2), ("half", (3,), 2, 3), ("cross", (4,), 3, 4),
            ("share", (5,), 4, None),
            ("cross", (half_c,), 0, 1), ("share", (7,), 1, None),
            ("line", (rest_d,), 0, 1), ("share", (9,), 1, None),
            ("share", (line_e,), 0, None),
        ),
    )
    grad, ngrad_a = more[1], more[2]
    out_b, out_a, out_c, out_d, out_e = (more[3 + k] for k in (2, 6, 8, 10, 11))
    (grad_g, grad_l, first_g, first_l), columns = run_last(
        geo, grad, hid, (out_a, out_b, out_c, out_d, out_e, out_f, out_s),
        global_views.shape, local_views.shape,
    )
    shard = lax.axis_index("fsdp")

    def own_columns(parts, width):
        whole = jnp.concatenate(parts, axis=1)
        return lax.dynamic_slice_in_dim(whole, shard * width, width, 1)

    return (
        first_g, first_l, second_g, second_l, grad_g, grad_l,
        *columns[0:3],
        own_columns((ngrad_a, ngrad_b, ngrad_c), first_norms.shape[1]),
        *columns[3:7],
        own_columns((ngrad_d, ngrad_e, ngrad_f, ngrad_s), second_norms.shape[1]),
        pooled_std,
    )


def solution(mesh):
    views = P(("rep", "fsdp"), None, None, None)
    columns = P(None, "fsdp")
    return jax.shard_map(
        functools.partial(body, mesh.shape["rep"], mesh.shape["fsdp"]),
        mesh=mesh,
        in_specs=(views, views, P(("rep", "fsdp"))) + (columns,) * 9 + (views, views),
        out_specs=(views,) * 6 + (columns,) * 9 + (P(),),
        check_vma=False,
    )
```

```python
import functools

import jax
import jax.numpy as jnp
from jax import lax
from jax.experimental import pallas as pl
from jax.experimental.pallas import tpu as pltpu
from jax.sharding import PartitionSpec as P

EPSILON = 1e-05
F32 = jnp.float32
BF16 = jnp.bfloat16
MESH = pl.DeviceIdType.MESH
CELLS = 16
PAIR, HALF, REST, LINE, SHARE, SPREAD, NEAR, OTHERS, JOIN, CROSS, ALL = range(11)
CORES, CHIPS, SHARDS, REPLICAS, CLOSE, APART, SLANTED = range(7)


def nt(left, right):
    return lax.dot_general(left, right, (((1,), (1,)), ((), ())), preferred_element_type=F32)


def nn(left, right):
    return lax.dot_general(left, right, (((1,), (0,)), ((), ())), preferred_element_type=F32)


def tn(left, right):
    return lax.dot_general(left, right, (((0,), (0,)), ((), ())), preferred_element_type=F32)


def sig(values):
    return 0.5 * jnp.tanh(0.5 * values) + 0.5


def silu(values):
    return values * sig(values)


def slope(values):
    gate = sig(values)
    held = values * gate
    return gate + held - held * gate


def lanes(tile, width):
    return jnp.concatenate([tile] * (width // tile.shape[1]), axis=1)


def fold(values):
    return jnp.sum(values.reshape(values.shape[0] // 8, 8, values.shape[1]), axis=0)


class Geometry:
    def __init__(self, views, side_global, side_local):
        self.slabs = views
        self.hg, self.hl = side_global, side_local
        assert side_global < CELLS and side_local < CELLS // 2
        self.rg, self.rl = side_global * CELLS, side_local * CELLS
        self.rows = self.rg + self.rl
        self.og, self.ol = (side_global - 1) // 2 + 1, (side_local - 1) // 2 + 1
        self.sg, self.sl = self.og * 8, self.ol * 8
        self.small = self.sg + self.sl
        self.total, self.small_total = self.slabs * self.rows, self.slabs * self.small
        self.halo = self.rows + 2 * CELLS
        self.halo_total = self.slabs * self.halo + CELLS
        self.chunk = 32
        assert self.rg % self.chunk == 0 and self.rl % self.chunk == 0 and self.small % 16 == 0

    def pieces(self, width):
        if width <= 256:
            return [(0, self.rg, 0), (self.rg, self.rl, 1)]
        step = self.chunk
        return [(start, step, 0) for start in range(0, self.rg, step)] + [
            (start, step, 1) for start in range(self.rg, self.rows, step)
        ]

    def mask(self, count, group, width):
        row = lax.broadcasted_iota(jnp.int32, (count, 128), 0)
        if group == 0:
            keep = (row & (CELLS - 1)) < self.hg
        else:
            keep = (row & (CELLS // 2 - 1)) < self.hl
        return lanes(keep.astype(F32), width)

    def small_mask(self, group, width):
        count = self.sl if group else self.sg
        row = lax.broadcasted_iota(jnp.int32, (count, 128), 0)
        keep = (row & 3) < self.ol if group else (row & 7) < self.og
        return lanes(keep.astype(F32), width)

    def small_pieces(self):
        return [(0, self.sg, 0), (self.sg, self.sl, 1)]


def alive(live, slab):
    return jnp.where(slab < 2 * live[0], 1.0, 0.0).astype(F32)


def cells(geo, count, group, width, small=False):
    images = lanes(count[8:9, 0:128], width)
    if small:
        return images * float(2 * geo.og * geo.og if group == 0 else 4 * geo.ol * geo.ol)
    return images * float(2 * geo.hg * geo.hg if group == 0 else 4 * geo.hl * geo.hl)


def member(sums, row, width):
    parts = width // sums.shape[1]
    return jnp.concatenate(
        [sums[row * parts + k : row * parts + k + 1, :] for k in range(parts)], axis=1
    )


def norm_terms(stats, norm, number, group):
    width = norm.shape[1]
    mean = member(stats, 2 * group, width) / number
    spread = member(stats, 2 * group + 1, width) / number - mean * mean
    inverse = lax.rsqrt(spread + EPSILON)
    scale = norm[0:1, :] * inverse
    return mean, inverse, scale, norm[1:2, :] - mean * scale


def back_terms(stats, norm, number, group, first, second_raw):
    mean, inverse, scale, unused = norm_terms(stats, norm, number, group)
    second = inverse * (second_raw - mean * first)
    by_value = -scale * inverse * (second / number)
    constant = -scale * (first / number) - by_value * mean
    return scale, by_value, constant, second


def forward_terms(geo, count, stats, norm, width, small=False):
    return [
        norm_terms(stats, norm, cells(geo, count, group, width, small), group)[2:]
        for group in range(2)
    ]


def backward_terms(geo, count, stats, norm, sums, out, width, small=False, rows=((0, 1), (2, 3))):
    terms = []
    seconds = []
    for group in range(2):
        number = cells(geo, count, group, width, small)
        first = member(sums, rows[group][0], width)
        raw = member(sums, rows[group][1], width)
        scale, by_value, constant, second = back_terms(stats, norm, number, group, first, raw)
        terms.append((scale, by_value, constant))
        seconds.append((second, first))
    out[0:1, :] = seconds[0][0] + seconds[1][0]
    out[1:2, :] = seconds[0][1] + seconds[1][1]
    return terms


def finish(stats, acc, members, begin=0):
    part = stats.shape[1]
    parts = acc.shape[2] // part
    for row in range(members):
        total = jnp.sum(acc[begin + row], axis=0, keepdims=True)
        for k in range(parts):
            stats[row * parts + k : row * parts + k + 1, :] = total[:, k * part : (k + 1) * part]


def put(store, place, values):
    for k in range(store.shape[0]):
        store[k, place, :] = values[:, k * 128 : (k + 1) * 128]


def take(store, place):
    return jnp.concatenate([store[k, place, :] for k in range(store.shape[0])], axis=1)


def put_pieces(pieces, first, values, begin=0):
    cores, chips, reps, size = pieces.shape[:4]
    cols = slice(begin, begin + values.shape[1])
    for k in range(values.shape[0] // size):
        index = first // size + k
        shard, rep = index // reps, index % reps
        part = values[k * size : (k + 1) * size]
        pieces[shard % cores, shard // cores, rep, :, cols] = part.astype(BF16)


def loop(count, step):
    def one(index, carry):
        step(index)
        return carry

    lax.fori_loop(0, count, one, 0)


def at(index, size):
    return pl.ds(pl.multiple_of(index * size, size), size)


def stage_a(geo, net, live, xg, xl, packed, conv, acc, pair, weight, own_g, own_l, arrive):
    loads = (
        pltpu.make_async_copy(xg, own_g, arrive.at[0]),
        pltpu.make_async_copy(xl, own_l, arrive.at[1]),
    )
    for load in loads:
        load.start()
    net.open()
    acc[...] = jnp.zeros(acc.shape, F32)
    blank = jnp.zeros((CELLS, packed.shape[1]), BF16)
    half = CELLS // 2
    pair[...] = jnp.zeros(pair.shape, F32)
    for load in loads:
        load.wait()

    def pack(s):
        base = s * geo.rows
        keep = alive(live, s).astype(BF16)
        for i in range(geo.hg):
            start = pl.multiple_of(base + i * CELLS, CELLS)
            packed[pl.ds(start, CELLS), :] = blank
            packed[pl.ds(start, geo.hg), :] = own_g[s, i] * keep
        for i in range(geo.hl):
            start = pl.multiple_of(base + geo.rg + i * CELLS, CELLS)
            for side in range(2):
                pair[side * half : side * half + geo.hl, :] = own_l[2 * s + side, i].astype(F32)
            packed[pl.ds(start, CELLS), :] = pair[...].astype(BF16) * keep

    part = geo.slabs // 4
    for number in range(4):
        begin = number * part
        size = part if number < 3 else geo.slabs - begin
        loop(size, lambda s: pack(s + begin))
        net.turn(number + 1)
    gathered = net.job_out(3)
    weight[...] = gathered[...].astype(F32).reshape(weight.shape).astype(BF16)

    def slab(s):
        result = nt(packed[at(s, geo.rows), :], weight[...])
        conv[at(s, geo.rows), :] = result.astype(BF16)
        for start, size, group in geo.pieces(256):
            piece = result[start : start + size]
            acc[2 * group] += fold(piece)
            acc[2 * group + 1] += fold(piece * piece)
        net.give(s, "packed", "za")

    loop(geo.slabs, slab)
    finish(net.own, acc, 4)
    net.own[8:16, :] = jnp.full((8, net.own.shape[1]), live[0], jnp.int32).astype(F32)
    net.turn(5)
    net.run()


def spread_taps(geo, store, s, values, reverse):
    width = values[0].shape[1]
    for group in range(2):
        rows = values[group]
        size = rows.shape[0]
        start = pl.multiple_of(s * geo.halo + CELLS + group * (geo.rg + CELLS), CELLS)
        before = pltpu.roll(rows, 1, 0)
        after = pltpu.roll(rows, size - 1, 0)
        order = (after, rows, before) if reverse else (before, rows, after)
        for tap in range(3):
            store[pl.ds(start, size), tap * width : (tap + 1) * width] = order[tap].astype(BF16)


def clear_halo(geo, store):
    blank = jnp.zeros((CELLS, store.shape[1]), BF16)

    def slab(s):
        store[pl.ds(pl.multiple_of(s * geo.halo, CELLS), CELLS), :] = blank
        store[pl.ds(pl.multiple_of(s * geo.halo + CELLS + geo.rg, CELLS), CELLS), :] = blank

    loop(geo.slabs, slab)
    store[geo.slabs * geo.halo : geo.slabs * geo.halo + CELLS, :] = blank


def activate(geo, live, conv, s, terms):
    values = []
    width = conv.shape[1]
    keep = alive(live, s)
    for group in range(2):
        start, size = (geo.rg, geo.rl) if group else (0, geo.rg)
        rows = conv[pl.ds(pl.multiple_of(s * geo.rows + start, CELLS), size), :].astype(F32)
        scale, shift = terms[group]
        values.append(silu(rows * scale + shift) * (geo.mask(size, group, width) * keep))
    return values


def stage_b(geo, net, live, count, za, stats_a, norm, weight, conv, taps, acc):
    acc[...] = jnp.zeros(acc.shape, F32)
    width = za.shape[1]
    terms = forward_terms(geo, count, stats_a, norm, width)
    clear_halo(geo, taps)

    def fill(s):
        net.need(s, "za")
        spread_taps(geo, taps, s, activate(geo, live, za, s, terms), False)

    loop(1, fill)
    net.open()
    loop(geo.slabs - 1, lambda s: fill(s + 1))
    net.turn(1)
    net.need(0, "wb")
    span = geo.halo - CELLS

    def slab(s):
        result = None
        for dy in range(3):
            rows = taps[pl.ds(pl.multiple_of(s * geo.halo + dy * CELLS, CELLS), span), :]
            term = nt(rows, weight[:, dy * 3 * width : (dy + 1) * 3 * width])
            result = term if result is None else result + term
        keep = alive(live, s)
        for group, (begin, size) in enumerate(((0, geo.rg), (geo.rg + CELLS, geo.rl))):
            piece = result[begin : begin + size]
            start = pl.multiple_of(s * geo.rows + group * geo.rg, CELLS)
            conv[pl.ds(start, size), :] = piece.astype(BF16)
            piece = piece * (geo.mask(size, group, width) * keep)
            acc[2 * group] += fold(piece)
            acc[2 * group + 1] += fold(piece * piece)
        net.give(s, "zb")

    loop(geo.slabs, slab)
    net.turn(2)
    finish(net.own, acc, 4)
    net.run()


def stage_c(geo, net, live, count, zb, stats_b, norm, weight, conv, act, acc):
    acc[...] = jnp.zeros(acc.shape, F32)
    terms = forward_terms(geo, count, stats_b, norm, zb.shape[1])
    step = 256

    def slab(s):
        net.need(s, "zb")
        values = activate(geo, live, zb, s, terms)
        act[0 : geo.rg, :] = values[0].astype(BF16)
        act[geo.rg : geo.rows, :] = values[1].astype(BF16)
        for c in range(0, weight.shape[0], step):
            result = nt(act[...], weight[c : c + step, :])
            conv[at(s, geo.rows), c : c + step] = result.astype(BF16)
            for start, size, group in geo.pieces(256):
                piece = result[start : start + size]
                acc[2 * group, :, c : c + step] += fold(piece)
                acc[2 * group + 1, :, c : c + step] += fold(piece * piece)
        net.give(s, "zc")

    loop(1, slab)
    net.open()
    loop(3, lambda s: slab(s + 1))
    net.turn(1)
    loop(geo.slabs - 4, lambda s: slab(s + 4))
    net.turn(2)
    finish(net.own, acc, 4)
    net.run()


def even_rows(geo):
    return [2 * i * CELLS for i in range(geo.og)] + [
        geo.rg + 2 * i * CELLS for i in range(geo.ol)
    ]


def stage_d(
    geo, net, live, count, zc, stats_c, norm, packed, weight, short, hid, conv, sub, conv_s, stats_s,
    full, acc, acc_s,
):
    acc[...] = jnp.zeros(acc.shape, F32)
    width = zc.shape[1]
    terms = forward_terms(geo, count, stats_c, norm, width)

    def slab(s):
        net.need(s, "zc", "packed")
        keep = alive(live, s)
        for start, size, group in geo.pieces(width):
            rows = pl.ds(pl.multiple_of(s * geo.rows + start, CELLS), size)
            scale, shift = terms[group]
            joined = zc[rows, :].astype(F32) * scale + shift + packed[rows, :].astype(F32)
            value = silu(joined) * (geo.mask(size, group, width) * keep)
            put(full, pl.ds(start, size), value)
            hid[rows, :] = value.astype(BF16)
        picked = [take(full, pl.ds(start, 8, stride=2)) for start in even_rows(geo)]
        sub[at(s, geo.small), :] = jnp.concatenate(picked, axis=0).astype(BF16)
        result = nt(hid[at(s, geo.rows), :], weight[...])
        conv[at(s, geo.rows), :] = result.astype(BF16)
        for start, size, group in geo.pieces(256):
            piece = result[start : start + size]
            acc[2 * group] += fold(piece)
            acc[2 * group + 1] += fold(piece * piece)
        net.give(s, "hid", "zd", "sub")

    net.need(0, "wd")
    loop(1, slab)
    net.open()
    loop(4, lambda s: slab(s + 1))
    net.turn(1)
    loop(geo.slabs - 5, lambda s: slab(s + 5))
    net.turn(2)
    finish(net.own, acc, 4)
    net.begin()
    acc_s[...] = jnp.zeros(acc_s.shape, F32)
    wide, step = short.shape[0], 256
    net.need(0, "ws")

    def pick(c):
        return short[c : c + step, :]

    small_product(geo, sub, pick, step, conv_s, acc_s, 0, wide // 4)
    net.step()
    small_product(geo, sub, pick, step, conv_s, acc_s, wide // 4, 5 * wide // 8)
    net.step()
    small_product(geo, sub, pick, step, conv_s, acc_s, 5 * wide // 8, wide)
    finish(stats_s, acc_s, 4)
    net.end()


def small_product(geo, left, pick, step, conv, acc, first, last):
    for c in range(first, last, step):
        result = nt(left[...], pick(c))
        conv[:, c : c + step] = result.astype(BF16)
        for s in range(geo.slabs):
            for start, size, group in geo.small_pieces():
                piece = result[s * geo.small + start : s * geo.small + start + size]
                acc[2 * group, :, c : c + step] += fold(piece)
                acc[2 * group + 1, :, c : c + step] += fold(piece * piece)


def gather_taps(geo, net, live, zd, terms, full, taps):
    width = zd.shape[1]
    blank = jnp.zeros((8, width), F32)
    full[:, 0:CELLS, :] = jnp.zeros((width // 128, CELLS, 128), F32)
    full[:, CELLS + geo.rg : 2 * CELLS + geo.rg, :] = jnp.zeros((width // 128, CELLS, 128), F32)

    def slab(s):
        net.need(s, "zd")
        keep = alive(live, s)
        for start, size, group in geo.pieces(width):
            rows = pl.ds(pl.multiple_of(s * geo.rows + start, CELLS), size)
            scale, shift = terms[group]
            value = silu(zd[rows, :].astype(F32) * scale + shift)
            begin = CELLS + start + group * CELLS
            put(full, pl.ds(begin, size), value * (geo.mask(size, group, width) * keep))
        for dy in range(3):
            for dx in range(3):
                picked = []
                for group in range(2):
                    for i in range(geo.ol if group else geo.og):
                        line = 2 * i + dy - 1
                        if line < 0:
                            picked.append(blank)
                            continue
                        begin = CELLS + group * (geo.rg + CELLS) + line * CELLS + dx - 1
                        picked.append(take(full, pl.ds(begin, 8, stride=2)))
                tap = dy * 3 + dx
                taps[at(s, geo.small), tap * width : (tap + 1) * width] = jnp.concatenate(
                    picked, axis=0
                ).astype(BF16)

    loop(1, slab)
    net.open()
    if net.side is not None:
        net.side.begin()
    loop(4, lambda s: slab(s + 1))
    if net.side is not None:
        net.side.step()
    loop(geo.slabs - 5, lambda s: slab(s + 5))


def stage_e(
    geo, net, live, count, zd, stats_d, norm, weight_0, weight_1, weight_2, conv, full, taps,
    acc,
):
    acc[...] = jnp.zeros(acc.shape, F32)
    terms = forward_terms(geo, count, stats_d, norm, zd.shape[1])
    gather_taps(geo, net, live, zd, terms, full, taps)
    net.turn(1)
    net.side.step()
    net.need(0, "we_0", "we_1", "we_2")
    step = 256
    third = weight_0.shape[1]
    for c in range(0, weight_0.shape[0], step):
        result = nt(taps[:, 0:third], weight_0[c : c + step, :])
        result = result + nt(taps[:, third : 2 * third], weight_1[c : c + step, :])
        result = result + nt(taps[:, 2 * third :], weight_2[c : c + step, :])
        conv[:, c : c + step] = result.astype(BF16)
        for s in range(geo.slabs):
            keep = alive(live, s)
            for start, size, group in geo.small_pieces():
                piece = result[s * geo.small + start : s * geo.small + start + size]
                piece = piece * (geo.small_mask(group, step) * keep)
                acc[2 * group, :, c : c + step] += fold(piece)
                acc[2 * group + 1, :, c : c + step] += fold(piece * piece)
    net.side.end()
    net.turn(2)
    finish(net.own, acc, 4)
    net.run()


def stage_f(geo, net, live, count, ze, stats_e, norm, weight, act, conv, acc):
    acc[...] = jnp.zeros(acc.shape, F32)
    width = ze.shape[1]
    terms = forward_terms(geo, count, stats_e, norm, width, True)

    def slab(s):
        keep = alive(live, s)
        rows = ze[at(s, geo.small), :].astype(F32)
        parts = []
        for start, size, group in geo.small_pieces():
            scale, shift = terms[group]
            value = silu(rows[start : start + size] * scale + shift)
            parts.append(value * (geo.small_mask(group, width) * keep))
        act[at(s, geo.small), :] = jnp.concatenate(parts, axis=0).astype(BF16)

    loop(geo.slabs, slab)
    half, step = weight.shape[0] // 2, 256
    net.need(0, "wf")

    def pick(c):
        return weight[c : c + step, :]

    small_product(geo, act, pick, step, conv, acc, 0, half)
    net.open()
    small_product(geo, act, pick, step, conv, acc, half, 2 * half)
    finish(net.own, acc, 4)
    net.run()


def stage_out(
    geo, net, live, count, zf, zs, stats_f, stats_s, norm_f, norm_s, cotg, cotl, outg, outl, grad,
    pooled_sums, pool, cot, acc,
):
    acc[...] = jnp.zeros(acc.shape, F32)
    cot[...] = jnp.zeros(cot.shape, F32)
    pool[...] = jnp.zeros(pool.shape, F32)
    width = zf.shape[1]
    step = 512
    terms_f = forward_terms(geo, count, stats_f, norm_f, width, True)
    terms_s = forward_terms(geo, count, stats_s, norm_s, width, True)

    def slab(s):
        net.need(s, "zf", "zs", "cotg", "cotl")
        keep = alive(live, s)
        for c in range(0, width, step):
            cols = slice(c, c + step)
            for i in range(geo.og):
                cot[i * 8 : i * 8 + geo.og, :] = cotg[s, i, :, cols].astype(F32)
            for i in range(geo.ol):
                for side in range(2):
                    begin = geo.sg + i * 8 + side * 4
                    cot[begin : begin + geo.ol, :] = cotl[2 * s + side, i, :, cols].astype(F32)
            rows_f = zf[at(s, geo.small), cols].astype(F32)
            rows_s = zs[at(s, geo.small), cols].astype(F32)
            grads = []
            for start, size, group in geo.small_pieces():
                part = slice(start, start + size)
                vf, vs = rows_f[part], rows_s[part]
                scale_f, shift_f = (item[:, cols] for item in terms_f[group])
                scale_s, shift_s = (item[:, cols] for item in terms_s[group])
                joined = vf * scale_f + vs * scale_s + (shift_f + shift_s)
                mask = geo.small_mask(group, step) * keep
                gate = sig(joined)
                held = joined * gate
                value = held * mask
                low = value.astype(BF16)
                dy = cot[part, :] * ((gate + held - held * gate) * mask)
                grads.append(dy)
                acc[3 * group, :, cols] += fold(dy)
                acc[3 * group + 1, :, cols] += fold(dy * vf)
                acc[3 * group + 2, :, cols] += fold(dy * vs)
                summed = fold(value)
                if group == 0:
                    for i in range(geo.og):
                        outg[s, i, :, cols] = value[i * 8 : i * 8 + geo.og].astype(BF16)
                    pool[s, 0:1, cols] = jnp.sum(summed, axis=0, keepdims=True) * (
                        1.0 / (geo.og * geo.og)
                    )
                else:
                    row = lax.broadcasted_iota(jnp.int32, (8, step), 0)
                    for side in range(2):
                        own = jnp.where((row >= 4) == (side == 1), summed, 0.0)
                        pool[s, 1 + side : 2 + side, cols] = jnp.sum(
                            own, axis=0, keepdims=True
                        ) * (1.0 / (geo.ol * geo.ol))
                        for i in range(geo.ol):
                            begin = i * 8 + side * 4
                            outl[2 * s + side, i, :, cols] = value[begin : begin + geo.ol].astype(
                                BF16
                            )
            grad[at(s, geo.small), cols] = jnp.concatenate(grads, axis=0).astype(BF16)
        net.give(s, "outg", "outl", "grad")
        pooled = pool[s]
        square = jnp.mean(pooled * pooled, axis=1, keepdims=True)
        normed = pooled * lax.rsqrt(square + 1e-06)
        acc[6] += normed
        acc[7] += normed * normed

    loop(geo.slabs, slab)
    finish(net.own, acc, 6)
    net.begin()
    finish(pooled_sums, acc, 2, 6)
    net.end()


def small_back(geo, live, s, grad, conv, terms, width, cols):
    keep = alive(live, s)
    rows_g = grad[at(s, geo.small), cols].astype(F32)
    rows_z = conv[at(s, geo.small), cols].astype(F32)
    parts = []
    for start, size, group in geo.small_pieces():
        scale, by_value, constant = (item[:, cols] for item in terms[group])
        part = slice(start, start + size)
        value = rows_g[part] * scale + rows_z[part] * by_value + constant
        parts.append(value * (geo.small_mask(group, width) * keep))
    return jnp.concatenate(parts, axis=0).astype(BF16)


def stage_f_back(
    geo, net, live, count, zf, zs, stats_f, stats_s, norm_f, norm_s, grad, sums, act, sub, weight,
    short, ze, stats_e, norm_e, wgrad_f, wgrad_s, back_sub, back_e, ngrad_f, ngrad_s, dzf, dzs, acc,
):
    acc[...] = jnp.zeros(acc.shape, F32)
    width = zf.shape[1]
    step = 512
    rows_f, rows_s = ((0, 1), (3, 4)), ((0, 2), (3, 5))
    terms_f = backward_terms(geo, count, stats_f, norm_f, sums, ngrad_f, width, True, rows_f)
    terms_s = backward_terms(geo, count, stats_s, norm_s, sums, ngrad_s, width, True, rows_s)

    def slab(s):
        net.need(s, "zf", "zs", "grad")
        for c in range(0, width, step):
            cols = slice(c, c + step)
            dzf[at(s, geo.small), cols] = small_back(geo, live, s, grad, zf, terms_f, step, cols)
            dzs[at(s, geo.small), cols] = small_back(geo, live, s, grad, zs, terms_s, step, cols)

    loop(geo.slabs, slab)
    net.open()
    net.side.begin()
    net.need(0, "wf")
    block = 256
    terms_e = forward_terms(geo, count, stats_e, norm_e, ze.shape[1], True)
    for c in range(0, act.shape[1], block):
        cols = slice(c, c + block)
        result = nn(dzf[...], weight[:, cols])
        for s in range(geo.slabs):
            keep = alive(live, s)
            rows = ze[s * geo.small : (s + 1) * geo.small, cols].astype(F32)
            parts = []
            for start, size, group in geo.small_pieces():
                scale, shift = (item[:, cols] for item in terms_e[group])
                value = rows[start : start + size]
                mask = geo.small_mask(group, block) * keep
                piece = result[s * geo.small + start : s * geo.small + start + size]
                piece = piece * (slope(value * scale + shift) * mask)
                parts.append(piece)
                acc[2 * group, :, cols] += fold(piece)
                acc[2 * group + 1, :, cols] += fold(piece * value)
            back_e[s * geo.small : (s + 1) * geo.small, cols] = jnp.concatenate(
                parts, axis=0
            ).astype(BF16)
    finish(net.own, acc, 4)
    net.begin()
    net.need(0, "sub", "act", "ws")
    for c in range(0, width, block):
        cols = slice(c, c + block)
        put_pieces(wgrad_s, c, tn(dzs[:, cols], sub[...]))
        if c == width // 4:
            net.step()
    net.step()
    net.turn(1)
    for c in range(0, width, block):
        cols = slice(c, c + block)
        put_pieces(wgrad_f, c, tn(dzf[:, cols], act[...]))
        if c == width // 4:
            net.side.step()
    net.side.step()
    net.turn(2)
    for c in range(0, sub.shape[1], block):
        cols = slice(c, c + block)
        back_sub[:, cols] = nn(dzs[...], short[:, cols]).astype(BF16)
    net.side.end()
    net.end()


def stage_e_back(
    geo, net, live, count, ze, stats_e, norm_e, back_e, sums_e, zd, stats_d, norm_d, weight_0, weight_1,
    weight_2, wgrad, back_d, ngrad, full, taps, dze, moved, parity, acc,
):
    acc[...] = jnp.zeros(acc.shape, F32)
    width = ze.shape[1]
    terms_e = backward_terms(geo, count, stats_e, norm_e, sums_e, ngrad, width, True)
    terms_d = forward_terms(geo, count, stats_d, norm_d, width)
    gather_taps(geo, net, live, zd, terms_d, full, taps)

    def shift(s):
        value = small_back(geo, live, s, back_e, ze, terms_e, width, slice(0, width)).astype(F32)
        blank = jnp.zeros((8, width), F32)
        down = jnp.concatenate(
            [value[8 : geo.sg], blank, value[geo.sg + 8 :], blank], axis=0
        )
        size = geo.small
        dze[at(s, size), :] = value.astype(BF16)
        moved[0, at(s, size), :] = pltpu.roll(value, size - 1, 0).astype(BF16)
        moved[1, at(s, size), :] = down.astype(BF16)
        moved[2, at(s, size), :] = pltpu.roll(down, size - 1, 0).astype(BF16)

    loop(geo.slabs, shift)

    net.need(0, "we_0", "we_1", "we_2")

    def tap(dy, dx):
        return (weight_0, weight_1, weight_2)[dy][:, dx * width : (dx + 1) * width]

    def grads(first, last):
        for t in range(first, last):
            result = tn(dze[...], taps[:, t * width : (t + 1) * width])
            put_pieces(wgrad, 0, result, t * width)

    parity[0] = nn(dze[...], tap(1, 1))
    parity[1] = nn(dze[...], tap(1, 2)) + nn(moved[0], tap(1, 0))
    parity[2] = nn(dze[...], tap(2, 1)) + nn(moved[1], tap(0, 1))
    parity[3] = (
        nn(dze[...], tap(2, 2))
        + nn(moved[0], tap(2, 0))
        + nn(moved[1], tap(0, 2))
        + nn(moved[2], tap(0, 0))
    )

    def slab(s):
        keep = alive(live, s)
        for group in range(2):
            for i in range(geo.ol if group else geo.og):
                for a in range(2):
                    for b in range(2):
                        begin = group * geo.rg + (2 * i + a) * CELLS + b
                        source = s * geo.small + group * geo.sg + i * 8
                        part = parity[2 * a + b, pl.ds(pl.multiple_of(source, 8), 8), :]
                        put(full, pl.ds(begin, 8, stride=2), part)
        for start, size, group in geo.pieces(width):
            rows = pl.ds(pl.multiple_of(s * geo.rows + start, CELLS), size)
            scale, shift_d = terms_d[group]
            value = zd[rows, :].astype(F32)
            mask = geo.mask(size, group, width) * keep
            piece = take(full, pl.ds(start, size)) * (slope(value * scale + shift_d) * mask)
            back_d[rows, :] = piece.astype(BF16)
            acc[2 * group] += fold(piece)
            acc[2 * group + 1] += fold(piece * value)
        net.give(s, "back_d")

    loop(geo.slabs, slab)
    finish(net.own, acc, 4)
    net.begin()
    grads(0, 3)
    net.step()
    grads(3, 6)
    net.step()
    grads(6, 9)
    net.end()


def wide_back(geo, live, s, grad, conv, terms, low):
    width = conv.shape[1]
    keep = alive(live, s)
    for start, size, group in geo.pieces(width):
        rows = pl.ds(pl.multiple_of(s * geo.rows + start, CELLS), size)
        scale, by_value, constant = terms[group]
        value = grad[rows, :].astype(F32) * scale + conv[rows, :].astype(F32) * by_value + constant
        low[rows, :] = (value * (geo.mask(size, group, width) * keep)).astype(BF16)


def stage_d_back(
    geo, net, live, count, zd, stats_d, norm_d, back_d, sums_d, hid, packed, zc, stats_c, norm_c,
    back_sub, weight, wgrad, joined, ngrad, dzd, full, acc,
):
    acc[...] = jnp.zeros(acc.shape, F32)
    width = zc.shape[1]
    terms_d = backward_terms(geo, count, stats_d, norm_d, sums_d, ngrad, zd.shape[1])
    terms_c = forward_terms(geo, count, stats_c, norm_c, width)

    def slab(s):
        net.need(s, "back_d", "zd", "zc", "packed")
        wide_back(geo, live, s, back_d, zd, terms_d, dzd)
        put(full, pl.ds(0, geo.rows), nn(dzd[at(s, geo.rows), :], weight[...]))
        extra = back_sub[at(s, geo.small), :].astype(F32)
        for k, start in enumerate(even_rows(geo)):
            place = pl.ds(start, 8, stride=2)
            put(full, place, take(full, place) + extra[k * 8 : k * 8 + 8])
        keep = alive(live, s)
        for start, size, group in geo.pieces(width):
            rows = pl.ds(pl.multiple_of(s * geo.rows + start, CELLS), size)
            scale, shift = terms_c[group]
            value = zc[rows, :].astype(F32)
            pre = value * scale + shift + packed[rows, :].astype(F32)
            mask = geo.mask(size, group, width) * keep
            piece = take(full, pl.ds(start, size)) * (slope(pre) * mask)
            joined[rows, :] = piece.astype(BF16)
            acc[2 * group] += fold(piece)
            acc[2 * group + 1] += fold(piece * value)
        net.give(s, "joined")

    loop(1, slab)
    net.open()
    loop(4, lambda s: slab(s + 1))
    net.turn(1)
    loop(geo.slabs - 5, lambda s: slab(s + 5))
    net.turn(2)
    finish(net.own, acc, 4)
    block = 256
    net.begin()
    net.need(0, "hid")
    for c in range(0, dzd.shape[1], block):
        put_pieces(wgrad, c, tn(dzd[:, c : c + block], hid[...]))
        net.step()
    net.end()


def stage_c_back(
    geo, net, live, count, zc, stats_c, norm_c, joined, sums_c, zb, stats_b, norm_b, weight, wgrad,
    back_b, ngrad, dzc, act, acc,
):
    acc[...] = jnp.zeros(acc.shape, F32)
    terms_c = backward_terms(geo, count, stats_c, norm_c, sums_c, ngrad, zc.shape[1])
    terms_b = forward_terms(geo, count, stats_b, norm_b, zb.shape[1])
    width = zb.shape[1]

    def slab(s):
        net.need(s, "joined", "zc", "zb")
        wide_back(geo, live, s, joined, zc, terms_c, dzc)
        result = nn(dzc[at(s, geo.rows), :], weight[...])
        keep = alive(live, s)
        for start, size, group in geo.pieces(width):
            rows = pl.ds(pl.multiple_of(s * geo.rows + start, CELLS), size)
            scale, shift = terms_b[group]
            value = zb[rows, :].astype(F32)
            pre = value * scale + shift
            mask = geo.mask(size, group, width) * keep
            gate = sig(pre)
            held = pre * gate
            act[rows, :] = (held * mask).astype(BF16)
            piece = result[start : start + size] * ((gate + held - held * gate) * mask)
            back_b[rows, :] = piece.astype(BF16)
            acc[2 * group] += fold(piece)
            acc[2 * group + 1] += fold(piece * value)
        net.give(s, "back_b")

    loop(1, slab)
    net.open()
    loop(geo.slabs - 1, lambda s: slab(s + 1))
    net.turn(2)
    finish(net.own, acc, 4)
    net.begin()
    block = 256
    for c in range(0, dzc.shape[1], block):
        put_pieces(wgrad, c, tn(dzc[:, c : c + block], act[...]))
        if c < 2 * block:
            net.step()
    net.end()


def stage_b_back(
    geo, net, live, count, zb, stats_b, norm_b, back_b, sums_b, za, stats_a, norm_a, weight, wgrad,
    back_a, ngrad, taps, dtaps, stacked, total, acc,
):
    acc[...] = jnp.zeros(acc.shape, F32)
    width = za.shape[1]
    terms_b = backward_terms(geo, count, stats_b, norm_b, sums_b, ngrad, width)
    terms_a = forward_terms(geo, count, stats_a, norm_a, width)
    clear_halo(geo, taps)
    clear_halo(geo, dtaps)
    for t in range(9):
        stacked[t * width : (t + 1) * width, :] = weight[:, t * width : (t + 1) * width]

    def fill(s):
        spread_taps(geo, taps, s, activate(geo, live, za, s, terms_a), False)
        keep = alive(live, s)
        values = []
        for start, size, group in geo.pieces(width):
            rows = pl.ds(pl.multiple_of(s * geo.rows + start, CELLS), size)
            scale, by_value, constant = terms_b[group]
            value = back_b[rows, :].astype(F32) * scale + zb[rows, :].astype(F32) * by_value
            values.append((value + constant) * (geo.mask(size, group, width) * keep))
        spread_taps(geo, dtaps, s, values, True)

    loop(2, fill)
    net.open()
    loop(geo.slabs - 2, lambda s: fill(s + 2))
    net.turn(1)
    span = geo.halo - CELLS
    total[...] = jnp.zeros(total.shape, F32)

    def slab(s):
        result = None
        for dy in range(3):
            begin = pl.multiple_of(s * geo.halo + (2 - dy) * CELLS, CELLS)
            term = nn(
                dtaps[pl.ds(begin, span), :], stacked[dy * 3 * width : (dy + 1) * 3 * width, :]
            )
            result = term if result is None else result + term
        keep = alive(live, s)
        for group, (begin, size) in enumerate(((0, geo.rg), (geo.rg + CELLS, geo.rl))):
            rows = pl.ds(pl.multiple_of(s * geo.rows + group * geo.rg, CELLS), size)
            scale, shift = terms_a[group]
            value = za[rows, :].astype(F32)
            mask = geo.mask(size, group, width) * keep
            piece = result[begin : begin + size] * (slope(value * scale + shift) * mask)
            back_a[rows, :] = piece.astype(BF16)
            acc[2 * group] += fold(piece)
            acc[2 * group + 1] += fold(piece * value)

    def grads(s):
        own = dtaps[
            pl.ds(pl.multiple_of(s * geo.halo + CELLS, CELLS), span), width : 2 * width
        ]
        for dy in range(3):
            begin = pl.multiple_of(s * geo.halo + dy * CELLS, CELLS)
            total[:, dy * 3 * width : (dy + 1) * 3 * width] += tn(own, taps[pl.ds(begin, span), :])

    loop(geo.slabs, slab)
    net.turn(2)
    finish(net.own, acc, 4)
    part = geo.slabs // 3
    net.begin()
    loop(part, grads)
    net.step()
    loop(part, lambda s: grads(s + part))
    net.step()
    loop(geo.slabs - 2 * part, lambda s: grads(s + 2 * part))
    put_pieces(wgrad, 0, total[...])
    net.end()


def stage_a_back(
    geo, net, live, count, za, stats_a, norm_a, back_a, sums_a, packed, joined, weight, wgrad, grad,
    ngrad, dza,
):
    terms_a = backward_terms(geo, count, stats_a, norm_a, sums_a, ngrad, za.shape[1])
    loop(2, lambda s: wide_back(geo, live, s, back_a, za, terms_a, dza))
    net.open()
    loop(geo.slabs - 2, lambda s: wide_back(geo, live, s + 2, back_a, za, terms_a, dza))
    net.need(0, "packed")
    put_pieces(wgrad, 0, tn(dza[...], packed[...]))
    net.turn(1)

    net.need(0, "joined")

    def slab(s):
        result = nn(dza[at(s, geo.rows), :], weight[...])
        rows = at(s, geo.rows)
        grad[rows, :] = (result + joined[rows, :].astype(F32)).astype(BF16)
        net.give(s, "grad")

    part = geo.slabs // 3
    for number in range(3):
        begin = number * part
        size = part if number < 2 else geo.slabs - begin
        loop(size, lambda s: slab(s + begin))
        net.turn(number + 2)
    net.turn(5)
    net.close()


def last_kernel(geo, upright, grad, hid, *refs):
    count = len(upright)
    rows_in, refs = refs[:count], refs[count:]
    dxg, dxl, outg, outl = refs[:4]
    targets = refs[4:]
    result = grad[...].astype(F32)
    half = CELLS // 2
    for i in range(geo.hg):
        dxg[0, i] = result[i * CELLS : i * CELLS + geo.hg]
        outg[0, i] = hid[i * CELLS : (i + 1) * CELLS, :][0 : geo.hg]
    for i in range(geo.hl):
        begin = geo.rg + i * CELLS
        low = hid[begin : begin + CELLS, :]
        for side in range(2):
            part = begin + side * half
            dxl[side, i] = result[part : part + geo.hl]
            outl[side, i] = low[side * half : side * half + geo.hl]

    def write(k):
        @pl.when(pl.program_id(0) == k % geo.slabs)
        def one():
            source, target = rows_in[k], targets[k]
            rows = source.shape[0] * source.shape[1]
            whole = source[...].astype(F32).reshape(rows, source.shape[2])
            target[...] = whole.T if upright[k] else whole

    for k in range(count):
        write(k)


def run_last(geo, grad, hid, parts, global_shape, local_shape):
    def whole(shape):
        return pl.BlockSpec(shape, lambda s: (0,) * len(shape))

    upright = [part.shape[0] * part.shape[1] >= 128 for part in parts]
    shapes = []
    for turn, part in zip(upright, parts):
        rows = part.shape[0] * part.shape[1]
        shapes.append((part.shape[2], rows) if turn else (rows, part.shape[2]))
    views = [
        pl.BlockSpec((1,) + global_shape[1:], lambda s: (s, 0, 0, 0)),
        pl.BlockSpec((2,) + local_shape[1:], lambda s: (s, 0, 0, 0)),
    ]
    outs = pl.pallas_call(
        functools.partial(last_kernel, geo, upright),
        grid=(geo.slabs,),
        out_shape=[
            jax.ShapeDtypeStruct(shape, dtype)
            for dtype in (F32, BF16)
            for shape in (global_shape, local_shape)
        ]
        + [jax.ShapeDtypeStruct(shape, F32) for shape in shapes],
        in_specs=[
            pl.BlockSpec((geo.rows, item.shape[1]), lambda s: (s, 0)) for item in (grad, hid)
        ]
        + [whole(part.shape) for part in parts],
        out_specs=views + views + [whole(shape) for shape in shapes],
        compiler_params=pltpu.CompilerParams(vmem_limit_bytes=VMEM_CAP),
        name="last",
    )(grad, hid, *parts)
    return outs[:4], [item if turn else item.T for turn, item in zip(upright, outs[4:])]


class Group:
    def __init__(self, kind, reps, shards):
        rep, shard = lax.axis_index("rep"), lax.axis_index("fsdp")
        chip, core = shard // 2, lax.rem(shard, 2)
        wide = reps // 2
        low, high = lax.rem(rep, 2), rep // wide
        first = core == 0
        if kind == CORES:
            self.size, self.me = 2, core
            self.address = lambda k: {"fsdp": chip * 2 + k}
        elif kind == CHIPS:
            self.size, self.me = shards // 2, chip
            self.address = lambda k: {"fsdp": k * 2 + core}
        elif kind == SHARDS:
            self.size, self.me = shards, shard
            self.address = lambda k: {"fsdp": k}
        elif kind == REPLICAS:
            self.size, self.me = reps, rep
            self.address = lambda k: {"rep": k}
        elif kind == CLOSE:
            self.size, self.me = 2, jnp.where(first, low, high)
            self.address = lambda k: {
                "rep": jnp.where(first, rep - low + k, rep - high * wide + k * wide)
            }
        elif kind == SLANTED:
            self.size = wide * (shards // 2)
            self.me = jnp.where(first, rep // 2, lax.rem(rep, wide)) * (shards // 2) + chip

            def across(k):
                far = k // (shards // 2)
                return {
                    "rep": jnp.where(first, far * 2 + low, high * wide + far),
                    "fsdp": lax.rem(k, shards // 2) * 2 + core,
                }

            self.address = across
        else:
            self.size = wide
            self.me = jnp.where(first, rep // 2, lax.rem(rep, wide))
            self.address = lambda k: {"rep": jnp.where(first, k * 2 + low, high * wide + k)}

    def other(self, hop):
        return lax.rem(self.me + hop, self.size)


class Sums:
    def __init__(self, reps, shards, own, out, buffers, sems):
        self.own, self.out, self.buffers, self.sems = own, out, buffers, sems
        self.groups = [Group(kind, reps, shards) for kind in (CORES, CHIPS, REPLICAS)]
        self.phase = 0
        self.copies = []

    def send(self, source):
        group, buffer = self.groups[self.phase], self.buffers[self.phase]
        self.copies = []
        for hop in range(1, group.size):
            copy = pltpu.make_async_remote_copy(
                source, buffer.at[group.me], self.sems[2 * self.phase].at[hop],
                self.sems[2 * self.phase + 1].at[hop], device_id=group.address(group.other(hop)),
                device_id_type=MESH,
            )
            copy.start()
            self.copies.append(copy)

    def begin(self):
        self.send(self.own)
        self.buffers[0][self.groups[0].me] = self.own[...]

    def total(self):
        for copy in self.copies:
            copy.wait()
        buffer = self.buffers[self.phase]
        total = buffer[0]
        for k in range(1, self.groups[self.phase].size):
            total = total + buffer[k]
        return total

    def step(self):
        total = self.total()
        self.phase += 1
        group, buffer = self.groups[self.phase], self.buffers[self.phase]
        buffer[group.me] = total
        self.send(buffer.at[group.me])

    def end(self):
        while self.phase < 2:
            self.step()
        self.out[...] = self.total()


class In:
    def __init__(self, name, array, rows=None):
        self.name, self.array, self.rows = name, array, rows


class Out:
    def __init__(self, name, shape, dtype, rows):
        self.name, self.shape, self.dtype, self.rows = name, shape, dtype, rows


class Stream:
    def __init__(self, source, target, sems, rows, slabs):
        self.source, self.target, self.sems, self.rows, self.slabs = source, target, sems, rows, slabs

    def copy(self, s):
        if self.rows is None:
            return pltpu.make_async_copy(self.source, self.target, self.sems.at[0])
        place = at(s, self.rows)
        return pltpu.make_async_copy(self.source.at[place], self.target.at[place], self.sems.at[s])


class Net:
    def __init__(self, reps, shards, sums=None, side=None, jobs=(), plans=(), ins=(), outs=()):
        self.ins, self.outs = dict(ins), dict(outs)
        self.reps, self.shards = reps, shards
        self.sums, self.side, self.jobs, self.plans = sums, side, jobs, plans
        self.own = None if sums is None else sums.own
        self.opened = False
        self.started, self.finished = set(), set()

    def enter(self):
        rep, shard = lax.axis_index("rep"), lax.axis_index("fsdp")
        barrier = pltpu.get_barrier_semaphore()
        for hop in range(1, self.shards):
            other = {"fsdp": lax.rem(shard + hop, self.shards)}
            pl.semaphore_signal(barrier, inc=1, device_id=other, device_id_type=MESH)
        for hop in range(1, self.reps):
            other = {"rep": lax.rem(rep + hop, self.reps)}
            pl.semaphore_signal(barrier, inc=1, device_id=other, device_id_type=MESH)
        self.greeted = self.shards + self.reps - 2
        if any(job.kind == CROSS for job in self.jobs):
            group = Group(SLANTED, self.reps, self.shards)
            chips = self.shards // 2
            for far in range(1, self.reps // 2):
                for step in range(1, chips):
                    other = lax.rem(group.me // chips + far, self.reps // 2) * chips
                    other = group.address(other + lax.rem(group.me + step, chips))
                    pl.semaphore_signal(barrier, inc=1, device_id=other, device_id_type=MESH)
                    self.greeted += 1

    def load(self):
        blocks = [stream for stream in self.ins.values() if stream.rows is not None]
        if blocks:

            def start(s):
                for stream in blocks:
                    stream.copy(s).start()

            loop(blocks[0].slabs, start)
        for stream in self.ins.values():
            if stream.rows is None:
                stream.copy(0).start()

    def need(self, s, *names):
        for name in names:
            self.ins[name].copy(s).wait()

    def give(self, s, *names):
        for name in names:
            self.outs[name].copy(s).start()

    def open(self):
        if not self.opened:
            self.opened = True
            pl.semaphore_wait(pltpu.get_barrier_semaphore(), self.greeted)
            self.turn(0)

    def turn(self, number):
        for k, (start, end) in enumerate(self.plans):
            if end == number:
                self.finish(k)
        for k, (start, end) in enumerate(self.plans):
            if start == number:
                self.started.add(k)
                self.jobs[k].start()

    def finish(self, k):
        assert k in self.started and k not in self.finished
        self.finished.add(k)
        self.jobs[k].finish()

    def job_out(self, k):
        return self.jobs[k].out

    def begin(self):
        self.open()
        self.sums.begin()

    def step(self):
        self.sums.step()

    def end(self):
        self.sums.end()
        self.close()

    def run(self):
        self.begin()
        self.end()

    def close(self):
        for k in range(len(self.jobs)):
            if k not in self.finished:
                self.finish(k)
        blocks = list(self.outs.values())
        if blocks:

            def wait(s):
                for stream in blocks:
                    stream.copy(s).wait()

            loop(blocks[0].slabs, wait)


class Job:
    GROUPS = {
        PAIR: CORES, JOIN: CORES, LINE: CHIPS, SPREAD: CHIPS, ALL: SHARDS, SHARE: REPLICAS,
        HALF: CLOSE, NEAR: CLOSE, REST: APART, OTHERS: APART, CROSS: SLANTED,
    }

    def __init__(self, kind, reps, shards, sources, out, held, send, recv):
        self.kind, self.sources, self.out, self.held = kind, sources, out, held
        self.send, self.recv = send, recv
        self.reps, self.chips = reps, shards // 2
        self.rep, shard = lax.axis_index("rep"), lax.axis_index("fsdp")
        self.chip, self.core = shard // 2, lax.rem(shard, 2)
        self.group = Group(self.GROUPS[kind], reps, shards)

    def give(self, source, target, hop):
        k = len(self.copies)
        if hop == 0:
            copy = pltpu.make_async_copy(source, target, self.send.at[k])
        else:
            copy = pltpu.make_async_remote_copy(
                source, target, self.send.at[k], self.recv.at[k],
                device_id=self.group.address(self.group.other(hop)), device_id_type=MESH,
            )
        copy.start()
        self.copies.append(copy)

    def start(self):
        self.copies = []
        kind, out, source, group = self.kind, self.out, self.sources[0], self.group
        order = list(range(1, group.size)) + [0]
        wide = self.reps // 2
        first = self.core == 0
        if kind == SPREAD:
            for hop in order[:-1]:
                self.give(source.at[self.rep], out.at[self.rep, group.size - hop - 1], hop)
        elif kind == NEAR:
            self.give(out.at[self.rep], out.at[self.rep], 1)
        elif kind == OTHERS:
            low, high = lax.rem(self.rep, 2), self.rep // wide
            partner = jnp.where(
                first, self.rep + 1 - 2 * low, self.rep + (1 - 2 * high) * wide
            )
            for hop in order[:-1]:
                for place in (self.rep, partner):
                    self.give(out.at[place], out.at[place], hop)
        elif kind == JOIN:
            for hop in order:
                for step in range(1, self.chips):
                    chip = lax.rem(self.chip + step, self.chips)
                    self.give(source.at[:, step - 1], out.at[chip, self.core], hop)
                self.give(self.sources[1], out.at[self.chip, self.core], hop)
        elif kind == CROSS:
            for hop in order:
                other = group.other(hop)
                block = source.at[other // self.chips, lax.rem(other, self.chips)]
                self.give(block, self.held.at[group.me], hop)
        elif kind in (ALL, SHARE):
            for hop in order:
                self.give(source, out.at[group.me], hop)
        elif kind == HALF:
            low, high = lax.rem(self.rep, 2), self.rep // wide
            mine = jnp.where(first, low, high * wide)
            theirs = jnp.where(first, 1 - low, (1 - high) * wide)
            step = jnp.where(first, 2, 1)
            for k in range(wide):
                self.give(source.at[theirs + k * step], self.held.at[1, k], 1)
            for k in range(wide):
                self.give(source.at[mine + k * step], self.held.at[0, k], 0)
        else:
            for hop in order:
                self.give(source.at[group.other(hop)], self.held.at[group.me], hop)

    def finish(self):
        for copy in self.copies:
            copy.wait()
        held, out = self.held, self.out
        if held is None:
            return
        members = held.shape[0]
        blocks = held.shape[1:-2]

        def one(index):
            place = (index // blocks[-1], lax.rem(index, blocks[-1])) if len(blocks) == 2 else (
                (index,) if blocks else ()
            )
            total = held[(0,) + place].astype(F32)
            for k in range(1, members):
                total = total + held[(k,) + place].astype(F32)
            out[place[::-1] if self.kind == PAIR else place] = total.astype(BF16)

        if blocks:
            loop(blocks[0] * (blocks[1] if len(blocks) == 2 else 1), one)
        else:
            total = held[0].astype(F32)
            for k in range(1, members):
                total = total + held[k].astype(F32)
            out[...] = total.astype(BF16)


def job_shapes(kind, reps, shards, shape):
    chips = shards // 2
    if kind == SPREAD:
        return None, (reps, chips - 1) + shape[1:], chips
    if kind in (NEAR, OTHERS):
        return None, shape, reps
    if kind == CROSS:
        return (shape[0] * shape[1],) + shape[2:], shape[2:], shape[0] * shape[1]
    if kind == JOIN:
        return None, (chips, 2, reps) + shape[2:], 2 * chips
    if kind == ALL:
        return None, (shards,) + shape, shards
    if kind == PAIR:
        return shape, (shape[2], shape[1]) + shape[3:], 2
    if kind == SHARE:
        return None, (reps,) + shape, reps
    if kind == HALF:
        return (2, reps // 2) + shape[1:], (reps // 2,) + shape[1:], reps
    return shape, shape[1:], shape[0]


VMEM_CAP = 60 << 20
FAR = (SPREAD, NEAR, OTHERS)


def sums_scratch(reps, shards, shape, own):
    sizes = (2, shards // 2, reps)
    return (
        [pltpu.VMEM(shape, F32)] * own
        + [pltpu.VMEM((size,) + shape, F32) for size in sizes]
        + [pltpu.SemaphoreType.DMA((size,)) for size in sizes for unused in range(2)]
    )


def run(kernel, geo, reps, shards, number, live, operands, results, scratch, sums, jobs, side, far=()):
    own_results = len(results)
    extra = []
    spaces = []
    flowing = []
    internal = []
    plain_results = []
    for k, item in enumerate(results):
        if isinstance(item, Out):
            extra.append(pltpu.VMEM(item.shape, item.dtype))
            if item.rows:
                extra.append(pltpu.SemaphoreType.DMA((geo.slabs,)))
            flowing.append((k, item))
            plain_results.append((item.shape, item.dtype))
        else:
            plain_results.append(item)
        internal.append(isinstance(item, Out) and not item.rows)
        spaces.append(pltpu.HBM if isinstance(item, Out) else pltpu.VMEM)
    results = plain_results
    streamed = [(k, item) for k, item in enumerate(operands) if isinstance(item, In)]
    operands = [item.array if isinstance(item, In) else item for item in operands]
    for k, item in streamed:
        extra.append(pltpu.VMEM(item.array.shape, item.array.dtype))
        extra.append(pltpu.SemaphoreType.DMA((1 if item.rows is None else geo.slabs,)))
    arrays = []
    shapes = []
    targets = []
    kept = {}
    for kind, sources, start, end in jobs:
        source = sources[0]
        if isinstance(source, int):
            shape, dtype = shapes[source]
        elif isinstance(source, str):
            shape, dtype = results[int(source)]
        else:
            shape, dtype = source.shape, source.dtype
        held, out, copies = job_shapes(kind, reps, shards, shape)
        shapes.append((out, dtype))
        extra += [] if held is None else [pltpu.VMEM(held, BF16)]
        extra += [pltpu.SemaphoreType.DMA((copies,))] * 2
        if kind in (NEAR, OTHERS) and isinstance(source, int):
            targets.append(targets[source])
        else:
            if kind in (NEAR, OTHERS):
                kept[len(arrays)] = len(results)
            targets.append(len(results))
            results.append(shapes[-1])
            spaces.append(pltpu.HBM if kind in FAR else pltpu.VMEM)
        arrays += [item for item in sources if not isinstance(item, (int, str))]
    own_or_job = len(results)
    keep = [k for k in range(own_or_job) if not (k < own_results and internal[k])]
    own_or_job = len(results)
    operands = tuple(operands)
    near = len(operands)
    if side is not None:
        operands += (side,)
        results.append((side.shape, F32))
        spaces.append(pltpu.VMEM)
        extra += sums_scratch(reps, shards, side.shape, 0)
    if sums is not None:
        results.append((sums, F32))
        spaces.append(pltpu.VMEM)
        extra += sums_scratch(reps, shards, sums, 1)
    inputs = 1 + len(operands)
    remote = bool(jobs) or sums is not None
    keep += list(range(own_or_job, len(results)))
    far = tuple(far) + tuple(k for k, unused in streamed)

    def whole(*refs):
        sources_in = list(refs[inputs : inputs + len(arrays)])
        first_out = inputs + len(arrays)
        outs = [None] * len(results)
        for place, k in enumerate(keep):
            outs[k] = refs[first_out + place]
        more = list(refs[first_out + len(keep) :])
        own_refs = list(outs[:own_results])
        out_streams, in_streams = [], []
        for k, item in flowing:
            own_refs[k] = more.pop(0)
            if item.rows:
                stream = Stream(own_refs[k], outs[k], more.pop(0), item.rows, geo.slabs)
                out_streams.append((item.name, stream))
            else:
                outs[k] = own_refs[k]
        given = list(refs[: 1 + len(operands)])
        for k, item in streamed:
            given[1 + k] = more.pop(0)
            stream = Stream(refs[1 + k], given[1 + k], more.pop(0), item.rows, geo.slabs)
            in_streams.append((item.name, stream))
        made = []
        for k, (kind, sources, start, end) in enumerate(jobs):
            refs_of = []
            for item in sources:
                if isinstance(item, int):
                    refs_of.append(made[item].out)
                elif isinstance(item, str):
                    refs_of.append(outs[int(item)])
                else:
                    refs_of.append(sources_in.pop(0))
            held = more.pop(0) if job_shapes(kind, reps, shards, refs_of[0].shape)[0] else None
            made.append(
                Job(kind, reps, shards, refs_of, outs[targets[k]], held, more.pop(0), more.pop(0))
            )
        beside, main = None, None
        if side is not None:
            beside = Sums(reps, shards, refs[near + 1], outs[own_or_job], more[0:3], more[3:9])
            more = more[9:]
        if sums is not None:
            main = Sums(reps, shards, more[0], outs[-1], more[1:4], more[4:10])
            more = more[10:]
        net = None
        if remote:
            plans = [job[2:] for job in jobs]
            net = Net(reps, shards, main, beside, made, plans, in_streams, out_streams)
            net.enter()
            net.load()
        kernel(geo, net, *given[: near + 1], *own_refs, *more)

    params = {"collective_id": number, "has_side_effects": True} if remote else {}
    outputs = pl.pallas_call(
        whole,
        out_shape=[jax.ShapeDtypeStruct(*results[k]) for k in keep],
        in_specs=[pl.BlockSpec(memory_space=pltpu.SMEM)]
        + [pl.BlockSpec(memory_space=pltpu.HBM if k in far else pltpu.VMEM) for k in range(len(operands))]
        + [
            pl.BlockSpec(memory_space=pltpu.HBM if k in kept else pl.ANY) for k in range(len(arrays))
        ],
        out_specs=[pl.BlockSpec(memory_space=spaces[k]) for k in keep],
        scratch_shapes=extra
        + [item if not isinstance(item, tuple) else pltpu.VMEM(*item) for item in scratch],
        input_output_aliases={inputs + k: keep.index(out) for k, out in kept.items()},
        compiler_params=pltpu.CompilerParams(vmem_limit_bytes=VMEM_CAP, **params),
        name=kernel.__name__,
    )(live, *operands, *arrays)
    placed = [None] * len(results)
    for place, k in enumerate(keep):
        placed[k] = outputs[place]
    return placed


def own_norms(first, second):
    flat = jnp.concatenate([first.reshape(-1), second.reshape(-1)]).astype(F32)
    size = -(-flat.shape[0] // 1024) * 1024
    return jnp.pad(flat, (0, size - flat.shape[0])).reshape(8, -1)


def all_norms(gathered, first, second):
    shards = gathered.shape[0]
    flat = gathered.reshape(shards, -1)
    split, last = first.size, first.size + second.size

    def whole(part):
        return part.reshape(shards, 2, -1).transpose(1, 0, 2).reshape(2, -1)

    return whole(flat[:, :split]), whole(flat[:, split:last])


def body(reps, shards, *arguments):
    (
        global_views, local_views, live, first_reduce, first_spatial, first_expand, first_norms,
        second_reduce, second_spatial, second_expand, second_short, second_norms, global_cotan,
        local_cotan,
    ) = arguments
    geo = Geometry(global_views.shape[0], global_views.shape[1], local_views.shape[1])
    assert local_views.shape[0] == 2 * geo.slabs
    channels = global_views.shape[3]
    ha, hb, hc, hd, he, hf, hs = (
        item.T.reshape(reps, -1, item.shape[0])
        for item in (
            first_reduce, first_spatial, first_expand, second_reduce, second_spatial,
            second_expand, second_short,
        )
    )
    he_0, he_1, he_2 = (he[:, :, k * he.shape[2] // 3 : (k + 1) * he.shape[2] // 3] for k in range(3))
    mid_1, mid_2 = first_reduce.shape[1] * shards, second_reduce.shape[1] * shards
    wide = second_expand.shape[1] * shards

    def rows_of(gathered):
        return gathered.reshape(-1, gathered.shape[-1])

    big, small = geo.total, geo.small_total

    numbers = iter(range(100))

    def go(kernel, operands, results, scratch, width=None, members=4, jobs=(), side=None, far=()):
        parts = {4: 2, 6: 4, 8: 2}[members]
        sums = None if width is None else (members * parts, width // parts)
        return run(
            kernel, geo, reps, shards, next(numbers), live, operands, results, scratch, sums,
            jobs, side, far,
        )

    def pieces(rows, columns):
        return ((2, shards // 2, reps, rows // (shards * reps), columns), BF16)

    def acc(width, members=4):
        return ((members, 8, width), F32)

    def stat(width):
        return ((8, width), F32)

    def both(width):
        return ((2, width), F32)

    more = go(
        stage_a, (global_views, local_views),
        [Out("packed", (big, channels), BF16, geo.rows), Out("za", (big, mid_1), BF16, geo.rows)],
        [
            acc(mid_1), ((CELLS, channels), F32), ((mid_1, channels), BF16), (global_views.shape, BF16),
            (local_views.shape, BF16), pltpu.SemaphoreType.DMA((2,)),
        ],
        mid_1, 8,
        jobs=(
            (SPREAD, (ha,), 0, 1), (NEAR, (0,), 1, 2), (OTHERS, (0,), 2, 3),
            (JOIN, (0, ha), 3, 4),
            (SPREAD, (hb,), 0, 2), (NEAR, (4,), 2, 3), (OTHERS, (4,), 3, 5),
            (JOIN, (4, hb), 5, None),
            (SPREAD, (hc,), 0, 3), (NEAR, (8,), 3, 5),
            (SPREAD, (hd,), 0, 3), (NEAR, (10,), 3, 5),
            (ALL, (own_norms(first_norms, second_norms),), 1, 5), (SPREAD, (hs,), 1, 5),
        ),
        far=(0, 1),
    )
    packed, za, unused, wa, unused, wb, far_c, far_d, norms, far_s, sa = more
    count = sa
    wa, wb = rows_of(wa), rows_of(wb)
    norms_1, norms_2 = all_norms(norms, first_norms, second_norms)
    na, nb, nc = norms_1[:, :mid_1], norms_1[:, mid_1 : 2 * mid_1], norms_1[:, 2 * mid_1 :]
    nd, ne = norms_2[:, :mid_2], norms_2[:, mid_2 : 2 * mid_2]
    nf, ns = norms_2[:, 2 * mid_2 : 2 * mid_2 + wide], norms_2[:, 2 * mid_2 + wide :]
    zb, far_c, wc, far_d, wd, far_s, far_e0, far_e1, far_e2, sb = go(
        stage_b, (count, In("za", za, geo.rows), sa, na, In("wb", wb)),
        [Out("zb", (big, mid_1), BF16, geo.rows)],
        [((geo.halo_total, 3 * mid_1), BF16), acc(mid_1)], mid_1,
        jobs=(
            (OTHERS, (far_c,), 0, 1), (JOIN, (0, hc), 1, 2), (OTHERS, (far_d,), 0, 1),
            (JOIN, (2, hd), 1, 2), (NEAR, (far_s,), 0, 1), (OTHERS, (4,), 1, 2),
            (SPREAD, (he_0,), 0, 2), (SPREAD, (he_1,), 0, 2), (SPREAD, (he_2,), 0, 2),
        ),
    )
    wc = rows_of(wc)
    zc, ws, far_e0, far_e1, far_f, sc = go(
        stage_c, (count, In("zb", zb, geo.rows), sb, nb, wc),
        [Out("zc", (big, channels), BF16, geo.rows)],
        [((geo.rows, mid_1), BF16), acc(channels)], channels,
        jobs=(
            (JOIN, (far_s, hs), 0, 2), (NEAR, (far_e0,), 0, 1), (OTHERS, (1,), 1, 2),
            (NEAR, (far_e1,), 0, 1), (OTHERS, (3,), 1, 2), (SPREAD, (hf,), 0, 2),
        ),
    )
    wd, ws = rows_of(wd), rows_of(ws)
    hid, zd, sub, zs, local_s, we_0, we_1, far_e2, we_2, far_f, sd = go(
        stage_d,
        (
            count, In("zc", zc, geo.rows), sc, nc, In("packed", packed, geo.rows), In("wd", wd),
            In("ws", ws),
        ),
        [
            Out("hid", (big, channels), BF16, geo.rows), Out("zd", (big, mid_2), BF16, geo.rows),
            Out("sub", (small, channels), BF16, geo.small),
            ((small, wide), BF16), stat(wide // 2),
        ],
        [((channels // 128, geo.rows, 128), F32), acc(mid_2), acc(wide)], mid_2,
        jobs=(
            (JOIN, (far_e0, he_0), 0, 2), (JOIN, (far_e1, he_1), 0, 2),
            (NEAR, (far_e2,), 0, 1), (OTHERS, (2,), 1, 2), (JOIN, (2, he_2), 2, None),
            (NEAR, (far_f,), 0, 1), (OTHERS, (5,), 1, 2),
        ),
    )
    we = tuple(rows_of(item) for item in (we_0, we_1, we_2))
    late_we = tuple(In(name, item) for name, item in zip(("we_0", "we_1", "we_2"), we))
    ze, wf, ss, se = go(
        stage_e, (count, In("zd", zd, geo.rows), sd, nd, *late_we),
        [((small, mid_2), BF16)],
        [((mid_2 // 128, geo.halo, 128), F32), ((small, 9 * mid_2), BF16), acc(mid_2)], mid_2,
        jobs=((JOIN, (far_f, hf), 0, 2),), side=local_s,
    )
    wf = rows_of(wf)
    act_e, zf, sf = go(
        stage_f, (count, ze, se, ne, In("wf", wf)),
        [((small, mid_2), BF16), ((small, wide), BF16)], [acc(wide)], wide,
    )
    second_g, second_l, grad, local_pool, so = go(
        stage_out,
        (
            count, In("zf", zf, geo.small), In("zs", zs, geo.small), sf, ss, nf, ns,
            In("cotg", global_cotan, 1), In("cotl", local_cotan, 2),
        ),
        [
            Out("outg", global_cotan.shape, BF16, 1), Out("outl", local_cotan.shape, BF16, 2),
            Out("grad", (small, wide), BF16, geo.small),
            stat(wide // 4),
        ],
        [((geo.slabs, 8, wide), F32), ((geo.small, 512), F32), acc(wide, 8)], wide, 6,
    )
    unused, unused, back_sub, back_e, ngrad_f, ngrad_s, pair_f, pair_s, pool, qe = go(
        stage_f_back,
        (
            count, In("zf", zf, geo.small), In("zs", zs, geo.small), sf, ss, nf, ns,
            In("grad", grad, geo.small), so, In("act", act_e), In("sub", sub), In("wf", wf),
            In("ws", ws), ze, se, ne,
        ),
        [
            Out("wgrad_f", *pieces(wide, mid_2), 0), Out("wgrad_s", *pieces(wide, channels), 0), ((small, channels), BF16), ((small, mid_2), BF16),
            both(wide), both(wide),
        ],
        [((small, wide), BF16), ((small, wide), BF16), acc(mid_2)], mid_2,
        jobs=((PAIR, ("0",), 2, None), (PAIR, ("1",), 1, None)), side=local_pool,
    )
    views = count[8, 0] * 6.0
    pool = pool.reshape(2, wide)
    center = pool[0] / views
    spread = pool[1] / views - center * center
    pooled_std = jnp.mean(jnp.sqrt(spread + 1e-06))
    wgrad_e, back_d, ngrad_e, half_f, half_s, qd = go(
        stage_e_back,
        (count, ze, se, ne, back_e, qe, In("zd", zd, geo.rows), sd, nd, *late_we),
        [
            pieces(mid_2, 9 * mid_2), Out("back_d", (big, mid_2), BF16, geo.rows), both(mid_2),
        ],
        [
            ((mid_2 // 128, geo.halo, 128), F32), ((small, 9 * mid_2), BF16),
            ((small, mid_2), BF16), ((3, small, mid_2), BF16), ((4, small, mid_2), F32),
            acc(mid_2),
        ],
        mid_2, jobs=((HALF, (pair_f,), 0, None), (HALF, (pair_s,), 0, None)),
    )
    wgrad_d, joined, ngrad_d, unused, half_e, unused, rest_s, line_f, qc = go(
        stage_d_back,
        (
            count, In("zd", zd, geo.rows), sd, nd, In("back_d", back_d, geo.rows), qd,
            In("hid", hid), In("packed", packed, geo.rows), In("zc", zc, geo.rows), sc, nc, back_sub,
            wd,
        ),
        [
            pieces(mid_2, channels), Out("joined", (big, channels), BF16, geo.rows), both(mid_2),
        ],
        [((big, mid_2), BF16), ((channels // 128, geo.rows, 128), F32), acc(channels)], channels,
        jobs=(
            (PAIR, (wgrad_e,), 0, 1), (HALF, (0,), 1, None),
            (REST, (half_f,), 0, 1), (REST, (half_s,), 0, 1), (LINE, (2,), 1, None),
        ),
    )
    wgrad_c, back_b, ngrad_c, pair_d, rest_e, line_s, qb = go(
        stage_c_back,
        (
            count, In("zc", zc, geo.rows), sc, nc, In("joined", joined, geo.rows), qc,
            In("zb", zb, geo.rows), sb, nb, wc,
        ),
        [
            pieces(channels, mid_1), Out("back_b", (big, mid_1), BF16, geo.rows), both(channels),
        ],
        [((big, channels), BF16), ((big, mid_1), BF16), acc(mid_1)], mid_1,
        jobs=(
            (PAIR, (wgrad_d,), 0, 2), (REST, (half_e,), 0, 2), (LINE, (rest_s,), 0, 2),
        ),
    )
    wgrad_b, back_a, ngrad_b, unused, rest_d, unused, half_c, line_e, out_f, out_s, qa = go(
        stage_b_back,
        (count, zb, sb, nb, back_b, qb, za, sa, na, wb),
        [pieces(mid_1, 9 * mid_1), ((big, mid_1), BF16), both(mid_1)],
        [
            ((geo.halo_total, 3 * mid_1), BF16), ((geo.halo_total, 3 * mid_1), BF16),
            ((9 * mid_1, mid_1), BF16), (wb.shape, F32), acc(mid_1),
        ],
        mid_1,
        jobs=(
            (HALF, (pair_d,), 0, 1), (REST, (0,), 1, 2), (PAIR, (wgrad_c,), 0, 1),
            (HALF, (2,), 1, 2), (LINE, (rest_e,), 0, 2), (SHARE, (line_f,), 0, 2),
            (SHARE, (line_s,), 0, 2),
        ),
    )
    more = go(
        stage_a_back,
        (count, za, sa, na, back_a, qa, In("packed", packed), In("joined", joined), wa),
        [
            pieces(mid_1, channels), Out("grad", (big, channels), BF16, geo.rows), both(mid_1),
        ],
        [((big, mid_1), BF16)],
        jobs=(
            (PAIR, (wgrad_b,), 0, 1), (HALF, (0,), 1, 2), (CROSS, (1,), 2, 3), (SHARE, (2,), 3, None),
            (PAIR, ("0",), 1, 2), (HALF, (4,), 2, 3), (CROSS, (5,), 3, 4), (SHARE, (6,), 4, None),
            (REST, (half_c,), 0, 1), (LINE, (8,), 1, 2), (SHARE, (9,), 2, None),
            (LINE, (rest_d,), 0, 1), (SHARE, (11,), 1, None), (SHARE, (line_e,), 0, None),
        ),
    )
    grad, ngrad_a = more[1], more[2]
    out_b, out_a, out_c, out_d, out_e = (more[3 + k] for k in (3, 7, 10, 12, 13))
    (grad_g, grad_l, first_g, first_l), columns = run_last(
        geo, grad, hid, (out_a, out_b, out_c, out_d, out_e, out_f, out_s),
        global_views.shape, local_views.shape,
    )
    shard = lax.axis_index("fsdp")

    def own_columns(parts, width):
        whole = jnp.concatenate(parts, axis=1)
        return lax.dynamic_slice_in_dim(whole, shard * width, width, 1)

    return (
        first_g, first_l, second_g, second_l, grad_g, grad_l,
        *columns[0:3],
        own_columns((ngrad_a, ngrad_b, ngrad_c), first_norms.shape[1]),
        *columns[3:7],
        own_columns((ngrad_d, ngrad_e, ngrad_f, ngrad_s), second_norms.shape[1]),
        pooled_std,
    )


def solution(mesh):
    views = P(("rep", "fsdp"), None, None, None)
    columns = P(None, "fsdp")
    return jax.shard_map(
        functools.partial(body, mesh.shape["rep"], mesh.shape["fsdp"]),
        mesh=mesh,
        in_specs=(views, views, P(("rep", "fsdp"))) + (columns,) * 9 + (views, views),
        out_specs=(views,) * 6 + (columns,) * 9 + (P(),),
        check_vma=False,
    )
```

```python
import functools

import jax
import jax.numpy as jnp
from jax import lax
from jax.experimental import pallas as pl
from jax.experimental.pallas import tpu as pltpu
from jax.sharding import PartitionSpec as P

EPSILON = 1e-05
F32 = jnp.float32
BF16 = jnp.bfloat16
MESH = pl.DeviceIdType.MESH
CELLS = 16
PAIR, HALF, REST, LINE, SHARE, SPREAD, NEAR, OTHERS, JOIN, CROSS, ALL = range(11)
CORES, CHIPS, SHARDS, REPLICAS, CLOSE, APART, SLANTED = range(7)


def nt(left, right):
    return lax.dot_general(left, right, (((1,), (1,)), ((), ())), preferred_element_type=F32)


def nn(left, right):
    return lax.dot_general(left, right, (((1,), (0,)), ((), ())), preferred_element_type=F32)


def tn(left, right):
    return lax.dot_general(left, right, (((0,), (0,)), ((), ())), preferred_element_type=F32)


def sig(values):
    return 0.5 * jnp.tanh(0.5 * values) + 0.5


def silu(values):
    return values * sig(values)


def slope(values):
    gate = sig(values)
    held = values * gate
    return gate + held - held * gate


def lanes(tile, width):
    return jnp.concatenate([tile] * (width // tile.shape[1]), axis=1)


def fold(values):
    return jnp.sum(values.reshape(values.shape[0] // 8, 8, values.shape[1]), axis=0)


class Geometry:
    def __init__(self, views, side_global, side_local):
        self.slabs = views
        self.hg, self.hl = side_global, side_local
        assert side_global < CELLS and side_local < CELLS // 2
        self.rg, self.rl = side_global * CELLS, side_local * CELLS
        self.rows = self.rg + self.rl
        self.og, self.ol = (side_global - 1) // 2 + 1, (side_local - 1) // 2 + 1
        self.sg, self.sl = self.og * 8, self.ol * 8
        self.small = self.sg + self.sl
        self.total, self.small_total = self.slabs * self.rows, self.slabs * self.small
        self.halo = self.rows + 3 * CELLS
        self.halo_total = self.slabs * self.halo
        self.chunk = 32
        assert self.rg % self.chunk == 0 and self.rl % self.chunk == 0 and self.small % 16 == 0

    def pieces(self, width):
        if width <= 256:
            return [(0, self.rg, 0), (self.rg, self.rl, 1)]
        step = self.chunk
        return [(start, step, 0) for start in range(0, self.rg, step)] + [
            (start, step, 1) for start in range(self.rg, self.rows, step)
        ]

    def mask(self, count, group, width):
        row = lax.broadcasted_iota(jnp.int32, (count, 128), 0)
        if group == 0:
            keep = (row & (CELLS - 1)) < self.hg
        else:
            keep = (row & (CELLS // 2 - 1)) < self.hl
        return lanes(keep.astype(F32), width)

    def small_mask(self, group, width):
        count = self.sl if group else self.sg
        row = lax.broadcasted_iota(jnp.int32, (count, 128), 0)
        keep = (row & 3) < self.ol if group else (row & 7) < self.og
        return lanes(keep.astype(F32), width)

    def small_pieces(self):
        return [(0, self.sg, 0), (self.sg, self.sl, 1)]


def alive(live, slab):
    return jnp.where(slab < 2 * live[0], 1.0, 0.0).astype(F32)


def cells(geo, count, group, width, small=False):
    images = lanes(count[8:9, 0:128], width)
    if small:
        return images * float(2 * geo.og * geo.og if group == 0 else 4 * geo.ol * geo.ol)
    return images * float(2 * geo.hg * geo.hg if group == 0 else 4 * geo.hl * geo.hl)


def member(sums, row, width):
    parts = width // sums.shape[1]
    return jnp.concatenate(
        [sums[row * parts + k : row * parts + k + 1, :] for k in range(parts)], axis=1
    )


def norm_terms(stats, norm, number, group):
    width = norm.shape[1]
    mean = member(stats, 2 * group, width) / number
    spread = member(stats, 2 * group + 1, width) / number - mean * mean
    inverse = lax.rsqrt(spread + EPSILON)
    scale = norm[0:1, :] * inverse
    return mean, inverse, scale, norm[1:2, :] - mean * scale


def back_terms(stats, norm, number, group, first, second_raw):
    mean, inverse, scale, unused = norm_terms(stats, norm, number, group)
    second = inverse * (second_raw - mean * first)
    by_value = -scale * inverse * (second / number)
    constant = -scale * (first / number) - by_value * mean
    return scale, by_value, constant, second


def forward_terms(geo, count, stats, norm, width, small=False):
    return [
        norm_terms(stats, norm, cells(geo, count, group, width, small), group)[2:]
        for group in range(2)
    ]


def backward_terms(geo, count, stats, norm, sums, out, width, small=False, rows=((0, 1), (2, 3))):
    terms = []
    seconds = []
    for group in range(2):
        number = cells(geo, count, group, width, small)
        first = member(sums, rows[group][0], width)
        raw = member(sums, rows[group][1], width)
        scale, by_value, constant, second = back_terms(stats, norm, number, group, first, raw)
        terms.append((scale, by_value, constant))
        seconds.append((second, first))
    out[0:1, :] = seconds[0][0] + seconds[1][0]
    out[1:2, :] = seconds[0][1] + seconds[1][1]
    return terms


def finish(stats, acc, members, begin=0):
    part = stats.shape[1]
    parts = acc.shape[2] // part
    for row in range(members):
        total = jnp.sum(acc[begin + row], axis=0, keepdims=True)
        for k in range(parts):
            stats[row * parts + k : row * parts + k + 1, :] = total[:, k * part : (k + 1) * part]


def put(store, place, values):
    for k in range(store.shape[0]):
        store[k, place, :] = values[:, k * 128 : (k + 1) * 128]


def take(store, place):
    return jnp.concatenate([store[k, place, :] for k in range(store.shape[0])], axis=1)


def put_pieces(pieces, first, values, begin=0):
    cores, chips, reps, size = pieces.shape[:4]
    cols = slice(begin, begin + values.shape[1])
    for k in range(values.shape[0] // size):
        index = first // size + k
        shard, rep = index // reps, index % reps
        part = values[k * size : (k + 1) * size]
        pieces[shard % cores, shard // cores, rep, :, cols] = part.astype(BF16)


def loop(count, step):
    def one(index, carry):
        step(index)
        return carry

    lax.fori_loop(0, count, one, 0)


def at(index, size):
    return pl.ds(pl.multiple_of(index * size, size), size)


def stage_a(geo, net, live, xg, xl, packed, conv, acc, pair, weight, own_g, own_l, arrive):
    loads = (
        pltpu.make_async_copy(xg, own_g, arrive.at[0]),
        pltpu.make_async_copy(xl, own_l, arrive.at[1]),
    )
    for load in loads:
        load.start()
    net.open()
    acc[...] = jnp.zeros(acc.shape, F32)
    blank = jnp.zeros((CELLS, packed.shape[1]), BF16)
    half = CELLS // 2
    pair[...] = jnp.zeros(pair.shape, F32)
    for load in loads:
        load.wait()

    def pack(s):
        base = s * geo.rows
        keep = alive(live, s).astype(BF16)
        for i in range(geo.hg):
            start = pl.multiple_of(base + i * CELLS, CELLS)
            packed[pl.ds(start, CELLS), :] = blank
            packed[pl.ds(start, geo.hg), :] = own_g[s, i] * keep
        for i in range(geo.hl):
            start = pl.multiple_of(base + geo.rg + i * CELLS, CELLS)
            for side in range(2):
                pair[side * half : side * half + geo.hl, :] = own_l[2 * s + side, i].astype(F32)
            packed[pl.ds(start, CELLS), :] = pair[...].astype(BF16) * keep

    part = geo.slabs // 4
    for number in range(4):
        begin = number * part
        size = part if number < 3 else geo.slabs - begin
        loop(size, lambda s: pack(s + begin))
        net.turn(number + 1)
    gathered = net.job_out(3)
    weight[...] = gathered[...].astype(F32).reshape(weight.shape).astype(BF16)

    def slab(s):
        result = nt(packed[at(s, geo.rows), :], weight[...])
        conv[at(s, geo.rows), :] = result.astype(BF16)
        for start, size, group in geo.pieces(256):
            piece = result[start : start + size]
            acc[2 * group] += fold(piece)
            acc[2 * group + 1] += fold(piece * piece)
        net.give(s, "packed", "za")

    loop(geo.slabs, slab)
    finish(net.own, acc, 4)
    net.own[8:16, :] = jnp.full((8, net.own.shape[1]), live[0], jnp.int32).astype(F32)
    net.turn(5)
    net.run()


def spread_taps(geo, store, s, values, reverse):
    width = values[0].shape[1]
    for group in range(2):
        rows = values[group]
        size = rows.shape[0]
        start = pl.multiple_of(s * geo.halo + CELLS + group * (geo.rg + CELLS), CELLS)
        before = pltpu.roll(rows, 1, 0)
        after = pltpu.roll(rows, size - 1, 0)
        order = (after, rows, before) if reverse else (before, rows, after)
        for tap in range(3):
            store[pl.ds(start, size), tap * width : (tap + 1) * width] = order[tap].astype(BF16)


def clear_halo(geo, store):
    blank = jnp.zeros((CELLS, store.shape[1]), BF16)

    def slab(s):
        store[pl.ds(pl.multiple_of(s * geo.halo, CELLS), CELLS), :] = blank
        store[pl.ds(pl.multiple_of(s * geo.halo + CELLS + geo.rg, CELLS), CELLS), :] = blank
        store[pl.ds(pl.multiple_of((s + 1) * geo.halo - CELLS, CELLS), CELLS), :] = blank

    loop(geo.slabs, slab)


def activate(geo, live, conv, s, terms):
    values = []
    width = conv.shape[1]
    keep = alive(live, s)
    for group in range(2):
        start, size = (geo.rg, geo.rl) if group else (0, geo.rg)
        rows = conv[pl.ds(pl.multiple_of(s * geo.rows + start, CELLS), size), :].astype(F32)
        scale, shift = terms[group]
        values.append(silu(rows * scale + shift) * (geo.mask(size, group, width) * keep))
    return values


def stage_b(geo, net, live, count, za, stats_a, norm, weight, conv, taps, acc):
    acc[...] = jnp.zeros(acc.shape, F32)
    width = za.shape[1]
    terms = forward_terms(geo, count, stats_a, norm, width)
    clear_halo(geo, taps)

    def fill(s):
        net.need(s, "za")
        spread_taps(geo, taps, s, activate(geo, live, za, s, terms), False)
        net.give(s, "taps")

    loop(1, fill)
    net.open()
    loop(geo.slabs - 1, lambda s: fill(s + 1))
    net.turn(1)
    net.need(0, "wb")
    span = geo.halo - 2 * CELLS

    def slab(s):
        result = None
        for dy in range(3):
            rows = taps[pl.ds(pl.multiple_of(s * geo.halo + dy * CELLS, CELLS), span), :]
            term = nt(rows, weight[:, dy * 3 * width : (dy + 1) * 3 * width])
            result = term if result is None else result + term
        keep = alive(live, s)
        for group, (begin, size) in enumerate(((0, geo.rg), (geo.rg + CELLS, geo.rl))):
            piece = result[begin : begin + size]
            start = pl.multiple_of(s * geo.rows + group * geo.rg, CELLS)
            conv[pl.ds(start, size), :] = piece.astype(BF16)
            piece = piece * (geo.mask(size, group, width) * keep)
            acc[2 * group] += fold(piece)
            acc[2 * group + 1] += fold(piece * piece)
        net.give(s, "zb")

    loop(geo.slabs, slab)
    net.turn(2)
    finish(net.own, acc, 4)
    net.run()


def stage_c(geo, net, live, count, zb, stats_b, norm, weight, conv, act, acc):
    acc[...] = jnp.zeros(acc.shape, F32)
    terms = forward_terms(geo, count, stats_b, norm, zb.shape[1])
    step = 256

    def slab(s):
        net.need(s, "zb")
        values = activate(geo, live, zb, s, terms)
        act[0 : geo.rg, :] = values[0].astype(BF16)
        act[geo.rg : geo.rows, :] = values[1].astype(BF16)
        for c in range(0, weight.shape[0], step):
            result = nt(act[...], weight[c : c + step, :])
            conv[at(s, geo.rows), c : c + step] = result.astype(BF16)
            for start, size, group in geo.pieces(256):
                piece = result[start : start + size]
                acc[2 * group, :, c : c + step] += fold(piece)
                acc[2 * group + 1, :, c : c + step] += fold(piece * piece)
        net.give(s, "zc")

    loop(1, slab)
    net.open()
    loop(3, lambda s: slab(s + 1))
    net.turn(1)
    loop(geo.slabs - 4, lambda s: slab(s + 4))
    net.turn(2)
    finish(net.own, acc, 4)
    net.run()


def even_rows(geo):
    return [2 * i * CELLS for i in range(geo.og)] + [
        geo.rg + 2 * i * CELLS for i in range(geo.ol)
    ]


def stage_d(
    geo, net, live, count, zc, stats_c, norm, packed, weight, short, hid, conv, sub, conv_s, stats_s,
    full, acc, acc_s,
):
    acc[...] = jnp.zeros(acc.shape, F32)
    width = zc.shape[1]
    terms = forward_terms(geo, count, stats_c, norm, width)

    def slab(s):
        net.need(s, "zc", "packed")
        keep = alive(live, s)
        for start, size, group in geo.pieces(width):
            rows = pl.ds(pl.multiple_of(s * geo.rows + start, CELLS), size)
            scale, shift = terms[group]
            joined = zc[rows, :].astype(F32) * scale + shift + packed[rows, :].astype(F32)
            value = silu(joined) * (geo.mask(size, group, width) * keep)
            put(full, pl.ds(start, size), value)
            hid[rows, :] = value.astype(BF16)
        picked = [take(full, pl.ds(start, 8, stride=2)) for start in even_rows(geo)]
        sub[at(s, geo.small), :] = jnp.concatenate(picked, axis=0).astype(BF16)
        result = nt(hid[at(s, geo.rows), :], weight[...])
        conv[at(s, geo.rows), :] = result.astype(BF16)
        for start, size, group in geo.pieces(256):
            piece = result[start : start + size]
            acc[2 * group] += fold(piece)
            acc[2 * group + 1] += fold(piece * piece)
        net.give(s, "hid", "zd", "sub")

    net.need(0, "wd")
    loop(1, slab)
    net.open()
    loop(4, lambda s: slab(s + 1))
    net.turn(1)
    loop(geo.slabs - 5, lambda s: slab(s + 5))
    net.turn(2)
    finish(net.own, acc, 4)
    net.begin()
    acc_s[...] = jnp.zeros(acc_s.shape, F32)
    wide, step = short.shape[0], 256
    net.need(0, "ws")

    def pick(c):
        return short[c : c + step, :]

    small_product(geo, sub, pick, step, conv_s, acc_s, 0, wide // 4)
    net.step()
    small_product(geo, sub, pick, step, conv_s, acc_s, wide // 4, 5 * wide // 8)
    net.step()
    small_product(geo, sub, pick, step, conv_s, acc_s, 5 * wide // 8, wide)
    finish(stats_s, acc_s, 4)
    net.end()


def small_product(geo, left, pick, step, conv, acc, first, last):
    for c in range(first, last, step):
        result = nt(left[...], pick(c))
        conv[:, c : c + step] = result.astype(BF16)
        for s in range(geo.slabs):
            for start, size, group in geo.small_pieces():
                piece = result[s * geo.small + start : s * geo.small + start + size]
                acc[2 * group, :, c : c + step] += fold(piece)
                acc[2 * group + 1, :, c : c + step] += fold(piece * piece)


def gather_taps(geo, net, live, zd, terms, full, taps):
    width = zd.shape[1]
    blank = jnp.zeros((8, width), F32)
    full[:, 0:CELLS, :] = jnp.zeros((width // 128, CELLS, 128), F32)
    full[:, CELLS + geo.rg : 2 * CELLS + geo.rg, :] = jnp.zeros((width // 128, CELLS, 128), F32)

    def slab(s):
        net.need(s, "zd")
        keep = alive(live, s)
        for start, size, group in geo.pieces(width):
            rows = pl.ds(pl.multiple_of(s * geo.rows + start, CELLS), size)
            scale, shift = terms[group]
            value = silu(zd[rows, :].astype(F32) * scale + shift)
            begin = CELLS + start + group * CELLS
            put(full, pl.ds(begin, size), value * (geo.mask(size, group, width) * keep))
        for dy in range(3):
            for dx in range(3):
                picked = []
                for group in range(2):
                    for i in range(geo.ol if group else geo.og):
                        line = 2 * i + dy - 1
                        if line < 0:
                            picked.append(blank)
                            continue
                        begin = CELLS + group * (geo.rg + CELLS) + line * CELLS + dx - 1
                        picked.append(take(full, pl.ds(begin, 8, stride=2)))
                tap = dy * 3 + dx
                taps[at(s, geo.small), tap * width : (tap + 1) * width] = jnp.concatenate(
                    picked, axis=0
                ).astype(BF16)
        net.give(s, "taps")

    loop(1, slab)
    net.open()
    net.side.begin()
    loop(4, lambda s: slab(s + 1))
    net.side.step()
    loop(geo.slabs - 5, lambda s: slab(s + 5))


def stage_e(
    geo, net, live, count, zd, stats_d, norm, weight_0, weight_1, weight_2, conv, taps, full,
    acc,
):
    acc[...] = jnp.zeros(acc.shape, F32)
    terms = forward_terms(geo, count, stats_d, norm, zd.shape[1])
    gather_taps(geo, net, live, zd, terms, full, taps)
    net.turn(1)
    net.side.step()
    net.need(0, "we_0", "we_1", "we_2")
    step = 256
    third = weight_0.shape[1]
    for c in range(0, weight_0.shape[0], step):
        result = nt(taps[:, 0:third], weight_0[c : c + step, :])
        result = result + nt(taps[:, third : 2 * third], weight_1[c : c + step, :])
        result = result + nt(taps[:, 2 * third :], weight_2[c : c + step, :])
        conv[:, c : c + step] = result.astype(BF16)
        for s in range(geo.slabs):
            keep = alive(live, s)
            for start, size, group in geo.small_pieces():
                piece = result[s * geo.small + start : s * geo.small + start + size]
                piece = piece * (geo.small_mask(group, step) * keep)
                acc[2 * group, :, c : c + step] += fold(piece)
                acc[2 * group + 1, :, c : c + step] += fold(piece * piece)
    net.side.end()
    net.turn(2)
    finish(net.own, acc, 4)
    net.run()


def stage_f(geo, net, live, count, ze, stats_e, norm, weight, act, conv, acc):
    acc[...] = jnp.zeros(acc.shape, F32)
    width = ze.shape[1]
    terms = forward_terms(geo, count, stats_e, norm, width, True)

    def slab(s):
        keep = alive(live, s)
        rows = ze[at(s, geo.small), :].astype(F32)
        parts = []
        for start, size, group in geo.small_pieces():
            scale, shift = terms[group]
            value = silu(rows[start : start + size] * scale + shift)
            parts.append(value * (geo.small_mask(group, width) * keep))
        act[at(s, geo.small), :] = jnp.concatenate(parts, axis=0).astype(BF16)

    loop(geo.slabs, slab)
    half, step = weight.shape[0] // 2, 256
    net.need(0, "wf")

    def pick(c):
        return weight[c : c + step, :]

    small_product(geo, act, pick, step, conv, acc, 0, half)
    net.open()
    small_product(geo, act, pick, step, conv, acc, half, 2 * half)
    finish(net.own, acc, 4)
    net.run()


def stage_out(
    geo, net, live, count, zf, zs, stats_f, stats_s, norm_f, norm_s, cotg, cotl, outg, outl, grad,
    pooled_sums, pool, cot, acc,
):
    acc[...] = jnp.zeros(acc.shape, F32)
    cot[...] = jnp.zeros(cot.shape, F32)
    pool[...] = jnp.zeros(pool.shape, F32)
    width = zf.shape[1]
    step = 512
    terms_f = forward_terms(geo, count, stats_f, norm_f, width, True)
    terms_s = forward_terms(geo, count, stats_s, norm_s, width, True)

    def slab(s):
        net.need(s, "zf", "zs", "cotg", "cotl")
        keep = alive(live, s)
        for c in range(0, width, step):
            cols = slice(c, c + step)
            for i in range(geo.og):
                cot[i * 8 : i * 8 + geo.og, :] = cotg[s, i, :, cols].astype(F32)
            for i in range(geo.ol):
                for side in range(2):
                    begin = geo.sg + i * 8 + side * 4
                    cot[begin : begin + geo.ol, :] = cotl[2 * s + side, i, :, cols].astype(F32)
            rows_f = zf[at(s, geo.small), cols].astype(F32)
            rows_s = zs[at(s, geo.small), cols].astype(F32)
            grads = []
            for start, size, group in geo.small_pieces():
                part = slice(start, start + size)
                vf, vs = rows_f[part], rows_s[part]
                scale_f, shift_f = (item[:, cols] for item in terms_f[group])
                scale_s, shift_s = (item[:, cols] for item in terms_s[group])
                joined = vf * scale_f + vs * scale_s + (shift_f + shift_s)
                mask = geo.small_mask(group, step) * keep
                gate = sig(joined)
                held = joined * gate
                value = held * mask
                low = value.astype(BF16)
                dy = cot[part, :] * ((gate + held - held * gate) * mask)
                grads.append(dy)
                acc[3 * group, :, cols] += fold(dy)
                acc[3 * group + 1, :, cols] += fold(dy * vf)
                acc[3 * group + 2, :, cols] += fold(dy * vs)
                summed = fold(value)
                if group == 0:
                    for i in range(geo.og):
                        outg[s, i, :, cols] = value[i * 8 : i * 8 + geo.og].astype(BF16)
                    pool[s, 0:1, cols] = jnp.sum(summed, axis=0, keepdims=True) * (
                        1.0 / (geo.og * geo.og)
                    )
                else:
                    row = lax.broadcasted_iota(jnp.int32, (8, step), 0)
                    for side in range(2):
                        own = jnp.where((row >= 4) == (side == 1), summed, 0.0)
                        pool[s, 1 + side : 2 + side, cols] = jnp.sum(
                            own, axis=0, keepdims=True
                        ) * (1.0 / (geo.ol * geo.ol))
                        for i in range(geo.ol):
                            begin = i * 8 + side * 4
                            outl[2 * s + side, i, :, cols] = value[begin : begin + geo.ol].astype(
                                BF16
                            )
            grad[at(s, geo.small), cols] = jnp.concatenate(grads, axis=0).astype(BF16)
        net.give(s, "outg", "outl", "grad")
        pooled = pool[s]
        square = jnp.mean(pooled * pooled, axis=1, keepdims=True)
        normed = pooled * lax.rsqrt(square + 1e-06)
        acc[6] += normed
        acc[7] += normed * normed

    loop(geo.slabs, slab)
    finish(net.own, acc, 6)
    net.begin()
    finish(pooled_sums, acc, 2, 6)
    net.end()


def small_back(geo, live, s, grad, conv, terms, width, cols):
    keep = alive(live, s)
    rows_g = grad[at(s, geo.small), cols].astype(F32)
    rows_z = conv[at(s, geo.small), cols].astype(F32)
    parts = []
    for start, size, group in geo.small_pieces():
        scale, by_value, constant = (item[:, cols] for item in terms[group])
        part = slice(start, start + size)
        value = rows_g[part] * scale + rows_z[part] * by_value + constant
        parts.append(value * (geo.small_mask(group, width) * keep))
    return jnp.concatenate(parts, axis=0).astype(BF16)


def stage_f_back(
    geo, net, live, count, zf, zs, stats_f, stats_s, norm_f, norm_s, grad, sums, act, sub, weight,
    short, ze, stats_e, norm_e, wgrad_f, wgrad_s, back_sub, back_e, ngrad_f, ngrad_s, dzf, dzs, acc,
):
    acc[...] = jnp.zeros(acc.shape, F32)
    width = zf.shape[1]
    step = 512
    rows_f, rows_s = ((0, 1), (3, 4)), ((0, 2), (3, 5))
    terms_f = backward_terms(geo, count, stats_f, norm_f, sums, ngrad_f, width, True, rows_f)
    terms_s = backward_terms(geo, count, stats_s, norm_s, sums, ngrad_s, width, True, rows_s)

    def slab(s):
        net.need(s, "zf", "zs", "grad")
        for c in range(0, width, step):
            cols = slice(c, c + step)
            dzf[at(s, geo.small), cols] = small_back(geo, live, s, grad, zf, terms_f, step, cols)
            dzs[at(s, geo.small), cols] = small_back(geo, live, s, grad, zs, terms_s, step, cols)

    loop(geo.slabs, slab)
    net.open()
    net.side.begin()
    net.need(0, "wf")
    block = 256
    terms_e = forward_terms(geo, count, stats_e, norm_e, ze.shape[1], True)
    for c in range(0, act.shape[1], block):
        cols = slice(c, c + block)
        result = nn(dzf[...], weight[:, cols])
        for s in range(geo.slabs):
            keep = alive(live, s)
            rows = ze[s * geo.small : (s + 1) * geo.small, cols].astype(F32)
            parts = []
            for start, size, group in geo.small_pieces():
                scale, shift = (item[:, cols] for item in terms_e[group])
                value = rows[start : start + size]
                mask = geo.small_mask(group, block) * keep
                piece = result[s * geo.small + start : s * geo.small + start + size]
                piece = piece * (slope(value * scale + shift) * mask)
                parts.append(piece)
                acc[2 * group, :, cols] += fold(piece)
                acc[2 * group + 1, :, cols] += fold(piece * value)
            back_e[s * geo.small : (s + 1) * geo.small, cols] = jnp.concatenate(
                parts, axis=0
            ).astype(BF16)
    finish(net.own, acc, 4)
    net.begin()
    net.need(0, "sub", "act", "ws")
    for c in range(0, width, block):
        cols = slice(c, c + block)
        put_pieces(wgrad_s, c, tn(dzs[:, cols], sub[...]))
        if c == width // 4:
            net.step()
    net.step()
    net.turn(1)
    for c in range(0, width, block):
        cols = slice(c, c + block)
        put_pieces(wgrad_f, c, tn(dzf[:, cols], act[...]))
        if c == width // 4:
            net.side.step()
    net.side.step()
    net.turn(2)
    for c in range(0, sub.shape[1], block):
        cols = slice(c, c + block)
        back_sub[:, cols] = nn(dzs[...], short[:, cols]).astype(BF16)
    net.side.end()
    net.end()


def stage_e_back(
    geo, net, live, count, ze, stats_e, norm_e, back_e, sums_e, zd, stats_d, norm_d, weight_0, weight_1,
    weight_2, taps, wgrad, back_d, ngrad, full, dze, moved, parity, acc,
):
    acc[...] = jnp.zeros(acc.shape, F32)
    width = ze.shape[1]
    terms_e = backward_terms(geo, count, stats_e, norm_e, sums_e, ngrad, width, True)
    terms_d = forward_terms(geo, count, stats_d, norm_d, width)

    def shift(s):
        value = small_back(geo, live, s, back_e, ze, terms_e, width, slice(0, width)).astype(F32)
        blank = jnp.zeros((8, width), F32)
        down = jnp.concatenate(
            [value[8 : geo.sg], blank, value[geo.sg + 8 :], blank], axis=0
        )
        size = geo.small
        dze[at(s, size), :] = value.astype(BF16)
        moved[0, at(s, size), :] = pltpu.roll(value, size - 1, 0).astype(BF16)
        moved[1, at(s, size), :] = down.astype(BF16)
        moved[2, at(s, size), :] = pltpu.roll(down, size - 1, 0).astype(BF16)

    loop(2, shift)
    net.open()
    loop(geo.slabs - 2, lambda s: shift(s + 2))

    net.need(0, "we_0", "we_1", "we_2")

    def tap(dy, dx):
        return (weight_0, weight_1, weight_2)[dy][:, dx * width : (dx + 1) * width]

    def grads(first, last):
        for t in range(first, last):
            result = tn(dze[...], taps[:, t * width : (t + 1) * width])
            put_pieces(wgrad, 0, result, t * width)

    parity[0] = nn(dze[...], tap(1, 1))
    parity[1] = nn(dze[...], tap(1, 2)) + nn(moved[0], tap(1, 0))
    parity[2] = nn(dze[...], tap(2, 1)) + nn(moved[1], tap(0, 1))
    parity[3] = (
        nn(dze[...], tap(2, 2))
        + nn(moved[0], tap(2, 0))
        + nn(moved[1], tap(0, 2))
        + nn(moved[2], tap(0, 0))
    )

    def slab(s):
        net.need(s, "zd")
        keep = alive(live, s)
        for group in range(2):
            for i in range(geo.ol if group else geo.og):
                for a in range(2):
                    for b in range(2):
                        begin = group * geo.rg + (2 * i + a) * CELLS + b
                        source = s * geo.small + group * geo.sg + i * 8
                        part = parity[2 * a + b, pl.ds(pl.multiple_of(source, 8), 8), :]
                        put(full, pl.ds(begin, 8, stride=2), part)
        for start, size, group in geo.pieces(width):
            rows = pl.ds(pl.multiple_of(s * geo.rows + start, CELLS), size)
            scale, shift_d = terms_d[group]
            value = zd[rows, :].astype(F32)
            mask = geo.mask(size, group, width) * keep
            piece = take(full, pl.ds(start, size)) * (slope(value * scale + shift_d) * mask)
            back_d[rows, :] = piece.astype(BF16)
            acc[2 * group] += fold(piece)
            acc[2 * group + 1] += fold(piece * value)
        net.give(s, "back_d")

    loop(geo.slabs, slab)
    finish(net.own, acc, 4)
    net.begin()
    net.need(0, "taps")
    grads(0, 3)
    net.step()
    grads(3, 6)
    net.step()
    grads(6, 9)
    net.end()


def wide_back(geo, live, s, grad, conv, terms, low):
    width = conv.shape[1]
    keep = alive(live, s)
    for start, size, group in geo.pieces(width):
        rows = pl.ds(pl.multiple_of(s * geo.rows + start, CELLS), size)
        scale, by_value, constant = terms[group]
        value = grad[rows, :].astype(F32) * scale + conv[rows, :].astype(F32) * by_value + constant
        low[rows, :] = (value * (geo.mask(size, group, width) * keep)).astype(BF16)


def stage_d_back(
    geo, net, live, count, zd, stats_d, norm_d, back_d, sums_d, hid, packed, zc, stats_c, norm_c,
    back_sub, weight, wgrad, joined, ngrad, dzd, full, acc,
):
    acc[...] = jnp.zeros(acc.shape, F32)
    width = zc.shape[1]
    terms_d = backward_terms(geo, count, stats_d, norm_d, sums_d, ngrad, zd.shape[1])
    terms_c = forward_terms(geo, count, stats_c, norm_c, width)

    def slab(s):
        net.need(s, "back_d", "zd", "zc", "packed")
        wide_back(geo, live, s, back_d, zd, terms_d, dzd)
        put(full, pl.ds(0, geo.rows), nn(dzd[at(s, geo.rows), :], weight[...]))
        extra = back_sub[at(s, geo.small), :].astype(F32)
        for k, start in enumerate(even_rows(geo)):
            place = pl.ds(start, 8, stride=2)
            put(full, place, take(full, place) + extra[k * 8 : k * 8 + 8])
        keep = alive(live, s)
        for start, size, group in geo.pieces(width):
            rows = pl.ds(pl.multiple_of(s * geo.rows + start, CELLS), size)
            scale, shift = terms_c[group]
            value = zc[rows, :].astype(F32)
            pre = value * scale + shift + packed[rows, :].astype(F32)
            mask = geo.mask(size, group, width) * keep
            piece = take(full, pl.ds(start, size)) * (slope(pre) * mask)
            joined[rows, :] = piece.astype(BF16)
            acc[2 * group] += fold(piece)
            acc[2 * group + 1] += fold(piece * value)
        net.give(s, "joined")

    loop(1, slab)
    net.open()
    loop(4, lambda s: slab(s + 1))
    net.turn(1)
    loop(geo.slabs - 5, lambda s: slab(s + 5))
    net.turn(2)
    finish(net.own, acc, 4)
    block = 256
    net.begin()
    net.need(0, "hid")
    for c in range(0, dzd.shape[1], block):
        put_pieces(wgrad, c, tn(dzd[:, c : c + block], hid[...]))
        net.step()
    net.end()


def stage_c_back(
    geo, net, live, count, zc, stats_c, norm_c, joined, sums_c, zb, stats_b, norm_b, weight, wgrad,
    back_b, ngrad, dzc, act, acc,
):
    acc[...] = jnp.zeros(acc.shape, F32)
    terms_c = backward_terms(geo, count, stats_c, norm_c, sums_c, ngrad, zc.shape[1])
    terms_b = forward_terms(geo, count, stats_b, norm_b, zb.shape[1])
    width = zb.shape[1]

    def slab(s):
        net.need(s, "joined", "zc", "zb")
        wide_back(geo, live, s, joined, zc, terms_c, dzc)
        result = nn(dzc[at(s, geo.rows), :], weight[...])
        keep = alive(live, s)
        for start, size, group in geo.pieces(width):
            rows = pl.ds(pl.multiple_of(s * geo.rows + start, CELLS), size)
            scale, shift = terms_b[group]
            value = zb[rows, :].astype(F32)
            pre = value * scale + shift
            mask = geo.mask(size, group, width) * keep
            gate = sig(pre)
            held = pre * gate
            act[rows, :] = (held * mask).astype(BF16)
            piece = result[start : start + size] * ((gate + held - held * gate) * mask)
            back_b[rows, :] = piece.astype(BF16)
            acc[2 * group] += fold(piece)
            acc[2 * group + 1] += fold(piece * value)
        net.give(s, "back_b")

    loop(1, slab)
    net.open()
    loop(geo.slabs - 1, lambda s: slab(s + 1))
    net.turn(2)
    finish(net.own, acc, 4)
    net.begin()
    block = 256
    for c in range(0, dzc.shape[1], block):
        put_pieces(wgrad, c, tn(dzc[:, c : c + block], act[...]))
        if c < 2 * block:
            net.step()
    net.end()


def stage_b_back(
    geo, net, live, count, zb, stats_b, norm_b, back_b, sums_b, za, stats_a, norm_a, weight, taps,
    wgrad, back_a, ngrad, dtaps, stacked, total, acc,
):
    acc[...] = jnp.zeros(acc.shape, F32)
    width = za.shape[1]
    terms_b = backward_terms(geo, count, stats_b, norm_b, sums_b, ngrad, width)
    terms_a = forward_terms(geo, count, stats_a, norm_a, width)
    clear_halo(geo, dtaps)
    for t in range(9):
        stacked[t * width : (t + 1) * width, :] = weight[:, t * width : (t + 1) * width]

    def fill(s):
        keep = alive(live, s)
        values = []
        for start, size, group in geo.pieces(width):
            rows = pl.ds(pl.multiple_of(s * geo.rows + start, CELLS), size)
            scale, by_value, constant = terms_b[group]
            value = back_b[rows, :].astype(F32) * scale + zb[rows, :].astype(F32) * by_value
            values.append((value + constant) * (geo.mask(size, group, width) * keep))
        spread_taps(geo, dtaps, s, values, True)

    loop(2, fill)
    net.open()
    loop(geo.slabs - 2, lambda s: fill(s + 2))
    net.turn(1)
    span = geo.halo - 2 * CELLS
    total[...] = jnp.zeros(total.shape, F32)

    def slab(s):
        result = None
        for dy in range(3):
            begin = pl.multiple_of(s * geo.halo + (2 - dy) * CELLS, CELLS)
            term = nn(
                dtaps[pl.ds(begin, span), :], stacked[dy * 3 * width : (dy + 1) * 3 * width, :]
            )
            result = term if result is None else result + term
        keep = alive(live, s)
        for group, (begin, size) in enumerate(((0, geo.rg), (geo.rg + CELLS, geo.rl))):
            rows = pl.ds(pl.multiple_of(s * geo.rows + group * geo.rg, CELLS), size)
            scale, shift = terms_a[group]
            value = za[rows, :].astype(F32)
            mask = geo.mask(size, group, width) * keep
            piece = result[begin : begin + size] * (slope(value * scale + shift) * mask)
            back_a[rows, :] = piece.astype(BF16)
            acc[2 * group] += fold(piece)
            acc[2 * group + 1] += fold(piece * value)

    def grads(s):
        net.need(s, "taps")
        own = dtaps[
            pl.ds(pl.multiple_of(s * geo.halo + CELLS, CELLS), span), width : 2 * width
        ]
        for dy in range(3):
            begin = pl.multiple_of(s * geo.halo + dy * CELLS, CELLS)
            total[:, dy * 3 * width : (dy + 1) * 3 * width] += tn(own, taps[pl.ds(begin, span), :])

    loop(geo.slabs, slab)
    net.turn(2)
    finish(net.own, acc, 4)
    part = geo.slabs // 3
    net.begin()
    loop(part, grads)
    net.step()
    loop(part, lambda s: grads(s + part))
    net.step()
    loop(geo.slabs - 2 * part, lambda s: grads(s + 2 * part))
    put_pieces(wgrad, 0, total[...])
    net.end()


def stage_a_back(
    geo, net, live, count, za, stats_a, norm_a, back_a, sums_a, packed, joined, weight, wgrad, grad,
    ngrad, dza,
):
    terms_a = backward_terms(geo, count, stats_a, norm_a, sums_a, ngrad, za.shape[1])
    loop(2, lambda s: wide_back(geo, live, s, back_a, za, terms_a, dza))
    net.open()
    loop(geo.slabs - 2, lambda s: wide_back(geo, live, s + 2, back_a, za, terms_a, dza))
    net.need(0, "packed")
    put_pieces(wgrad, 0, tn(dza[...], packed[...]))
    net.turn(1)

    net.need(0, "joined")

    def slab(s):
        result = nn(dza[at(s, geo.rows), :], weight[...])
        rows = at(s, geo.rows)
        grad[rows, :] = (result + joined[rows, :].astype(F32)).astype(BF16)
        net.give(s, "grad")

    part = geo.slabs // 3
    for number in range(3):
        begin = number * part
        size = part if number < 2 else geo.slabs - begin
        loop(size, lambda s: slab(s + begin))
        net.turn(number + 2)
    net.turn(5)
    net.close()


def last_kernel(geo, upright, grad, hid, *refs):
    count = len(upright)
    rows_in, refs = refs[:count], refs[count:]
    dxg, dxl, outg, outl = refs[:4]
    targets = refs[4:]
    result = grad[...].astype(F32)
    half = CELLS // 2
    for i in range(geo.hg):
        dxg[0, i] = result[i * CELLS : i * CELLS + geo.hg]
        outg[0, i] = hid[i * CELLS : (i + 1) * CELLS, :][0 : geo.hg]
    for i in range(geo.hl):
        begin = geo.rg + i * CELLS
        low = hid[begin : begin + CELLS, :]
        for side in range(2):
            part = begin + side * half
            dxl[side, i] = result[part : part + geo.hl]
            outl[side, i] = low[side * half : side * half + geo.hl]

    def write(k):
        @pl.when(pl.program_id(0) == k % geo.slabs)
        def one():
            source, target = rows_in[k], targets[k]
            rows = source.shape[0] * source.shape[1]
            whole = source[...].astype(F32).reshape(rows, source.shape[2])
            target[...] = whole.T if upright[k] else whole

    for k in range(count):
        write(k)


def run_last(geo, grad, hid, parts, global_shape, local_shape):
    def whole(shape):
        return pl.BlockSpec(shape, lambda s: (0,) * len(shape))

    upright = [part.shape[0] * part.shape[1] >= 128 for part in parts]
    shapes = []
    for turn, part in zip(upright, parts):
        rows = part.shape[0] * part.shape[1]
        shapes.append((part.shape[2], rows) if turn else (rows, part.shape[2]))
    views = [
        pl.BlockSpec((1,) + global_shape[1:], lambda s: (s, 0, 0, 0)),
        pl.BlockSpec((2,) + local_shape[1:], lambda s: (s, 0, 0, 0)),
    ]
    outs = pl.pallas_call(
        functools.partial(last_kernel, geo, upright),
        grid=(geo.slabs,),
        out_shape=[
            jax.ShapeDtypeStruct(shape, dtype)
            for dtype in (F32, BF16)
            for shape in (global_shape, local_shape)
        ]
        + [jax.ShapeDtypeStruct(shape, F32) for shape in shapes],
        in_specs=[
            pl.BlockSpec((geo.rows, item.shape[1]), lambda s: (s, 0)) for item in (grad, hid)
        ]
        + [whole(part.shape) for part in parts],
        out_specs=views + views + [whole(shape) for shape in shapes],
        compiler_params=pltpu.CompilerParams(vmem_limit_bytes=VMEM_CAP),
        name="last",
    )(grad, hid, *parts)
    return outs[:4], [item if turn else item.T for turn, item in zip(upright, outs[4:])]


class Group:
    def __init__(self, kind, reps, shards):
        rep, shard = lax.axis_index("rep"), lax.axis_index("fsdp")
        chip, core = shard // 2, lax.rem(shard, 2)
        wide = reps // 2
        low, high = lax.rem(rep, 2), rep // wide
        first = core == 0
        if kind == CORES:
            self.size, self.me = 2, core
            self.address = lambda k: {"fsdp": chip * 2 + k}
        elif kind == CHIPS:
            self.size, self.me = shards // 2, chip
            self.address = lambda k: {"fsdp": k * 2 + core}
        elif kind == SHARDS:
            self.size, self.me = shards, shard
            self.address = lambda k: {"fsdp": k}
        elif kind == REPLICAS:
            self.size, self.me = reps, rep
            self.address = lambda k: {"rep": k}
        elif kind == CLOSE:
            self.size, self.me = 2, jnp.where(first, low, high)
            self.address = lambda k: {
                "rep": jnp.where(first, rep - low + k, rep - high * wide + k * wide)
            }
        elif kind == SLANTED:
            self.size = wide * (shards // 2)
            self.me = jnp.where(first, rep // 2, lax.rem(rep, wide)) * (shards // 2) + chip

            def across(k):
                far = k // (shards // 2)
                return {
                    "rep": jnp.where(first, far * 2 + low, high * wide + far),
                    "fsdp": lax.rem(k, shards // 2) * 2 + core,
                }

            self.address = across
        else:
            self.size = wide
            self.me = jnp.where(first, rep // 2, lax.rem(rep, wide))
            self.address = lambda k: {"rep": jnp.where(first, k * 2 + low, high * wide + k)}

    def other(self, hop):
        return lax.rem(self.me + hop, self.size)


class Sums:
    def __init__(self, reps, shards, own, out, buffers, sems):
        self.own, self.out, self.buffers, self.sems = own, out, buffers, sems
        self.groups = [Group(kind, reps, shards) for kind in (CORES, CHIPS, REPLICAS)]
        self.phase = 0
        self.copies = []

    def send(self, source):
        group, buffer = self.groups[self.phase], self.buffers[self.phase]
        self.copies = []
        for hop in range(1, group.size):
            copy = pltpu.make_async_remote_copy(
                source, buffer.at[group.me], self.sems[2 * self.phase].at[hop],
                self.sems[2 * self.phase + 1].at[hop], device_id=group.address(group.other(hop)),
                device_id_type=MESH,
            )
            copy.start()
            self.copies.append(copy)

    def begin(self):
        self.send(self.own)
        self.buffers[0][self.groups[0].me] = self.own[...]

    def total(self):
        for copy in self.copies:
            copy.wait()
        buffer = self.buffers[self.phase]
        total = buffer[0]
        for k in range(1, self.groups[self.phase].size):
            total = total + buffer[k]
        return total

    def step(self):
        total = self.total()
        self.phase += 1
        group, buffer = self.groups[self.phase], self.buffers[self.phase]
        buffer[group.me] = total
        self.send(buffer.at[group.me])

    def end(self):
        while self.phase < 2:
            self.step()
        self.out[...] = self.total()


class In:
    def __init__(self, name, array, rows=None):
        self.name, self.array, self.rows = name, array, rows


class Out:
    def __init__(self, name, shape, dtype, rows):
        self.name, self.shape, self.dtype, self.rows = name, shape, dtype, rows


class Stream:
    def __init__(self, source, target, sems, rows, slabs):
        self.source, self.target, self.sems, self.rows, self.slabs = source, target, sems, rows, slabs

    def copy(self, s):
        if self.rows is None:
            return pltpu.make_async_copy(self.source, self.target, self.sems.at[0])
        place = at(s, self.rows)
        return pltpu.make_async_copy(self.source.at[place], self.target.at[place], self.sems.at[s])


class Net:
    def __init__(self, reps, shards, sums=None, side=None, jobs=(), plans=(), ins=(), outs=()):
        self.ins, self.outs = dict(ins), dict(outs)
        self.reps, self.shards = reps, shards
        self.sums, self.side, self.jobs, self.plans = sums, side, jobs, plans
        self.own = None if sums is None else sums.own
        self.opened = False
        self.started, self.finished = set(), set()

    def enter(self):
        rep, shard = lax.axis_index("rep"), lax.axis_index("fsdp")
        barrier = pltpu.get_barrier_semaphore()
        for hop in range(1, self.shards):
            other = {"fsdp": lax.rem(shard + hop, self.shards)}
            pl.semaphore_signal(barrier, inc=1, device_id=other, device_id_type=MESH)
        for hop in range(1, self.reps):
            other = {"rep": lax.rem(rep + hop, self.reps)}
            pl.semaphore_signal(barrier, inc=1, device_id=other, device_id_type=MESH)
        self.greeted = self.shards + self.reps - 2
        if any(job.kind == CROSS for job in self.jobs):
            group = Group(SLANTED, self.reps, self.shards)
            chips = self.shards // 2
            for far in range(1, self.reps // 2):
                for step in range(1, chips):
                    other = lax.rem(group.me // chips + far, self.reps // 2) * chips
                    other = group.address(other + lax.rem(group.me + step, chips))
                    pl.semaphore_signal(barrier, inc=1, device_id=other, device_id_type=MESH)
                    self.greeted += 1

    def load(self):
        blocks = [stream for stream in self.ins.values() if stream.rows is not None]
        if blocks:

            def start(s):
                for stream in blocks:
                    stream.copy(s).start()

            loop(blocks[0].slabs, start)
        for stream in self.ins.values():
            if stream.rows is None:
                stream.copy(0).start()

    def need(self, s, *names):
        for name in names:
            self.ins[name].copy(s).wait()

    def give(self, s, *names):
        for name in names:
            self.outs[name].copy(s).start()

    def open(self):
        if not self.opened:
            self.opened = True
            pl.semaphore_wait(pltpu.get_barrier_semaphore(), self.greeted)
            self.turn(0)

    def turn(self, number):
        for k, (start, end) in enumerate(self.plans):
            if end == number:
                self.finish(k)
        for k, (start, end) in enumerate(self.plans):
            if start == number:
                self.started.add(k)
                self.jobs[k].start()

    def finish(self, k):
        assert k in self.started and k not in self.finished
        self.finished.add(k)
        self.jobs[k].finish()

    def job_out(self, k):
        return self.jobs[k].out

    def begin(self):
        self.open()
        self.sums.begin()

    def step(self):
        self.sums.step()

    def end(self):
        self.sums.end()
        self.close()

    def run(self):
        self.begin()
        self.end()

    def close(self):
        for k in range(len(self.jobs)):
            if k not in self.finished:
                self.finish(k)
        blocks = list(self.outs.values())
        if blocks:

            def wait(s):
                for stream in blocks:
                    stream.copy(s).wait()

            loop(blocks[0].slabs, wait)


class Job:
    GROUPS = {
        PAIR: CORES, JOIN: CORES, LINE: CHIPS, SPREAD: CHIPS, ALL: SHARDS, SHARE: REPLICAS,
        HALF: CLOSE, NEAR: CLOSE, REST: APART, OTHERS: APART, CROSS: SLANTED,
    }

    def __init__(self, kind, reps, shards, sources, out, held, send, recv):
        self.kind, self.sources, self.out, self.held = kind, sources, out, held
        self.send, self.recv = send, recv
        self.reps, self.chips = reps, shards // 2
        self.rep, shard = lax.axis_index("rep"), lax.axis_index("fsdp")
        self.chip, self.core = shard // 2, lax.rem(shard, 2)
        self.group = Group(self.GROUPS[kind], reps, shards)

    def give(self, source, target, hop):
        k = len(self.copies)
        if hop == 0:
            copy = pltpu.make_async_copy(source, target, self.send.at[k])
        else:
            copy = pltpu.make_async_remote_copy(
                source, target, self.send.at[k], self.recv.at[k],
                device_id=self.group.address(self.group.other(hop)), device_id_type=MESH,
            )
        copy.start()
        self.copies.append(copy)

    def start(self):
        self.copies = []
        kind, out, source, group = self.kind, self.out, self.sources[0], self.group
        order = list(range(1, group.size)) + [0]
        wide = self.reps // 2
        first = self.core == 0
        if kind == SPREAD:
            for hop in order[:-1]:
                self.give(source.at[self.rep], out.at[self.rep, group.size - hop - 1], hop)
        elif kind == NEAR:
            self.give(out.at[self.rep], out.at[self.rep], 1)
        elif kind == OTHERS:
            low, high = lax.rem(self.rep, 2), self.rep // wide
            partner = jnp.where(
                first, self.rep + 1 - 2 * low, self.rep + (1 - 2 * high) * wide
            )
            for hop in order[:-1]:
                for place in (self.rep, partner):
                    self.give(out.at[place], out.at[place], hop)
        elif kind == JOIN:
            for hop in order:
                for step in range(1, self.chips):
                    chip = lax.rem(self.chip + step, self.chips)
                    self.give(source.at[:, step - 1], out.at[chip, self.core], hop)
                self.give(self.sources[1], out.at[self.chip, self.core], hop)
        elif kind == CROSS:
            for hop in order:
                other = group.other(hop)
                block = source.at[other // self.chips, lax.rem(other, self.chips)]
                self.give(block, self.held.at[group.me], hop)
        elif kind in (ALL, SHARE):
            for hop in order:
                self.give(source, out.at[group.me], hop)
        elif kind == HALF:
            low, high = lax.rem(self.rep, 2), self.rep // wide
            mine = jnp.where(first, low, high * wide)
            theirs = jnp.where(first, 1 - low, (1 - high) * wide)
            step = jnp.where(first, 2, 1)
            for k in range(wide):
                self.give(source.at[theirs + k * step], self.held.at[1, k], 1)
            for k in range(wide):
                self.give(source.at[mine + k * step], self.held.at[0, k], 0)
        else:
            for hop in order:
                self.give(source.at[group.other(hop)], self.held.at[group.me], hop)

    def finish(self):
        for copy in self.copies:
            copy.wait()
        held, out = self.held, self.out
        if held is None:
            return
        members = held.shape[0]
        blocks = held.shape[1:-2]

        def one(index):
            place = (index // blocks[-1], lax.rem(index, blocks[-1])) if len(blocks) == 2 else (
                (index,) if blocks else ()
            )
            total = held[(0,) + place].astype(F32)
            for k in range(1, members):
                total = total + held[(k,) + place].astype(F32)
            out[place[::-1] if self.kind == PAIR else place] = total.astype(BF16)

        if blocks:
            loop(blocks[0] * (blocks[1] if len(blocks) == 2 else 1), one)
        else:
            total = held[0].astype(F32)
            for k in range(1, members):
                total = total + held[k].astype(F32)
            out[...] = total.astype(BF16)


def job_shapes(kind, reps, shards, shape):
    chips = shards // 2
    if kind == SPREAD:
        return None, (reps, chips - 1) + shape[1:], chips
    if kind in (NEAR, OTHERS):
        return None, shape, reps
    if kind == CROSS:
        return (shape[0] * shape[1],) + shape[2:], shape[2:], shape[0] * shape[1]
    if kind == JOIN:
        return None, (chips, 2, reps) + shape[2:], 2 * chips
    if kind == ALL:
        return None, (shards,) + shape, shards
    if kind == PAIR:
        return shape, (shape[2], shape[1]) + shape[3:], 2
    if kind == SHARE:
        return None, (reps,) + shape, reps
    if kind == HALF:
        return (2, reps // 2) + shape[1:], (reps // 2,) + shape[1:], reps
    return shape, shape[1:], shape[0]


VMEM_CAP = 60 << 20
FAR = (SPREAD, NEAR, OTHERS)


def sums_scratch(reps, shards, shape, own):
    sizes = (2, shards // 2, reps)
    return (
        [pltpu.VMEM(shape, F32)] * own
        + [pltpu.VMEM((size,) + shape, F32) for size in sizes]
        + [pltpu.SemaphoreType.DMA((size,)) for size in sizes for unused in range(2)]
    )


def run(kernel, geo, reps, shards, number, live, operands, results, scratch, sums, jobs, side, far=()):
    own_results = len(results)
    extra = []
    spaces = []
    flowing = []
    internal = []
    plain_results = []
    for k, item in enumerate(results):
        if isinstance(item, Out):
            extra.append(pltpu.VMEM(item.shape, item.dtype))
            if item.rows:
                extra.append(pltpu.SemaphoreType.DMA((geo.slabs,)))
            flowing.append((k, item))
            plain_results.append((item.shape, item.dtype))
        else:
            plain_results.append(item)
        internal.append(isinstance(item, Out) and not item.rows)
        spaces.append(pltpu.HBM if isinstance(item, Out) else pltpu.VMEM)
    results = plain_results
    streamed = [(k, item) for k, item in enumerate(operands) if isinstance(item, In)]
    operands = [item.array if isinstance(item, In) else item for item in operands]
    for k, item in streamed:
        extra.append(pltpu.VMEM(item.array.shape, item.array.dtype))
        extra.append(pltpu.SemaphoreType.DMA((1 if item.rows is None else geo.slabs,)))
    arrays = []
    shapes = []
    targets = []
    kept = {}
    for kind, sources, start, end in jobs:
        source = sources[0]
        if isinstance(source, int):
            shape, dtype = shapes[source]
        elif isinstance(source, str):
            shape, dtype = results[int(source)]
        else:
            shape, dtype = source.shape, source.dtype
        held, out, copies = job_shapes(kind, reps, shards, shape)
        shapes.append((out, dtype))
        extra += [] if held is None else [pltpu.VMEM(held, BF16)]
        extra += [pltpu.SemaphoreType.DMA((copies,))] * 2
        if kind in (NEAR, OTHERS) and isinstance(source, int):
            targets.append(targets[source])
        else:
            if kind in (NEAR, OTHERS):
                kept[len(arrays)] = len(results)
            targets.append(len(results))
            results.append(shapes[-1])
            spaces.append(pltpu.HBM if kind in FAR else pltpu.VMEM)
        arrays += [item for item in sources if not isinstance(item, (int, str))]
    own_or_job = len(results)
    keep = [k for k in range(own_or_job) if not (k < own_results and internal[k])]
    own_or_job = len(results)
    operands = tuple(operands)
    near = len(operands)
    if side is not None:
        operands += (side,)
        results.append((side.shape, F32))
        spaces.append(pltpu.VMEM)
        extra += sums_scratch(reps, shards, side.shape, 0)
    if sums is not None:
        results.append((sums, F32))
        spaces.append(pltpu.VMEM)
        extra += sums_scratch(reps, shards, sums, 1)
    inputs = 1 + len(operands)
    remote = bool(jobs) or sums is not None
    keep += list(range(own_or_job, len(results)))
    far = tuple(far) + tuple(k for k, unused in streamed)

    def whole(*refs):
        sources_in = list(refs[inputs : inputs + len(arrays)])
        first_out = inputs + len(arrays)
        outs = [None] * len(results)
        for place, k in enumerate(keep):
            outs[k] = refs[first_out + place]
        more = list(refs[first_out + len(keep) :])
        own_refs = list(outs[:own_results])
        out_streams, in_streams = [], []
        for k, item in flowing:
            own_refs[k] = more.pop(0)
            if item.rows:
                stream = Stream(own_refs[k], outs[k], more.pop(0), item.rows, geo.slabs)
                out_streams.append((item.name, stream))
            else:
                outs[k] = own_refs[k]
        given = list(refs[: 1 + len(operands)])
        for k, item in streamed:
            given[1 + k] = more.pop(0)
            stream = Stream(refs[1 + k], given[1 + k], more.pop(0), item.rows, geo.slabs)
            in_streams.append((item.name, stream))
        made = []
        for k, (kind, sources, start, end) in enumerate(jobs):
            refs_of = []
            for item in sources:
                if isinstance(item, int):
                    refs_of.append(made[item].out)
                elif isinstance(item, str):
                    refs_of.append(outs[int(item)])
                else:
                    refs_of.append(sources_in.pop(0))
            held = more.pop(0) if job_shapes(kind, reps, shards, refs_of[0].shape)[0] else None
            made.append(
                Job(kind, reps, shards, refs_of, outs[targets[k]], held, more.pop(0), more.pop(0))
            )
        beside, main = None, None
        if side is not None:
            beside = Sums(reps, shards, refs[near + 1], outs[own_or_job], more[0:3], more[3:9])
            more = more[9:]
        if sums is not None:
            main = Sums(reps, shards, more[0], outs[-1], more[1:4], more[4:10])
            more = more[10:]
        net = None
        if remote:
            plans = [job[2:] for job in jobs]
            net = Net(reps, shards, main, beside, made, plans, in_streams, out_streams)
            net.enter()
            net.load()
        kernel(geo, net, *given[: near + 1], *own_refs, *more)

    params = {"collective_id": number, "has_side_effects": True} if remote else {}
    outputs = pl.pallas_call(
        whole,
        out_shape=[jax.ShapeDtypeStruct(*results[k]) for k in keep],
        in_specs=[pl.BlockSpec(memory_space=pltpu.SMEM)]
        + [pl.BlockSpec(memory_space=pltpu.HBM if k in far else pltpu.VMEM) for k in range(len(operands))]
        + [
            pl.BlockSpec(memory_space=pltpu.HBM if k in kept else pl.ANY) for k in range(len(arrays))
        ],
        out_specs=[pl.BlockSpec(memory_space=spaces[k]) for k in keep],
        scratch_shapes=extra
        + [item if not isinstance(item, tuple) else pltpu.VMEM(*item) for item in scratch],
        input_output_aliases={inputs + k: keep.index(out) for k, out in kept.items()},
        compiler_params=pltpu.CompilerParams(vmem_limit_bytes=VMEM_CAP, **params),
        name=kernel.__name__,
    )(live, *operands, *arrays)
    placed = [None] * len(results)
    for place, k in enumerate(keep):
        placed[k] = outputs[place]
    return placed


def own_norms(first, second):
    flat = jnp.concatenate([first.reshape(-1), second.reshape(-1)]).astype(F32)
    size = -(-flat.shape[0] // 1024) * 1024
    return jnp.pad(flat, (0, size - flat.shape[0])).reshape(8, -1)


def all_norms(gathered, first, second):
    shards = gathered.shape[0]
    flat = gathered.reshape(shards, -1)
    split, last = first.size, first.size + second.size

    def whole(part):
        return part.reshape(shards, 2, -1).transpose(1, 0, 2).reshape(2, -1)

    return whole(flat[:, :split]), whole(flat[:, split:last])


def body(reps, shards, *arguments):
    (
        global_views, local_views, live, first_reduce, first_spatial, first_expand, first_norms,
        second_reduce, second_spatial, second_expand, second_short, second_norms, global_cotan,
        local_cotan,
    ) = arguments
    geo = Geometry(global_views.shape[0], global_views.shape[1], local_views.shape[1])
    assert local_views.shape[0] == 2 * geo.slabs
    channels = global_views.shape[3]
    ha, hb, hc, hd, he, hf, hs = (
        item.T.reshape(reps, -1, item.shape[0])
        for item in (
            first_reduce, first_spatial, first_expand, second_reduce, second_spatial,
            second_expand, second_short,
        )
    )
    he_0, he_1, he_2 = (he[:, :, k * he.shape[2] // 3 : (k + 1) * he.shape[2] // 3] for k in range(3))
    mid_1, mid_2 = first_reduce.shape[1] * shards, second_reduce.shape[1] * shards
    wide = second_expand.shape[1] * shards

    def rows_of(gathered):
        return gathered.reshape(-1, gathered.shape[-1])

    big, small = geo.total, geo.small_total

    numbers = iter(range(100))

    def go(kernel, operands, results, scratch, width=None, members=4, jobs=(), side=None, far=()):
        parts = {4: 2, 6: 4, 8: 2}[members]
        sums = None if width is None else (members * parts, width // parts)
        return run(
            kernel, geo, reps, shards, next(numbers), live, operands, results, scratch, sums,
            jobs, side, far,
        )

    def pieces(rows, columns):
        return ((2, shards // 2, reps, rows // (shards * reps), columns), BF16)

    def acc(width, members=4):
        return ((members, 8, width), F32)

    def stat(width):
        return ((8, width), F32)

    def both(width):
        return ((2, width), F32)

    more = go(
        stage_a, (global_views, local_views),
        [Out("packed", (big, channels), BF16, geo.rows), Out("za", (big, mid_1), BF16, geo.rows)],
        [
            acc(mid_1), ((CELLS, channels), F32), ((mid_1, channels), BF16), (global_views.shape, BF16),
            (local_views.shape, BF16), pltpu.SemaphoreType.DMA((2,)),
        ],
        mid_1, 8,
        jobs=(
            (SPREAD, (ha,), 0, 1), (NEAR, (0,), 1, 2), (OTHERS, (0,), 2, 3),
            (JOIN, (0, ha), 3, 4),
            (SPREAD, (hb,), 0, 2), (NEAR, (4,), 2, 3), (OTHERS, (4,), 3, 5),
            (JOIN, (4, hb), 5, None),
            (SPREAD, (hc,), 0, 3), (NEAR, (8,), 3, 5), (OTHERS, (8,), 5, None),
            (SPREAD, (hd,), 0, 3), (NEAR, (11,), 3, 5), (OTHERS, (11,), 5, None),
            (ALL, (own_norms(first_norms, second_norms),), 1, 5), (SPREAD, (hs,), 1, 5),
        ),
        far=(0, 1),
    )
    packed, za, unused, wa, unused, wb, far_c, far_d, norms, far_s, sa = more
    count = sa
    wa, wb = rows_of(wa), rows_of(wb)
    norms_1, norms_2 = all_norms(norms, first_norms, second_norms)
    na, nb, nc = norms_1[:, :mid_1], norms_1[:, mid_1 : 2 * mid_1], norms_1[:, 2 * mid_1 :]
    nd, ne = norms_2[:, :mid_2], norms_2[:, mid_2 : 2 * mid_2]
    nf, ns = norms_2[:, 2 * mid_2 : 2 * mid_2 + wide], norms_2[:, 2 * mid_2 + wide :]
    zb, taps_b, wc, wd, far_s, far_e0, far_e1, far_e2, sb = go(
        stage_b, (count, In("za", za, geo.rows), sa, na, In("wb", wb)),
        [
            Out("zb", (big, mid_1), BF16, geo.rows),
            Out("taps", (geo.halo_total, 3 * mid_1), BF16, geo.halo),
        ],
        [acc(mid_1)], mid_1,
        jobs=(
            (JOIN, (far_c, hc), 0, 2), (JOIN, (far_d, hd), 0, 2),
            (NEAR, (far_s,), 0, 1), (OTHERS, (2,), 1, 2),
            (SPREAD, (he_0,), 0, 2), (SPREAD, (he_1,), 0, 2), (SPREAD, (he_2,), 0, 2),
        ),
    )
    wc = rows_of(wc)
    zc, ws, far_e0, far_e1, far_f, sc = go(
        stage_c, (count, In("zb", zb, geo.rows), sb, nb, wc),
        [Out("zc", (big, channels), BF16, geo.rows)],
        [((geo.rows, mid_1), BF16), acc(channels)], channels,
        jobs=(
            (JOIN, (far_s, hs), 0, 2), (NEAR, (far_e0,), 0, 1), (OTHERS, (1,), 1, 2),
            (NEAR, (far_e1,), 0, 1), (OTHERS, (3,), 1, 2), (SPREAD, (hf,), 0, 2),
        ),
    )
    wd, ws = rows_of(wd), rows_of(ws)
    hid, zd, sub, zs, local_s, we_0, we_1, far_e2, we_2, far_f, sd = go(
        stage_d,
        (
            count, In("zc", zc, geo.rows), sc, nc, In("packed", packed, geo.rows), In("wd", wd),
            In("ws", ws),
        ),
        [
            Out("hid", (big, channels), BF16, geo.rows), Out("zd", (big, mid_2), BF16, geo.rows),
            Out("sub", (small, channels), BF16, geo.small),
            ((small, wide), BF16), stat(wide // 2),
        ],
        [((channels // 128, geo.rows, 128), F32), acc(mid_2), acc(wide)], mid_2,
        jobs=(
            (JOIN, (far_e0, he_0), 0, 2), (JOIN, (far_e1, he_1), 0, 2),
            (NEAR, (far_e2,), 0, 1), (OTHERS, (2,), 1, 2), (JOIN, (2, he_2), 2, None),
            (NEAR, (far_f,), 0, 1), (OTHERS, (5,), 1, 2),
        ),
    )
    we = tuple(rows_of(item) for item in (we_0, we_1, we_2))
    late_we = tuple(In(name, item) for name, item in zip(("we_0", "we_1", "we_2"), we))
    ze, taps_e, wf, ss, se = go(
        stage_e, (count, In("zd", zd, geo.rows), sd, nd, *late_we),
        [((small, mid_2), BF16), Out("taps", (small, 9 * mid_2), BF16, geo.small)],
        [((mid_2 // 128, geo.halo, 128), F32), acc(mid_2)], mid_2,
        jobs=((JOIN, (far_f, hf), 0, 2),), side=local_s,
    )
    wf = rows_of(wf)
    act_e, zf, sf = go(
        stage_f, (count, ze, se, ne, In("wf", wf)),
        [((small, mid_2), BF16), ((small, wide), BF16)], [acc(wide)], wide,
    )
    second_g, second_l, grad, local_pool, so = go(
        stage_out,
        (
            count, In("zf", zf, geo.small), In("zs", zs, geo.small), sf, ss, nf, ns,
            In("cotg", global_cotan, 1), In("cotl", local_cotan, 2),
        ),
        [
            Out("outg", global_cotan.shape, BF16, 1), Out("outl", local_cotan.shape, BF16, 2),
            Out("grad", (small, wide), BF16, geo.small),
            stat(wide // 4),
        ],
        [((geo.slabs, 8, wide), F32), ((geo.small, 512), F32), acc(wide, 8)], wide, 6,
    )
    unused, unused, back_sub, back_e, ngrad_f, ngrad_s, pair_f, pair_s, pool, qe = go(
        stage_f_back,
        (
            count, In("zf", zf, geo.small), In("zs", zs, geo.small), sf, ss, nf, ns,
            In("grad", grad, geo.small), so, In("act", act_e), In("sub", sub), In("wf", wf),
            In("ws", ws), ze, se, ne,
        ),
        [
            Out("wgrad_f", *pieces(wide, mid_2), 0), Out("wgrad_s", *pieces(wide, channels), 0), ((small, channels), BF16), ((small, mid_2), BF16),
            both(wide), both(wide),
        ],
        [((small, wide), BF16), ((small, wide), BF16), acc(mid_2)], mid_2,
        jobs=((PAIR, ("0",), 2, None), (PAIR, ("1",), 1, None)), side=local_pool,
    )
    views = count[8, 0] * 6.0
    pool = pool.reshape(2, wide)
    center = pool[0] / views
    spread = pool[1] / views - center * center
    pooled_std = jnp.mean(jnp.sqrt(spread + 1e-06))
    wgrad_e, back_d, ngrad_e, half_f, half_s, qd = go(
        stage_e_back,
        (
            count, ze, se, ne, back_e, qe, In("zd", zd, geo.rows), sd, nd, *late_we,
            In("taps", taps_e),
        ),
        [
            pieces(mid_2, 9 * mid_2), Out("back_d", (big, mid_2), BF16, geo.rows), both(mid_2),
        ],
        [
            ((mid_2 // 128, geo.halo, 128), F32), ((small, mid_2), BF16), ((3, small, mid_2), BF16), ((4, small, mid_2), F32),
            acc(mid_2),
        ],
        mid_2, jobs=((HALF, (pair_f,), 0, None), (HALF, (pair_s,), 0, None)),
    )
    wgrad_d, joined, ngrad_d, unused, half_e, unused, rest_s, line_f, qc = go(
        stage_d_back,
        (
            count, In("zd", zd, geo.rows), sd, nd, In("back_d", back_d, geo.rows), qd,
            In("hid", hid), In("packed", packed, geo.rows), In("zc", zc, geo.rows), sc, nc, back_sub,
            wd,
        ),
        [
            pieces(mid_2, channels), Out("joined", (big, channels), BF16, geo.rows), both(mid_2),
        ],
        [((big, mid_2), BF16), ((channels // 128, geo.rows, 128), F32), acc(channels)], channels,
        jobs=(
            (PAIR, (wgrad_e,), 0, 1), (HALF, (0,), 1, None),
            (REST, (half_f,), 0, 1), (REST, (half_s,), 0, 1), (LINE, (2,), 1, None),
        ),
    )
    wgrad_c, back_b, ngrad_c, pair_d, rest_e, line_s, qb = go(
        stage_c_back,
        (
            count, In("zc", zc, geo.rows), sc, nc, In("joined", joined, geo.rows), qc,
            In("zb", zb, geo.rows), sb, nb, wc,
        ),
        [
            pieces(channels, mid_1), Out("back_b", (big, mid_1), BF16, geo.rows), both(channels),
        ],
        [((big, channels), BF16), ((big, mid_1), BF16), acc(mid_1)], mid_1,
        jobs=(
            (PAIR, (wgrad_d,), 0, 2), (REST, (half_e,), 0, 2), (LINE, (rest_s,), 0, 2),
        ),
    )
    wgrad_b, back_a, ngrad_b, unused, rest_d, unused, half_c, line_e, out_f, out_s, qa = go(
        stage_b_back,
        (count, zb, sb, nb, back_b, qb, za, sa, na, wb, In("taps", taps_b, geo.halo)),
        [pieces(mid_1, 9 * mid_1), ((big, mid_1), BF16), both(mid_1)],
        [
            ((geo.halo_total, 3 * mid_1), BF16), ((9 * mid_1, mid_1), BF16), (wb.shape, F32), acc(mid_1),
        ],
        mid_1,
        jobs=(
            (HALF, (pair_d,), 0, 1), (REST, (0,), 1, 2), (PAIR, (wgrad_c,), 0, 1),
            (HALF, (2,), 1, 2), (LINE, (rest_e,), 0, 2), (SHARE, (line_f,), 0, 2),
            (SHARE, (line_s,), 0, 2),
        ),
    )
    more = go(
        stage_a_back,
        (count, za, sa, na, back_a, qa, In("packed", packed), In("joined", joined), wa),
        [
            pieces(mid_1, channels), Out("grad", (big, channels), BF16, geo.rows), both(mid_1),
        ],
        [((big, mid_1), BF16)],
        jobs=(
            (PAIR, (wgrad_b,), 0, 1), (HALF, (0,), 1, 2), (CROSS, (1,), 2, 3), (SHARE, (2,), 3, None),
            (PAIR, ("0",), 1, 2), (HALF, (4,), 2, 3), (CROSS, (5,), 3, 4), (SHARE, (6,), 4, None),
            (REST, (half_c,), 0, 1), (LINE, (8,), 1, 2), (SHARE, (9,), 2, None),
            (LINE, (rest_d,), 0, 1), (SHARE, (11,), 1, None), (SHARE, (line_e,), 0, None),
        ),
    )
    grad, ngrad_a = more[1], more[2]
    out_b, out_a, out_c, out_d, out_e = (more[3 + k] for k in (3, 7, 10, 12, 13))
    (grad_g, grad_l, first_g, first_l), columns = run_last(
        geo, grad, hid, (out_a, out_b, out_c, out_d, out_e, out_f, out_s),
        global_views.shape, local_views.shape,
    )
    shard = lax.axis_index("fsdp")

    def own_columns(parts, width):
        whole = jnp.concatenate(parts, axis=1)
        return lax.dynamic_slice_in_dim(whole, shard * width, width, 1)

    return (
        first_g, first_l, second_g, second_l, grad_g, grad_l,
        *columns[0:3],
        own_columns((ngrad_a, ngrad_b, ngrad_c), first_norms.shape[1]),
        *columns[3:7],
        own_columns((ngrad_d, ngrad_e, ngrad_f, ngrad_s), second_norms.shape[1]),
        pooled_std,
    )


def solution(mesh):
    views = P(("rep", "fsdp"), None, None, None)
    columns = P(None, "fsdp")
    return jax.shard_map(
        functools.partial(body, mesh.shape["rep"], mesh.shape["fsdp"]),
        mesh=mesh,
        in_specs=(views, views, P(("rep", "fsdp"))) + (columns,) * 9 + (views, views),
        out_specs=(views,) * 6 + (columns,) * 9 + (P(),),
        check_vma=False,
    )
```

```python
import functools

import jax
import jax.numpy as jnp
from jax import lax
from jax.experimental import pallas as pl
from jax.experimental.pallas import tpu as pltpu
from jax.sharding import PartitionSpec as P

EPSILON = 1e-05
F32 = jnp.float32
BF16 = jnp.bfloat16
MESH = pl.DeviceIdType.MESH
CELLS = 16
PAIR, HALF, REST, LINE, SHARE, SPREAD, NEAR, OTHERS, JOIN, CROSS, ALL = range(11)
CORES, CHIPS, SHARDS, REPLICAS, CLOSE, APART, SLANTED = range(7)


def nt(left, right):
    return lax.dot_general(left, right, (((1,), (1,)), ((), ())), preferred_element_type=F32)


def nn(left, right):
    return lax.dot_general(left, right, (((1,), (0,)), ((), ())), preferred_element_type=F32)


def tn(left, right):
    return lax.dot_general(left, right, (((0,), (0,)), ((), ())), preferred_element_type=F32)


def sig(values):
    return 0.5 * jnp.tanh(0.5 * values) + 0.5


def silu(values):
    return values * sig(values)


def slope(values):
    gate = sig(values)
    held = values * gate
    return gate + held - held * gate


def lanes(tile, width):
    return jnp.concatenate([tile] * (width // tile.shape[1]), axis=1)


def fold(values):
    return jnp.sum(values.reshape(values.shape[0] // 8, 8, values.shape[1]), axis=0)


class Geometry:
    def __init__(self, views, side_global, side_local):
        self.slabs = views
        self.hg, self.hl = side_global, side_local
        assert side_global < CELLS and side_local < CELLS // 2
        self.rg, self.rl = side_global * CELLS, side_local * CELLS
        self.rows = self.rg + self.rl
        self.og, self.ol = (side_global - 1) // 2 + 1, (side_local - 1) // 2 + 1
        self.sg, self.sl = self.og * 8, self.ol * 8
        self.small = self.sg + self.sl
        self.total, self.small_total = self.slabs * self.rows, self.slabs * self.small
        self.halo = self.rows + 3 * CELLS
        self.halo_total = self.slabs * self.halo
        self.chunk = 32
        assert self.rg % self.chunk == 0 and self.rl % self.chunk == 0 and self.small % 16 == 0

    def pieces(self, width):
        if width <= 256:
            return [(0, self.rg, 0), (self.rg, self.rl, 1)]
        step = self.chunk
        return [(start, step, 0) for start in range(0, self.rg, step)] + [
            (start, step, 1) for start in range(self.rg, self.rows, step)
        ]

    def mask(self, count, group, width):
        row = lax.broadcasted_iota(jnp.int32, (count, 128), 0)
        if group == 0:
            keep = (row & (CELLS - 1)) < self.hg
        else:
            keep = (row & (CELLS // 2 - 1)) < self.hl
        return lanes(keep.astype(F32), width)

    def small_mask(self, group, width):
        count = self.sl if group else self.sg
        row = lax.broadcasted_iota(jnp.int32, (count, 128), 0)
        keep = (row & 3) < self.ol if group else (row & 7) < self.og
        return lanes(keep.astype(F32), width)

    def small_pieces(self):
        return [(0, self.sg, 0), (self.sg, self.sl, 1)]


def alive(live, slab):
    return jnp.where(slab < 2 * live[0], 1.0, 0.0).astype(F32)


def cells(geo, count, group, width, small=False):
    images = lanes(count[8:9, 0:128], width)
    if small:
        return images * float(2 * geo.og * geo.og if group == 0 else 4 * geo.ol * geo.ol)
    return images * float(2 * geo.hg * geo.hg if group == 0 else 4 * geo.hl * geo.hl)


def member(sums, row, width):
    parts = width // sums.shape[1]
    return jnp.concatenate(
        [sums[row * parts + k : row * parts + k + 1, :] for k in range(parts)], axis=1
    )


def norm_terms(stats, norm, number, group):
    width = norm.shape[1]
    mean = member(stats, 2 * group, width) / number
    spread = member(stats, 2 * group + 1, width) / number - mean * mean
    inverse = lax.rsqrt(spread + EPSILON)
    scale = norm[0:1, :] * inverse
    return mean, inverse, scale, norm[1:2, :] - mean * scale


def back_terms(stats, norm, number, group, first, second_raw):
    mean, inverse, scale, unused = norm_terms(stats, norm, number, group)
    second = inverse * (second_raw - mean * first)
    by_value = -scale * inverse * (second / number)
    constant = -scale * (first / number) - by_value * mean
    return scale, by_value, constant, second


def forward_terms(geo, count, stats, norm, width, small=False):
    return [
        norm_terms(stats, norm, cells(geo, count, group, width, small), group)[2:]
        for group in range(2)
    ]


def backward_terms(geo, count, stats, norm, sums, out, width, small=False, rows=((0, 1), (2, 3))):
    terms = []
    seconds = []
    for group in range(2):
        number = cells(geo, count, group, width, small)
        first = member(sums, rows[group][0], width)
        raw = member(sums, rows[group][1], width)
        scale, by_value, constant, second = back_terms(stats, norm, number, group, first, raw)
        terms.append((scale, by_value, constant))
        seconds.append((second, first))
    out[0:1, :] = seconds[0][0] + seconds[1][0]
    out[1:2, :] = seconds[0][1] + seconds[1][1]
    return terms


def finish(stats, acc, members, begin=0):
    part = stats.shape[1]
    parts = acc.shape[2] // part
    for row in range(members):
        total = jnp.sum(acc[begin + row], axis=0, keepdims=True)
        for k in range(parts):
            stats[row * parts + k : row * parts + k + 1, :] = total[:, k * part : (k + 1) * part]


def put(store, place, values):
    for k in range(store.shape[0]):
        store[k, place, :] = values[:, k * 128 : (k + 1) * 128]


def take(store, place):
    return jnp.concatenate([store[k, place, :] for k in range(store.shape[0])], axis=1)


def put_pieces(pieces, first, values, begin=0):
    cores, chips, reps, size = pieces.shape[:4]
    cols = slice(begin, begin + values.shape[1])
    for k in range(values.shape[0] // size):
        index = first // size + k
        shard, rep = index // reps, index % reps
        part = values[k * size : (k + 1) * size]
        pieces[shard % cores, shard // cores, rep, :, cols] = part.astype(BF16)


def loop(count, step):
    def one(index, carry):
        step(index)
        return carry

    lax.fori_loop(0, count, one, 0)


def at(index, size):
    return pl.ds(pl.multiple_of(index * size, size), size)


def stage_a(
    geo, net, live, xg, xl, short, expand, packed, conv, short_rows, expand_rows, acc, pair, weight,
    own_g, own_l, arrive,
):
    loads = (
        pltpu.make_async_copy(xg, own_g, arrive.at[0]),
        pltpu.make_async_copy(xl, own_l, arrive.at[1]),
    )
    for load in loads:
        load.start()
    net.open()
    acc[...] = jnp.zeros(acc.shape, F32)
    blank = jnp.zeros((CELLS, packed.shape[1]), BF16)
    half = CELLS // 2
    pair[...] = jnp.zeros(pair.shape, F32)
    for columns, rows in ((short, short_rows), (expand, expand_rows)):
        rows[...] = columns[...].astype(F32).T.reshape(rows.shape).astype(BF16)
    for load in loads:
        load.wait()

    def pack(s):
        base = s * geo.rows
        keep = alive(live, s).astype(BF16)
        for i in range(geo.hg):
            start = pl.multiple_of(base + i * CELLS, CELLS)
            packed[pl.ds(start, CELLS), :] = blank
            packed[pl.ds(start, geo.hg), :] = own_g[s, i] * keep
        for i in range(geo.hl):
            start = pl.multiple_of(base + geo.rg + i * CELLS, CELLS)
            for side in range(2):
                pair[side * half : side * half + geo.hl, :] = own_l[2 * s + side, i].astype(F32)
            packed[pl.ds(start, CELLS), :] = pair[...].astype(BF16) * keep

    part = geo.slabs // 4
    for number in range(4):
        begin = number * part
        size = part if number < 3 else geo.slabs - begin
        loop(size, lambda s: pack(s + begin))
        net.turn(number + 1)
    gathered = net.job_out(3)
    weight[...] = gathered[...].astype(F32).reshape(weight.shape).astype(BF16)

    def slab(s):
        result = nt(packed[at(s, geo.rows), :], weight[...])
        conv[at(s, geo.rows), :] = result.astype(BF16)
        for start, size, group in geo.pieces(256):
            piece = result[start : start + size]
            acc[2 * group] += fold(piece)
            acc[2 * group + 1] += fold(piece * piece)
        net.give(s, "packed", "za")

    loop(geo.slabs, slab)
    finish(net.own, acc, 4)
    net.own[8:16, :] = jnp.full((8, net.own.shape[1]), live[0], jnp.int32).astype(F32)
    net.turn(5)
    net.run()


def spread_taps(geo, store, s, values, reverse):
    width = values[0].shape[1]
    for group in range(2):
        rows = values[group]
        size = rows.shape[0]
        start = pl.multiple_of(s * geo.halo + CELLS + group * (geo.rg + CELLS), CELLS)
        before = pltpu.roll(rows, 1, 0)
        after = pltpu.roll(rows, size - 1, 0)
        order = (after, rows, before) if reverse else (before, rows, after)
        for tap in range(3):
            store[pl.ds(start, size), tap * width : (tap + 1) * width] = order[tap].astype(BF16)


def clear_halo(geo, store):
    blank = jnp.zeros((CELLS, store.shape[1]), BF16)

    def slab(s):
        store[pl.ds(pl.multiple_of(s * geo.halo, CELLS), CELLS), :] = blank
        store[pl.ds(pl.multiple_of(s * geo.halo + CELLS + geo.rg, CELLS), CELLS), :] = blank
        store[pl.ds(pl.multiple_of((s + 1) * geo.halo - CELLS, CELLS), CELLS), :] = blank

    loop(geo.slabs, slab)


def activate(geo, live, conv, s, terms):
    values = []
    width = conv.shape[1]
    keep = alive(live, s)
    for group in range(2):
        start, size = (geo.rg, geo.rl) if group else (0, geo.rg)
        rows = conv[pl.ds(pl.multiple_of(s * geo.rows + start, CELLS), size), :].astype(F32)
        scale, shift = terms[group]
        values.append(silu(rows * scale + shift) * (geo.mask(size, group, width) * keep))
    return values


def stage_b(geo, net, live, count, za, stats_a, norm, weight, conv, taps, acc):
    acc[...] = jnp.zeros(acc.shape, F32)
    width = za.shape[1]
    terms = forward_terms(geo, count, stats_a, norm, width)
    clear_halo(geo, taps)

    def fill(s):
        net.need(s, "za")
        spread_taps(geo, taps, s, activate(geo, live, za, s, terms), False)
        net.give(s, "taps")

    loop(1, fill)
    net.open()
    loop(geo.slabs - 1, lambda s: fill(s + 1))
    net.turn(1)
    net.need(0, "wb")
    span = geo.halo - 2 * CELLS

    def slab(s):
        result = None
        for dy in range(3):
            rows = taps[pl.ds(pl.multiple_of(s * geo.halo + dy * CELLS, CELLS), span), :]
            term = nt(rows, weight[:, dy * 3 * width : (dy + 1) * 3 * width])
            result = term if result is None else result + term
        keep = alive(live, s)
        for group, (begin, size) in enumerate(((0, geo.rg), (geo.rg + CELLS, geo.rl))):
            piece = result[begin : begin + size]
            start = pl.multiple_of(s * geo.rows + group * geo.rg, CELLS)
            conv[pl.ds(start, size), :] = piece.astype(BF16)
            piece = piece * (geo.mask(size, group, width) * keep)
            acc[2 * group] += fold(piece)
            acc[2 * group + 1] += fold(piece * piece)
        net.give(s, "zb")

    loop(geo.slabs, slab)
    net.turn(2)
    finish(net.own, acc, 4)
    net.run()


def stage_c(geo, net, live, count, zb, stats_b, norm, weight, conv, act, acc):
    acc[...] = jnp.zeros(acc.shape, F32)
    terms = forward_terms(geo, count, stats_b, norm, zb.shape[1])
    step = 256

    def slab(s):
        net.need(s, "zb")
        values = activate(geo, live, zb, s, terms)
        act[0 : geo.rg, :] = values[0].astype(BF16)
        act[geo.rg : geo.rows, :] = values[1].astype(BF16)
        for c in range(0, weight.shape[0], step):
            result = nt(act[...], weight[c : c + step, :])
            conv[at(s, geo.rows), c : c + step] = result.astype(BF16)
            for start, size, group in geo.pieces(256):
                piece = result[start : start + size]
                acc[2 * group, :, c : c + step] += fold(piece)
                acc[2 * group + 1, :, c : c + step] += fold(piece * piece)
        net.give(s, "zc")

    loop(1, slab)
    net.open()
    loop(3, lambda s: slab(s + 1))
    net.turn(1)
    loop(geo.slabs - 4, lambda s: slab(s + 4))
    net.turn(2)
    finish(net.own, acc, 4)
    net.run()


def even_rows(geo):
    return [2 * i * CELLS for i in range(geo.og)] + [
        geo.rg + 2 * i * CELLS for i in range(geo.ol)
    ]


def stage_d(
    geo, net, live, count, zc, stats_c, norm, packed, weight, short, hid, conv, sub, conv_s, stats_s,
    full, acc, acc_s,
):
    acc[...] = jnp.zeros(acc.shape, F32)
    width = zc.shape[1]
    terms = forward_terms(geo, count, stats_c, norm, width)

    def slab(s):
        net.need(s, "zc", "packed")
        keep = alive(live, s)
        for start, size, group in geo.pieces(width):
            rows = pl.ds(pl.multiple_of(s * geo.rows + start, CELLS), size)
            scale, shift = terms[group]
            joined = zc[rows, :].astype(F32) * scale + shift + packed[rows, :].astype(F32)
            value = silu(joined) * (geo.mask(size, group, width) * keep)
            put(full, pl.ds(start, size), value)
            hid[rows, :] = value.astype(BF16)
        picked = [take(full, pl.ds(start, 8, stride=2)) for start in even_rows(geo)]
        sub[at(s, geo.small), :] = jnp.concatenate(picked, axis=0).astype(BF16)
        result = nt(hid[at(s, geo.rows), :], weight[...])
        conv[at(s, geo.rows), :] = result.astype(BF16)
        for start, size, group in geo.pieces(256):
            piece = result[start : start + size]
            acc[2 * group] += fold(piece)
            acc[2 * group + 1] += fold(piece * piece)
        net.give(s, "hid", "zd", "sub")

    net.need(0, "wd")
    loop(1, slab)
    net.open()
    loop(4, lambda s: slab(s + 1))
    net.turn(1)
    loop(geo.slabs - 5, lambda s: slab(s + 5))
    net.turn(2)
    finish(net.own, acc, 4)
    net.begin()
    acc_s[...] = jnp.zeros(acc_s.shape, F32)
    wide, step = short.shape[0], 256
    net.need(0, "ws")

    def pick(c):
        return short[c : c + step, :]

    small_product(geo, sub, pick, step, conv_s, acc_s, 0, wide // 4)
    net.step()
    small_product(geo, sub, pick, step, conv_s, acc_s, wide // 4, 5 * wide // 8)
    net.step()
    small_product(geo, sub, pick, step, conv_s, acc_s, 5 * wide // 8, wide)
    finish(stats_s, acc_s, 4)
    net.end()


def small_product(geo, left, pick, step, conv, acc, first, last):
    for c in range(first, last, step):
        result = nt(left[...], pick(c))
        conv[:, c : c + step] = result.astype(BF16)
        for s in range(geo.slabs):
            for start, size, group in geo.small_pieces():
                piece = result[s * geo.small + start : s * geo.small + start + size]
                acc[2 * group, :, c : c + step] += fold(piece)
                acc[2 * group + 1, :, c : c + step] += fold(piece * piece)


def gather_taps(geo, net, live, zd, terms, full, taps):
    width = zd.shape[1]
    blank = jnp.zeros((8, width), F32)
    full[:, 0:CELLS, :] = jnp.zeros((width // 128, CELLS, 128), F32)
    full[:, CELLS + geo.rg : 2 * CELLS + geo.rg, :] = jnp.zeros((width // 128, CELLS, 128), F32)

    def slab(s):
        net.need(s, "zd")
        keep = alive(live, s)
        for start, size, group in geo.pieces(width):
            rows = pl.ds(pl.multiple_of(s * geo.rows + start, CELLS), size)
            scale, shift = terms[group]
            value = silu(zd[rows, :].astype(F32) * scale + shift)
            begin = CELLS + start + group * CELLS
            put(full, pl.ds(begin, size), value * (geo.mask(size, group, width) * keep))
        for dy in range(3):
            for dx in range(3):
                picked = []
                for group in range(2):
                    for i in range(geo.ol if group else geo.og):
                        line = 2 * i + dy - 1
                        if line < 0:
                            picked.append(blank)
                            continue
                        begin = CELLS + group * (geo.rg + CELLS) + line * CELLS + dx - 1
                        picked.append(take(full, pl.ds(begin, 8, stride=2)))
                tap = dy * 3 + dx
                taps[at(s, geo.small), tap * width : (tap + 1) * width] = jnp.concatenate(
                    picked, axis=0
                ).astype(BF16)
        net.give(s, "taps")

    loop(1, slab)
    net.open()
    net.side.begin()
    loop(4, lambda s: slab(s + 1))
    net.side.step()
    loop(geo.slabs - 5, lambda s: slab(s + 5))


def stage_e(
    geo, net, live, count, zd, stats_d, norm, weight_0, weight_1, weight_2, conv, taps, full,
    acc,
):
    acc[...] = jnp.zeros(acc.shape, F32)
    terms = forward_terms(geo, count, stats_d, norm, zd.shape[1])
    gather_taps(geo, net, live, zd, terms, full, taps)
    net.turn(1)
    net.side.step()
    net.need(0, "we_0", "we_1", "we_2")
    step = 256
    third = weight_0.shape[1]
    for c in range(0, weight_0.shape[0], step):
        result = nt(taps[:, 0:third], weight_0[c : c + step, :])
        result = result + nt(taps[:, third : 2 * third], weight_1[c : c + step, :])
        result = result + nt(taps[:, 2 * third :], weight_2[c : c + step, :])
        conv[:, c : c + step] = result.astype(BF16)
        for s in range(geo.slabs):
            keep = alive(live, s)
            for start, size, group in geo.small_pieces():
                piece = result[s * geo.small + start : s * geo.small + start + size]
                piece = piece * (geo.small_mask(group, step) * keep)
                acc[2 * group, :, c : c + step] += fold(piece)
                acc[2 * group + 1, :, c : c + step] += fold(piece * piece)
    net.side.end()
    net.turn(2)
    finish(net.own, acc, 4)
    net.run()


def stage_f(geo, net, live, count, ze, stats_e, norm, weight, act, conv, acc):
    acc[...] = jnp.zeros(acc.shape, F32)
    width = ze.shape[1]
    terms = forward_terms(geo, count, stats_e, norm, width, True)

    def slab(s):
        keep = alive(live, s)
        rows = ze[at(s, geo.small), :].astype(F32)
        parts = []
        for start, size, group in geo.small_pieces():
            scale, shift = terms[group]
            value = silu(rows[start : start + size] * scale + shift)
            parts.append(value * (geo.small_mask(group, width) * keep))
        act[at(s, geo.small), :] = jnp.concatenate(parts, axis=0).astype(BF16)

    loop(geo.slabs, slab)
    half, step = weight.shape[0] // 2, 256
    net.need(0, "wf")

    def pick(c):
        return weight[c : c + step, :]

    small_product(geo, act, pick, step, conv, acc, 0, half)
    net.open()
    small_product(geo, act, pick, step, conv, acc, half, 2 * half)
    finish(net.own, acc, 4)
    net.run()


def stage_out(
    geo, net, live, count, zf, zs, stats_f, stats_s, norm_f, norm_s, cotg, cotl, outg, outl, grad,
    pooled_sums, pool, cot, acc,
):
    acc[...] = jnp.zeros(acc.shape, F32)
    cot[...] = jnp.zeros(cot.shape, F32)
    pool[...] = jnp.zeros(pool.shape, F32)
    width = zf.shape[1]
    step = 512
    terms_f = forward_terms(geo, count, stats_f, norm_f, width, True)
    terms_s = forward_terms(geo, count, stats_s, norm_s, width, True)

    def slab(s):
        net.need(s, "zf", "zs", "cotg", "cotl")
        keep = alive(live, s)
        for c in range(0, width, step):
            cols = slice(c, c + step)
            for i in range(geo.og):
                cot[i * 8 : i * 8 + geo.og, :] = cotg[s, i, :, cols].astype(F32)
            for i in range(geo.ol):
                for side in range(2):
                    begin = geo.sg + i * 8 + side * 4
                    cot[begin : begin + geo.ol, :] = cotl[2 * s + side, i, :, cols].astype(F32)
            rows_f = zf[at(s, geo.small), cols].astype(F32)
            rows_s = zs[at(s, geo.small), cols].astype(F32)
            grads = []
            for start, size, group in geo.small_pieces():
                part = slice(start, start + size)
                vf, vs = rows_f[part], rows_s[part]
                scale_f, shift_f = (item[:, cols] for item in terms_f[group])
                scale_s, shift_s = (item[:, cols] for item in terms_s[group])
                joined = vf * scale_f + vs * scale_s + (shift_f + shift_s)
                mask = geo.small_mask(group, step) * keep
                gate = sig(joined)
                held = joined * gate
                value = held * mask
                low = value.astype(BF16)
                dy = cot[part, :] * ((gate + held - held * gate) * mask)
                grads.append(dy)
                acc[3 * group, :, cols] += fold(dy)
                acc[3 * group + 1, :, cols] += fold(dy * vf)
                acc[3 * group + 2, :, cols] += fold(dy * vs)
                summed = fold(value)
                if group == 0:
                    for i in range(geo.og):
                        outg[s, i, :, cols] = value[i * 8 : i * 8 + geo.og].astype(BF16)
                    pool[s, 0:1, cols] = jnp.sum(summed, axis=0, keepdims=True) * (
                        1.0 / (geo.og * geo.og)
                    )
                else:
                    row = lax.broadcasted_iota(jnp.int32, (8, step), 0)
                    for side in range(2):
                        own = jnp.where((row >= 4) == (side == 1), summed, 0.0)
                        pool[s, 1 + side : 2 + side, cols] = jnp.sum(
                            own, axis=0, keepdims=True
                        ) * (1.0 / (geo.ol * geo.ol))
                        for i in range(geo.ol):
                            begin = i * 8 + side * 4
                            outl[2 * s + side, i, :, cols] = value[begin : begin + geo.ol].astype(
                                BF16
                            )
            grad[at(s, geo.small), cols] = jnp.concatenate(grads, axis=0).astype(BF16)
        net.give(s, "outg", "outl", "grad")
        pooled = pool[s]
        square = jnp.mean(pooled * pooled, axis=1, keepdims=True)
        normed = pooled * lax.rsqrt(square + 1e-06)
        acc[6] += normed
        acc[7] += normed * normed

    loop(geo.slabs, slab)
    finish(net.own, acc, 6)
    net.begin()
    finish(pooled_sums, acc, 2, 6)
    net.end()


def small_back(geo, live, s, grad, conv, terms, width, cols):
    keep = alive(live, s)
    rows_g = grad[at(s, geo.small), cols].astype(F32)
    rows_z = conv[at(s, geo.small), cols].astype(F32)
    parts = []
    for start, size, group in geo.small_pieces():
        scale, by_value, constant = (item[:, cols] for item in terms[group])
        part = slice(start, start + size)
        value = rows_g[part] * scale + rows_z[part] * by_value + constant
        parts.append(value * (geo.small_mask(group, width) * keep))
    return jnp.concatenate(parts, axis=0).astype(BF16)


def stage_f_back(
    geo, net, live, count, zf, zs, stats_f, stats_s, norm_f, norm_s, grad, sums, act, sub, weight,
    short, ze, stats_e, norm_e, wgrad_f, wgrad_s, back_sub, back_e, ngrad_f, ngrad_s, dzf, dzs, acc,
):
    acc[...] = jnp.zeros(acc.shape, F32)
    width = zf.shape[1]
    step = 512
    rows_f, rows_s = ((0, 1), (3, 4)), ((0, 2), (3, 5))
    terms_f = backward_terms(geo, count, stats_f, norm_f, sums, ngrad_f, width, True, rows_f)
    terms_s = backward_terms(geo, count, stats_s, norm_s, sums, ngrad_s, width, True, rows_s)

    def slab(s):
        net.need(s, "zf", "zs", "grad")
        for c in range(0, width, step):
            cols = slice(c, c + step)
            dzf[at(s, geo.small), cols] = small_back(geo, live, s, grad, zf, terms_f, step, cols)
            dzs[at(s, geo.small), cols] = small_back(geo, live, s, grad, zs, terms_s, step, cols)

    loop(geo.slabs, slab)
    net.open()
    net.side.begin()
    net.need(0, "wf")
    block = 256
    terms_e = forward_terms(geo, count, stats_e, norm_e, ze.shape[1], True)
    for c in range(0, act.shape[1], block):
        cols = slice(c, c + block)
        result = nn(dzf[...], weight[:, cols])
        for s in range(geo.slabs):
            keep = alive(live, s)
            rows = ze[s * geo.small : (s + 1) * geo.small, cols].astype(F32)
            parts = []
            for start, size, group in geo.small_pieces():
                scale, shift = (item[:, cols] for item in terms_e[group])
                value = rows[start : start + size]
                mask = geo.small_mask(group, block) * keep
                piece = result[s * geo.small + start : s * geo.small + start + size]
                piece = piece * (slope(value * scale + shift) * mask)
                parts.append(piece)
                acc[2 * group, :, cols] += fold(piece)
                acc[2 * group + 1, :, cols] += fold(piece * value)
            back_e[s * geo.small : (s + 1) * geo.small, cols] = jnp.concatenate(
                parts, axis=0
            ).astype(BF16)
    finish(net.own, acc, 4)
    net.begin()
    net.need(0, "sub", "act", "ws")
    for c in range(0, width, block):
        cols = slice(c, c + block)
        put_pieces(wgrad_s, c, tn(dzs[:, cols], sub[...]))
        if c == width // 4:
            net.step()
    net.step()
    net.turn(1)
    for c in range(0, width, block):
        cols = slice(c, c + block)
        put_pieces(wgrad_f, c, tn(dzf[:, cols], act[...]))
        if c == width // 4:
            net.side.step()
    net.side.step()
    net.turn(2)
    for c in range(0, sub.shape[1], block):
        cols = slice(c, c + block)
        back_sub[:, cols] = nn(dzs[...], short[:, cols]).astype(BF16)
    net.side.end()
    net.end()


def stage_e_back(
    geo, net, live, count, ze, stats_e, norm_e, back_e, sums_e, zd, stats_d, norm_d, weight_0, weight_1,
    weight_2, taps, wgrad, back_d, ngrad, full, dze, moved, parity, acc,
):
    acc[...] = jnp.zeros(acc.shape, F32)
    width = ze.shape[1]
    terms_e = backward_terms(geo, count, stats_e, norm_e, sums_e, ngrad, width, True)
    terms_d = forward_terms(geo, count, stats_d, norm_d, width)

    def shift(s):
        value = small_back(geo, live, s, back_e, ze, terms_e, width, slice(0, width)).astype(F32)
        blank = jnp.zeros((8, width), F32)
        down = jnp.concatenate(
            [value[8 : geo.sg], blank, value[geo.sg + 8 :], blank], axis=0
        )
        size = geo.small
        dze[at(s, size), :] = value.astype(BF16)
        moved[0, at(s, size), :] = pltpu.roll(value, size - 1, 0).astype(BF16)
        moved[1, at(s, size), :] = down.astype(BF16)
        moved[2, at(s, size), :] = pltpu.roll(down, size - 1, 0).astype(BF16)

    loop(2, shift)
    net.open()
    loop(geo.slabs - 2, lambda s: shift(s + 2))

    net.need(0, "we_0", "we_1", "we_2")

    def tap(dy, dx):
        return (weight_0, weight_1, weight_2)[dy][:, dx * width : (dx + 1) * width]

    def grads(first, last):
        for t in range(first, last):
            result = tn(dze[...], taps[:, t * width : (t + 1) * width])
            put_pieces(wgrad, 0, result, t * width)

    parity[0] = nn(dze[...], tap(1, 1))
    parity[1] = nn(dze[...], tap(1, 2)) + nn(moved[0], tap(1, 0))
    parity[2] = nn(dze[...], tap(2, 1)) + nn(moved[1], tap(0, 1))
    parity[3] = (
        nn(dze[...], tap(2, 2))
        + nn(moved[0], tap(2, 0))
        + nn(moved[1], tap(0, 2))
        + nn(moved[2], tap(0, 0))
    )

    def slab(s):
        net.need(s, "zd")
        keep = alive(live, s)
        for group in range(2):
            for i in range(geo.ol if group else geo.og):
                for a in range(2):
                    for b in range(2):
                        begin = group * geo.rg + (2 * i + a) * CELLS + b
                        source = s * geo.small + group * geo.sg + i * 8
                        part = parity[2 * a + b, pl.ds(pl.multiple_of(source, 8), 8), :]
                        put(full, pl.ds(begin, 8, stride=2), part)
        for start, size, group in geo.pieces(width):
            rows = pl.ds(pl.multiple_of(s * geo.rows + start, CELLS), size)
            scale, shift_d = terms_d[group]
            value = zd[rows, :].astype(F32)
            mask = geo.mask(size, group, width) * keep
            piece = take(full, pl.ds(start, size)) * (slope(value * scale + shift_d) * mask)
            back_d[rows, :] = piece.astype(BF16)
            acc[2 * group] += fold(piece)
            acc[2 * group + 1] += fold(piece * value)
        net.give(s, "back_d")

    loop(geo.slabs, slab)
    finish(net.own, acc, 4)
    net.begin()
    net.need(0, "taps")
    grads(0, 3)
    net.step()
    grads(3, 6)
    net.step()
    grads(6, 9)
    net.end()


def wide_back(geo, live, s, grad, conv, terms, low):
    width = conv.shape[1]
    keep = alive(live, s)
    for start, size, group in geo.pieces(width):
        rows = pl.ds(pl.multiple_of(s * geo.rows + start, CELLS), size)
        scale, by_value, constant = terms[group]
        value = grad[rows, :].astype(F32) * scale + conv[rows, :].astype(F32) * by_value + constant
        low[rows, :] = (value * (geo.mask(size, group, width) * keep)).astype(BF16)


def stage_d_back(
    geo, net, live, count, zd, stats_d, norm_d, back_d, sums_d, hid, packed, zc, stats_c, norm_c,
    back_sub, weight, wgrad, joined, ngrad, dzd, full, acc,
):
    acc[...] = jnp.zeros(acc.shape, F32)
    width = zc.shape[1]
    terms_d = backward_terms(geo, count, stats_d, norm_d, sums_d, ngrad, zd.shape[1])
    terms_c = forward_terms(geo, count, stats_c, norm_c, width)

    def slab(s):
        net.need(s, "back_d", "zd", "zc", "packed")
        wide_back(geo, live, s, back_d, zd, terms_d, dzd)
        put(full, pl.ds(0, geo.rows), nn(dzd[at(s, geo.rows), :], weight[...]))
        extra = back_sub[at(s, geo.small), :].astype(F32)
        for k, start in enumerate(even_rows(geo)):
            place = pl.ds(start, 8, stride=2)
            put(full, place, take(full, place) + extra[k * 8 : k * 8 + 8])
        keep = alive(live, s)
        for start, size, group in geo.pieces(width):
            rows = pl.ds(pl.multiple_of(s * geo.rows + start, CELLS), size)
            scale, shift = terms_c[group]
            value = zc[rows, :].astype(F32)
            pre = value * scale + shift + packed[rows, :].astype(F32)
            mask = geo.mask(size, group, width) * keep
            piece = take(full, pl.ds(start, size)) * (slope(pre) * mask)
            joined[rows, :] = piece.astype(BF16)
            acc[2 * group] += fold(piece)
            acc[2 * group + 1] += fold(piece * value)
        net.give(s, "joined")

    loop(1, slab)
    net.open()
    loop(4, lambda s: slab(s + 1))
    net.turn(1)
    loop(geo.slabs - 5, lambda s: slab(s + 5))
    net.turn(2)
    finish(net.own, acc, 4)
    block = 256
    net.begin()
    net.need(0, "hid")
    for c in range(0, dzd.shape[1], block):
        put_pieces(wgrad, c, tn(dzd[:, c : c + block], hid[...]))
        net.step()
    net.end()


def stage_c_back(
    geo, net, live, count, zc, stats_c, norm_c, joined, sums_c, zb, stats_b, norm_b, weight, wgrad,
    back_b, ngrad, dzc, act, acc,
):
    acc[...] = jnp.zeros(acc.shape, F32)
    terms_c = backward_terms(geo, count, stats_c, norm_c, sums_c, ngrad, zc.shape[1])
    terms_b = forward_terms(geo, count, stats_b, norm_b, zb.shape[1])
    width = zb.shape[1]

    def slab(s):
        net.need(s, "joined", "zc", "zb")
        wide_back(geo, live, s, joined, zc, terms_c, dzc)
        result = nn(dzc[at(s, geo.rows), :], weight[...])
        keep = alive(live, s)
        for start, size, group in geo.pieces(width):
            rows = pl.ds(pl.multiple_of(s * geo.rows + start, CELLS), size)
            scale, shift = terms_b[group]
            value = zb[rows, :].astype(F32)
            pre = value * scale + shift
            mask = geo.mask(size, group, width) * keep
            gate = sig(pre)
            held = pre * gate
            act[rows, :] = (held * mask).astype(BF16)
            piece = result[start : start + size] * ((gate + held - held * gate) * mask)
            back_b[rows, :] = piece.astype(BF16)
            acc[2 * group] += fold(piece)
            acc[2 * group + 1] += fold(piece * value)
        net.give(s, "back_b")

    loop(1, slab)
    net.open()
    loop(geo.slabs - 1, lambda s: slab(s + 1))
    net.turn(2)
    finish(net.own, acc, 4)
    net.begin()
    block = 256
    for c in range(0, dzc.shape[1], block):
        put_pieces(wgrad, c, tn(dzc[:, c : c + block], act[...]))
        if c < 2 * block:
            net.step()
    net.end()


def stage_b_back(
    geo, net, live, count, zb, stats_b, norm_b, back_b, sums_b, za, stats_a, norm_a, weight, taps,
    wgrad, back_a, ngrad, dtaps, stacked, total, acc,
):
    acc[...] = jnp.zeros(acc.shape, F32)
    width = za.shape[1]
    terms_b = backward_terms(geo, count, stats_b, norm_b, sums_b, ngrad, width)
    terms_a = forward_terms(geo, count, stats_a, norm_a, width)
    clear_halo(geo, dtaps)
    for t in range(9):
        stacked[t * width : (t + 1) * width, :] = weight[:, t * width : (t + 1) * width]

    def fill(s):
        keep = alive(live, s)
        values = []
        for start, size, group in geo.pieces(width):
            rows = pl.ds(pl.multiple_of(s * geo.rows + start, CELLS), size)
            scale, by_value, constant = terms_b[group]
            value = back_b[rows, :].astype(F32) * scale + zb[rows, :].astype(F32) * by_value
            values.append((value + constant) * (geo.mask(size, group, width) * keep))
        spread_taps(geo, dtaps, s, values, True)

    loop(2, fill)
    net.open()
    loop(geo.slabs - 2, lambda s: fill(s + 2))
    net.turn(1)
    span = geo.halo - 2 * CELLS
    total[...] = jnp.zeros(total.shape, F32)

    def slab(s):
        result = None
        for dy in range(3):
            begin = pl.multiple_of(s * geo.halo + (2 - dy) * CELLS, CELLS)
            term = nn(
                dtaps[pl.ds(begin, span), :], stacked[dy * 3 * width : (dy + 1) * 3 * width, :]
            )
            result = term if result is None else result + term
        keep = alive(live, s)
        for group, (begin, size) in enumerate(((0, geo.rg), (geo.rg + CELLS, geo.rl))):
            rows = pl.ds(pl.multiple_of(s * geo.rows + group * geo.rg, CELLS), size)
            scale, shift = terms_a[group]
            value = za[rows, :].astype(F32)
            mask = geo.mask(size, group, width) * keep
            piece = result[begin : begin + size] * (slope(value * scale + shift) * mask)
            back_a[rows, :] = piece.astype(BF16)
            acc[2 * group] += fold(piece)
            acc[2 * group + 1] += fold(piece * value)

    def grads(s):
        net.need(s, "taps")
        own = dtaps[
            pl.ds(pl.multiple_of(s * geo.halo + CELLS, CELLS), span), width : 2 * width
        ]
        for dy in range(3):
            begin = pl.multiple_of(s * geo.halo + dy * CELLS, CELLS)
            total[:, dy * 3 * width : (dy + 1) * 3 * width] += tn(own, taps[pl.ds(begin, span), :])

    loop(geo.slabs, slab)
    net.turn(2)
    finish(net.own, acc, 4)
    part = geo.slabs // 3
    net.begin()
    loop(part, grads)
    net.step()
    loop(part, lambda s: grads(s + part))
    net.step()
    loop(geo.slabs - 2 * part, lambda s: grads(s + 2 * part))
    put_pieces(wgrad, 0, total[...])
    net.end()


def stage_a_back(
    geo, net, live, count, za, stats_a, norm_a, back_a, sums_a, packed, joined, weight, wgrad, grad,
    ngrad, dza,
):
    terms_a = backward_terms(geo, count, stats_a, norm_a, sums_a, ngrad, za.shape[1])
    loop(2, lambda s: wide_back(geo, live, s, back_a, za, terms_a, dza))
    net.open()
    loop(geo.slabs - 2, lambda s: wide_back(geo, live, s + 2, back_a, za, terms_a, dza))
    net.need(0, "packed")
    put_pieces(wgrad, 0, tn(dza[...], packed[...]))
    net.turn(1)

    net.need(0, "joined")

    def slab(s):
        result = nn(dza[at(s, geo.rows), :], weight[...])
        rows = at(s, geo.rows)
        grad[rows, :] = (result + joined[rows, :].astype(F32)).astype(BF16)
        net.give(s, "grad")

    part = geo.slabs // 3
    for number in range(3):
        begin = number * part
        size = part if number < 2 else geo.slabs - begin
        loop(size, lambda s: slab(s + begin))
        net.turn(number + 2)
    net.turn(5)
    net.close()


def last_kernel(geo, upright, grad, hid, *refs):
    count = len(upright)
    rows_in, refs = refs[:count], refs[count:]
    dxg, dxl, outg, outl = refs[:4]
    targets = refs[4:]
    result = grad[...].astype(F32)
    half = CELLS // 2
    for i in range(geo.hg):
        dxg[0, i] = result[i * CELLS : i * CELLS + geo.hg]
        outg[0, i] = hid[i * CELLS : (i + 1) * CELLS, :][0 : geo.hg]
    for i in range(geo.hl):
        begin = geo.rg + i * CELLS
        low = hid[begin : begin + CELLS, :]
        for side in range(2):
            part = begin + side * half
            dxl[side, i] = result[part : part + geo.hl]
            outl[side, i] = low[side * half : side * half + geo.hl]

    def write(k):
        @pl.when(pl.program_id(0) == k % geo.slabs)
        def one():
            source, target = rows_in[k], targets[k]
            rows = source.shape[0] * source.shape[1]
            whole = source[...].astype(F32).reshape(rows, source.shape[2])
            target[...] = whole.T if upright[k] else whole

    for k in range(count):
        write(k)


def run_last(geo, grad, hid, parts, global_shape, local_shape):
    def whole(shape):
        return pl.BlockSpec(shape, lambda s: (0,) * len(shape))

    upright = [part.shape[0] * part.shape[1] >= 128 for part in parts]
    shapes = []
    for turn, part in zip(upright, parts):
        rows = part.shape[0] * part.shape[1]
        shapes.append((part.shape[2], rows) if turn else (rows, part.shape[2]))
    views = [
        pl.BlockSpec((1,) + global_shape[1:], lambda s: (s, 0, 0, 0)),
        pl.BlockSpec((2,) + local_shape[1:], lambda s: (s, 0, 0, 0)),
    ]
    outs = pl.pallas_call(
        functools.partial(last_kernel, geo, upright),
        grid=(geo.slabs,),
        out_shape=[
            jax.ShapeDtypeStruct(shape, dtype)
            for dtype in (F32, BF16)
            for shape in (global_shape, local_shape)
        ]
        + [jax.ShapeDtypeStruct(shape, F32) for shape in shapes],
        in_specs=[
            pl.BlockSpec((geo.rows, item.shape[1]), lambda s: (s, 0)) for item in (grad, hid)
        ]
        + [whole(part.shape) for part in parts],
        out_specs=views + views + [whole(shape) for shape in shapes],
        compiler_params=pltpu.CompilerParams(vmem_limit_bytes=VMEM_CAP),
        name="last",
    )(grad, hid, *parts)
    return outs[:4], [item if turn else item.T for turn, item in zip(upright, outs[4:])]


class Group:
    def __init__(self, kind, reps, shards):
        rep, shard = lax.axis_index("rep"), lax.axis_index("fsdp")
        chip, core = shard // 2, lax.rem(shard, 2)
        wide = reps // 2
        low, high = lax.rem(rep, 2), rep // wide
        first = core == 0
        if kind == CORES:
            self.size, self.me = 2, core
            self.address = lambda k: {"fsdp": chip * 2 + k}
        elif kind == CHIPS:
            self.size, self.me = shards // 2, chip
            self.address = lambda k: {"fsdp": k * 2 + core}
        elif kind == SHARDS:
            self.size, self.me = shards, shard
            self.address = lambda k: {"fsdp": k}
        elif kind == REPLICAS:
            self.size, self.me = reps, rep
            self.address = lambda k: {"rep": k}
        elif kind == CLOSE:
            self.size, self.me = 2, jnp.where(first, low, high)
            self.address = lambda k: {
                "rep": jnp.where(first, rep - low + k, rep - high * wide + k * wide)
            }
        elif kind == SLANTED:
            self.size = wide * (shards // 2)
            self.me = jnp.where(first, rep // 2, lax.rem(rep, wide)) * (shards // 2) + chip

            def across(k):
                far = k // (shards // 2)
                return {
                    "rep": jnp.where(first, far * 2 + low, high * wide + far),
                    "fsdp": lax.rem(k, shards // 2) * 2 + core,
                }

            self.address = across
        else:
            self.size = wide
            self.me = jnp.where(first, rep // 2, lax.rem(rep, wide))
            self.address = lambda k: {"rep": jnp.where(first, k * 2 + low, high * wide + k)}

    def other(self, hop):
        return lax.rem(self.me + hop, self.size)


class Sums:
    def __init__(self, reps, shards, own, out, buffers, sems):
        self.own, self.out, self.buffers, self.sems = own, out, buffers, sems
        self.groups = [Group(kind, reps, shards) for kind in (CORES, CHIPS, REPLICAS)]
        self.phase = 0
        self.copies = []

    def send(self, source):
        group, buffer = self.groups[self.phase], self.buffers[self.phase]
        self.copies = []
        for hop in range(1, group.size):
            copy = pltpu.make_async_remote_copy(
                source, buffer.at[group.me], self.sems[2 * self.phase].at[hop],
                self.sems[2 * self.phase + 1].at[hop], device_id=group.address(group.other(hop)),
                device_id_type=MESH,
            )
            copy.start()
            self.copies.append(copy)

    def begin(self):
        self.send(self.own)
        self.buffers[0][self.groups[0].me] = self.own[...]

    def total(self):
        for copy in self.copies:
            copy.wait()
        buffer = self.buffers[self.phase]
        total = buffer[0]
        for k in range(1, self.groups[self.phase].size):
            total = total + buffer[k]
        return total

    def step(self):
        total = self.total()
        self.phase += 1
        group, buffer = self.groups[self.phase], self.buffers[self.phase]
        buffer[group.me] = total
        self.send(buffer.at[group.me])

    def end(self):
        while self.phase < 2:
            self.step()
        self.out[...] = self.total()


class In:
    def __init__(self, name, array, rows=None):
        self.name, self.array, self.rows = name, array, rows


class Out:
    def __init__(self, name, shape, dtype, rows):
        self.name, self.shape, self.dtype, self.rows = name, shape, dtype, rows


class Stream:
    def __init__(self, source, target, sems, rows, slabs):
        self.source, self.target, self.sems, self.rows, self.slabs = source, target, sems, rows, slabs

    def copy(self, s):
        if self.rows is None:
            return pltpu.make_async_copy(self.source, self.target, self.sems.at[0])
        place = at(s, self.rows)
        return pltpu.make_async_copy(self.source.at[place], self.target.at[place], self.sems.at[s])


class Net:
    def __init__(self, reps, shards, sums=None, side=None, jobs=(), plans=(), ins=(), outs=()):
        self.ins, self.outs = dict(ins), dict(outs)
        self.reps, self.shards = reps, shards
        self.sums, self.side, self.jobs, self.plans = sums, side, jobs, plans
        self.own = None if sums is None else sums.own
        self.opened = False
        self.started, self.finished = set(), set()

    def enter(self):
        rep, shard = lax.axis_index("rep"), lax.axis_index("fsdp")
        barrier = pltpu.get_barrier_semaphore()
        for hop in range(1, self.shards):
            other = {"fsdp": lax.rem(shard + hop, self.shards)}
            pl.semaphore_signal(barrier, inc=1, device_id=other, device_id_type=MESH)
        for hop in range(1, self.reps):
            other = {"rep": lax.rem(rep + hop, self.reps)}
            pl.semaphore_signal(barrier, inc=1, device_id=other, device_id_type=MESH)
        self.greeted = self.shards + self.reps - 2
        if any(job.kind == CROSS for job in self.jobs):
            group = Group(SLANTED, self.reps, self.shards)
            chips = self.shards // 2
            for far in range(1, self.reps // 2):
                for step in range(1, chips):
                    other = lax.rem(group.me // chips + far, self.reps // 2) * chips
                    other = group.address(other + lax.rem(group.me + step, chips))
                    pl.semaphore_signal(barrier, inc=1, device_id=other, device_id_type=MESH)
                    self.greeted += 1

    def load(self):
        blocks = [stream for stream in self.ins.values() if stream.rows is not None]
        if blocks:

            def start(s):
                for stream in blocks:
                    stream.copy(s).start()

            loop(blocks[0].slabs, start)
        for stream in self.ins.values():
            if stream.rows is None:
                stream.copy(0).start()

    def need(self, s, *names):
        for name in names:
            self.ins[name].copy(s).wait()

    def give(self, s, *names):
        for name in names:
            self.outs[name].copy(s).start()

    def open(self):
        if not self.opened:
            self.opened = True
            pl.semaphore_wait(pltpu.get_barrier_semaphore(), self.greeted)
            self.turn(0)

    def turn(self, number):
        for k, (start, end) in enumerate(self.plans):
            if end == number:
                self.finish(k)
        for k, (start, end) in enumerate(self.plans):
            if start == number:
                self.started.add(k)
                self.jobs[k].start()

    def finish(self, k):
        assert k in self.started and k not in self.finished
        self.finished.add(k)
        self.jobs[k].finish()

    def job_out(self, k):
        return self.jobs[k].out

    def begin(self):
        self.open()
        self.sums.begin()

    def step(self):
        self.sums.step()

    def end(self):
        self.sums.end()
        self.close()

    def run(self):
        self.begin()
        self.end()

    def close(self):
        for k in range(len(self.jobs)):
            if k not in self.finished:
                self.finish(k)
        blocks = list(self.outs.values())
        if blocks:

            def wait(s):
                for stream in blocks:
                    stream.copy(s).wait()

            loop(blocks[0].slabs, wait)


class Job:
    GROUPS = {
        PAIR: CORES, JOIN: CORES, LINE: CHIPS, SPREAD: CHIPS, ALL: SHARDS, SHARE: REPLICAS,
        HALF: CLOSE, NEAR: CLOSE, REST: APART, OTHERS: APART, CROSS: SLANTED,
    }

    def __init__(self, kind, reps, shards, sources, out, held, send, recv):
        self.kind, self.sources, self.out, self.held = kind, sources, out, held
        self.send, self.recv = send, recv
        self.reps, self.chips = reps, shards // 2
        self.rep, shard = lax.axis_index("rep"), lax.axis_index("fsdp")
        self.chip, self.core = shard // 2, lax.rem(shard, 2)
        self.group = Group(self.GROUPS[kind], reps, shards)

    def give(self, source, target, hop):
        k = len(self.copies)
        if hop == 0:
            copy = pltpu.make_async_copy(source, target, self.send.at[k])
        else:
            copy = pltpu.make_async_remote_copy(
                source, target, self.send.at[k], self.recv.at[k],
                device_id=self.group.address(self.group.other(hop)), device_id_type=MESH,
            )
        copy.start()
        self.copies.append(copy)

    def start(self):
        self.copies = []
        kind, out, source, group = self.kind, self.out, self.sources[0], self.group
        order = list(range(1, group.size)) + [0]
        wide = self.reps // 2
        first = self.core == 0
        if kind == SPREAD:
            for hop in order[:-1]:
                self.give(source.at[self.rep], out.at[self.rep, group.size - hop - 1], hop)
        elif kind == NEAR:
            self.give(out.at[self.rep], out.at[self.rep], 1)
        elif kind == OTHERS:
            low, high = lax.rem(self.rep, 2), self.rep // wide
            partner = jnp.where(
                first, self.rep + 1 - 2 * low, self.rep + (1 - 2 * high) * wide
            )
            for hop in order[:-1]:
                for place in (self.rep, partner):
                    self.give(out.at[place], out.at[place], hop)
        elif kind == JOIN:
            for hop in order:
                for step in range(1, self.chips):
                    chip = lax.rem(self.chip + step, self.chips)
                    self.give(source.at[:, step - 1], out.at[chip, self.core], hop)
                self.give(self.sources[1], out.at[self.chip, self.core], hop)
        elif kind == CROSS:
            for hop in order:
                other = group.other(hop)
                block = source.at[other // self.chips, lax.rem(other, self.chips)]
                self.give(block, self.held.at[group.me], hop)
        elif kind in (ALL, SHARE):
            for hop in order:
                self.give(source, out.at[group.me], hop)
        elif kind == HALF:
            low, high = lax.rem(self.rep, 2), self.rep // wide
            mine = jnp.where(first, low, high * wide)
            theirs = jnp.where(first, 1 - low, (1 - high) * wide)
            step = jnp.where(first, 2, 1)
            for k in range(wide):
                self.give(source.at[theirs + k * step], self.held.at[1, k], 1)
            for k in range(wide):
                self.give(source.at[mine + k * step], self.held.at[0, k], 0)
        else:
            for hop in order:
                self.give(source.at[group.other(hop)], self.held.at[group.me], hop)

    def finish(self):
        for copy in self.copies:
            copy.wait()
        held, out = self.held, self.out
        if held is None:
            return
        members = held.shape[0]
        blocks = held.shape[1:-2]

        def one(index):
            place = (index // blocks[-1], lax.rem(index, blocks[-1])) if len(blocks) == 2 else (
                (index,) if blocks else ()
            )
            total = held[(0,) + place].astype(F32)
            for k in range(1, members):
                total = total + held[(k,) + place].astype(F32)
            out[place[::-1] if self.kind == PAIR else place] = total.astype(BF16)

        if blocks:
            loop(blocks[0] * (blocks[1] if len(blocks) == 2 else 1), one)
        else:
            total = held[0].astype(F32)
            for k in range(1, members):
                total = total + held[k].astype(F32)
            out[...] = total.astype(BF16)


def job_shapes(kind, reps, shards, shape):
    chips = shards // 2
    if kind == SPREAD:
        return None, (reps, chips - 1) + shape[1:], chips
    if kind in (NEAR, OTHERS):
        return None, shape, reps
    if kind == CROSS:
        return (shape[0] * shape[1],) + shape[2:], shape[2:], shape[0] * shape[1]
    if kind == JOIN:
        return None, (chips, 2, reps) + shape[2:], 2 * chips
    if kind == ALL:
        return None, (shards,) + shape, shards
    if kind == PAIR:
        return shape, (shape[2], shape[1]) + shape[3:], 2
    if kind == SHARE:
        return None, (reps,) + shape, reps
    if kind == HALF:
        return (2, reps // 2) + shape[1:], (reps // 2,) + shape[1:], reps
    return shape, shape[1:], shape[0]


VMEM_CAP = 60 << 20
FAR = (SPREAD, NEAR, OTHERS)


def sums_scratch(reps, shards, shape, own):
    sizes = (2, shards // 2, reps)
    return (
        [pltpu.VMEM(shape, F32)] * own
        + [pltpu.VMEM((size,) + shape, F32) for size in sizes]
        + [pltpu.SemaphoreType.DMA((size,)) for size in sizes for unused in range(2)]
    )


def run(kernel, geo, reps, shards, number, live, operands, results, scratch, sums, jobs, side, far=()):
    own_results = len(results)
    extra = []
    spaces = []
    flowing = []
    internal = []
    plain_results = []
    for k, item in enumerate(results):
        if isinstance(item, Out):
            extra.append(pltpu.VMEM(item.shape, item.dtype))
            if item.rows:
                extra.append(pltpu.SemaphoreType.DMA((geo.slabs,)))
            flowing.append((k, item))
            plain_results.append((item.shape, item.dtype))
        else:
            plain_results.append(item)
        internal.append(isinstance(item, Out) and not item.rows)
        spaces.append(pltpu.HBM if isinstance(item, Out) else pltpu.VMEM)
    results = plain_results
    streamed = [(k, item) for k, item in enumerate(operands) if isinstance(item, In)]
    operands = [item.array if isinstance(item, In) else item for item in operands]
    for k, item in streamed:
        extra.append(pltpu.VMEM(item.array.shape, item.array.dtype))
        extra.append(pltpu.SemaphoreType.DMA((1 if item.rows is None else geo.slabs,)))
    arrays = []
    shapes = []
    targets = []
    kept = {}
    for kind, sources, start, end in jobs:
        source = sources[0]
        if isinstance(source, int):
            shape, dtype = shapes[source]
        elif isinstance(source, str):
            shape, dtype = results[int(source)]
        else:
            shape, dtype = source.shape, source.dtype
        held, out, copies = job_shapes(kind, reps, shards, shape)
        shapes.append((out, dtype))
        extra += [] if held is None else [pltpu.VMEM(held, BF16)]
        extra += [pltpu.SemaphoreType.DMA((copies,))] * 2
        if kind in (NEAR, OTHERS) and isinstance(source, int):
            targets.append(targets[source])
        else:
            if kind in (NEAR, OTHERS):
                kept[len(arrays)] = len(results)
            targets.append(len(results))
            results.append(shapes[-1])
            spaces.append(pltpu.HBM if kind in FAR else pltpu.VMEM)
        arrays += [item for item in sources if not isinstance(item, (int, str))]
    own_or_job = len(results)
    keep = [k for k in range(own_or_job) if not (k < own_results and internal[k])]
    own_or_job = len(results)
    operands = tuple(operands)
    near = len(operands)
    if side is not None:
        operands += (side,)
        results.append((side.shape, F32))
        spaces.append(pltpu.VMEM)
        extra += sums_scratch(reps, shards, side.shape, 0)
    if sums is not None:
        results.append((sums, F32))
        spaces.append(pltpu.VMEM)
        extra += sums_scratch(reps, shards, sums, 1)
    inputs = 1 + len(operands)
    remote = bool(jobs) or sums is not None
    keep += list(range(own_or_job, len(results)))
    far = tuple(far) + tuple(k for k, unused in streamed)

    def whole(*refs):
        sources_in = list(refs[inputs : inputs + len(arrays)])
        first_out = inputs + len(arrays)
        outs = [None] * len(results)
        for place, k in enumerate(keep):
            outs[k] = refs[first_out + place]
        more = list(refs[first_out + len(keep) :])
        own_refs = list(outs[:own_results])
        out_streams, in_streams = [], []
        for k, item in flowing:
            own_refs[k] = more.pop(0)
            if item.rows:
                stream = Stream(own_refs[k], outs[k], more.pop(0), item.rows, geo.slabs)
                out_streams.append((item.name, stream))
            else:
                outs[k] = own_refs[k]
        given = list(refs[: 1 + len(operands)])
        for k, item in streamed:
            given[1 + k] = more.pop(0)
            stream = Stream(refs[1 + k], given[1 + k], more.pop(0), item.rows, geo.slabs)
            in_streams.append((item.name, stream))
        made = []
        for k, (kind, sources, start, end) in enumerate(jobs):
            refs_of = []
            for item in sources:
                if isinstance(item, int):
                    refs_of.append(made[item].out)
                elif isinstance(item, str):
                    refs_of.append(outs[int(item)])
                else:
                    refs_of.append(sources_in.pop(0))
            held = more.pop(0) if job_shapes(kind, reps, shards, refs_of[0].shape)[0] else None
            made.append(
                Job(kind, reps, shards, refs_of, outs[targets[k]], held, more.pop(0), more.pop(0))
            )
        beside, main = None, None
        if side is not None:
            beside = Sums(reps, shards, refs[near + 1], outs[own_or_job], more[0:3], more[3:9])
            more = more[9:]
        if sums is not None:
            main = Sums(reps, shards, more[0], outs[-1], more[1:4], more[4:10])
            more = more[10:]
        net = None
        if remote:
            plans = [job[2:] for job in jobs]
            net = Net(reps, shards, main, beside, made, plans, in_streams, out_streams)
            net.enter()
            net.load()
        kernel(geo, net, *given[: near + 1], *own_refs, *more)

    params = {"collective_id": number, "has_side_effects": True} if remote else {}
    outputs = pl.pallas_call(
        whole,
        out_shape=[jax.ShapeDtypeStruct(*results[k]) for k in keep],
        in_specs=[pl.BlockSpec(memory_space=pltpu.SMEM)]
        + [pl.BlockSpec(memory_space=pltpu.HBM if k in far else pltpu.VMEM) for k in range(len(operands))]
        + [
            pl.BlockSpec(memory_space=pltpu.HBM if k in kept else pl.ANY) for k in range(len(arrays))
        ],
        out_specs=[pl.BlockSpec(memory_space=spaces[k]) for k in keep],
        scratch_shapes=extra
        + [item if not isinstance(item, tuple) else pltpu.VMEM(*item) for item in scratch],
        input_output_aliases={inputs + k: keep.index(out) for k, out in kept.items()},
        compiler_params=pltpu.CompilerParams(vmem_limit_bytes=VMEM_CAP, **params),
        name=kernel.__name__,
    )(live, *operands, *arrays)
    placed = [None] * len(results)
    for place, k in enumerate(keep):
        placed[k] = outputs[place]
    return placed


def own_norms(first, second):
    flat = jnp.concatenate([first.reshape(-1), second.reshape(-1)]).astype(F32)
    size = -(-flat.shape[0] // 1024) * 1024
    return jnp.pad(flat, (0, size - flat.shape[0])).reshape(8, -1)


def all_norms(gathered, first, second):
    shards = gathered.shape[0]
    flat = gathered.reshape(shards, -1)
    split, last = first.size, first.size + second.size

    def whole(part):
        return part.reshape(shards, 2, -1).transpose(1, 0, 2).reshape(2, -1)

    return whole(flat[:, :split]), whole(flat[:, split:last])


def body(reps, shards, *arguments):
    (
        global_views, local_views, live, first_reduce, first_spatial, first_expand, first_norms,
        second_reduce, second_spatial, second_expand, second_short, second_norms, global_cotan,
        local_cotan,
    ) = arguments
    geo = Geometry(global_views.shape[0], global_views.shape[1], local_views.shape[1])
    assert local_views.shape[0] == 2 * geo.slabs
    channels = global_views.shape[3]
    ha, hb, hc, hd, he = (
        item.T.reshape(reps, -1, item.shape[0])
        for item in (first_reduce, first_spatial, first_expand, second_reduce, second_spatial)
    )
    he_0, he_1, he_2 = (he[:, :, k * he.shape[2] // 3 : (k + 1) * he.shape[2] // 3] for k in range(3))
    mid_1, mid_2 = first_reduce.shape[1] * shards, second_reduce.shape[1] * shards
    wide = second_expand.shape[1] * shards

    def rows_of(gathered):
        return gathered.reshape(-1, gathered.shape[-1])

    big, small = geo.total, geo.small_total

    numbers = iter(range(100))

    def go(kernel, operands, results, scratch, width=None, members=4, jobs=(), side=None, far=()):
        parts = {4: 2, 6: 4, 8: 2}[members]
        sums = None if width is None else (members * parts, width // parts)
        return run(
            kernel, geo, reps, shards, next(numbers), live, operands, results, scratch, sums,
            jobs, side, far,
        )

    def pieces(rows, columns):
        return ((2, shards // 2, reps, rows // (shards * reps), columns), BF16)

    def acc(width, members=4):
        return ((members, 8, width), F32)

    def stat(width):
        return ((8, width), F32)

    def both(width):
        return ((2, width), F32)

    more = go(
        stage_a, (global_views, local_views, second_short, second_expand),
        [
            Out("packed", (big, channels), BF16, geo.rows), Out("za", (big, mid_1), BF16, geo.rows),
            ((reps, second_short.shape[1] // reps, channels), BF16),
            ((reps, second_expand.shape[1] // reps, mid_2), BF16),
        ],
        [
            acc(mid_1), ((CELLS, channels), F32), ((mid_1, channels), BF16), (global_views.shape, BF16),
            (local_views.shape, BF16), pltpu.SemaphoreType.DMA((2,)),
        ],
        mid_1, 8,
        jobs=(
            (SPREAD, (ha,), 0, 1), (NEAR, (0,), 1, 2), (OTHERS, (0,), 2, 3),
            (JOIN, (0, ha), 3, 4),
            (SPREAD, (hb,), 0, 2), (NEAR, (4,), 2, 3), (OTHERS, (4,), 3, 5),
            (JOIN, (4, hb), 5, None),
            (SPREAD, (hc,), 0, 3), (NEAR, (8,), 3, 5), (OTHERS, (8,), 5, None),
            (SPREAD, (hd,), 0, 3), (NEAR, (11,), 3, 5), (OTHERS, (11,), 5, None),
            (ALL, (own_norms(first_norms, second_norms),), 1, 5), (SPREAD, ("2",), 1, 5),
        ),
        far=(0, 1),
    )
    packed, za, hs, hf, unused, wa, unused, wb, far_c, far_d, norms, far_s, sa = more
    count = sa
    wa, wb = rows_of(wa), rows_of(wb)
    norms_1, norms_2 = all_norms(norms, first_norms, second_norms)
    na, nb, nc = norms_1[:, :mid_1], norms_1[:, mid_1 : 2 * mid_1], norms_1[:, 2 * mid_1 :]
    nd, ne = norms_2[:, :mid_2], norms_2[:, mid_2 : 2 * mid_2]
    nf, ns = norms_2[:, 2 * mid_2 : 2 * mid_2 + wide], norms_2[:, 2 * mid_2 + wide :]
    zb, taps_b, wc, wd, far_s, far_e0, far_e1, far_e2, sb = go(
        stage_b, (count, In("za", za, geo.rows), sa, na, In("wb", wb)),
        [
            Out("zb", (big, mid_1), BF16, geo.rows),
            Out("taps", (geo.halo_total, 3 * mid_1), BF16, geo.halo),
        ],
        [acc(mid_1)], mid_1,
        jobs=(
            (JOIN, (far_c, hc), 0, 2), (JOIN, (far_d, hd), 0, 2),
            (NEAR, (far_s,), 0, 1), (OTHERS, (2,), 1, 2),
            (SPREAD, (he_0,), 0, 2), (SPREAD, (he_1,), 0, 2), (SPREAD, (he_2,), 0, 2),
        ),
    )
    wc = rows_of(wc)
    zc, ws, far_e0, far_f, sc = go(
        stage_c, (count, In("zb", zb, geo.rows), sb, nb, wc),
        [Out("zc", (big, channels), BF16, geo.rows)],
        [((geo.rows, mid_1), BF16), acc(channels)], channels,
        jobs=(
            (JOIN, (far_s, hs), 0, 2), (NEAR, (far_e0,), 0, 1), (OTHERS, (1,), 1, 2),
            (SPREAD, (hf,), 0, 2),
        ),
    )
    wd, ws = rows_of(wd), rows_of(ws)
    hid, zd, sub, zs, local_s, we_0, far_e1, we_1, far_e2, we_2, far_f, sd = go(
        stage_d,
        (
            count, In("zc", zc, geo.rows), sc, nc, In("packed", packed, geo.rows), In("wd", wd),
            In("ws", ws),
        ),
        [
            Out("hid", (big, channels), BF16, geo.rows), Out("zd", (big, mid_2), BF16, geo.rows),
            Out("sub", (small, channels), BF16, geo.small),
            ((small, wide), BF16), stat(wide // 2),
        ],
        [((channels // 128, geo.rows, 128), F32), acc(mid_2), acc(wide)], mid_2,
        jobs=(
            (JOIN, (far_e0, he_0), 0, 1),
            (NEAR, (far_e1,), 0, 1), (OTHERS, (1,), 1, 2), (JOIN, (1, he_1), 2, None),
            (NEAR, (far_e2,), 0, 1), (OTHERS, (4,), 1, 2), (JOIN, (4, he_2), 2, None),
            (NEAR, (far_f,), 1, 2),
        ),
    )
    we = tuple(rows_of(item) for item in (we_0, we_1, we_2))
    late_we = tuple(In(name, item) for name, item in zip(("we_0", "we_1", "we_2"), we))
    ze, taps_e, unused, wf, ss, se = go(
        stage_e, (count, In("zd", zd, geo.rows), sd, nd, *late_we),
        [((small, mid_2), BF16), Out("taps", (small, 9 * mid_2), BF16, geo.small)],
        [((mid_2 // 128, geo.halo, 128), F32), acc(mid_2)], mid_2,
        jobs=((OTHERS, (far_f,), 0, 1), (JOIN, (0, hf), 1, 2)), side=local_s,
    )
    wf = rows_of(wf)
    act_e, zf, sf = go(
        stage_f, (count, ze, se, ne, In("wf", wf)),
        [((small, mid_2), BF16), ((small, wide), BF16)], [acc(wide)], wide,
    )
    second_g, second_l, grad, local_pool, so = go(
        stage_out,
        (
            count, In("zf", zf, geo.small), In("zs", zs, geo.small), sf, ss, nf, ns,
            In("cotg", global_cotan, 1), In("cotl", local_cotan, 2),
        ),
        [
            Out("outg", global_cotan.shape, BF16, 1), Out("outl", local_cotan.shape, BF16, 2),
            Out("grad", (small, wide), BF16, geo.small),
            stat(wide // 4),
        ],
        [((geo.slabs, 8, wide), F32), ((geo.small, 512), F32), acc(wide, 8)], wide, 6,
    )
    unused, unused, back_sub, back_e, ngrad_f, ngrad_s, pair_f, pair_s, pool, qe = go(
        stage_f_back,
        (
            count, In("zf", zf, geo.small), In("zs", zs, geo.small), sf, ss, nf, ns,
            In("grad", grad, geo.small), so, In("act", act_e), In("sub", sub), In("wf", wf),
            In("ws", ws), ze, se, ne,
        ),
        [
            Out("wgrad_f", *pieces(wide, mid_2), 0), Out("wgrad_s", *pieces(wide, channels), 0), ((small, channels), BF16), ((small, mid_2), BF16),
            both(wide), both(wide),
        ],
        [((small, wide), BF16), ((small, wide), BF16), acc(mid_2)], mid_2,
        jobs=((PAIR, ("0",), 2, None), (PAIR, ("1",), 1, None)), side=local_pool,
    )
    views = count[8, 0] * 6.0
    pool = pool.reshape(2, wide)
    center = pool[0] / views
    spread = pool[1] / views - center * center
    pooled_std = jnp.mean(jnp.sqrt(spread + 1e-06))
    wgrad_e, back_d, ngrad_e, half_f, half_s, qd = go(
        stage_e_back,
        (
            count, ze, se, ne, back_e, qe, In("zd", zd, geo.rows), sd, nd, *late_we,
            In("taps", taps_e),
        ),
        [
            pieces(mid_2, 9 * mid_2), Out("back_d", (big, mid_2), BF16, geo.rows), both(mid_2),
        ],
        [
            ((mid_2 // 128, geo.halo, 128), F32), ((small, mid_2), BF16), ((3, small, mid_2), BF16), ((4, small, mid_2), F32),
            acc(mid_2),
        ],
        mid_2, jobs=((HALF, (pair_f,), 0, None), (HALF, (pair_s,), 0, None)),
    )
    wgrad_d, joined, ngrad_d, unused, half_e, unused, rest_s, line_f, qc = go(
        stage_d_back,
        (
            count, In("zd", zd, geo.rows), sd, nd, In("back_d", back_d, geo.rows), qd,
            In("hid", hid), In("packed", packed, geo.rows), In("zc", zc, geo.rows), sc, nc, back_sub,
            wd,
        ),
        [
            pieces(mid_2, channels), Out("joined", (big, channels), BF16, geo.rows), both(mid_2),
        ],
        [((big, mid_2), BF16), ((channels // 128, geo.rows, 128), F32), acc(channels)], channels,
        jobs=(
            (PAIR, (wgrad_e,), 0, 1), (HALF, (0,), 1, None),
            (REST, (half_f,), 0, 1), (REST, (half_s,), 0, 1), (LINE, (2,), 1, None),
        ),
    )
    wgrad_c, back_b, ngrad_c, pair_d, rest_e, line_s, qb = go(
        stage_c_back,
        (
            count, In("zc", zc, geo.rows), sc, nc, In("joined", joined, geo.rows), qc,
            In("zb", zb, geo.rows), sb, nb, wc,
        ),
        [
            pieces(channels, mid_1), Out("back_b", (big, mid_1), BF16, geo.rows), both(channels),
        ],
        [((big, channels), BF16), ((big, mid_1), BF16), acc(mid_1)], mid_1,
        jobs=(
            (PAIR, (wgrad_d,), 0, 2), (REST, (half_e,), 0, 2), (LINE, (rest_s,), 0, 2),
        ),
    )
    wgrad_b, back_a, ngrad_b, unused, rest_d, unused, half_c, line_e, out_f, out_s, qa = go(
        stage_b_back,
        (count, zb, sb, nb, back_b, qb, za, sa, na, wb, In("taps", taps_b, geo.halo)),
        [pieces(mid_1, 9 * mid_1), ((big, mid_1), BF16), both(mid_1)],
        [
            ((geo.halo_total, 3 * mid_1), BF16), ((9 * mid_1, mid_1), BF16), (wb.shape, F32), acc(mid_1),
        ],
        mid_1,
        jobs=(
            (HALF, (pair_d,), 0, 1), (REST, (0,), 1, 2), (PAIR, (wgrad_c,), 0, 1),
            (HALF, (2,), 1, 2), (LINE, (rest_e,), 0, 2), (SHARE, (line_f,), 1, 2),
            (SHARE, (line_s,), 1, 2),
        ),
    )
    more = go(
        stage_a_back,
        (count, za, sa, na, back_a, qa, In("packed", packed), In("joined", joined), wa),
        [
            pieces(mid_1, channels), Out("grad", (big, channels), BF16, geo.rows), both(mid_1),
        ],
        [((big, mid_1), BF16)],
        jobs=(
            (PAIR, (wgrad_b,), 0, 1), (HALF, (0,), 1, 2), (CROSS, (1,), 2, 3), (SHARE, (2,), 3, None),
            (PAIR, ("0",), 1, 2), (HALF, (4,), 2, 3), (CROSS, (5,), 3, 4), (SHARE, (6,), 4, None),
            (REST, (half_c,), 0, 1), (LINE, (8,), 1, 2), (SHARE, (9,), 2, None),
            (LINE, (rest_d,), 0, 1), (SHARE, (11,), 1, None), (SHARE, (line_e,), 0, None),
        ),
    )
    grad, ngrad_a = more[1], more[2]
    out_b, out_a, out_c, out_d, out_e = (more[3 + k] for k in (3, 7, 10, 12, 13))
    (grad_g, grad_l, first_g, first_l), columns = run_last(
        geo, grad, hid, (out_a, out_b, out_c, out_d, out_e, out_f, out_s),
        global_views.shape, local_views.shape,
    )
    shard = lax.axis_index("fsdp")

    def own_columns(parts, width):
        whole = jnp.concatenate(parts, axis=1)
        return lax.dynamic_slice_in_dim(whole, shard * width, width, 1)

    return (
        first_g, first_l, second_g, second_l, grad_g, grad_l,
        *columns[0:3],
        own_columns((ngrad_a, ngrad_b, ngrad_c), first_norms.shape[1]),
        *columns[3:7],
        own_columns((ngrad_d, ngrad_e, ngrad_f, ngrad_s), second_norms.shape[1]),
        pooled_std,
    )


def solution(mesh):
    views = P(("rep", "fsdp"), None, None, None)
    columns = P(None, "fsdp")
    return jax.shard_map(
        functools.partial(body, mesh.shape["rep"], mesh.shape["fsdp"]),
        mesh=mesh,
        in_specs=(views, views, P(("rep", "fsdp"))) + (columns,) * 9 + (views, views),
        out_specs=(views,) * 6 + (columns,) * 9 + (P(),),
        check_vma=False,
    )
```

```python
import functools

import jax
import jax.numpy as jnp
from jax import lax
from jax.experimental import pallas as pl
from jax.experimental.pallas import tpu as pltpu
from jax.sharding import PartitionSpec as P

EPSILON = 1e-05
F32 = jnp.float32
BF16 = jnp.bfloat16
MESH = pl.DeviceIdType.MESH
CELLS = 16
PAIR, HALF, REST, LINE, SHARE, SPREAD, NEAR, OTHERS, JOIN, CROSS, ALL = range(11)
CORES, CHIPS, SHARDS, REPLICAS, CLOSE, APART, SLANTED = range(7)


def nt(left, right):
    return lax.dot_general(left, right, (((1,), (1,)), ((), ())), preferred_element_type=F32)


def nn(left, right):
    return lax.dot_general(left, right, (((1,), (0,)), ((), ())), preferred_element_type=F32)


def tn(left, right):
    return lax.dot_general(left, right, (((0,), (0,)), ((), ())), preferred_element_type=F32)


def sig(values):
    return 0.5 * jnp.tanh(0.5 * values) + 0.5


def silu(values):
    return values * sig(values)


def slope(values):
    gate = sig(values)
    held = values * gate
    return gate + held - held * gate


def lanes(tile, width):
    return jnp.concatenate([tile] * (width // tile.shape[1]), axis=1)


def fold(values):
    return jnp.sum(values.reshape(values.shape[0] // 8, 8, values.shape[1]), axis=0)


class Geometry:
    def __init__(self, views, side_global, side_local):
        self.slabs = views
        self.hg, self.hl = side_global, side_local
        assert side_global < CELLS and side_local < CELLS // 2
        self.rg, self.rl = side_global * CELLS, side_local * CELLS
        self.rows = self.rg + self.rl
        self.og, self.ol = (side_global - 1) // 2 + 1, (side_local - 1) // 2 + 1
        self.sg, self.sl = self.og * 8, self.ol * 8
        self.small = self.sg + self.sl
        self.total, self.small_total = self.slabs * self.rows, self.slabs * self.small
        self.halo = self.rows + 3 * CELLS
        self.halo_total = self.slabs * self.halo
        self.chunk = 32
        assert self.rg % self.chunk == 0 and self.rl % self.chunk == 0 and self.small % 16 == 0

    def pieces(self, width):
        if width <= 256:
            return [(0, self.rg, 0), (self.rg, self.rl, 1)]
        step = self.chunk
        return [(start, step, 0) for start in range(0, self.rg, step)] + [
            (start, step, 1) for start in range(self.rg, self.rows, step)
        ]

    def mask(self, count, group, width):
        row = lax.broadcasted_iota(jnp.int32, (count, 128), 0)
        if group == 0:
            keep = (row & (CELLS - 1)) < self.hg
        else:
            keep = (row & (CELLS // 2 - 1)) < self.hl
        return lanes(keep.astype(F32), width)

    def small_mask(self, group, width):
        count = self.sl if group else self.sg
        row = lax.broadcasted_iota(jnp.int32, (count, 128), 0)
        keep = (row & 3) < self.ol if group else (row & 7) < self.og
        return lanes(keep.astype(F32), width)

    def small_pieces(self):
        return [(0, self.sg, 0), (self.sg, self.sl, 1)]


def alive(live, slab):
    return jnp.where(slab < 2 * live[0], 1.0, 0.0).astype(F32)


def cells(geo, count, group, width, small=False):
    images = lanes(count[8:9, 0:128], width)
    if small:
        return images * float(2 * geo.og * geo.og if group == 0 else 4 * geo.ol * geo.ol)
    return images * float(2 * geo.hg * geo.hg if group == 0 else 4 * geo.hl * geo.hl)


def member(sums, row, width):
    parts = width // sums.shape[1]
    return jnp.concatenate(
        [sums[row * parts + k : row * parts + k + 1, :] for k in range(parts)], axis=1
    )


def norm_terms(stats, norm, number, group):
    width = norm.shape[1]
    mean = member(stats, 2 * group, width) / number
    spread = member(stats, 2 * group + 1, width) / number - mean * mean
    inverse = lax.rsqrt(spread + EPSILON)
    scale = norm[0:1, :] * inverse
    return mean, inverse, scale, norm[1:2, :] - mean * scale


def back_terms(stats, norm, number, group, first, second_raw):
    mean, inverse, scale, unused = norm_terms(stats, norm, number, group)
    second = inverse * (second_raw - mean * first)
    by_value = -scale * inverse * (second / number)
    constant = -scale * (first / number) - by_value * mean
    return scale, by_value, constant, second


def forward_terms(geo, count, stats, norm, width, small=False):
    return [
        norm_terms(stats, norm, cells(geo, count, group, width, small), group)[2:]
        for group in range(2)
    ]


def backward_terms(geo, count, stats, norm, sums, out, width, small=False, rows=((0, 1), (2, 3))):
    terms = []
    seconds = []
    for group in range(2):
        number = cells(geo, count, group, width, small)
        first = member(sums, rows[group][0], width)
        raw = member(sums, rows[group][1], width)
        scale, by_value, constant, second = back_terms(stats, norm, number, group, first, raw)
        terms.append((scale, by_value, constant))
        seconds.append((second, first))
    out[0:1, :] = seconds[0][0] + seconds[1][0]
    out[1:2, :] = seconds[0][1] + seconds[1][1]
    return terms


def finish(stats, acc, members, begin=0):
    part = stats.shape[1]
    parts = acc.shape[2] // part
    for row in range(members):
        total = jnp.sum(acc[begin + row], axis=0, keepdims=True)
        for k in range(parts):
            stats[row * parts + k : row * parts + k + 1, :] = total[:, k * part : (k + 1) * part]


def put(store, place, values):
    for k in range(store.shape[0]):
        store[k, place, :] = values[:, k * 128 : (k + 1) * 128]


def take(store, place):
    return jnp.concatenate([store[k, place, :] for k in range(store.shape[0])], axis=1)


def put_pieces(pieces, first, values, begin=0):
    cores, chips, reps, size = pieces.shape[:4]
    cols = slice(begin, begin + values.shape[1])
    for k in range(values.shape[0] // size):
        index = first // size + k
        shard, rep = index // reps, index % reps
        part = values[k * size : (k + 1) * size]
        pieces[shard % cores, shard // cores, rep, :, cols] = part.astype(BF16)


def loop(count, step):
    def one(index, carry):
        step(index)
        return carry

    lax.fori_loop(0, count, one, 0)


def at(index, size):
    return pl.ds(pl.multiple_of(index * size, size), size)


def stage_a(
    geo, net, live, xg, xl, short, expand, packed, conv, short_rows, expand_rows, acc, pair, weight,
    own_g, own_l, arrive,
):
    loads = (
        pltpu.make_async_copy(xg, own_g, arrive.at[0]),
        pltpu.make_async_copy(xl, own_l, arrive.at[1]),
    )
    for load in loads:
        load.start()
    net.open()
    acc[...] = jnp.zeros(acc.shape, F32)
    blank = jnp.zeros((CELLS, packed.shape[1]), BF16)
    half = CELLS // 2
    pair[...] = jnp.zeros(pair.shape, F32)
    for columns, rows in ((short, short_rows), (expand, expand_rows)):
        rows[...] = columns[...].astype(F32).T.reshape(rows.shape).astype(BF16)
    for load in loads:
        load.wait()

    def pack(s):
        base = s * geo.rows
        keep = alive(live, s).astype(BF16)
        for i in range(geo.hg):
            start = pl.multiple_of(base + i * CELLS, CELLS)
            packed[pl.ds(start, CELLS), :] = blank
            packed[pl.ds(start, geo.hg), :] = own_g[s, i] * keep
        for i in range(geo.hl):
            start = pl.multiple_of(base + geo.rg + i * CELLS, CELLS)
            for side in range(2):
                pair[side * half : side * half + geo.hl, :] = own_l[2 * s + side, i].astype(F32)
            packed[pl.ds(start, CELLS), :] = pair[...].astype(BF16) * keep

    part = geo.slabs // 4
    for number in range(4):
        begin = number * part
        size = part if number < 3 else geo.slabs - begin
        loop(size, lambda s: pack(s + begin))
        net.turn(number + 1)
    gathered = net.job_out(3)
    weight[...] = gathered[...].astype(F32).reshape(weight.shape).astype(BF16)

    def slab(s):
        result = nt(packed[at(s, geo.rows), :], weight[...])
        conv[at(s, geo.rows), :] = result.astype(BF16)
        for start, size, group in geo.pieces(256):
            piece = result[start : start + size]
            acc[2 * group] += fold(piece)
            acc[2 * group + 1] += fold(piece * piece)
        net.give(s, "packed", "za")

    loop(geo.slabs, slab)
    finish(net.own, acc, 4)
    net.own[8:16, :] = jnp.full((8, net.own.shape[1]), live[0], jnp.int32).astype(F32)
    net.begin()
    net.turn(5)
    net.end()


def spread_taps(geo, store, s, values, reverse):
    width = values[0].shape[1]
    for group in range(2):
        rows = values[group]
        size = rows.shape[0]
        start = pl.multiple_of(s * geo.halo + CELLS + group * (geo.rg + CELLS), CELLS)
        before = pltpu.roll(rows, 1, 0)
        after = pltpu.roll(rows, size - 1, 0)
        order = (after, rows, before) if reverse else (before, rows, after)
        for tap in range(3):
            store[pl.ds(start, size), tap * width : (tap + 1) * width] = order[tap].astype(BF16)


def clear_halo(geo, store):
    blank = jnp.zeros((CELLS, store.shape[1]), BF16)

    def slab(s):
        store[pl.ds(pl.multiple_of(s * geo.halo, CELLS), CELLS), :] = blank
        store[pl.ds(pl.multiple_of(s * geo.halo + CELLS + geo.rg, CELLS), CELLS), :] = blank
        store[pl.ds(pl.multiple_of((s + 1) * geo.halo - CELLS, CELLS), CELLS), :] = blank

    loop(geo.slabs, slab)


def activate(geo, live, conv, s, terms):
    values = []
    width = conv.shape[1]
    keep = alive(live, s)
    for group in range(2):
        start, size = (geo.rg, geo.rl) if group else (0, geo.rg)
        rows = conv[pl.ds(pl.multiple_of(s * geo.rows + start, CELLS), size), :].astype(F32)
        scale, shift = terms[group]
        values.append(silu(rows * scale + shift) * (geo.mask(size, group, width) * keep))
    return values


def stage_b(geo, net, live, count, za, stats_a, norm, weight, conv, taps, acc):
    acc[...] = jnp.zeros(acc.shape, F32)
    width = za.shape[1]
    terms = forward_terms(geo, count, stats_a, norm, width)
    clear_halo(geo, taps)

    def fill(s):
        net.need(s, "za")
        spread_taps(geo, taps, s, activate(geo, live, za, s, terms), False)
        net.give(s, "taps")

    loop(1, fill)
    net.open()
    loop(geo.slabs - 1, lambda s: fill(s + 1))
    net.turn(1)
    net.need(0, "wb")
    span = geo.halo - 2 * CELLS

    def slab(s):
        result = None
        for dy in range(3):
            rows = taps[pl.ds(pl.multiple_of(s * geo.halo + dy * CELLS, CELLS), span), :]
            term = nt(rows, weight[:, dy * 3 * width : (dy + 1) * 3 * width])
            result = term if result is None else result + term
        keep = alive(live, s)
        for group, (begin, size) in enumerate(((0, geo.rg), (geo.rg + CELLS, geo.rl))):
            piece = result[begin : begin + size]
            start = pl.multiple_of(s * geo.rows + group * geo.rg, CELLS)
            conv[pl.ds(start, size), :] = piece.astype(BF16)
            piece = piece * (geo.mask(size, group, width) * keep)
            acc[2 * group] += fold(piece)
            acc[2 * group + 1] += fold(piece * piece)
        net.give(s, "zb")

    loop(geo.slabs, slab)
    net.turn(2)
    finish(net.own, acc, 4)
    net.run()


def stage_c(geo, net, live, count, zb, stats_b, norm, weight, conv, act, acc):
    acc[...] = jnp.zeros(acc.shape, F32)
    terms = forward_terms(geo, count, stats_b, norm, zb.shape[1])
    step = 256

    def slab(s):
        net.need(s, "zb")
        values = activate(geo, live, zb, s, terms)
        act[0 : geo.rg, :] = values[0].astype(BF16)
        act[geo.rg : geo.rows, :] = values[1].astype(BF16)
        for c in range(0, weight.shape[0], step):
            result = nt(act[...], weight[c : c + step, :])
            conv[at(s, geo.rows), c : c + step] = result.astype(BF16)
            for start, size, group in geo.pieces(256):
                piece = result[start : start + size]
                acc[2 * group, :, c : c + step] += fold(piece)
                acc[2 * group + 1, :, c : c + step] += fold(piece * piece)
        net.give(s, "zc")

    loop(1, slab)
    net.open()
    loop(3, lambda s: slab(s + 1))
    net.turn(1)
    loop(geo.slabs - 4, lambda s: slab(s + 4))
    net.turn(2)
    finish(net.own, acc, 4)
    net.run()


def even_rows(geo):
    return [2 * i * CELLS for i in range(geo.og)] + [
        geo.rg + 2 * i * CELLS for i in range(geo.ol)
    ]


def stage_d(
    geo, net, live, count, zc, stats_c, norm, packed, weight, short, hid, conv, sub, conv_s, stats_s,
    full, acc, acc_s,
):
    acc[...] = jnp.zeros(acc.shape, F32)
    width = zc.shape[1]
    terms = forward_terms(geo, count, stats_c, norm, width)

    def slab(s):
        net.need(s, "zc", "packed")
        keep = alive(live, s)
        for start, size, group in geo.pieces(width):
            rows = pl.ds(pl.multiple_of(s * geo.rows + start, CELLS), size)
            scale, shift = terms[group]
            joined = zc[rows, :].astype(F32) * scale + shift + packed[rows, :].astype(F32)
            value = silu(joined) * (geo.mask(size, group, width) * keep)
            put(full, pl.ds(start, size), value)
            hid[rows, :] = value.astype(BF16)
        picked = [take(full, pl.ds(start, 8, stride=2)) for start in even_rows(geo)]
        sub[at(s, geo.small), :] = jnp.concatenate(picked, axis=0).astype(BF16)
        result = nt(hid[at(s, geo.rows), :], weight[...])
        conv[at(s, geo.rows), :] = result.astype(BF16)
        for start, size, group in geo.pieces(256):
            piece = result[start : start + size]
            acc[2 * group] += fold(piece)
            acc[2 * group + 1] += fold(piece * piece)
        net.give(s, "hid", "zd", "sub")

    net.need(0, "wd")
    loop(1, slab)
    net.open()
    loop(4, lambda s: slab(s + 1))
    net.turn(1)
    loop(geo.slabs - 5, lambda s: slab(s + 5))
    finish(net.own, acc, 4)
    net.begin()
    acc_s[...] = jnp.zeros(acc_s.shape, F32)
    wide, step = short.shape[0], 256
    net.need(0, "ws")

    def pick(c):
        return short[c : c + step, :]

    small_product(geo, sub, pick, step, conv_s, acc_s, 0, wide // 4)
    net.turn(2)
    net.step()
    small_product(geo, sub, pick, step, conv_s, acc_s, wide // 4, 5 * wide // 8)
    net.step()
    small_product(geo, sub, pick, step, conv_s, acc_s, 5 * wide // 8, wide)
    finish(stats_s, acc_s, 4)
    net.end()


def small_product(geo, left, pick, step, conv, acc, first, last):
    for c in range(first, last, step):
        result = nt(left[...], pick(c))
        conv[:, c : c + step] = result.astype(BF16)
        for s in range(geo.slabs):
            for start, size, group in geo.small_pieces():
                piece = result[s * geo.small + start : s * geo.small + start + size]
                acc[2 * group, :, c : c + step] += fold(piece)
                acc[2 * group + 1, :, c : c + step] += fold(piece * piece)


def gather_taps(geo, net, live, zd, terms, full, taps):
    width = zd.shape[1]
    blank = jnp.zeros((8, width), F32)
    full[:, 0:CELLS, :] = jnp.zeros((width // 128, CELLS, 128), F32)
    full[:, CELLS + geo.rg : 2 * CELLS + geo.rg, :] = jnp.zeros((width // 128, CELLS, 128), F32)

    def slab(s):
        net.need(s, "zd")
        keep = alive(live, s)
        for start, size, group in geo.pieces(width):
            rows = pl.ds(pl.multiple_of(s * geo.rows + start, CELLS), size)
            scale, shift = terms[group]
            value = silu(zd[rows, :].astype(F32) * scale + shift)
            begin = CELLS + start + group * CELLS
            put(full, pl.ds(begin, size), value * (geo.mask(size, group, width) * keep))
        for dy in range(3):
            for dx in range(3):
                picked = []
                for group in range(2):
                    for i in range(geo.ol if group else geo.og):
                        line = 2 * i + dy - 1
                        if line < 0:
                            picked.append(blank)
                            continue
                        begin = CELLS + group * (geo.rg + CELLS) + line * CELLS + dx - 1
                        picked.append(take(full, pl.ds(begin, 8, stride=2)))
                tap = dy * 3 + dx
                taps[at(s, geo.small), tap * width : (tap + 1) * width] = jnp.concatenate(
                    picked, axis=0
                ).astype(BF16)
        net.give(s, "taps")

    loop(1, slab)
    net.open()
    net.side.begin()
    loop(4, lambda s: slab(s + 1))
    net.side.step()
    loop(geo.slabs - 5, lambda s: slab(s + 5))


def stage_e(
    geo, net, live, count, zd, stats_d, norm, weight_0, weight_1, weight_2, conv, taps, full,
    acc,
):
    acc[...] = jnp.zeros(acc.shape, F32)
    terms = forward_terms(geo, count, stats_d, norm, zd.shape[1])
    gather_taps(geo, net, live, zd, terms, full, taps)
    net.turn(1)
    net.side.step()
    net.need(0, "we_0", "we_1", "we_2")
    step = 256
    third = weight_0.shape[1]
    for c in range(0, weight_0.shape[0], step):
        result = nt(taps[:, 0:third], weight_0[c : c + step, :])
        result = result + nt(taps[:, third : 2 * third], weight_1[c : c + step, :])
        result = result + nt(taps[:, 2 * third :], weight_2[c : c + step, :])
        conv[:, c : c + step] = result.astype(BF16)
        for s in range(geo.slabs):
            keep = alive(live, s)
            for start, size, group in geo.small_pieces():
                piece = result[s * geo.small + start : s * geo.small + start + size]
                piece = piece * (geo.small_mask(group, step) * keep)
                acc[2 * group, :, c : c + step] += fold(piece)
                acc[2 * group + 1, :, c : c + step] += fold(piece * piece)
    net.side.end()
    net.turn(2)
    finish(net.own, acc, 4)
    net.run()


def stage_f(geo, net, live, count, ze, stats_e, norm, weight, act, conv, acc):
    acc[...] = jnp.zeros(acc.shape, F32)
    width = ze.shape[1]
    terms = forward_terms(geo, count, stats_e, norm, width, True)

    def slab(s):
        keep = alive(live, s)
        rows = ze[at(s, geo.small), :].astype(F32)
        parts = []
        for start, size, group in geo.small_pieces():
            scale, shift = terms[group]
            value = silu(rows[start : start + size] * scale + shift)
            parts.append(value * (geo.small_mask(group, width) * keep))
        act[at(s, geo.small), :] = jnp.concatenate(parts, axis=0).astype(BF16)

    loop(geo.slabs, slab)
    half, step = weight.shape[0] // 2, 256
    net.need(0, "wf")

    def pick(c):
        return weight[c : c + step, :]

    small_product(geo, act, pick, step, conv, acc, 0, half)
    net.open()
    small_product(geo, act, pick, step, conv, acc, half, 2 * half)
    finish(net.own, acc, 4)
    net.run()


def stage_out(
    geo, net, live, count, zf, zs, stats_f, stats_s, norm_f, norm_s, cotg, cotl, outg, outl, grad,
    pooled_sums, pool, cot, acc,
):
    acc[...] = jnp.zeros(acc.shape, F32)
    cot[...] = jnp.zeros(cot.shape, F32)
    pool[...] = jnp.zeros(pool.shape, F32)
    width = zf.shape[1]
    step = 512
    terms_f = forward_terms(geo, count, stats_f, norm_f, width, True)
    terms_s = forward_terms(geo, count, stats_s, norm_s, width, True)

    def slab(s):
        net.need(s, "zf", "zs", "cotg", "cotl")
        keep = alive(live, s)
        for c in range(0, width, step):
            cols = slice(c, c + step)
            for i in range(geo.og):
                cot[i * 8 : i * 8 + geo.og, :] = cotg[s, i, :, cols].astype(F32)
            for i in range(geo.ol):
                for side in range(2):
                    begin = geo.sg + i * 8 + side * 4
                    cot[begin : begin + geo.ol, :] = cotl[2 * s + side, i, :, cols].astype(F32)
            rows_f = zf[at(s, geo.small), cols].astype(F32)
            rows_s = zs[at(s, geo.small), cols].astype(F32)
            grads = []
            for start, size, group in geo.small_pieces():
                part = slice(start, start + size)
                vf, vs = rows_f[part], rows_s[part]
                scale_f, shift_f = (item[:, cols] for item in terms_f[group])
                scale_s, shift_s = (item[:, cols] for item in terms_s[group])
                joined = vf * scale_f + vs * scale_s + (shift_f + shift_s)
                mask = geo.small_mask(group, step) * keep
                gate = sig(joined)
                held = joined * gate
                value = held * mask
                low = value.astype(BF16)
                dy = cot[part, :] * ((gate + held - held * gate) * mask)
                grads.append(dy)
                acc[3 * group, :, cols] += fold(dy)
                acc[3 * group + 1, :, cols] += fold(dy * vf)
                acc[3 * group + 2, :, cols] += fold(dy * vs)
                summed = fold(value)
                if group == 0:
                    for i in range(geo.og):
                        outg[s, i, :, cols] = value[i * 8 : i * 8 + geo.og].astype(BF16)
                    pool[s, 0:1, cols] = jnp.sum(summed, axis=0, keepdims=True) * (
                        1.0 / (geo.og * geo.og)
                    )
                else:
                    row = lax.broadcasted_iota(jnp.int32, (8, step), 0)
                    for side in range(2):
                        own = jnp.where((row >= 4) == (side == 1), summed, 0.0)
                        pool[s, 1 + side : 2 + side, cols] = jnp.sum(
                            own, axis=0, keepdims=True
                        ) * (1.0 / (geo.ol * geo.ol))
                        for i in range(geo.ol):
                            begin = i * 8 + side * 4
                            outl[2 * s + side, i, :, cols] = value[begin : begin + geo.ol].astype(
                                BF16
                            )
            grad[at(s, geo.small), cols] = jnp.concatenate(grads, axis=0).astype(BF16)
        net.give(s, "outg", "outl", "grad")
        pooled = pool[s]
        square = jnp.mean(pooled * pooled, axis=1, keepdims=True)
        normed = pooled * lax.rsqrt(square + 1e-06)
        acc[6] += normed
        acc[7] += normed * normed

    loop(geo.slabs, slab)
    finish(net.own, acc, 6)
    net.begin()
    finish(pooled_sums, acc, 2, 6)
    net.end()


def small_back(geo, live, s, grad, conv, terms, width, cols):
    keep = alive(live, s)
    rows_g = grad[at(s, geo.small), cols].astype(F32)
    rows_z = conv[at(s, geo.small), cols].astype(F32)
    parts = []
    for start, size, group in geo.small_pieces():
        scale, by_value, constant = (item[:, cols] for item in terms[group])
        part = slice(start, start + size)
        value = rows_g[part] * scale + rows_z[part] * by_value + constant
        parts.append(value * (geo.small_mask(group, width) * keep))
    return jnp.concatenate(parts, axis=0).astype(BF16)


def stage_f_back(
    geo, net, live, count, zf, zs, stats_f, stats_s, norm_f, norm_s, grad, sums, act, sub, weight,
    short, ze, stats_e, norm_e, wgrad_f, wgrad_s, back_sub, back_e, ngrad_f, ngrad_s, dzf, dzs, acc,
):
    acc[...] = jnp.zeros(acc.shape, F32)
    width = zf.shape[1]
    step = 512
    rows_f, rows_s = ((0, 1), (3, 4)), ((0, 2), (3, 5))
    terms_f = backward_terms(geo, count, stats_f, norm_f, sums, ngrad_f, width, True, rows_f)
    terms_s = backward_terms(geo, count, stats_s, norm_s, sums, ngrad_s, width, True, rows_s)

    def slab(s):
        net.need(s, "zf", "zs", "grad")
        for c in range(0, width, step):
            cols = slice(c, c + step)
            dzf[at(s, geo.small), cols] = small_back(geo, live, s, grad, zf, terms_f, step, cols)
            dzs[at(s, geo.small), cols] = small_back(geo, live, s, grad, zs, terms_s, step, cols)

    loop(geo.slabs, slab)
    net.open()
    net.side.begin()
    net.need(0, "wf")
    block = 256
    terms_e = forward_terms(geo, count, stats_e, norm_e, ze.shape[1], True)
    for c in range(0, act.shape[1], block):
        cols = slice(c, c + block)
        result = nn(dzf[...], weight[:, cols])
        for s in range(geo.slabs):
            keep = alive(live, s)
            rows = ze[s * geo.small : (s + 1) * geo.small, cols].astype(F32)
            parts = []
            for start, size, group in geo.small_pieces():
                scale, shift = (item[:, cols] for item in terms_e[group])
                value = rows[start : start + size]
                mask = geo.small_mask(group, block) * keep
                piece = result[s * geo.small + start : s * geo.small + start + size]
                piece = piece * (slope(value * scale + shift) * mask)
                parts.append(piece)
                acc[2 * group, :, cols] += fold(piece)
                acc[2 * group + 1, :, cols] += fold(piece * value)
            back_e[s * geo.small : (s + 1) * geo.small, cols] = jnp.concatenate(
                parts, axis=0
            ).astype(BF16)
    finish(net.own, acc, 4)
    net.begin()
    net.need(0, "sub", "act", "ws")
    for c in range(0, width, block):
        cols = slice(c, c + block)
        put_pieces(wgrad_s, c, tn(dzs[:, cols], sub[...]))
        if c == width // 4:
            net.step()
    net.step()
    net.turn(1)
    for c in range(0, width, block):
        cols = slice(c, c + block)
        put_pieces(wgrad_f, c, tn(dzf[:, cols], act[...]))
        if c == width // 4:
            net.side.step()
    net.side.step()
    net.turn(2)
    for c in range(0, sub.shape[1], block):
        cols = slice(c, c + block)
        back_sub[:, cols] = nn(dzs[...], short[:, cols]).astype(BF16)
    net.side.end()
    net.end()


def stage_e_back(
    geo, net, live, count, ze, stats_e, norm_e, back_e, sums_e, zd, stats_d, norm_d, weight_0, weight_1,
    weight_2, taps, wgrad, back_d, ngrad, full, dze, moved, parity, acc,
):
    acc[...] = jnp.zeros(acc.shape, F32)
    width = ze.shape[1]
    terms_e = backward_terms(geo, count, stats_e, norm_e, sums_e, ngrad, width, True)
    terms_d = forward_terms(geo, count, stats_d, norm_d, width)

    def shift(s):
        value = small_back(geo, live, s, back_e, ze, terms_e, width, slice(0, width)).astype(F32)
        blank = jnp.zeros((8, width), F32)
        down = jnp.concatenate(
            [value[8 : geo.sg], blank, value[geo.sg + 8 :], blank], axis=0
        )
        size = geo.small
        dze[at(s, size), :] = value.astype(BF16)
        moved[0, at(s, size), :] = pltpu.roll(value, size - 1, 0).astype(BF16)
        moved[1, at(s, size), :] = down.astype(BF16)
        moved[2, at(s, size), :] = pltpu.roll(down, size - 1, 0).astype(BF16)

    loop(2, shift)
    net.open()
    loop(geo.slabs - 2, lambda s: shift(s + 2))

    net.need(0, "we_0", "we_1", "we_2")

    def tap(dy, dx):
        return (weight_0, weight_1, weight_2)[dy][:, dx * width : (dx + 1) * width]

    def grads(first, last):
        for t in range(first, last):
            result = tn(dze[...], taps[:, t * width : (t + 1) * width])
            put_pieces(wgrad, 0, result, t * width)

    parity[0] = nn(dze[...], tap(1, 1))
    parity[1] = nn(dze[...], tap(1, 2)) + nn(moved[0], tap(1, 0))
    parity[2] = nn(dze[...], tap(2, 1)) + nn(moved[1], tap(0, 1))
    parity[3] = (
        nn(dze[...], tap(2, 2))
        + nn(moved[0], tap(2, 0))
        + nn(moved[1], tap(0, 2))
        + nn(moved[2], tap(0, 0))
    )

    def slab(s):
        net.need(s, "zd")
        keep = alive(live, s)
        for group in range(2):
            for i in range(geo.ol if group else geo.og):
                for a in range(2):
                    for b in range(2):
                        begin = group * geo.rg + (2 * i + a) * CELLS + b
                        source = s * geo.small + group * geo.sg + i * 8
                        part = parity[2 * a + b, pl.ds(pl.multiple_of(source, 8), 8), :]
                        put(full, pl.ds(begin, 8, stride=2), part)
        for start, size, group in geo.pieces(width):
            rows = pl.ds(pl.multiple_of(s * geo.rows + start, CELLS), size)
            scale, shift_d = terms_d[group]
            value = zd[rows, :].astype(F32)
            mask = geo.mask(size, group, width) * keep
            piece = take(full, pl.ds(start, size)) * (slope(value * scale + shift_d) * mask)
            back_d[rows, :] = piece.astype(BF16)
            acc[2 * group] += fold(piece)
            acc[2 * group + 1] += fold(piece * value)
        net.give(s, "back_d")

    loop(geo.slabs, slab)
    finish(net.own, acc, 4)
    net.begin()
    net.need(0, "taps")
    grads(0, 3)
    net.step()
    grads(3, 6)
    net.step()
    grads(6, 9)
    net.end()


def wide_back(geo, live, s, grad, conv, terms, low):
    width = conv.shape[1]
    keep = alive(live, s)
    for start, size, group in geo.pieces(width):
        rows = pl.ds(pl.multiple_of(s * geo.rows + start, CELLS), size)
        scale, by_value, constant = terms[group]
        value = grad[rows, :].astype(F32) * scale + conv[rows, :].astype(F32) * by_value + constant
        low[rows, :] = (value * (geo.mask(size, group, width) * keep)).astype(BF16)


def stage_d_back(
    geo, net, live, count, zd, stats_d, norm_d, back_d, sums_d, hid, packed, zc, stats_c, norm_c,
    back_sub, weight, wgrad, joined, ngrad, dzd, full, acc,
):
    acc[...] = jnp.zeros(acc.shape, F32)
    width = zc.shape[1]
    terms_d = backward_terms(geo, count, stats_d, norm_d, sums_d, ngrad, zd.shape[1])
    terms_c = forward_terms(geo, count, stats_c, norm_c, width)

    def slab(s):
        net.need(s, "back_d", "zd", "zc", "packed")
        wide_back(geo, live, s, back_d, zd, terms_d, dzd)
        put(full, pl.ds(0, geo.rows), nn(dzd[at(s, geo.rows), :], weight[...]))
        extra = back_sub[at(s, geo.small), :].astype(F32)
        for k, start in enumerate(even_rows(geo)):
            place = pl.ds(start, 8, stride=2)
            put(full, place, take(full, place) + extra[k * 8 : k * 8 + 8])
        keep = alive(live, s)
        for start, size, group in geo.pieces(width):
            rows = pl.ds(pl.multiple_of(s * geo.rows + start, CELLS), size)
            scale, shift = terms_c[group]
            value = zc[rows, :].astype(F32)
            pre = value * scale + shift + packed[rows, :].astype(F32)
            mask = geo.mask(size, group, width) * keep
            piece = take(full, pl.ds(start, size)) * (slope(pre) * mask)
            joined[rows, :] = piece.astype(BF16)
            acc[2 * group] += fold(piece)
            acc[2 * group + 1] += fold(piece * value)
        net.give(s, "joined")

    loop(1, slab)
    net.open()
    loop(4, lambda s: slab(s + 1))
    net.turn(1)
    loop(geo.slabs - 5, lambda s: slab(s + 5))
    net.turn(2)
    finish(net.own, acc, 4)
    block = 256
    net.begin()
    net.need(0, "hid")
    for c in range(0, dzd.shape[1], block):
        put_pieces(wgrad, c, tn(dzd[:, c : c + block], hid[...]))
        net.step()
    net.end()


def stage_c_back(
    geo, net, live, count, zc, stats_c, norm_c, joined, sums_c, zb, stats_b, norm_b, weight, wgrad,
    back_b, ngrad, dzc, act, acc,
):
    acc[...] = jnp.zeros(acc.shape, F32)
    terms_c = backward_terms(geo, count, stats_c, norm_c, sums_c, ngrad, zc.shape[1])
    terms_b = forward_terms(geo, count, stats_b, norm_b, zb.shape[1])
    width = zb.shape[1]

    def slab(s):
        net.need(s, "joined", "zc", "zb")
        wide_back(geo, live, s, joined, zc, terms_c, dzc)
        result = nn(dzc[at(s, geo.rows), :], weight[...])
        keep = alive(live, s)
        for start, size, group in geo.pieces(width):
            rows = pl.ds(pl.multiple_of(s * geo.rows + start, CELLS), size)
            scale, shift = terms_b[group]
            value = zb[rows, :].astype(F32)
            pre = value * scale + shift
            mask = geo.mask(size, group, width) * keep
            gate = sig(pre)
            held = pre * gate
            act[rows, :] = (held * mask).astype(BF16)
            piece = result[start : start + size] * ((gate + held - held * gate) * mask)
            back_b[rows, :] = piece.astype(BF16)
            acc[2 * group] += fold(piece)
            acc[2 * group + 1] += fold(piece * value)
        net.give(s, "back_b")

    loop(1, slab)
    net.open()
    loop(geo.slabs - 1, lambda s: slab(s + 1))
    net.turn(2)
    finish(net.own, acc, 4)
    net.begin()
    block = 256
    for c in range(0, dzc.shape[1], block):
        put_pieces(wgrad, c, tn(dzc[:, c : c + block], act[...]))
        if c < 2 * block:
            net.step()
    net.end()


def stage_b_back(
    geo, net, live, count, zb, stats_b, norm_b, back_b, sums_b, za, stats_a, norm_a, weight, taps,
    wgrad, back_a, ngrad, dtaps, stacked, total, acc,
):
    acc[...] = jnp.zeros(acc.shape, F32)
    width = za.shape[1]
    terms_b = backward_terms(geo, count, stats_b, norm_b, sums_b, ngrad, width)
    terms_a = forward_terms(geo, count, stats_a, norm_a, width)
    clear_halo(geo, dtaps)
    for t in range(9):
        stacked[t * width : (t + 1) * width, :] = weight[:, t * width : (t + 1) * width]

    def fill(s):
        keep = alive(live, s)
        values = []
        for start, size, group in geo.pieces(width):
            rows = pl.ds(pl.multiple_of(s * geo.rows + start, CELLS), size)
            scale, by_value, constant = terms_b[group]
            value = back_b[rows, :].astype(F32) * scale + zb[rows, :].astype(F32) * by_value
            values.append((value + constant) * (geo.mask(size, group, width) * keep))
        spread_taps(geo, dtaps, s, values, True)

    loop(2, fill)
    net.open()
    loop(geo.slabs - 2, lambda s: fill(s + 2))
    net.turn(1)
    span = geo.halo - 2 * CELLS
    total[...] = jnp.zeros(total.shape, F32)

    def slab(s):
        result = None
        for dy in range(3):
            begin = pl.multiple_of(s * geo.halo + (2 - dy) * CELLS, CELLS)
            term = nn(
                dtaps[pl.ds(begin, span), :], stacked[dy * 3 * width : (dy + 1) * 3 * width, :]
            )
            result = term if result is None else result + term
        keep = alive(live, s)
        for group, (begin, size) in enumerate(((0, geo.rg), (geo.rg + CELLS, geo.rl))):
            rows = pl.ds(pl.multiple_of(s * geo.rows + group * geo.rg, CELLS), size)
            scale, shift = terms_a[group]
            value = za[rows, :].astype(F32)
            mask = geo.mask(size, group, width) * keep
            piece = result[begin : begin + size] * (slope(value * scale + shift) * mask)
            back_a[rows, :] = piece.astype(BF16)
            acc[2 * group] += fold(piece)
            acc[2 * group + 1] += fold(piece * value)

    def grads(s):
        net.need(s, "taps")
        own = dtaps[
            pl.ds(pl.multiple_of(s * geo.halo + CELLS, CELLS), span), width : 2 * width
        ]
        for dy in range(3):
            begin = pl.multiple_of(s * geo.halo + dy * CELLS, CELLS)
            total[:, dy * 3 * width : (dy + 1) * 3 * width] += tn(own, taps[pl.ds(begin, span), :])

    loop(geo.slabs, slab)
    net.turn(2)
    finish(net.own, acc, 4)
    part = geo.slabs // 3
    net.begin()
    loop(part, grads)
    net.step()
    loop(part, lambda s: grads(s + part))
    net.step()
    loop(geo.slabs - 2 * part, lambda s: grads(s + 2 * part))
    put_pieces(wgrad, 0, total[...])
    net.end()


def stage_a_back(
    geo, net, live, count, za, stats_a, norm_a, back_a, sums_a, packed, joined, weight, wgrad, grad,
    ngrad, dza,
):
    terms_a = backward_terms(geo, count, stats_a, norm_a, sums_a, ngrad, za.shape[1])
    loop(2, lambda s: wide_back(geo, live, s, back_a, za, terms_a, dza))
    net.open()
    loop(geo.slabs - 2, lambda s: wide_back(geo, live, s + 2, back_a, za, terms_a, dza))
    net.need(0, "packed")
    put_pieces(wgrad, 0, tn(dza[...], packed[...]))
    net.turn(1)

    net.need(0, "joined")

    def slab(s):
        result = nn(dza[at(s, geo.rows), :], weight[...])
        rows = at(s, geo.rows)
        grad[rows, :] = (result + joined[rows, :].astype(F32)).astype(BF16)
        net.give(s, "grad")

    part = geo.slabs // 3
    for number in range(3):
        begin = number * part
        size = part if number < 2 else geo.slabs - begin
        loop(size, lambda s: slab(s + begin))
        net.turn(number + 2)
    net.turn(5)
    net.close()


def last_kernel(geo, upright, grad, hid, *refs):
    count = len(upright)
    rows_in, refs = refs[:count], refs[count:]
    dxg, dxl, outg, outl = refs[:4]
    targets = refs[4:]
    result = grad[...].astype(F32)
    half = CELLS // 2
    for i in range(geo.hg):
        dxg[0, i] = result[i * CELLS : i * CELLS + geo.hg]
        outg[0, i] = hid[i * CELLS : (i + 1) * CELLS, :][0 : geo.hg]
    for i in range(geo.hl):
        begin = geo.rg + i * CELLS
        low = hid[begin : begin + CELLS, :]
        for side in range(2):
            part = begin + side * half
            dxl[side, i] = result[part : part + geo.hl]
            outl[side, i] = low[side * half : side * half + geo.hl]

    def write(k):
        @pl.when(pl.program_id(0) == k % geo.slabs)
        def one():
            source, target = rows_in[k], targets[k]
            rows = source.shape[0] * source.shape[1]
            whole = source[...].astype(F32).reshape(rows, source.shape[2])
            target[...] = whole.T if upright[k] else whole

    for k in range(count):
        write(k)


def run_last(geo, grad, hid, parts, global_shape, local_shape):
    def whole(shape):
        return pl.BlockSpec(shape, lambda s: (0,) * len(shape))

    upright = [part.shape[0] * part.shape[1] >= 128 for part in parts]
    shapes = []
    for turn, part in zip(upright, parts):
        rows = part.shape[0] * part.shape[1]
        shapes.append((part.shape[2], rows) if turn else (rows, part.shape[2]))
    views = [
        pl.BlockSpec((1,) + global_shape[1:], lambda s: (s, 0, 0, 0)),
        pl.BlockSpec((2,) + local_shape[1:], lambda s: (s, 0, 0, 0)),
    ]
    outs = pl.pallas_call(
        functools.partial(last_kernel, geo, upright),
        grid=(geo.slabs,),
        out_shape=[
            jax.ShapeDtypeStruct(shape, dtype)
            for dtype in (F32, BF16)
            for shape in (global_shape, local_shape)
        ]
        + [jax.ShapeDtypeStruct(shape, F32) for shape in shapes],
        in_specs=[
            pl.BlockSpec((geo.rows, item.shape[1]), lambda s: (s, 0)) for item in (grad, hid)
        ]
        + [whole(part.shape) for part in parts],
        out_specs=views + views + [whole(shape) for shape in shapes],
        compiler_params=pltpu.CompilerParams(vmem_limit_bytes=VMEM_CAP),
        name="last",
    )(grad, hid, *parts)
    return outs[:4], [item if turn else item.T for turn, item in zip(upright, outs[4:])]


class Group:
    def __init__(self, kind, reps, shards):
        rep, shard = lax.axis_index("rep"), lax.axis_index("fsdp")
        chip, core = shard // 2, lax.rem(shard, 2)
        wide = reps // 2
        low, high = lax.rem(rep, 2), rep // wide
        first = core == 0
        if kind == CORES:
            self.size, self.me = 2, core
            self.address = lambda k: {"fsdp": chip * 2 + k}
        elif kind == CHIPS:
            self.size, self.me = shards // 2, chip
            self.address = lambda k: {"fsdp": k * 2 + core}
        elif kind == SHARDS:
            self.size, self.me = shards, shard
            self.address = lambda k: {"fsdp": k}
        elif kind == REPLICAS:
            self.size, self.me = reps, rep
            self.address = lambda k: {"rep": k}
        elif kind == CLOSE:
            self.size, self.me = 2, jnp.where(first, low, high)
            self.address = lambda k: {
                "rep": jnp.where(first, rep - low + k, rep - high * wide + k * wide)
            }
        elif kind == SLANTED:
            self.size = wide * (shards // 2)
            self.me = jnp.where(first, rep // 2, lax.rem(rep, wide)) * (shards // 2) + chip

            def across(k):
                far = k // (shards // 2)
                return {
                    "rep": jnp.where(first, far * 2 + low, high * wide + far),
                    "fsdp": lax.rem(k, shards // 2) * 2 + core,
                }

            self.address = across
        else:
            self.size = wide
            self.me = jnp.where(first, rep // 2, lax.rem(rep, wide))
            self.address = lambda k: {"rep": jnp.where(first, k * 2 + low, high * wide + k)}

    def other(self, hop):
        return lax.rem(self.me + hop, self.size)


class Sums:
    def __init__(self, reps, shards, own, out, buffers, sems):
        self.own, self.out, self.buffers, self.sems = own, out, buffers, sems
        self.groups = [Group(kind, reps, shards) for kind in (CORES, CHIPS, REPLICAS)]
        self.phase = 0
        self.copies = []

    def send(self, source):
        group, buffer = self.groups[self.phase], self.buffers[self.phase]
        self.copies = []
        for hop in range(1, group.size):
            copy = pltpu.make_async_remote_copy(
                source, buffer.at[group.me], self.sems[2 * self.phase].at[hop],
                self.sems[2 * self.phase + 1].at[hop], device_id=group.address(group.other(hop)),
                device_id_type=MESH,
            )
            copy.start()
            self.copies.append(copy)

    def begin(self):
        self.send(self.own)
        self.buffers[0][self.groups[0].me] = self.own[...]

    def total(self):
        for copy in self.copies:
            copy.wait()
        buffer = self.buffers[self.phase]
        total = buffer[0]
        for k in range(1, self.groups[self.phase].size):
            total = total + buffer[k]
        return total

    def step(self):
        total = self.total()
        self.phase += 1
        group, buffer = self.groups[self.phase], self.buffers[self.phase]
        buffer[group.me] = total
        self.send(buffer.at[group.me])

    def end(self):
        while self.phase < 2:
            self.step()
        self.out[...] = self.total()


class In:
    def __init__(self, name, array, rows=None):
        self.name, self.array, self.rows = name, array, rows


class Out:
    def __init__(self, name, shape, dtype, rows):
        self.name, self.shape, self.dtype, self.rows = name, shape, dtype, rows


class Stream:
    def __init__(self, source, target, sems, rows, slabs):
        self.source, self.target, self.sems, self.rows, self.slabs = source, target, sems, rows, slabs

    def copy(self, s):
        if self.rows is None:
            return pltpu.make_async_copy(self.source, self.target, self.sems.at[0])
        place = at(s, self.rows)
        return pltpu.make_async_copy(self.source.at[place], self.target.at[place], self.sems.at[s])


class Net:
    def __init__(self, reps, shards, sums=None, side=None, jobs=(), plans=(), ins=(), outs=()):
        self.ins, self.outs = dict(ins), dict(outs)
        self.reps, self.shards = reps, shards
        self.sums, self.side, self.jobs, self.plans = sums, side, jobs, plans
        self.own = None if sums is None else sums.own
        self.opened = False
        self.started, self.finished = set(), set()

    def enter(self):
        rep, shard = lax.axis_index("rep"), lax.axis_index("fsdp")
        barrier = pltpu.get_barrier_semaphore()
        for hop in range(1, self.shards):
            other = {"fsdp": lax.rem(shard + hop, self.shards)}
            pl.semaphore_signal(barrier, inc=1, device_id=other, device_id_type=MESH)
        for hop in range(1, self.reps):
            other = {"rep": lax.rem(rep + hop, self.reps)}
            pl.semaphore_signal(barrier, inc=1, device_id=other, device_id_type=MESH)
        self.greeted = self.shards + self.reps - 2
        if any(job.kind == CROSS for job in self.jobs):
            group = Group(SLANTED, self.reps, self.shards)
            chips = self.shards // 2
            for far in range(1, self.reps // 2):
                for step in range(1, chips):
                    other = lax.rem(group.me // chips + far, self.reps // 2) * chips
                    other = group.address(other + lax.rem(group.me + step, chips))
                    pl.semaphore_signal(barrier, inc=1, device_id=other, device_id_type=MESH)
                    self.greeted += 1

    def load(self):
        blocks = [stream for stream in self.ins.values() if stream.rows is not None]
        if blocks:

            def start(s):
                for stream in blocks:
                    stream.copy(s).start()

            loop(blocks[0].slabs, start)
        for stream in self.ins.values():
            if stream.rows is None:
                stream.copy(0).start()

    def need(self, s, *names):
        for name in names:
            self.ins[name].copy(s).wait()

    def give(self, s, *names):
        for name in names:
            self.outs[name].copy(s).start()

    def open(self):
        if not self.opened:
            self.opened = True
            pl.semaphore_wait(pltpu.get_barrier_semaphore(), self.greeted)
            self.turn(0)

    def turn(self, number):
        for k, (start, end) in enumerate(self.plans):
            if end == number:
                self.finish(k)
        for k, (start, end) in enumerate(self.plans):
            if start == number:
                self.started.add(k)
                self.jobs[k].start()

    def finish(self, k):
        assert k in self.started and k not in self.finished
        self.finished.add(k)
        self.jobs[k].finish()

    def job_out(self, k):
        return self.jobs[k].out

    def begin(self):
        self.open()
        self.sums.begin()

    def step(self):
        self.sums.step()

    def end(self):
        self.sums.end()
        self.close()

    def run(self):
        self.begin()
        self.end()

    def close(self):
        for k in range(len(self.jobs)):
            if k not in self.finished:
                self.finish(k)
        blocks = list(self.outs.values())
        if blocks:

            def wait(s):
                for stream in blocks:
                    stream.copy(s).wait()

            loop(blocks[0].slabs, wait)


class Job:
    GROUPS = {
        PAIR: CORES, JOIN: CORES, LINE: CHIPS, SPREAD: CHIPS, ALL: SHARDS, SHARE: REPLICAS,
        HALF: CLOSE, NEAR: CLOSE, REST: APART, OTHERS: APART, CROSS: SLANTED,
    }

    def __init__(self, kind, reps, shards, sources, out, held, send, recv):
        self.kind, self.sources, self.out, self.held = kind, sources, out, held
        self.send, self.recv = send, recv
        self.reps, self.chips = reps, shards // 2
        self.rep, shard = lax.axis_index("rep"), lax.axis_index("fsdp")
        self.chip, self.core = shard // 2, lax.rem(shard, 2)
        self.group = Group(self.GROUPS[kind], reps, shards)

    def give(self, source, target, hop):
        k = len(self.copies)
        if hop == 0:
            copy = pltpu.make_async_copy(source, target, self.send.at[k])
        else:
            copy = pltpu.make_async_remote_copy(
                source, target, self.send.at[k], self.recv.at[k],
                device_id=self.group.address(self.group.other(hop)), device_id_type=MESH,
            )
        copy.start()
        self.copies.append(copy)

    def start(self):
        self.copies = []
        kind, out, source, group = self.kind, self.out, self.sources[0], self.group
        order = list(range(1, group.size)) + [0]
        wide = self.reps // 2
        first = self.core == 0
        if kind == SPREAD:
            for hop in order[:-1]:
                self.give(source.at[self.rep], out.at[self.rep, group.size - hop - 1], hop)
        elif kind == NEAR:
            self.give(out.at[self.rep], out.at[self.rep], 1)
        elif kind == OTHERS:
            low, high = lax.rem(self.rep, 2), self.rep // wide
            partner = jnp.where(
                first, self.rep + 1 - 2 * low, self.rep + (1 - 2 * high) * wide
            )
            for hop in order[:-1]:
                for place in (self.rep, partner):
                    self.give(out.at[place], out.at[place], hop)
        elif kind == JOIN:
            for hop in order:
                for step in range(1, self.chips):
                    chip = lax.rem(self.chip + step, self.chips)
                    self.give(source.at[:, step - 1], out.at[chip, self.core], hop)
                self.give(self.sources[1], out.at[self.chip, self.core], hop)
        elif kind == CROSS:
            for hop in order:
                other = group.other(hop)
                block = source.at[other // self.chips, lax.rem(other, self.chips)]
                self.give(block, self.held.at[group.me], hop)
        elif kind in (ALL, SHARE):
            for hop in order:
                self.give(source, out.at[group.me], hop)
        elif kind == HALF:
            low, high = lax.rem(self.rep, 2), self.rep // wide
            mine = jnp.where(first, low, high * wide)
            theirs = jnp.where(first, 1 - low, (1 - high) * wide)
            step = jnp.where(first, 2, 1)
            for k in range(wide):
                self.give(source.at[theirs + k * step], self.held.at[1, k], 1)
            for k in range(wide):
                self.give(source.at[mine + k * step], self.held.at[0, k], 0)
        else:
            for hop in order:
                self.give(source.at[group.other(hop)], self.held.at[group.me], hop)

    def finish(self):
        for copy in self.copies:
            copy.wait()
        held, out = self.held, self.out
        if held is None:
            return
        members = held.shape[0]
        blocks = held.shape[1:-2]

        def one(index):
            place = (index // blocks[-1], lax.rem(index, blocks[-1])) if len(blocks) == 2 else (
                (index,) if blocks else ()
            )
            total = held[(0,) + place].astype(F32)
            for k in range(1, members):
                total = total + held[(k,) + place].astype(F32)
            out[place[::-1] if self.kind == PAIR else place] = total.astype(BF16)

        if blocks:
            loop(blocks[0] * (blocks[1] if len(blocks) == 2 else 1), one)
        else:
            total = held[0].astype(F32)
            for k in range(1, members):
                total = total + held[k].astype(F32)
            out[...] = total.astype(BF16)


def job_shapes(kind, reps, shards, shape):
    chips = shards // 2
    if kind == SPREAD:
        return None, (reps, chips - 1) + shape[1:], chips
    if kind in (NEAR, OTHERS):
        return None, shape, reps
    if kind == CROSS:
        return (shape[0] * shape[1],) + shape[2:], shape[2:], shape[0] * shape[1]
    if kind == JOIN:
        return None, (chips, 2, reps) + shape[2:], 2 * chips
    if kind == ALL:
        return None, (shards,) + shape, shards
    if kind == PAIR:
        return shape, (shape[2], shape[1]) + shape[3:], 2
    if kind == SHARE:
        return None, (reps,) + shape, reps
    if kind == HALF:
        return (2, reps // 2) + shape[1:], (reps // 2,) + shape[1:], reps
    return shape, shape[1:], shape[0]


VMEM_CAP = 60 << 20
FAR = (SPREAD, NEAR, OTHERS)


def sums_scratch(reps, shards, shape, own):
    sizes = (2, shards // 2, reps)
    return (
        [pltpu.VMEM(shape, F32)] * own
        + [pltpu.VMEM((size,) + shape, F32) for size in sizes]
        + [pltpu.SemaphoreType.DMA((size,)) for size in sizes for unused in range(2)]
    )


def run(kernel, geo, reps, shards, number, live, operands, results, scratch, sums, jobs, side, far=()):
    own_results = len(results)
    extra = []
    spaces = []
    flowing = []
    internal = []
    plain_results = []
    for k, item in enumerate(results):
        if isinstance(item, Out):
            extra.append(pltpu.VMEM(item.shape, item.dtype))
            if item.rows:
                extra.append(pltpu.SemaphoreType.DMA((geo.slabs,)))
            flowing.append((k, item))
            plain_results.append((item.shape, item.dtype))
        else:
            plain_results.append(item)
        internal.append(isinstance(item, Out) and not item.rows)
        spaces.append(pltpu.HBM if isinstance(item, Out) else pltpu.VMEM)
    results = plain_results
    streamed = [(k, item) for k, item in enumerate(operands) if isinstance(item, In)]
    operands = [item.array if isinstance(item, In) else item for item in operands]
    for k, item in streamed:
        extra.append(pltpu.VMEM(item.array.shape, item.array.dtype))
        extra.append(pltpu.SemaphoreType.DMA((1 if item.rows is None else geo.slabs,)))
    arrays = []
    shapes = []
    targets = []
    kept = {}
    for kind, sources, start, end in jobs:
        source = sources[0]
        if isinstance(source, int):
            shape, dtype = shapes[source]
        elif isinstance(source, str):
            shape, dtype = results[int(source)]
        else:
            shape, dtype = source.shape, source.dtype
        held, out, copies = job_shapes(kind, reps, shards, shape)
        shapes.append((out, dtype))
        extra += [] if held is None else [pltpu.VMEM(held, BF16)]
        extra += [pltpu.SemaphoreType.DMA((copies,))] * 2
        if kind in (NEAR, OTHERS) and isinstance(source, int):
            targets.append(targets[source])
        else:
            if kind in (NEAR, OTHERS):
                kept[len(arrays)] = len(results)
            targets.append(len(results))
            results.append(shapes[-1])
            spaces.append(pltpu.HBM if kind in FAR else pltpu.VMEM)
        arrays += [item for item in sources if not isinstance(item, (int, str))]
    own_or_job = len(results)
    keep = [k for k in range(own_or_job) if not (k < own_results and internal[k])]
    own_or_job = len(results)
    operands = tuple(operands)
    near = len(operands)
    if side is not None:
        operands += (side,)
        results.append((side.shape, F32))
        spaces.append(pltpu.VMEM)
        extra += sums_scratch(reps, shards, side.shape, 0)
    if sums is not None:
        results.append((sums, F32))
        spaces.append(pltpu.VMEM)
        extra += sums_scratch(reps, shards, sums, 1)
    inputs = 1 + len(operands)
    remote = bool(jobs) or sums is not None
    keep += list(range(own_or_job, len(results)))
    far = tuple(far) + tuple(k for k, unused in streamed)

    def whole(*refs):
        sources_in = list(refs[inputs : inputs + len(arrays)])
        first_out = inputs + len(arrays)
        outs = [None] * len(results)
        for place, k in enumerate(keep):
            outs[k] = refs[first_out + place]
        more = list(refs[first_out + len(keep) :])
        own_refs = list(outs[:own_results])
        out_streams, in_streams = [], []
        for k, item in flowing:
            own_refs[k] = more.pop(0)
            if item.rows:
                stream = Stream(own_refs[k], outs[k], more.pop(0), item.rows, geo.slabs)
                out_streams.append((item.name, stream))
            else:
                outs[k] = own_refs[k]
        given = list(refs[: 1 + len(operands)])
        for k, item in streamed:
            given[1 + k] = more.pop(0)
            stream = Stream(refs[1 + k], given[1 + k], more.pop(0), item.rows, geo.slabs)
            in_streams.append((item.name, stream))
        made = []
        for k, (kind, sources, start, end) in enumerate(jobs):
            refs_of = []
            for item in sources:
                if isinstance(item, int):
                    refs_of.append(made[item].out)
                elif isinstance(item, str):
                    refs_of.append(outs[int(item)])
                else:
                    refs_of.append(sources_in.pop(0))
            held = more.pop(0) if job_shapes(kind, reps, shards, refs_of[0].shape)[0] else None
            made.append(
                Job(kind, reps, shards, refs_of, outs[targets[k]], held, more.pop(0), more.pop(0))
            )
        beside, main = None, None
        if side is not None:
            beside = Sums(reps, shards, refs[near + 1], outs[own_or_job], more[0:3], more[3:9])
            more = more[9:]
        if sums is not None:
            main = Sums(reps, shards, more[0], outs[-1], more[1:4], more[4:10])
            more = more[10:]
        net = None
        if remote:
            plans = [job[2:] for job in jobs]
            net = Net(reps, shards, main, beside, made, plans, in_streams, out_streams)
            net.enter()
            net.load()
        kernel(geo, net, *given[: near + 1], *own_refs, *more)

    params = {"collective_id": number, "has_side_effects": True} if remote else {}
    outputs = pl.pallas_call(
        whole,
        out_shape=[jax.ShapeDtypeStruct(*results[k]) for k in keep],
        in_specs=[pl.BlockSpec(memory_space=pltpu.SMEM)]
        + [pl.BlockSpec(memory_space=pltpu.HBM if k in far else pltpu.VMEM) for k in range(len(operands))]
        + [
            pl.BlockSpec(memory_space=pltpu.HBM if k in kept else pl.ANY) for k in range(len(arrays))
        ],
        out_specs=[pl.BlockSpec(memory_space=spaces[k]) for k in keep],
        scratch_shapes=extra
        + [item if not isinstance(item, tuple) else pltpu.VMEM(*item) for item in scratch],
        input_output_aliases={inputs + k: keep.index(out) for k, out in kept.items()},
        compiler_params=pltpu.CompilerParams(vmem_limit_bytes=VMEM_CAP, **params),
        name=kernel.__name__,
    )(live, *operands, *arrays)
    placed = [None] * len(results)
    for place, k in enumerate(keep):
        placed[k] = outputs[place]
    return placed


def own_norms(first, second):
    flat = jnp.concatenate([first.reshape(-1), second.reshape(-1)]).astype(F32)
    size = -(-flat.shape[0] // 1024) * 1024
    return jnp.pad(flat, (0, size - flat.shape[0])).reshape(8, -1)


def all_norms(gathered, first, second):
    shards = gathered.shape[0]
    flat = gathered.reshape(shards, -1)
    split, last = first.size, first.size + second.size

    def whole(part):
        return part.reshape(shards, 2, -1).transpose(1, 0, 2).reshape(2, -1)

    return whole(flat[:, :split]), whole(flat[:, split:last])


def body(reps, shards, *arguments):
    (
        global_views, local_views, live, first_reduce, first_spatial, first_expand, first_norms,
        second_reduce, second_spatial, second_expand, second_short, second_norms, global_cotan,
        local_cotan,
    ) = arguments
    geo = Geometry(global_views.shape[0], global_views.shape[1], local_views.shape[1])
    assert local_views.shape[0] == 2 * geo.slabs
    channels = global_views.shape[3]
    ha, hb, hc, hd, he = (
        item.T.reshape(reps, -1, item.shape[0])
        for item in (first_reduce, first_spatial, first_expand, second_reduce, second_spatial)
    )
    he_0, he_1, he_2 = (he[:, :, k * he.shape[2] // 3 : (k + 1) * he.shape[2] // 3] for k in range(3))
    mid_1, mid_2 = first_reduce.shape[1] * shards, second_reduce.shape[1] * shards
    wide = second_expand.shape[1] * shards

    def rows_of(gathered):
        return gathered.reshape(-1, gathered.shape[-1])

    big, small = geo.total, geo.small_total

    numbers = iter(range(100))

    def go(kernel, operands, results, scratch, width=None, members=4, jobs=(), side=None, far=()):
        parts = {4: 2, 6: 4, 8: 2}[members]
        sums = None if width is None else (members * parts, width // parts)
        return run(
            kernel, geo, reps, shards, next(numbers), live, operands, results, scratch, sums,
            jobs, side, far,
        )

    def pieces(rows, columns):
        return ((2, shards // 2, reps, rows // (shards * reps), columns), BF16)

    def acc(width, members=4):
        return ((members, 8, width), F32)

    def stat(width):
        return ((8, width), F32)

    def both(width):
        return ((2, width), F32)

    more = go(
        stage_a, (global_views, local_views, second_short, second_expand),
        [
            Out("packed", (big, channels), BF16, geo.rows), Out("za", (big, mid_1), BF16, geo.rows),
            ((reps, second_short.shape[1] // reps, channels), BF16),
            ((reps, second_expand.shape[1] // reps, mid_2), BF16),
        ],
        [
            acc(mid_1), ((CELLS, channels), F32), ((mid_1, channels), BF16), (global_views.shape, BF16),
            (local_views.shape, BF16), pltpu.SemaphoreType.DMA((2,)),
        ],
        mid_1, 8,
        jobs=(
            (SPREAD, (ha,), 0, 1), (NEAR, (0,), 1, 2), (OTHERS, (0,), 2, 3),
            (JOIN, (0, ha), 3, 4),
            (SPREAD, (hb,), 0, 2), (NEAR, (4,), 2, 3), (OTHERS, (4,), 3, 5),
            (JOIN, (4, hb), 5, None),
            (SPREAD, (hc,), 0, 3), (NEAR, (8,), 3, 5), (OTHERS, (8,), 5, None),
            (SPREAD, (hd,), 0, 3), (NEAR, (11,), 3, 5), (OTHERS, (11,), 5, None),
            (ALL, (own_norms(first_norms, second_norms),), 1, None), (SPREAD, ("2",), 1, None),
        ),
        far=(0, 1),
    )
    packed, za, hs, hf, unused, wa, unused, wb, far_c, far_d, norms, far_s, sa = more
    count = sa
    wa, wb = rows_of(wa), rows_of(wb)
    norms_1, norms_2 = all_norms(norms, first_norms, second_norms)
    na, nb, nc = norms_1[:, :mid_1], norms_1[:, mid_1 : 2 * mid_1], norms_1[:, 2 * mid_1 :]
    nd, ne = norms_2[:, :mid_2], norms_2[:, mid_2 : 2 * mid_2]
    nf, ns = norms_2[:, 2 * mid_2 : 2 * mid_2 + wide], norms_2[:, 2 * mid_2 + wide :]
    zb, taps_b, wc, wd, far_s, far_e0, far_e1, far_e2, sb = go(
        stage_b, (count, In("za", za, geo.rows), sa, na, In("wb", wb)),
        [
            Out("zb", (big, mid_1), BF16, geo.rows),
            Out("taps", (geo.halo_total, 3 * mid_1), BF16, geo.halo),
        ],
        [acc(mid_1)], mid_1,
        jobs=(
            (JOIN, (far_c, hc), 0, None), (JOIN, (far_d, hd), 0, None),
            (NEAR, (far_s,), 0, 1), (OTHERS, (2,), 1, None),
            (SPREAD, (he_0,), 0, None), (SPREAD, (he_1,), 0, None), (SPREAD, (he_2,), 0, None),
        ),
    )
    wc = rows_of(wc)
    zc, ws, far_e0, far_f, sc = go(
        stage_c, (count, In("zb", zb, geo.rows), sb, nb, wc),
        [Out("zc", (big, channels), BF16, geo.rows)],
        [((geo.rows, mid_1), BF16), acc(channels)], channels,
        jobs=(
            (JOIN, (far_s, hs), 0, None), (NEAR, (far_e0,), 0, 1), (OTHERS, (1,), 1, None),
            (SPREAD, (hf,), 0, None),
        ),
    )
    wd, ws = rows_of(wd), rows_of(ws)
    hid, zd, sub, zs, local_s, we_0, far_e1, we_1, far_e2, we_2, far_f, sd = go(
        stage_d,
        (
            count, In("zc", zc, geo.rows), sc, nc, In("packed", packed, geo.rows), In("wd", wd),
            In("ws", ws),
        ),
        [
            Out("hid", (big, channels), BF16, geo.rows), Out("zd", (big, mid_2), BF16, geo.rows),
            Out("sub", (small, channels), BF16, geo.small),
            ((small, wide), BF16), stat(wide // 2),
        ],
        [((channels // 128, geo.rows, 128), F32), acc(mid_2), acc(wide)], mid_2,
        jobs=(
            (JOIN, (far_e0, he_0), 0, 1),
            (NEAR, (far_e1,), 0, 1), (OTHERS, (1,), 1, 2), (JOIN, (1, he_1), 2, None),
            (NEAR, (far_e2,), 0, 1), (OTHERS, (4,), 1, 2), (JOIN, (4, he_2), 2, None),
            (NEAR, (far_f,), 1, None),
        ),
    )
    we = tuple(rows_of(item) for item in (we_0, we_1, we_2))
    late_we = tuple(In(name, item) for name, item in zip(("we_0", "we_1", "we_2"), we))
    ze, taps_e, unused, wf, ss, se = go(
        stage_e, (count, In("zd", zd, geo.rows), sd, nd, *late_we),
        [((small, mid_2), BF16), Out("taps", (small, 9 * mid_2), BF16, geo.small)],
        [((mid_2 // 128, geo.halo, 128), F32), acc(mid_2)], mid_2,
        jobs=((OTHERS, (far_f,), 0, 1), (JOIN, (0, hf), 1, None)), side=local_s,
    )
    wf = rows_of(wf)
    act_e, zf, sf = go(
        stage_f, (count, ze, se, ne, In("wf", wf)),
        [((small, mid_2), BF16), ((small, wide), BF16)], [acc(wide)], wide,
    )
    second_g, second_l, grad, local_pool, so = go(
        stage_out,
        (
            count, In("zf", zf, geo.small), In("zs", zs, geo.small), sf, ss, nf, ns,
            In("cotg", global_cotan, 1), In("cotl", local_cotan, 2),
        ),
        [
            Out("outg", global_cotan.shape, BF16, 1), Out("outl", local_cotan.shape, BF16, 2),
            Out("grad", (small, wide), BF16, geo.small),
            stat(wide // 4),
        ],
        [((geo.slabs, 8, wide), F32), ((geo.small, 512), F32), acc(wide, 8)], wide, 6,
    )
    unused, unused, back_sub, back_e, ngrad_f, ngrad_s, pair_f, pair_s, pool, qe = go(
        stage_f_back,
        (
            count, In("zf", zf, geo.small), In("zs", zs, geo.small), sf, ss, nf, ns,
            In("grad", grad, geo.small), so, In("act", act_e), In("sub", sub), In("wf", wf),
            In("ws", ws), ze, se, ne,
        ),
        [
            Out("wgrad_f", *pieces(wide, mid_2), 0), Out("wgrad_s", *pieces(wide, channels), 0), ((small, channels), BF16), ((small, mid_2), BF16),
            both(wide), both(wide),
        ],
        [((small, wide), BF16), ((small, wide), BF16), acc(mid_2)], mid_2,
        jobs=((PAIR, ("0",), 2, None), (PAIR, ("1",), 1, None)), side=local_pool,
    )
    views = count[8, 0] * 6.0
    pool = pool.reshape(2, wide)
    center = pool[0] / views
    spread = pool[1] / views - center * center
    pooled_std = jnp.mean(jnp.sqrt(spread + 1e-06))
    wgrad_e, back_d, ngrad_e, half_f, half_s, qd = go(
        stage_e_back,
        (
            count, ze, se, ne, back_e, qe, In("zd", zd, geo.rows), sd, nd, *late_we,
            In("taps", taps_e),
        ),
        [
            pieces(mid_2, 9 * mid_2), Out("back_d", (big, mid_2), BF16, geo.rows), both(mid_2),
        ],
        [
            ((mid_2 // 128, geo.halo, 128), F32), ((small, mid_2), BF16), ((3, small, mid_2), BF16), ((4, small, mid_2), F32),
            acc(mid_2),
        ],
        mid_2, jobs=((HALF, (pair_f,), 0, None), (HALF, (pair_s,), 0, None)),
    )
    wgrad_d, joined, ngrad_d, unused, half_e, unused, rest_s, line_f, qc = go(
        stage_d_back,
        (
            count, In("zd", zd, geo.rows), sd, nd, In("back_d", back_d, geo.rows), qd,
            In("hid", hid), In("packed", packed, geo.rows), In("zc", zc, geo.rows), sc, nc, back_sub,
            wd,
        ),
        [
            pieces(mid_2, channels), Out("joined", (big, channels), BF16, geo.rows), both(mid_2),
        ],
        [((big, mid_2), BF16), ((channels // 128, geo.rows, 128), F32), acc(channels)], channels,
        jobs=(
            (PAIR, (wgrad_e,), 0, 1), (HALF, (0,), 1, None),
            (REST, (half_f,), 0, 1), (REST, (half_s,), 0, 1), (LINE, (2,), 1, None),
        ),
    )
    wgrad_c, back_b, ngrad_c, pair_d, rest_e, line_s, qb = go(
        stage_c_back,
        (
            count, In("zc", zc, geo.rows), sc, nc, In("joined", joined, geo.rows), qc,
            In("zb", zb, geo.rows), sb, nb, wc,
        ),
        [
            pieces(channels, mid_1), Out("back_b", (big, mid_1), BF16, geo.rows), both(channels),
        ],
        [((big, channels), BF16), ((big, mid_1), BF16), acc(mid_1)], mid_1,
        jobs=(
            (PAIR, (wgrad_d,), 0, None), (REST, (half_e,), 0, None), (LINE, (rest_s,), 0, None),
        ),
    )
    wgrad_b, back_a, ngrad_b, unused, rest_d, unused, half_c, line_e, out_f, out_s, qa = go(
        stage_b_back,
        (count, zb, sb, nb, back_b, qb, za, sa, na, wb, In("taps", taps_b, geo.halo)),
        [pieces(mid_1, 9 * mid_1), ((big, mid_1), BF16), both(mid_1)],
        [
            ((geo.halo_total, 3 * mid_1), BF16), ((9 * mid_1, mid_1), BF16), (wb.shape, F32), acc(mid_1),
        ],
        mid_1,
        jobs=(
            (HALF, (pair_d,), 0, 1), (REST, (0,), 1, None), (PAIR, (wgrad_c,), 0, 1),
            (HALF, (2,), 1, None), (LINE, (rest_e,), 0, None), (SHARE, (line_f,), 1, None),
            (SHARE, (line_s,), 1, None),
        ),
    )
    more = go(
        stage_a_back,
        (count, za, sa, na, back_a, qa, In("packed", packed), In("joined", joined), wa),
        [
            pieces(mid_1, channels), Out("grad", (big, channels), BF16, geo.rows), both(mid_1),
        ],
        [((big, mid_1), BF16)],
        jobs=(
            (PAIR, (wgrad_b,), 0, 1), (HALF, (0,), 1, 2), (CROSS, (1,), 2, 3), (SHARE, (2,), 3, None),
            (PAIR, ("0",), 1, 2), (HALF, (4,), 2, 3), (CROSS, (5,), 3, 4), (SHARE, (6,), 4, None),
            (REST, (half_c,), 0, 1), (LINE, (8,), 1, 2), (SHARE, (9,), 2, None),
            (LINE, (rest_d,), 0, 1), (SHARE, (11,), 1, None), (SHARE, (line_e,), 0, None),
        ),
    )
    grad, ngrad_a = more[1], more[2]
    out_b, out_a, out_c, out_d, out_e = (more[3 + k] for k in (3, 7, 10, 12, 13))
    (grad_g, grad_l, first_g, first_l), columns = run_last(
        geo, grad, hid, (out_a, out_b, out_c, out_d, out_e, out_f, out_s),
        global_views.shape, local_views.shape,
    )
    shard = lax.axis_index("fsdp")

    def own_columns(parts, width):
        whole = jnp.concatenate(parts, axis=1)
        return lax.dynamic_slice_in_dim(whole, shard * width, width, 1)

    return (
        first_g, first_l, second_g, second_l, grad_g, grad_l,
        *columns[0:3],
        own_columns((ngrad_a, ngrad_b, ngrad_c), first_norms.shape[1]),
        *columns[3:7],
        own_columns((ngrad_d, ngrad_e, ngrad_f, ngrad_s), second_norms.shape[1]),
        pooled_std,
    )


def solution(mesh):
    views = P(("rep", "fsdp"), None, None, None)
    columns = P(None, "fsdp")
    return jax.shard_map(
        functools.partial(body, mesh.shape["rep"], mesh.shape["fsdp"]),
        mesh=mesh,
        in_specs=(views, views, P(("rep", "fsdp"))) + (columns,) * 9 + (views, views),
        out_specs=(views,) * 6 + (columns,) * 9 + (P(),),
        check_vma=False,
    )
```

```python
import functools

import jax
import jax.numpy as jnp
from jax import lax
from jax.experimental import pallas as pl
from jax.experimental.pallas import tpu as pltpu
from jax.sharding import PartitionSpec as P

EPSILON = 1e-05
F32 = jnp.float32
BF16 = jnp.bfloat16
MESH = pl.DeviceIdType.MESH
CELLS = 16
PAIR, HALF, REST, LINE, SHARE, SPREAD, NEAR, OTHERS, JOIN, CROSS, ALL = range(11)
CORES, CHIPS, SHARDS, REPLICAS, CLOSE, APART, SLANTED = range(7)


def nt(left, right):
    return lax.dot_general(left, right, (((1,), (1,)), ((), ())), preferred_element_type=F32)


def nn(left, right):
    return lax.dot_general(left, right, (((1,), (0,)), ((), ())), preferred_element_type=F32)


def tn(left, right):
    return lax.dot_general(left, right, (((0,), (0,)), ((), ())), preferred_element_type=F32)


def sig(values):
    return 0.5 * jnp.tanh(0.5 * values) + 0.5


def silu(values):
    return values * sig(values)


def slope(values):
    gate = sig(values)
    held = values * gate
    return gate + held - held * gate


def lanes(tile, width):
    return jnp.concatenate([tile] * (width // tile.shape[1]), axis=1)


def fold(values):
    return jnp.sum(values.reshape(values.shape[0] // 8, 8, values.shape[1]), axis=0)


class Geometry:
    def __init__(self, views, side_global, side_local):
        self.slabs = views
        self.hg, self.hl = side_global, side_local
        assert side_global < CELLS and side_local < CELLS // 2
        self.rg, self.rl = side_global * CELLS, side_local * CELLS
        self.rows = self.rg + self.rl
        self.og, self.ol = (side_global - 1) // 2 + 1, (side_local - 1) // 2 + 1
        self.sg, self.sl = self.og * 8, self.ol * 8
        self.small = self.sg + self.sl
        self.total, self.small_total = self.slabs * self.rows, self.slabs * self.small
        self.halo = self.rows + 3 * CELLS
        self.halo_total = self.slabs * self.halo
        self.chunk = 32
        assert self.rg % self.chunk == 0 and self.rl % self.chunk == 0 and self.small % 16 == 0

    def pieces(self, width):
        if width <= 256:
            return [(0, self.rg, 0), (self.rg, self.rl, 1)]
        step = self.chunk
        return [(start, step, 0) for start in range(0, self.rg, step)] + [
            (start, step, 1) for start in range(self.rg, self.rows, step)
        ]

    def mask(self, count, group, width):
        row = lax.broadcasted_iota(jnp.int32, (count, 128), 0)
        if group == 0:
            keep = (row & (CELLS - 1)) < self.hg
        else:
            keep = (row & (CELLS // 2 - 1)) < self.hl
        return lanes(keep.astype(F32), width)

    def small_mask(self, group, width):
        count = self.sl if group else self.sg
        row = lax.broadcasted_iota(jnp.int32, (count, 128), 0)
        keep = (row & 3) < self.ol if group else (row & 7) < self.og
        return lanes(keep.astype(F32), width)

    def small_pieces(self):
        return [(0, self.sg, 0), (self.sg, self.sl, 1)]


def alive(live, slab):
    return jnp.where(slab < 2 * live[0], 1.0, 0.0).astype(F32)


def cells(geo, count, group, width, small=False):
    images = lanes(count[8:9, 0:128], width)
    if small:
        return images * float(2 * geo.og * geo.og if group == 0 else 4 * geo.ol * geo.ol)
    return images * float(2 * geo.hg * geo.hg if group == 0 else 4 * geo.hl * geo.hl)


def member(sums, row, width):
    parts = width // sums.shape[1]
    return jnp.concatenate(
        [sums[row * parts + k : row * parts + k + 1, :] for k in range(parts)], axis=1
    )


def norm_terms(stats, norm, number, group):
    width = norm.shape[1]
    mean = member(stats, 2 * group, width) / number
    spread = member(stats, 2 * group + 1, width) / number - mean * mean
    inverse = lax.rsqrt(spread + EPSILON)
    scale = norm[0:1, :] * inverse
    return mean, inverse, scale, norm[1:2, :] - mean * scale


def back_terms(stats, norm, number, group, first, second_raw):
    mean, inverse, scale, unused = norm_terms(stats, norm, number, group)
    second = inverse * (second_raw - mean * first)
    by_value = -scale * inverse * (second / number)
    constant = -scale * (first / number) - by_value * mean
    return scale, by_value, constant, second


def forward_terms(geo, count, stats, norm, width, small=False):
    return [
        norm_terms(stats, norm, cells(geo, count, group, width, small), group)[2:]
        for group in range(2)
    ]


def backward_terms(geo, count, stats, norm, sums, out, width, small=False, rows=((0, 1), (2, 3))):
    terms = []
    seconds = []
    for group in range(2):
        number = cells(geo, count, group, width, small)
        first = member(sums, rows[group][0], width)
        raw = member(sums, rows[group][1], width)
        scale, by_value, constant, second = back_terms(stats, norm, number, group, first, raw)
        terms.append((scale, by_value, constant))
        seconds.append((second, first))
    out[0:1, :] = seconds[0][0] + seconds[1][0]
    out[1:2, :] = seconds[0][1] + seconds[1][1]
    return terms


def finish(stats, acc, members, begin=0):
    part = stats.shape[1]
    parts = acc.shape[2] // part
    for row in range(members):
        total = jnp.sum(acc[begin + row], axis=0, keepdims=True)
        for k in range(parts):
            stats[row * parts + k : row * parts + k + 1, :] = total[:, k * part : (k + 1) * part]


def put(store, place, values):
    for k in range(store.shape[0]):
        store[k, place, :] = values[:, k * 128 : (k + 1) * 128]


def take(store, place):
    return jnp.concatenate([store[k, place, :] for k in range(store.shape[0])], axis=1)


def put_pieces(pieces, first, values, begin=0):
    cores, chips, reps, size = pieces.shape[:4]
    cols = slice(begin, begin + values.shape[1])
    for k in range(values.shape[0] // size):
        index = first // size + k
        shard, rep = index // reps, index % reps
        part = values[k * size : (k + 1) * size]
        pieces[shard % cores, shard // cores, rep, :, cols] = part.astype(BF16)


def loop(count, step):
    def one(index, carry):
        step(index)
        return carry

    lax.fori_loop(0, count, one, 0)


def at(index, size):
    return pl.ds(pl.multiple_of(index * size, size), size)


def stage_a(
    geo, net, live, xg, xl, short, expand, packed, conv, short_rows, expand_rows, acc, pair, weight,
    own_g, own_l, arrive,
):
    loads = (
        pltpu.make_async_copy(xg, own_g, arrive.at[0]),
        pltpu.make_async_copy(xl, own_l, arrive.at[1]),
    )
    for load in loads:
        load.start()
    net.open()
    acc[...] = jnp.zeros(acc.shape, F32)
    blank = jnp.zeros((CELLS, packed.shape[1]), BF16)
    half = CELLS // 2
    pair[...] = jnp.zeros(pair.shape, F32)
    for columns, rows in ((short, short_rows), (expand, expand_rows)):
        rows[...] = columns[...].astype(F32).T.reshape(rows.shape).astype(BF16)
    for load in loads:
        load.wait()

    def pack(s):
        base = s * geo.rows
        keep = alive(live, s).astype(BF16)
        for i in range(geo.hg):
            start = pl.multiple_of(base + i * CELLS, CELLS)
            packed[pl.ds(start, CELLS), :] = blank
            packed[pl.ds(start, geo.hg), :] = own_g[s, i] * keep
        for i in range(geo.hl):
            start = pl.multiple_of(base + geo.rg + i * CELLS, CELLS)
            for side in range(2):
                pair[side * half : side * half + geo.hl, :] = own_l[2 * s + side, i].astype(F32)
            packed[pl.ds(start, CELLS), :] = pair[...].astype(BF16) * keep

    part = geo.slabs // 4
    for number in range(4):
        begin = number * part
        size = part if number < 3 else geo.slabs - begin
        loop(size, lambda s: pack(s + begin))
        net.turn(number + 1)
    gathered = net.job_out(3)
    weight[...] = gathered[...].astype(F32).reshape(weight.shape).astype(BF16)

    def slab(s):
        result = nt(packed[at(s, geo.rows), :], weight[...])
        conv[at(s, geo.rows), :] = result.astype(BF16)
        for start, size, group in geo.pieces(256):
            piece = result[start : start + size]
            acc[2 * group] += fold(piece)
            acc[2 * group + 1] += fold(piece * piece)
        net.give(s, "packed", "za")

    loop(geo.slabs, slab)
    finish(net.own, acc, 4)
    net.own[8:16, :] = jnp.full((8, net.own.shape[1]), live[0], jnp.int32).astype(F32)
    net.begin()
    net.turn(5)
    net.end()


def spread_taps(geo, store, s, values, reverse):
    width = values[0].shape[1]
    for group in range(2):
        rows = values[group]
        size = rows.shape[0]
        start = pl.multiple_of(s * geo.halo + CELLS + group * (geo.rg + CELLS), CELLS)
        before = pltpu.roll(rows, 1, 0)
        after = pltpu.roll(rows, size - 1, 0)
        order = (after, rows, before) if reverse else (before, rows, after)
        for tap in range(3):
            store[pl.ds(start, size), tap * width : (tap + 1) * width] = order[tap].astype(BF16)


def clear_halo(geo, store):
    blank = jnp.zeros((CELLS, store.shape[1]), BF16)

    def slab(s):
        store[pl.ds(pl.multiple_of(s * geo.halo, CELLS), CELLS), :] = blank
        store[pl.ds(pl.multiple_of(s * geo.halo + CELLS + geo.rg, CELLS), CELLS), :] = blank
        store[pl.ds(pl.multiple_of((s + 1) * geo.halo - CELLS, CELLS), CELLS), :] = blank

    loop(geo.slabs, slab)


def activate(geo, live, conv, s, terms):
    values = []
    width = conv.shape[1]
    keep = alive(live, s)
    for group in range(2):
        start, size = (geo.rg, geo.rl) if group else (0, geo.rg)
        rows = conv[pl.ds(pl.multiple_of(s * geo.rows + start, CELLS), size), :].astype(F32)
        scale, shift = terms[group]
        values.append(silu(rows * scale + shift) * (geo.mask(size, group, width) * keep))
    return values


def stage_b(geo, net, live, count, za, stats_a, norm, weight, conv, taps, acc):
    acc[...] = jnp.zeros(acc.shape, F32)
    width = za.shape[1]
    terms = forward_terms(geo, count, stats_a, norm, width)
    clear_halo(geo, taps)

    def fill(s):
        net.need(s, "za")
        spread_taps(geo, taps, s, activate(geo, live, za, s, terms), False)
        net.give(s, "taps")

    loop(1, fill)
    net.open()
    loop(geo.slabs - 1, lambda s: fill(s + 1))
    net.need(0, "wb")
    span = geo.halo - 2 * CELLS

    def slab(s):
        result = None
        for dy in range(3):
            rows = taps[pl.ds(pl.multiple_of(s * geo.halo + dy * CELLS, CELLS), span), :]
            term = nt(rows, weight[:, dy * 3 * width : (dy + 1) * 3 * width])
            result = term if result is None else result + term
        keep = alive(live, s)
        for group, (begin, size) in enumerate(((0, geo.rg), (geo.rg + CELLS, geo.rl))):
            piece = result[begin : begin + size]
            start = pl.multiple_of(s * geo.rows + group * geo.rg, CELLS)
            conv[pl.ds(start, size), :] = piece.astype(BF16)
            piece = piece * (geo.mask(size, group, width) * keep)
            acc[2 * group] += fold(piece)
            acc[2 * group + 1] += fold(piece * piece)
        net.give(s, "zb")

    loop(2, slab)
    net.turn(1)
    loop(geo.slabs - 2, lambda s: slab(s + 2))
    net.turn(2)
    finish(net.own, acc, 4)
    net.run()


def stage_c(geo, net, live, count, zb, stats_b, norm, weight, conv, act, acc):
    acc[...] = jnp.zeros(acc.shape, F32)
    terms = forward_terms(geo, count, stats_b, norm, zb.shape[1])
    step = 256

    def slab(s):
        net.need(s, "zb")
        values = activate(geo, live, zb, s, terms)
        act[0 : geo.rg, :] = values[0].astype(BF16)
        act[geo.rg : geo.rows, :] = values[1].astype(BF16)
        for c in range(0, weight.shape[0], step):
            result = nt(act[...], weight[c : c + step, :])
            conv[at(s, geo.rows), c : c + step] = result.astype(BF16)
            for start, size, group in geo.pieces(256):
                piece = result[start : start + size]
                acc[2 * group, :, c : c + step] += fold(piece)
                acc[2 * group + 1, :, c : c + step] += fold(piece * piece)
        net.give(s, "zc")

    loop(1, slab)
    net.open()
    loop(3, lambda s: slab(s + 1))
    net.turn(1)
    loop(geo.slabs - 4, lambda s: slab(s + 4))
    net.turn(2)
    finish(net.own, acc, 4)
    net.run()


def even_rows(geo):
    return [2 * i * CELLS for i in range(geo.og)] + [
        geo.rg + 2 * i * CELLS for i in range(geo.ol)
    ]


def stage_d(
    geo, net, live, count, zc, stats_c, norm, packed, weight, short, hid, conv, sub, conv_s, stats_s,
    full, acc, acc_s,
):
    acc[...] = jnp.zeros(acc.shape, F32)
    width = zc.shape[1]
    terms = forward_terms(geo, count, stats_c, norm, width)

    def slab(s):
        net.need(s, "zc", "packed")
        keep = alive(live, s)
        for start, size, group in geo.pieces(width):
            rows = pl.ds(pl.multiple_of(s * geo.rows + start, CELLS), size)
            scale, shift = terms[group]
            joined = zc[rows, :].astype(F32) * scale + shift + packed[rows, :].astype(F32)
            value = silu(joined) * (geo.mask(size, group, width) * keep)
            put(full, pl.ds(start, size), value)
            hid[rows, :] = value.astype(BF16)
        picked = [take(full, pl.ds(start, 8, stride=2)) for start in even_rows(geo)]
        sub[at(s, geo.small), :] = jnp.concatenate(picked, axis=0).astype(BF16)
        result = nt(hid[at(s, geo.rows), :], weight[...])
        conv[at(s, geo.rows), :] = result.astype(BF16)
        for start, size, group in geo.pieces(256):
            piece = result[start : start + size]
            acc[2 * group] += fold(piece)
            acc[2 * group + 1] += fold(piece * piece)
        net.give(s, "hid", "zd", "sub")

    net.need(0, "wd")
    loop(1, slab)
    net.open()
    loop(4, lambda s: slab(s + 1))
    net.turn(1)
    loop(geo.slabs - 5, lambda s: slab(s + 5))
    finish(net.own, acc, 4)
    net.begin()
    acc_s[...] = jnp.zeros(acc_s.shape, F32)
    wide, step = short.shape[0], 256
    net.need(0, "ws")

    def pick(c):
        return short[c : c + step, :]

    small_product(geo, sub, pick, step, conv_s, acc_s, 0, wide // 4)
    net.turn(2)
    net.step()
    small_product(geo, sub, pick, step, conv_s, acc_s, wide // 4, 5 * wide // 8)
    net.step()
    small_product(geo, sub, pick, step, conv_s, acc_s, 5 * wide // 8, wide)
    finish(stats_s, acc_s, 4)
    net.end()


def small_product(geo, left, pick, step, conv, acc, first, last):
    for c in range(first, last, step):
        result = nt(left[...], pick(c))
        conv[:, c : c + step] = result.astype(BF16)
        for s in range(geo.slabs):
            for start, size, group in geo.small_pieces():
                piece = result[s * geo.small + start : s * geo.small + start + size]
                acc[2 * group, :, c : c + step] += fold(piece)
                acc[2 * group + 1, :, c : c + step] += fold(piece * piece)


def gather_taps(geo, net, live, zd, terms, full, taps):
    width = zd.shape[1]
    blank = jnp.zeros((8, width), F32)
    full[:, 0:CELLS, :] = jnp.zeros((width // 128, CELLS, 128), F32)
    full[:, CELLS + geo.rg : 2 * CELLS + geo.rg, :] = jnp.zeros((width // 128, CELLS, 128), F32)

    def slab(s):
        net.need(s, "zd")
        keep = alive(live, s)
        for start, size, group in geo.pieces(width):
            rows = pl.ds(pl.multiple_of(s * geo.rows + start, CELLS), size)
            scale, shift = terms[group]
            value = silu(zd[rows, :].astype(F32) * scale + shift)
            begin = CELLS + start + group * CELLS
            put(full, pl.ds(begin, size), value * (geo.mask(size, group, width) * keep))
        for dy in range(3):
            for dx in range(3):
                picked = []
                for group in range(2):
                    for i in range(geo.ol if group else geo.og):
                        line = 2 * i + dy - 1
                        if line < 0:
                            picked.append(blank)
                            continue
                        begin = CELLS + group * (geo.rg + CELLS) + line * CELLS + dx - 1
                        picked.append(take(full, pl.ds(begin, 8, stride=2)))
                tap = dy * 3 + dx
                taps[at(s, geo.small), tap * width : (tap + 1) * width] = jnp.concatenate(
                    picked, axis=0
                ).astype(BF16)
        net.give(s, "taps")

    loop(1, slab)
    net.open()
    net.side.begin()
    loop(4, lambda s: slab(s + 1))
    net.side.step()
    loop(geo.slabs - 5, lambda s: slab(s + 5))


def stage_e(
    geo, net, live, count, zd, stats_d, norm, weight_0, weight_1, weight_2, conv, taps, full,
    acc,
):
    acc[...] = jnp.zeros(acc.shape, F32)
    terms = forward_terms(geo, count, stats_d, norm, zd.shape[1])
    gather_taps(geo, net, live, zd, terms, full, taps)
    net.turn(1)
    net.side.step()
    net.need(0, "we_0", "we_1", "we_2")
    step = 256
    third = weight_0.shape[1]
    for c in range(0, weight_0.shape[0], step):
        result = nt(taps[:, 0:third], weight_0[c : c + step, :])
        result = result + nt(taps[:, third : 2 * third], weight_1[c : c + step, :])
        result = result + nt(taps[:, 2 * third :], weight_2[c : c + step, :])
        conv[:, c : c + step] = result.astype(BF16)
        for s in range(geo.slabs):
            keep = alive(live, s)
            for start, size, group in geo.small_pieces():
                piece = result[s * geo.small + start : s * geo.small + start + size]
                piece = piece * (geo.small_mask(group, step) * keep)
                acc[2 * group, :, c : c + step] += fold(piece)
                acc[2 * group + 1, :, c : c + step] += fold(piece * piece)
    net.side.end()
    net.turn(2)
    finish(net.own, acc, 4)
    net.run()


def stage_f(geo, net, live, count, ze, stats_e, norm, weight, act, conv, acc):
    acc[...] = jnp.zeros(acc.shape, F32)
    width = ze.shape[1]
    terms = forward_terms(geo, count, stats_e, norm, width, True)

    def slab(s):
        keep = alive(live, s)
        rows = ze[at(s, geo.small), :].astype(F32)
        parts = []
        for start, size, group in geo.small_pieces():
            scale, shift = terms[group]
            value = silu(rows[start : start + size] * scale + shift)
            parts.append(value * (geo.small_mask(group, width) * keep))
        act[at(s, geo.small), :] = jnp.concatenate(parts, axis=0).astype(BF16)

    loop(geo.slabs, slab)
    half, step = weight.shape[0] // 2, 256
    net.need(0, "wf")

    def pick(c):
        return weight[c : c + step, :]

    small_product(geo, act, pick, step, conv, acc, 0, half)
    net.open()
    small_product(geo, act, pick, step, conv, acc, half, 2 * half)
    finish(net.own, acc, 4)
    net.run()


def stage_out(
    geo, net, live, count, zf, zs, stats_f, stats_s, norm_f, norm_s, cotg, cotl, outg, outl, grad,
    pooled_sums, pool, cot, acc,
):
    acc[...] = jnp.zeros(acc.shape, F32)
    cot[...] = jnp.zeros(cot.shape, F32)
    pool[...] = jnp.zeros(pool.shape, F32)
    width = zf.shape[1]
    step = 512
    terms_f = forward_terms(geo, count, stats_f, norm_f, width, True)
    terms_s = forward_terms(geo, count, stats_s, norm_s, width, True)

    def slab(s):
        net.need(s, "zf", "zs", "cotg", "cotl")
        keep = alive(live, s)
        for c in range(0, width, step):
            cols = slice(c, c + step)
            for i in range(geo.og):
                cot[i * 8 : i * 8 + geo.og, :] = cotg[s, i, :, cols].astype(F32)
            for i in range(geo.ol):
                for side in range(2):
                    begin = geo.sg + i * 8 + side * 4
                    cot[begin : begin + geo.ol, :] = cotl[2 * s + side, i, :, cols].astype(F32)
            rows_f = zf[at(s, geo.small), cols].astype(F32)
            rows_s = zs[at(s, geo.small), cols].astype(F32)
            grads = []
            for start, size, group in geo.small_pieces():
                part = slice(start, start + size)
                vf, vs = rows_f[part], rows_s[part]
                scale_f, shift_f = (item[:, cols] for item in terms_f[group])
                scale_s, shift_s = (item[:, cols] for item in terms_s[group])
                joined = vf * scale_f + vs * scale_s + (shift_f + shift_s)
                mask = geo.small_mask(group, step) * keep
                gate = sig(joined)
                held = joined * gate
                value = held * mask
                low = value.astype(BF16)
                dy = cot[part, :] * ((gate + held - held * gate) * mask)
                grads.append(dy)
                acc[3 * group, :, cols] += fold(dy)
                acc[3 * group + 1, :, cols] += fold(dy * vf)
                acc[3 * group + 2, :, cols] += fold(dy * vs)
                summed = fold(value)
                if group == 0:
                    for i in range(geo.og):
                        outg[s, i, :, cols] = value[i * 8 : i * 8 + geo.og].astype(BF16)
                    pool[s, 0:1, cols] = jnp.sum(summed, axis=0, keepdims=True) * (
                        1.0 / (geo.og * geo.og)
                    )
                else:
                    row = lax.broadcasted_iota(jnp.int32, (8, step), 0)
                    for side in range(2):
                        own = jnp.where((row >= 4) == (side == 1), summed, 0.0)
                        pool[s, 1 + side : 2 + side, cols] = jnp.sum(
                            own, axis=0, keepdims=True
                        ) * (1.0 / (geo.ol * geo.ol))
                        for i in range(geo.ol):
                            begin = i * 8 + side * 4
                            outl[2 * s + side, i, :, cols] = value[begin : begin + geo.ol].astype(
                                BF16
                            )
            grad[at(s, geo.small), cols] = jnp.concatenate(grads, axis=0).astype(BF16)
        net.give(s, "outg", "outl", "grad")
        pooled = pool[s]
        square = jnp.mean(pooled * pooled, axis=1, keepdims=True)
        normed = pooled * lax.rsqrt(square + 1e-06)
        acc[6] += normed
        acc[7] += normed * normed

    loop(geo.slabs, slab)
    finish(net.own, acc, 6)
    net.begin()
    finish(pooled_sums, acc, 2, 6)
    net.end()


def small_back(geo, live, s, grad, conv, terms, width, cols):
    keep = alive(live, s)
    rows_g = grad[at(s, geo.small), cols].astype(F32)
    rows_z = conv[at(s, geo.small), cols].astype(F32)
    parts = []
    for start, size, group in geo.small_pieces():
        scale, by_value, constant = (item[:, cols] for item in terms[group])
        part = slice(start, start + size)
        value = rows_g[part] * scale + rows_z[part] * by_value + constant
        parts.append(value * (geo.small_mask(group, width) * keep))
    return jnp.concatenate(parts, axis=0).astype(BF16)


def stage_f_back(
    geo, net, live, count, zf, zs, stats_f, stats_s, norm_f, norm_s, grad, sums, act, sub, weight,
    short, ze, stats_e, norm_e, wgrad_f, wgrad_s, back_sub, back_e, ngrad_f, ngrad_s, dzf, dzs, acc,
):
    acc[...] = jnp.zeros(acc.shape, F32)
    width = zf.shape[1]
    step = 512
    rows_f, rows_s = ((0, 1), (3, 4)), ((0, 2), (3, 5))
    terms_f = backward_terms(geo, count, stats_f, norm_f, sums, ngrad_f, width, True, rows_f)
    terms_s = backward_terms(geo, count, stats_s, norm_s, sums, ngrad_s, width, True, rows_s)

    def slab(s):
        net.need(s, "zf", "zs", "grad")
        for c in range(0, width, step):
            cols = slice(c, c + step)
            dzf[at(s, geo.small), cols] = small_back(geo, live, s, grad, zf, terms_f, step, cols)
            dzs[at(s, geo.small), cols] = small_back(geo, live, s, grad, zs, terms_s, step, cols)

    loop(geo.slabs, slab)
    net.open()
    net.side.begin()
    net.need(0, "wf")
    block = 256
    terms_e = forward_terms(geo, count, stats_e, norm_e, ze.shape[1], True)
    for c in range(0, act.shape[1], block):
        cols = slice(c, c + block)
        result = nn(dzf[...], weight[:, cols])
        for s in range(geo.slabs):
            keep = alive(live, s)
            rows = ze[s * geo.small : (s + 1) * geo.small, cols].astype(F32)
            parts = []
            for start, size, group in geo.small_pieces():
                scale, shift = (item[:, cols] for item in terms_e[group])
                value = rows[start : start + size]
                mask = geo.small_mask(group, block) * keep
                piece = result[s * geo.small + start : s * geo.small + start + size]
                piece = piece * (slope(value * scale + shift) * mask)
                parts.append(piece)
                acc[2 * group, :, cols] += fold(piece)
                acc[2 * group + 1, :, cols] += fold(piece * value)
            back_e[s * geo.small : (s + 1) * geo.small, cols] = jnp.concatenate(
                parts, axis=0
            ).astype(BF16)
    finish(net.own, acc, 4)
    net.begin()
    net.need(0, "sub", "act", "ws")
    for c in range(0, width, block):
        cols = slice(c, c + block)
        put_pieces(wgrad_s, c, tn(dzs[:, cols], sub[...]))
        if c == width // 4:
            net.step()
    net.step()
    net.turn(1)
    for c in range(0, width, block):
        cols = slice(c, c + block)
        put_pieces(wgrad_f, c, tn(dzf[:, cols], act[...]))
        if c == width // 4:
            net.side.step()
    net.side.step()
    net.turn(2)
    for c in range(0, sub.shape[1], block):
        cols = slice(c, c + block)
        back_sub[:, cols] = nn(dzs[...], short[:, cols]).astype(BF16)
    net.side.end()
    net.end()


def stage_e_back(
    geo, net, live, count, ze, stats_e, norm_e, back_e, sums_e, zd, stats_d, norm_d, weight_0, weight_1,
    weight_2, taps, wgrad, back_d, ngrad, full, dze, moved, parity, acc,
):
    acc[...] = jnp.zeros(acc.shape, F32)
    width = ze.shape[1]
    terms_e = backward_terms(geo, count, stats_e, norm_e, sums_e, ngrad, width, True)
    terms_d = forward_terms(geo, count, stats_d, norm_d, width)

    def shift(s):
        value = small_back(geo, live, s, back_e, ze, terms_e, width, slice(0, width)).astype(F32)
        blank = jnp.zeros((8, width), F32)
        down = jnp.concatenate(
            [value[8 : geo.sg], blank, value[geo.sg + 8 :], blank], axis=0
        )
        size = geo.small
        dze[at(s, size), :] = value.astype(BF16)
        moved[0, at(s, size), :] = pltpu.roll(value, size - 1, 0).astype(BF16)
        moved[1, at(s, size), :] = down.astype(BF16)
        moved[2, at(s, size), :] = pltpu.roll(down, size - 1, 0).astype(BF16)

    loop(2, shift)
    net.open()
    loop(geo.slabs - 2, lambda s: shift(s + 2))

    net.need(0, "we_0", "we_1", "we_2")

    def tap(dy, dx):
        return (weight_0, weight_1, weight_2)[dy][:, dx * width : (dx + 1) * width]

    def grads(first, last):
        for t in range(first, last):
            result = tn(dze[...], taps[:, t * width : (t + 1) * width])
            put_pieces(wgrad, 0, result, t * width)

    parity[0] = nn(dze[...], tap(1, 1))
    parity[1] = nn(dze[...], tap(1, 2)) + nn(moved[0], tap(1, 0))
    parity[2] = nn(dze[...], tap(2, 1)) + nn(moved[1], tap(0, 1))
    parity[3] = (
        nn(dze[...], tap(2, 2))
        + nn(moved[0], tap(2, 0))
        + nn(moved[1], tap(0, 2))
        + nn(moved[2], tap(0, 0))
    )

    def slab(s):
        net.need(s, "zd")
        keep = alive(live, s)
        for group in range(2):
            for i in range(geo.ol if group else geo.og):
                for a in range(2):
                    for b in range(2):
                        begin = group * geo.rg + (2 * i + a) * CELLS + b
                        source = s * geo.small + group * geo.sg + i * 8
                        part = parity[2 * a + b, pl.ds(pl.multiple_of(source, 8), 8), :]
                        put(full, pl.ds(begin, 8, stride=2), part)
        for start, size, group in geo.pieces(width):
            rows = pl.ds(pl.multiple_of(s * geo.rows + start, CELLS), size)
            scale, shift_d = terms_d[group]
            value = zd[rows, :].astype(F32)
            mask = geo.mask(size, group, width) * keep
            piece = take(full, pl.ds(start, size)) * (slope(value * scale + shift_d) * mask)
            back_d[rows, :] = piece.astype(BF16)
            acc[2 * group] += fold(piece)
            acc[2 * group + 1] += fold(piece * value)
        net.give(s, "back_d")

    loop(geo.slabs, slab)
    finish(net.own, acc, 4)
    net.begin()
    net.need(0, "taps")
    grads(0, 3)
    net.step()
    grads(3, 6)
    net.step()
    grads(6, 9)
    net.end()


def wide_back(geo, live, s, grad, conv, terms, low):
    width = conv.shape[1]
    keep = alive(live, s)
    for start, size, group in geo.pieces(width):
        rows = pl.ds(pl.multiple_of(s * geo.rows + start, CELLS), size)
        scale, by_value, constant = terms[group]
        value = grad[rows, :].astype(F32) * scale + conv[rows, :].astype(F32) * by_value + constant
        low[rows, :] = (value * (geo.mask(size, group, width) * keep)).astype(BF16)


def stage_d_back(
    geo, net, live, count, zd, stats_d, norm_d, back_d, sums_d, hid, packed, zc, stats_c, norm_c,
    back_sub, weight, wgrad, joined, ngrad, dzd, full, acc,
):
    acc[...] = jnp.zeros(acc.shape, F32)
    width = zc.shape[1]
    terms_d = backward_terms(geo, count, stats_d, norm_d, sums_d, ngrad, zd.shape[1])
    terms_c = forward_terms(geo, count, stats_c, norm_c, width)

    def slab(s):
        net.need(s, "back_d", "zd", "zc", "packed")
        wide_back(geo, live, s, back_d, zd, terms_d, dzd)
        put(full, pl.ds(0, geo.rows), nn(dzd[at(s, geo.rows), :], weight[...]))
        extra = back_sub[at(s, geo.small), :].astype(F32)
        for k, start in enumerate(even_rows(geo)):
            place = pl.ds(start, 8, stride=2)
            put(full, place, take(full, place) + extra[k * 8 : k * 8 + 8])
        keep = alive(live, s)
        for start, size, group in geo.pieces(width):
            rows = pl.ds(pl.multiple_of(s * geo.rows + start, CELLS), size)
            scale, shift = terms_c[group]
            value = zc[rows, :].astype(F32)
            pre = value * scale + shift + packed[rows, :].astype(F32)
            mask = geo.mask(size, group, width) * keep
            piece = take(full, pl.ds(start, size)) * (slope(pre) * mask)
            joined[rows, :] = piece.astype(BF16)
            acc[2 * group] += fold(piece)
            acc[2 * group + 1] += fold(piece * value)
        net.give(s, "joined")

    loop(1, slab)
    net.open()
    loop(4, lambda s: slab(s + 1))
    net.turn(1)
    loop(geo.slabs - 5, lambda s: slab(s + 5))
    net.turn(2)
    finish(net.own, acc, 4)
    block = 256
    net.begin()
    net.need(0, "hid")
    for c in range(0, dzd.shape[1], block):
        put_pieces(wgrad, c, tn(dzd[:, c : c + block], hid[...]))
        net.step()
    net.end()


def stage_c_back(
    geo, net, live, count, zc, stats_c, norm_c, joined, sums_c, zb, stats_b, norm_b, weight, wgrad,
    back_b, ngrad, dzc, act, acc,
):
    acc[...] = jnp.zeros(acc.shape, F32)
    terms_c = backward_terms(geo, count, stats_c, norm_c, sums_c, ngrad, zc.shape[1])
    terms_b = forward_terms(geo, count, stats_b, norm_b, zb.shape[1])
    width = zb.shape[1]

    def slab(s):
        net.need(s, "joined", "zc", "zb")
        wide_back(geo, live, s, joined, zc, terms_c, dzc)
        result = nn(dzc[at(s, geo.rows), :], weight[...])
        keep = alive(live, s)
        for start, size, group in geo.pieces(width):
            rows = pl.ds(pl.multiple_of(s * geo.rows + start, CELLS), size)
            scale, shift = terms_b[group]
            value = zb[rows, :].astype(F32)
            pre = value * scale + shift
            mask = geo.mask(size, group, width) * keep
            gate = sig(pre)
            held = pre * gate
            act[rows, :] = (held * mask).astype(BF16)
            piece = result[start : start + size] * ((gate + held - held * gate) * mask)
            back_b[rows, :] = piece.astype(BF16)
            acc[2 * group] += fold(piece)
            acc[2 * group + 1] += fold(piece * value)
        net.give(s, "back_b")

    loop(1, slab)
    net.open()
    loop(geo.slabs - 1, lambda s: slab(s + 1))
    net.turn(2)
    finish(net.own, acc, 4)
    net.begin()
    block = 256
    for c in range(0, dzc.shape[1], block):
        put_pieces(wgrad, c, tn(dzc[:, c : c + block], act[...]))
        if c < 2 * block:
            net.step()
    net.end()


def stage_b_back(
    geo, net, live, count, zb, stats_b, norm_b, back_b, sums_b, za, stats_a, norm_a, weight, taps,
    wgrad, back_a, ngrad, dtaps, stacked, total, acc,
):
    acc[...] = jnp.zeros(acc.shape, F32)
    width = za.shape[1]
    terms_b = backward_terms(geo, count, stats_b, norm_b, sums_b, ngrad, width)
    terms_a = forward_terms(geo, count, stats_a, norm_a, width)
    clear_halo(geo, dtaps)
    for t in range(9):
        stacked[t * width : (t + 1) * width, :] = weight[:, t * width : (t + 1) * width]

    def fill(s):
        keep = alive(live, s)
        values = []
        for start, size, group in geo.pieces(width):
            rows = pl.ds(pl.multiple_of(s * geo.rows + start, CELLS), size)
            scale, by_value, constant = terms_b[group]
            value = back_b[rows, :].astype(F32) * scale + zb[rows, :].astype(F32) * by_value
            values.append((value + constant) * (geo.mask(size, group, width) * keep))
        spread_taps(geo, dtaps, s, values, True)

    loop(2, fill)
    net.open()
    loop(geo.slabs - 2, lambda s: fill(s + 2))
    net.turn(1)
    span = geo.halo - 2 * CELLS
    total[...] = jnp.zeros(total.shape, F32)

    def slab(s):
        result = None
        for dy in range(3):
            begin = pl.multiple_of(s * geo.halo + (2 - dy) * CELLS, CELLS)
            term = nn(
                dtaps[pl.ds(begin, span), :], stacked[dy * 3 * width : (dy + 1) * 3 * width, :]
            )
            result = term if result is None else result + term
        keep = alive(live, s)
        for group, (begin, size) in enumerate(((0, geo.rg), (geo.rg + CELLS, geo.rl))):
            rows = pl.ds(pl.multiple_of(s * geo.rows + group * geo.rg, CELLS), size)
            scale, shift = terms_a[group]
            value = za[rows, :].astype(F32)
            mask = geo.mask(size, group, width) * keep
            piece = result[begin : begin + size] * (slope(value * scale + shift) * mask)
            back_a[rows, :] = piece.astype(BF16)
            acc[2 * group] += fold(piece)
            acc[2 * group + 1] += fold(piece * value)

    def grads(s):
        net.need(s, "taps")
        own = dtaps[
            pl.ds(pl.multiple_of(s * geo.halo + CELLS, CELLS), span), width : 2 * width
        ]
        for dy in range(3):
            begin = pl.multiple_of(s * geo.halo + dy * CELLS, CELLS)
            total[:, dy * 3 * width : (dy + 1) * 3 * width] += tn(own, taps[pl.ds(begin, span), :])

    loop(geo.slabs, slab)
    net.turn(2)
    finish(net.own, acc, 4)
    part = geo.slabs // 3
    net.begin()
    loop(part, grads)
    net.step()
    loop(part, lambda s: grads(s + part))
    net.step()
    loop(geo.slabs - 2 * part, lambda s: grads(s + 2 * part))
    put_pieces(wgrad, 0, total[...])
    net.end()


def stage_a_back(
    geo, net, live, count, za, stats_a, norm_a, back_a, sums_a, packed, joined, weight, wgrad, grad,
    ngrad, dza,
):
    terms_a = backward_terms(geo, count, stats_a, norm_a, sums_a, ngrad, za.shape[1])
    loop(2, lambda s: wide_back(geo, live, s, back_a, za, terms_a, dza))
    net.open()
    loop(geo.slabs - 2, lambda s: wide_back(geo, live, s + 2, back_a, za, terms_a, dza))
    net.need(0, "packed")
    put_pieces(wgrad, 0, tn(dza[...], packed[...]))
    net.turn(1)

    net.need(0, "joined")

    def slab(s):
        result = nn(dza[at(s, geo.rows), :], weight[...])
        rows = at(s, geo.rows)
        grad[rows, :] = (result + joined[rows, :].astype(F32)).astype(BF16)
        net.give(s, "grad")

    part = geo.slabs // 3
    for number in range(3):
        begin = number * part
        size = part if number < 2 else geo.slabs - begin
        loop(size, lambda s: slab(s + begin))
        net.turn(number + 2)
    net.turn(5)
    net.close()


def last_kernel(geo, upright, grad, hid, *refs):
    count = len(upright)
    rows_in, refs = refs[:count], refs[count:]
    dxg, dxl, outg, outl = refs[:4]
    targets = refs[4:]
    result = grad[...].astype(F32)
    half = CELLS // 2
    for i in range(geo.hg):
        dxg[0, i] = result[i * CELLS : i * CELLS + geo.hg]
        outg[0, i] = hid[i * CELLS : (i + 1) * CELLS, :][0 : geo.hg]
    for i in range(geo.hl):
        begin = geo.rg + i * CELLS
        low = hid[begin : begin + CELLS, :]
        for side in range(2):
            part = begin + side * half
            dxl[side, i] = result[part : part + geo.hl]
            outl[side, i] = low[side * half : side * half + geo.hl]

    def write(k):
        @pl.when(pl.program_id(0) == k % geo.slabs)
        def one():
            source, target = rows_in[k], targets[k]
            rows = source.shape[0] * source.shape[1]
            whole = source[...].astype(F32).reshape(rows, source.shape[2])
            target[...] = whole.T if upright[k] else whole

    for k in range(count):
        write(k)


def run_last(geo, grad, hid, parts, global_shape, local_shape):
    def whole(shape):
        return pl.BlockSpec(shape, lambda s: (0,) * len(shape))

    upright = [part.shape[0] * part.shape[1] >= 128 for part in parts]
    shapes = []
    for turn, part in zip(upright, parts):
        rows = part.shape[0] * part.shape[1]
        shapes.append((part.shape[2], rows) if turn else (rows, part.shape[2]))
    views = [
        pl.BlockSpec((1,) + global_shape[1:], lambda s: (s, 0, 0, 0)),
        pl.BlockSpec((2,) + local_shape[1:], lambda s: (s, 0, 0, 0)),
    ]
    outs = pl.pallas_call(
        functools.partial(last_kernel, geo, upright),
        grid=(geo.slabs,),
        out_shape=[
            jax.ShapeDtypeStruct(shape, dtype)
            for dtype in (F32, BF16)
            for shape in (global_shape, local_shape)
        ]
        + [jax.ShapeDtypeStruct(shape, F32) for shape in shapes],
        in_specs=[
            pl.BlockSpec((geo.rows, item.shape[1]), lambda s: (s, 0)) for item in (grad, hid)
        ]
        + [whole(part.shape) for part in parts],
        out_specs=views + views + [whole(shape) for shape in shapes],
        compiler_params=pltpu.CompilerParams(vmem_limit_bytes=VMEM_CAP),
        name="last",
    )(grad, hid, *parts)
    return outs[:4], [item if turn else item.T for turn, item in zip(upright, outs[4:])]


class Group:
    def __init__(self, kind, reps, shards):
        rep, shard = lax.axis_index("rep"), lax.axis_index("fsdp")
        chip, core = shard // 2, lax.rem(shard, 2)
        wide = reps // 2
        low, high = lax.rem(rep, 2), rep // wide
        first = core == 0
        if kind == CORES:
            self.size, self.me = 2, core
            self.address = lambda k: {"fsdp": chip * 2 + k}
        elif kind == CHIPS:
            self.size, self.me = shards // 2, chip
            self.address = lambda k: {"fsdp": k * 2 + core}
        elif kind == SHARDS:
            self.size, self.me = shards, shard
            self.address = lambda k: {"fsdp": k}
        elif kind == REPLICAS:
            self.size, self.me = reps, rep
            self.address = lambda k: {"rep": k}
        elif kind == CLOSE:
            self.size, self.me = 2, jnp.where(first, low, high)
            self.address = lambda k: {
                "rep": jnp.where(first, rep - low + k, rep - high * wide + k * wide)
            }
        elif kind == SLANTED:
            self.size = wide * (shards // 2)
            self.me = jnp.where(first, rep // 2, lax.rem(rep, wide)) * (shards // 2) + chip

            def across(k):
                far = k // (shards // 2)
                return {
                    "rep": jnp.where(first, far * 2 + low, high * wide + far),
                    "fsdp": lax.rem(k, shards // 2) * 2 + core,
                }

            self.address = across
        else:
            self.size = wide
            self.me = jnp.where(first, rep // 2, lax.rem(rep, wide))
            self.address = lambda k: {"rep": jnp.where(first, k * 2 + low, high * wide + k)}

    def other(self, hop):
        return lax.rem(self.me + hop, self.size)


class Sums:
    def __init__(self, reps, shards, own, out, buffers, sems):
        self.own, self.out, self.buffers, self.sems = own, out, buffers, sems
        self.groups = [Group(kind, reps, shards) for kind in (CORES, CHIPS, REPLICAS)]
        self.phase = 0
        self.copies = []

    def send(self, source):
        group, buffer = self.groups[self.phase], self.buffers[self.phase]
        self.copies = []
        for hop in range(1, group.size):
            copy = pltpu.make_async_remote_copy(
                source, buffer.at[group.me], self.sems[2 * self.phase].at[hop],
                self.sems[2 * self.phase + 1].at[hop], device_id=group.address(group.other(hop)),
                device_id_type=MESH,
            )
            copy.start()
            self.copies.append(copy)

    def begin(self):
        self.send(self.own)
        self.buffers[0][self.groups[0].me] = self.own[...]

    def total(self):
        for copy in self.copies:
            copy.wait()
        buffer = self.buffers[self.phase]
        total = buffer[0]
        for k in range(1, self.groups[self.phase].size):
            total = total + buffer[k]
        return total

    def step(self):
        total = self.total()
        self.phase += 1
        group, buffer = self.groups[self.phase], self.buffers[self.phase]
        buffer[group.me] = total
        self.send(buffer.at[group.me])

    def end(self):
        while self.phase < 2:
            self.step()
        self.out[...] = self.total()


class In:
    def __init__(self, name, array, rows=None):
        self.name, self.array, self.rows = name, array, rows


class Out:
    def __init__(self, name, shape, dtype, rows):
        self.name, self.shape, self.dtype, self.rows = name, shape, dtype, rows


class Stream:
    def __init__(self, source, target, sems, rows, slabs):
        self.source, self.target, self.sems, self.rows, self.slabs = source, target, sems, rows, slabs

    def copy(self, s):
        if self.rows is None:
            return pltpu.make_async_copy(self.source, self.target, self.sems.at[0])
        place = at(s, self.rows)
        return pltpu.make_async_copy(self.source.at[place], self.target.at[place], self.sems.at[s])


class Net:
    def __init__(self, reps, shards, sums=None, side=None, jobs=(), plans=(), ins=(), outs=()):
        self.ins, self.outs = dict(ins), dict(outs)
        self.reps, self.shards = reps, shards
        self.sums, self.side, self.jobs, self.plans = sums, side, jobs, plans
        self.own = None if sums is None else sums.own
        self.opened = False
        self.started, self.finished = set(), set()

    def enter(self):
        rep, shard = lax.axis_index("rep"), lax.axis_index("fsdp")
        barrier = pltpu.get_barrier_semaphore()
        for hop in range(1, self.shards):
            other = {"fsdp": lax.rem(shard + hop, self.shards)}
            pl.semaphore_signal(barrier, inc=1, device_id=other, device_id_type=MESH)
        for hop in range(1, self.reps):
            other = {"rep": lax.rem(rep + hop, self.reps)}
            pl.semaphore_signal(barrier, inc=1, device_id=other, device_id_type=MESH)
        self.greeted = self.shards + self.reps - 2
        if any(job.kind == CROSS for job in self.jobs):
            group = Group(SLANTED, self.reps, self.shards)
            chips = self.shards // 2
            for far in range(1, self.reps // 2):
                for step in range(1, chips):
                    other = lax.rem(group.me // chips + far, self.reps // 2) * chips
                    other = group.address(other + lax.rem(group.me + step, chips))
                    pl.semaphore_signal(barrier, inc=1, device_id=other, device_id_type=MESH)
                    self.greeted += 1

    def load(self):
        blocks = [stream for stream in self.ins.values() if stream.rows is not None]
        if blocks:

            def start(s):
                for stream in blocks:
                    stream.copy(s).start()

            loop(blocks[0].slabs, start)
        for stream in self.ins.values():
            if stream.rows is None:
                stream.copy(0).start()

    def need(self, s, *names):
        for name in names:
            self.ins[name].copy(s).wait()

    def give(self, s, *names):
        for name in names:
            self.outs[name].copy(s).start()

    def open(self):
        if not self.opened:
            self.opened = True
            pl.semaphore_wait(pltpu.get_barrier_semaphore(), self.greeted)
            self.turn(0)

    def turn(self, number):
        for k, (start, end) in enumerate(self.plans):
            if end == number:
                self.finish(k)
        for k, (start, end) in enumerate(self.plans):
            if start == number:
                self.started.add(k)
                self.jobs[k].start()

    def finish(self, k):
        assert k in self.started and k not in self.finished
        self.finished.add(k)
        self.jobs[k].finish()

    def job_out(self, k):
        return self.jobs[k].out

    def begin(self):
        self.open()
        self.sums.begin()

    def step(self):
        self.sums.step()

    def end(self):
        self.sums.end()
        self.close()

    def run(self):
        self.begin()
        self.end()

    def close(self):
        for k in range(len(self.jobs)):
            if k not in self.finished:
                self.finish(k)
        blocks = list(self.outs.values())
        if blocks:

            def wait(s):
                for stream in blocks:
                    stream.copy(s).wait()

            loop(blocks[0].slabs, wait)


class Job:
    GROUPS = {
        PAIR: CORES, JOIN: CORES, LINE: CHIPS, SPREAD: CHIPS, ALL: SHARDS, SHARE: REPLICAS,
        HALF: CLOSE, NEAR: CLOSE, REST: APART, OTHERS: APART, CROSS: SLANTED,
    }

    def __init__(self, kind, reps, shards, sources, out, held, send, recv):
        self.kind, self.sources, self.out, self.held = kind, sources, out, held
        self.send, self.recv = send, recv
        self.reps, self.chips = reps, shards // 2
        self.rep, shard = lax.axis_index("rep"), lax.axis_index("fsdp")
        self.chip, self.core = shard // 2, lax.rem(shard, 2)
        self.group = Group(self.GROUPS[kind], reps, shards)

    def give(self, source, target, hop):
        k = len(self.copies)
        if hop == 0:
            copy = pltpu.make_async_copy(source, target, self.send.at[k])
        else:
            copy = pltpu.make_async_remote_copy(
                source, target, self.send.at[k], self.recv.at[k],
                device_id=self.group.address(self.group.other(hop)), device_id_type=MESH,
            )
        copy.start()
        self.copies.append(copy)

    def start(self):
        self.copies = []
        kind, out, source, group = self.kind, self.out, self.sources[0], self.group
        order = list(range(1, group.size)) + [0]
        wide = self.reps // 2
        first = self.core == 0
        if kind == SPREAD:
            for hop in order[:-1]:
                self.give(source.at[self.rep], out.at[self.rep, group.size - hop - 1], hop)
        elif kind == NEAR:
            self.give(out.at[self.rep], out.at[self.rep], 1)
        elif kind == OTHERS:
            low, high = lax.rem(self.rep, 2), self.rep // wide
            partner = jnp.where(
                first, self.rep + 1 - 2 * low, self.rep + (1 - 2 * high) * wide
            )
            for hop in order[:-1]:
                for place in (self.rep, partner):
                    self.give(out.at[place], out.at[place], hop)
        elif kind == JOIN:
            for hop in order:
                for step in range(1, self.chips):
                    chip = lax.rem(self.chip + step, self.chips)
                    self.give(source.at[:, step - 1], out.at[chip, self.core], hop)
                self.give(self.sources[1], out.at[self.chip, self.core], hop)
        elif kind == CROSS:
            for hop in order:
                other = group.other(hop)
                block = source.at[other // self.chips, lax.rem(other, self.chips)]
                self.give(block, self.held.at[group.me], hop)
        elif kind in (ALL, SHARE):
            for hop in order:
                self.give(source, out.at[group.me], hop)
        elif kind == HALF:
            low, high = lax.rem(self.rep, 2), self.rep // wide
            mine = jnp.where(first, low, high * wide)
            theirs = jnp.where(first, 1 - low, (1 - high) * wide)
            step = jnp.where(first, 2, 1)
            for k in range(wide):
                self.give(source.at[theirs + k * step], self.held.at[1, k], 1)
            for k in range(wide):
                self.give(source.at[mine + k * step], self.held.at[0, k], 0)
        else:
            for hop in order:
                self.give(source.at[group.other(hop)], self.held.at[group.me], hop)

    def finish(self):
        for copy in self.copies:
            copy.wait()
        held, out = self.held, self.out
        if held is None:
            return
        members = held.shape[0]
        blocks = held.shape[1:-2]

        def one(index):
            place = (index // blocks[-1], lax.rem(index, blocks[-1])) if len(blocks) == 2 else (
                (index,) if blocks else ()
            )
            total = held[(0,) + place].astype(F32)
            for k in range(1, members):
                total = total + held[(k,) + place].astype(F32)
            out[place[::-1] if self.kind == PAIR else place] = total.astype(BF16)

        if blocks:
            loop(blocks[0] * (blocks[1] if len(blocks) == 2 else 1), one)
        else:
            total = held[0].astype(F32)
            for k in range(1, members):
                total = total + held[k].astype(F32)
            out[...] = total.astype(BF16)


def job_shapes(kind, reps, shards, shape):
    chips = shards // 2
    if kind == SPREAD:
        return None, (reps, chips - 1) + shape[1:], chips
    if kind in (NEAR, OTHERS):
        return None, shape, reps
    if kind == CROSS:
        return (shape[0] * shape[1],) + shape[2:], shape[2:], shape[0] * shape[1]
    if kind == JOIN:
        return None, (chips, 2, reps) + shape[2:], 2 * chips
    if kind == ALL:
        return None, (shards,) + shape, shards
    if kind == PAIR:
        return shape, (shape[2], shape[1]) + shape[3:], 2
    if kind == SHARE:
        return None, (reps,) + shape, reps
    if kind == HALF:
        return (2, reps // 2) + shape[1:], (reps // 2,) + shape[1:], reps
    return shape, shape[1:], shape[0]


VMEM_CAP = 60 << 20
FAR = (SPREAD, NEAR, OTHERS)


def sums_scratch(reps, shards, shape, own):
    sizes = (2, shards // 2, reps)
    return (
        [pltpu.VMEM(shape, F32)] * own
        + [pltpu.VMEM((size,) + shape, F32) for size in sizes]
        + [pltpu.SemaphoreType.DMA((size,)) for size in sizes for unused in range(2)]
    )


def run(kernel, geo, reps, shards, number, live, operands, results, scratch, sums, jobs, side, far=()):
    own_results = len(results)
    extra = []
    spaces = []
    flowing = []
    internal = []
    plain_results = []
    for k, item in enumerate(results):
        if isinstance(item, Out):
            extra.append(pltpu.VMEM(item.shape, item.dtype))
            if item.rows:
                extra.append(pltpu.SemaphoreType.DMA((geo.slabs,)))
            flowing.append((k, item))
            plain_results.append((item.shape, item.dtype))
        else:
            plain_results.append(item)
        internal.append(isinstance(item, Out) and not item.rows)
        spaces.append(pltpu.HBM if isinstance(item, Out) else pltpu.VMEM)
    results = plain_results
    streamed = [(k, item) for k, item in enumerate(operands) if isinstance(item, In)]
    operands = [item.array if isinstance(item, In) else item for item in operands]
    for k, item in streamed:
        extra.append(pltpu.VMEM(item.array.shape, item.array.dtype))
        extra.append(pltpu.SemaphoreType.DMA((1 if item.rows is None else geo.slabs,)))
    arrays = []
    shapes = []
    targets = []
    kept = {}
    for kind, sources, start, end in jobs:
        source = sources[0]
        if isinstance(source, int):
            shape, dtype = shapes[source]
        elif isinstance(source, str):
            shape, dtype = results[int(source)]
        else:
            shape, dtype = source.shape, source.dtype
        held, out, copies = job_shapes(kind, reps, shards, shape)
        shapes.append((out, dtype))
        extra += [] if held is None else [pltpu.VMEM(held, BF16)]
        extra += [pltpu.SemaphoreType.DMA((copies,))] * 2
        if kind in (NEAR, OTHERS) and isinstance(source, int):
            targets.append(targets[source])
        else:
            if kind in (NEAR, OTHERS):
                kept[len(arrays)] = len(results)
            targets.append(len(results))
            results.append(shapes[-1])
            spaces.append(pltpu.HBM if kind in FAR else pltpu.VMEM)
        arrays += [item for item in sources if not isinstance(item, (int, str))]
    own_or_job = len(results)
    keep = [k for k in range(own_or_job) if not (k < own_results and internal[k])]
    own_or_job = len(results)
    operands = tuple(operands)
    near = len(operands)
    if side is not None:
        operands += (side,)
        results.append((side.shape, F32))
        spaces.append(pltpu.VMEM)
        extra += sums_scratch(reps, shards, side.shape, 0)
    if sums is not None:
        results.append((sums, F32))
        spaces.append(pltpu.VMEM)
        extra += sums_scratch(reps, shards, sums, 1)
    inputs = 1 + len(operands)
    remote = bool(jobs) or sums is not None
    keep += list(range(own_or_job, len(results)))
    far = tuple(far) + tuple(k for k, unused in streamed)

    def whole(*refs):
        sources_in = list(refs[inputs : inputs + len(arrays)])
        first_out = inputs + len(arrays)
        outs = [None] * len(results)
        for place, k in enumerate(keep):
            outs[k] = refs[first_out + place]
        more = list(refs[first_out + len(keep) :])
        own_refs = list(outs[:own_results])
        out_streams, in_streams = [], []
        for k, item in flowing:
            own_refs[k] = more.pop(0)
            if item.rows:
                stream = Stream(own_refs[k], outs[k], more.pop(0), item.rows, geo.slabs)
                out_streams.append((item.name, stream))
            else:
                outs[k] = own_refs[k]
        given = list(refs[: 1 + len(operands)])
        for k, item in streamed:
            given[1 + k] = more.pop(0)
            stream = Stream(refs[1 + k], given[1 + k], more.pop(0), item.rows, geo.slabs)
            in_streams.append((item.name, stream))
        made = []
        for k, (kind, sources, start, end) in enumerate(jobs):
            refs_of = []
            for item in sources:
                if isinstance(item, int):
                    refs_of.append(made[item].out)
                elif isinstance(item, str):
                    refs_of.append(outs[int(item)])
                else:
                    refs_of.append(sources_in.pop(0))
            held = more.pop(0) if job_shapes(kind, reps, shards, refs_of[0].shape)[0] else None
            made.append(
                Job(kind, reps, shards, refs_of, outs[targets[k]], held, more.pop(0), more.pop(0))
            )
        beside, main = None, None
        if side is not None:
            beside = Sums(reps, shards, refs[near + 1], outs[own_or_job], more[0:3], more[3:9])
            more = more[9:]
        if sums is not None:
            main = Sums(reps, shards, more[0], outs[-1], more[1:4], more[4:10])
            more = more[10:]
        net = None
        if remote:
            plans = [job[2:] for job in jobs]
            net = Net(reps, shards, main, beside, made, plans, in_streams, out_streams)
            net.enter()
            net.load()
        kernel(geo, net, *given[: near + 1], *own_refs, *more)

    params = {"collective_id": number, "has_side_effects": True} if remote else {}
    outputs = pl.pallas_call(
        whole,
        out_shape=[jax.ShapeDtypeStruct(*results[k]) for k in keep],
        in_specs=[pl.BlockSpec(memory_space=pltpu.SMEM)]
        + [pl.BlockSpec(memory_space=pltpu.HBM if k in far else pltpu.VMEM) for k in range(len(operands))]
        + [
            pl.BlockSpec(memory_space=pltpu.HBM if k in kept else pl.ANY) for k in range(len(arrays))
        ],
        out_specs=[pl.BlockSpec(memory_space=spaces[k]) for k in keep],
        scratch_shapes=extra
        + [item if not isinstance(item, tuple) else pltpu.VMEM(*item) for item in scratch],
        input_output_aliases={inputs + k: keep.index(out) for k, out in kept.items()},
        compiler_params=pltpu.CompilerParams(vmem_limit_bytes=VMEM_CAP, **params),
        name=kernel.__name__,
    )(live, *operands, *arrays)
    placed = [None] * len(results)
    for place, k in enumerate(keep):
        placed[k] = outputs[place]
    return placed


def own_norms(first, second):
    flat = jnp.concatenate([first.reshape(-1), second.reshape(-1)]).astype(F32)
    size = -(-flat.shape[0] // 1024) * 1024
    return jnp.pad(flat, (0, size - flat.shape[0])).reshape(8, -1)


def all_norms(gathered, first, second):
    shards = gathered.shape[0]
    flat = gathered.reshape(shards, -1)
    split, last = first.size, first.size + second.size

    def whole(part):
        return part.reshape(shards, 2, -1).transpose(1, 0, 2).reshape(2, -1)

    return whole(flat[:, :split]), whole(flat[:, split:last])


def body(reps, shards, *arguments):
    (
        global_views, local_views, live, first_reduce, first_spatial, first_expand, first_norms,
        second_reduce, second_spatial, second_expand, second_short, second_norms, global_cotan,
        local_cotan,
    ) = arguments
    geo = Geometry(global_views.shape[0], global_views.shape[1], local_views.shape[1])
    assert local_views.shape[0] == 2 * geo.slabs
    channels = global_views.shape[3]
    ha, hb, hc, hd, he = (
        item.T.reshape(reps, -1, item.shape[0])
        for item in (first_reduce, first_spatial, first_expand, second_reduce, second_spatial)
    )
    he_0, he_1, he_2 = (he[:, :, k * he.shape[2] // 3 : (k + 1) * he.shape[2] // 3] for k in range(3))
    mid_1, mid_2 = first_reduce.shape[1] * shards, second_reduce.shape[1] * shards
    wide = second_expand.shape[1] * shards

    def rows_of(gathered):
        return gathered.reshape(-1, gathered.shape[-1])

    big, small = geo.total, geo.small_total

    numbers = iter(range(100))

    def go(kernel, operands, results, scratch, width=None, members=4, jobs=(), side=None, far=()):
        parts = {4: 2, 6: 4, 8: 2}[members]
        sums = None if width is None else (members * parts, width // parts)
        return run(
            kernel, geo, reps, shards, next(numbers), live, operands, results, scratch, sums,
            jobs, side, far,
        )

    def pieces(rows, columns):
        return ((2, shards // 2, reps, rows // (shards * reps), columns), BF16)

    def acc(width, members=4):
        return ((members, 8, width), F32)

    def stat(width):
        return ((8, width), F32)

    def both(width):
        return ((2, width), F32)

    more = go(
        stage_a, (global_views, local_views, second_short, second_expand),
        [
            Out("packed", (big, channels), BF16, geo.rows), Out("za", (big, mid_1), BF16, geo.rows),
            ((reps, second_short.shape[1] // reps, channels), BF16),
            ((reps, second_expand.shape[1] // reps, mid_2), BF16),
        ],
        [
            acc(mid_1), ((CELLS, channels), F32), ((mid_1, channels), BF16), (global_views.shape, BF16),
            (local_views.shape, BF16), pltpu.SemaphoreType.DMA((2,)),
        ],
        mid_1, 8,
        jobs=(
            (SPREAD, (ha,), 0, 1), (NEAR, (0,), 1, 2), (OTHERS, (0,), 2, 3),
            (JOIN, (0, ha), 3, 4),
            (SPREAD, (hb,), 0, 2), (NEAR, (4,), 2, 3), (OTHERS, (4,), 3, 5),
            (JOIN, (4, hb), 5, None),
            (SPREAD, (hc,), 0, 3), (NEAR, (8,), 3, 5), (OTHERS, (8,), 5, None),
            (SPREAD, (hd,), 0, 3), (NEAR, (11,), 3, 5), (OTHERS, (11,), 5, None),
            (ALL, (own_norms(first_norms, second_norms),), 1, None), (SPREAD, ("2",), 1, None),
        ),
        far=(0, 1),
    )
    packed, za, hs, hf, unused, wa, unused, wb, far_c, far_d, norms, far_s, sa = more
    count = sa
    wa, wb = rows_of(wa), rows_of(wb)
    norms_1, norms_2 = all_norms(norms, first_norms, second_norms)
    na, nb, nc = norms_1[:, :mid_1], norms_1[:, mid_1 : 2 * mid_1], norms_1[:, 2 * mid_1 :]
    nd, ne = norms_2[:, :mid_2], norms_2[:, mid_2 : 2 * mid_2]
    nf, ns = norms_2[:, 2 * mid_2 : 2 * mid_2 + wide], norms_2[:, 2 * mid_2 + wide :]
    zb, taps_b, wc, wd, far_s, far_e0, far_e1, far_e2, sb = go(
        stage_b, (count, In("za", za, geo.rows), sa, na, In("wb", wb)),
        [
            Out("zb", (big, mid_1), BF16, geo.rows),
            Out("taps", (geo.halo_total, 3 * mid_1), BF16, geo.halo),
        ],
        [acc(mid_1)], mid_1,
        jobs=(
            (JOIN, (far_c, hc), 0, None), (JOIN, (far_d, hd), 0, None),
            (NEAR, (far_s,), 0, 1), (OTHERS, (2,), 1, None),
            (SPREAD, (he_0,), 0, None), (SPREAD, (he_1,), 0, None), (SPREAD, (he_2,), 0, None),
        ),
    )
    wc = rows_of(wc)
    zc, ws, far_e0, far_f, sc = go(
        stage_c, (count, In("zb", zb, geo.rows), sb, nb, wc),
        [Out("zc", (big, channels), BF16, geo.rows)],
        [((geo.rows, mid_1), BF16), acc(channels)], channels,
        jobs=(
            (JOIN, (far_s, hs), 0, None), (NEAR, (far_e0,), 0, 1), (OTHERS, (1,), 1, None),
            (SPREAD, (hf,), 0, None),
        ),
    )
    wd, ws = rows_of(wd), rows_of(ws)
    hid, zd, sub, zs, local_s, we_0, far_e1, we_1, far_e2, we_2, far_f, sd = go(
        stage_d,
        (
            count, In("zc", zc, geo.rows), sc, nc, In("packed", packed, geo.rows), In("wd", wd),
            In("ws", ws),
        ),
        [
            Out("hid", (big, channels), BF16, geo.rows), Out("zd", (big, mid_2), BF16, geo.rows),
            Out("sub", (small, channels), BF16, geo.small),
            ((small, wide), BF16), stat(wide // 2),
        ],
        [((channels // 128, geo.rows, 128), F32), acc(mid_2), acc(wide)], mid_2,
        jobs=(
            (JOIN, (far_e0, he_0), 0, 1),
            (NEAR, (far_e1,), 0, 1), (OTHERS, (1,), 1, 2), (JOIN, (1, he_1), 2, None),
            (NEAR, (far_e2,), 0, 1), (OTHERS, (4,), 1, 2), (JOIN, (4, he_2), 2, None),
            (NEAR, (far_f,), 1, None),
        ),
    )
    we = tuple(rows_of(item) for item in (we_0, we_1, we_2))
    late_we = tuple(In(name, item) for name, item in zip(("we_0", "we_1", "we_2"), we))
    ze, taps_e, unused, wf, ss, se = go(
        stage_e, (count, In("zd", zd, geo.rows), sd, nd, *late_we),
        [((small, mid_2), BF16), Out("taps", (small, 9 * mid_2), BF16, geo.small)],
        [((mid_2 // 128, geo.halo, 128), F32), acc(mid_2)], mid_2,
        jobs=((OTHERS, (far_f,), 0, 1), (JOIN, (0, hf), 1, None)), side=local_s,
    )
    wf = rows_of(wf)
    act_e, zf, sf = go(
        stage_f, (count, ze, se, ne, In("wf", wf)),
        [((small, mid_2), BF16), ((small, wide), BF16)], [acc(wide)], wide,
    )
    second_g, second_l, grad, local_pool, so = go(
        stage_out,
        (
            count, In("zf", zf, geo.small), In("zs", zs, geo.small), sf, ss, nf, ns,
            In("cotg", global_cotan, 1), In("cotl", local_cotan, 2),
        ),
        [
            Out("outg", global_cotan.shape, BF16, 1), Out("outl", local_cotan.shape, BF16, 2),
            Out("grad", (small, wide), BF16, geo.small),
            stat(wide // 4),
        ],
        [((geo.slabs, 8, wide), F32), ((geo.small, 512), F32), acc(wide, 8)], wide, 6,
    )
    unused, unused, back_sub, back_e, ngrad_f, ngrad_s, pair_f, pair_s, pool, qe = go(
        stage_f_back,
        (
            count, In("zf", zf, geo.small), In("zs", zs, geo.small), sf, ss, nf, ns,
            In("grad", grad, geo.small), so, In("act", act_e), In("sub", sub), In("wf", wf),
            In("ws", ws), ze, se, ne,
        ),
        [
            Out("wgrad_f", *pieces(wide, mid_2), 0), Out("wgrad_s", *pieces(wide, channels), 0), ((small, channels), BF16), ((small, mid_2), BF16),
            both(wide), both(wide),
        ],
        [((small, wide), BF16), ((small, wide), BF16), acc(mid_2)], mid_2,
        jobs=((PAIR, ("0",), 2, None), (PAIR, ("1",), 1, None)), side=local_pool,
    )
    views = count[8, 0] * 6.0
    pool = pool.reshape(2, wide)
    center = pool[0] / views
    spread = pool[1] / views - center * center
    pooled_std = jnp.mean(jnp.sqrt(spread + 1e-06))
    wgrad_e, back_d, ngrad_e, half_f, half_s, qd = go(
        stage_e_back,
        (
            count, ze, se, ne, back_e, qe, In("zd", zd, geo.rows), sd, nd, *late_we,
            In("taps", taps_e),
        ),
        [
            pieces(mid_2, 9 * mid_2), Out("back_d", (big, mid_2), BF16, geo.rows), both(mid_2),
        ],
        [
            ((mid_2 // 128, geo.halo, 128), F32), ((small, mid_2), BF16), ((3, small, mid_2), BF16), ((4, small, mid_2), F32),
            acc(mid_2),
        ],
        mid_2, jobs=((HALF, (pair_f,), 0, None), (HALF, (pair_s,), 0, None)),
    )
    wgrad_d, joined, ngrad_d, unused, half_e, unused, rest_s, line_f, qc = go(
        stage_d_back,
        (
            count, In("zd", zd, geo.rows), sd, nd, In("back_d", back_d, geo.rows), qd,
            In("hid", hid), In("packed", packed, geo.rows), In("zc", zc, geo.rows), sc, nc, back_sub,
            wd,
        ),
        [
            pieces(mid_2, channels), Out("joined", (big, channels), BF16, geo.rows), both(mid_2),
        ],
        [((big, mid_2), BF16), ((channels // 128, geo.rows, 128), F32), acc(channels)], channels,
        jobs=(
            (PAIR, (wgrad_e,), 0, 1), (HALF, (0,), 1, None),
            (REST, (half_f,), 0, 1), (REST, (half_s,), 0, 1), (LINE, (2,), 1, None),
        ),
    )
    wgrad_c, back_b, ngrad_c, pair_d, rest_e, line_s, qb = go(
        stage_c_back,
        (
            count, In("zc", zc, geo.rows), sc, nc, In("joined", joined, geo.rows), qc,
            In("zb", zb, geo.rows), sb, nb, wc,
        ),
        [
            pieces(channels, mid_1), Out("back_b", (big, mid_1), BF16, geo.rows), both(channels),
        ],
        [((big, channels), BF16), ((big, mid_1), BF16), acc(mid_1)], mid_1,
        jobs=(
            (PAIR, (wgrad_d,), 0, None), (REST, (half_e,), 0, None), (LINE, (rest_s,), 0, None),
        ),
    )
    wgrad_b, back_a, ngrad_b, unused, rest_d, unused, half_c, line_e, out_f, out_s, qa = go(
        stage_b_back,
        (count, zb, sb, nb, back_b, qb, za, sa, na, wb, In("taps", taps_b, geo.halo)),
        [pieces(mid_1, 9 * mid_1), ((big, mid_1), BF16), both(mid_1)],
        [
            ((geo.halo_total, 3 * mid_1), BF16), ((9 * mid_1, mid_1), BF16), (wb.shape, F32), acc(mid_1),
        ],
        mid_1,
        jobs=(
            (HALF, (pair_d,), 0, 1), (REST, (0,), 1, None), (PAIR, (wgrad_c,), 0, 1),
            (HALF, (2,), 1, None), (LINE, (rest_e,), 0, None), (SHARE, (line_f,), 1, None),
            (SHARE, (line_s,), 1, None),
        ),
    )
    more = go(
        stage_a_back,
        (count, za, sa, na, back_a, qa, In("packed", packed), In("joined", joined), wa),
        [
            pieces(mid_1, channels), Out("grad", (big, channels), BF16, geo.rows), both(mid_1),
        ],
        [((big, mid_1), BF16)],
        jobs=(
            (PAIR, (wgrad_b,), 0, 1), (HALF, (0,), 1, 2), (CROSS, (1,), 2, 3), (SHARE, (2,), 3, None),
            (PAIR, ("0",), 1, 2), (HALF, (4,), 2, 3), (CROSS, (5,), 3, 4), (SHARE, (6,), 4, None),
            (REST, (half_c,), 0, 1), (LINE, (8,), 1, 2), (SHARE, (9,), 2, None),
            (LINE, (rest_d,), 0, 1), (SHARE, (11,), 1, None), (SHARE, (line_e,), 0, None),
        ),
    )
    grad, ngrad_a = more[1], more[2]
    out_b, out_a, out_c, out_d, out_e = (more[3 + k] for k in (3, 7, 10, 12, 13))
    (grad_g, grad_l, first_g, first_l), columns = run_last(
        geo, grad, hid, (out_a, out_b, out_c, out_d, out_e, out_f, out_s),
        global_views.shape, local_views.shape,
    )
    shard = lax.axis_index("fsdp")

    def own_columns(parts, width):
        whole = jnp.concatenate(parts, axis=1)
        return lax.dynamic_slice_in_dim(whole, shard * width, width, 1)

    return (
        first_g, first_l, second_g, second_l, grad_g, grad_l,
        *columns[0:3],
        own_columns((ngrad_a, ngrad_b, ngrad_c), first_norms.shape[1]),
        *columns[3:7],
        own_columns((ngrad_d, ngrad_e, ngrad_f, ngrad_s), second_norms.shape[1]),
        pooled_std,
    )


def solution(mesh):
    views = P(("rep", "fsdp"), None, None, None)
    columns = P(None, "fsdp")
    return jax.shard_map(
        functools.partial(body, mesh.shape["rep"], mesh.shape["fsdp"]),
        mesh=mesh,
        in_specs=(views, views, P(("rep", "fsdp"))) + (columns,) * 9 + (views, views),
        out_specs=(views,) * 6 + (columns,) * 9 + (P(),),
        check_vma=False,
    )
```
